128 devices in a mesh: rows: 8 (over z, core), cols: 16 (over y, x).
Axes of the slice: x: 4, y: 4, z: 4, core: 2. Of those that a mesh axis runs over, the one named last changes fastest.
Arguments:
- model_dir: float32 [131072, 128], P('cols'), may hold values from -6 to 6
- sens_blocks: bfloat16 [8, 6144, 128, 128], P('rows', 'cols'), may hold values from -0.0625 to 0.0625
- blk_row: int32 [8, 6144], P('rows', 'cols'), may hold values from 0 to 31, as said below
- blk_col: int32 [8, 6144], P('rows', 'cols'), may hold values from 0 to 63, as said below
- blk_count: int32 [8, 16], P('rows', 'cols'), may hold values from 48 to 384, as said below
- send_order: int32 [16, 64], P('cols'), may hold values from 0 to 63, each once within a row
- neighbors: int32 [4, 131072], P(None, 'cols'), may hold values from 0 to 131071, as said below
- face_weight: float32 [4, 131072], P(None, 'cols'), may hold values from 0.05 to 0.5
Outputs:
- data_image: float32 [32768, 128], P('rows')
- normal_product: float32 [131072, 128], P('cols')
The draws below stay inside these ranges and needn't reach their ends.
Inputs may be any that keep to these rules, and one draw needn't show every extreme that they name: Within one device's 384 slots the pairs (blk_row, blk_col) are all different. `blk_col`: paired with blk_row as stated there. The live slots of a device are its first blk_count slots; some device has all 384 live. `send_order`: each row is a permutation. `neighbors`: every neighbour lies within 64 of the cell's own number.
All inputs are finite; a program needn't handle non-finite values.
Results may differ from the reference program's by a relative error of at most 0.0029.
Values may be sent and summed in bfloat16 or wider, within the bound.
A program may use at most 192 MiB of HBM per device.

```python
import math
import jax
import jax.numpy as jnp
from jax import lax

BLK = 128
NV = 128
RB_DEV = 32
NB_DEV = 64
KB = 384
RIM = 64
PER = 4
CB = 1024
NCELL = 131072
ND = 32768
N_ROWS = 8
N_COLS = 16


def block_pairs(key):
    key_list = jax.random.split(jax.random.fold_in(key, 7), N_ROWS * N_COLS)

    def pick_one(subkey):
        return jax.random.permutation(subkey, RB_DEV * NB_DEV)[:KB]
    chosen = jax.vmap(pick_one)(key_list)
    return chosen.reshape(N_ROWS, N_COLS * KB).astype(jnp.int32)


def draw_blk_row(key, part):
    return block_pairs(key) // NB_DEV


def draw_blk_col(key, part):
    return block_pairs(key) % NB_DEV


def draw_blk_count(key, part):
    lowest = KB // 8
    first_draw = jax.random.randint(jax.random.fold_in(key, 3), (N_ROWS * N_COLS,), 0, KB + 1)
    second_draw = jax.random.randint(jax.random.fold_in(key, 4), (N_ROWS * N_COLS,), 0, KB + 1)
    counts = lowest + (KB - lowest) * first_draw * second_draw // (KB * KB)
    busiest = jax.random.randint(jax.random.fold_in(key, 5), (), 0, N_ROWS * N_COLS)
    counts = jnp.where(jnp.arange(N_ROWS * N_COLS) == busiest, KB, counts)
    return counts.reshape(N_ROWS, N_COLS).astype(jnp.int32)


def draw_neighbors(key, part):
    offsets = jax.random.randint(jax.random.fold_in(key, 9), (4, NCELL), -RIM, RIM + 1)
    own_index = jnp.arange(NCELL, dtype=jnp.int32)[None, :]
    return jnp.clip(own_index + offsets, 0, NCELL - 1).astype(jnp.int32)


def block_scale(rng, dims, pieces, least, largest):
    def one(axis_at, parts):
        heights = jax.random.uniform(jax.random.fold_in(jax.random.fold_in(rng, 6), axis_at), (parts,), jnp.float32, least / len(pieces), largest / len(pieces))
        return jnp.repeat(jnp.exp(heights), dims[axis_at] // parts).reshape((-1,) + (1,) * (len(dims) - axis_at - 1))

    level = one(*pieces[0])
    for cut in pieces[1:]:
        level = level * one(*cut)
    return level


def normal_values(rng, extent, spread, limit, cuts=(), kind=jnp.bfloat16):
    entries = spread * jax.random.normal(rng, extent, jnp.float32)
    if cuts:
        entries = entries * block_scale(rng, extent, cuts, -0.22, 0.18)
    return jnp.clip(entries, -limit, limit).astype(kind)


def setup_inputs(seed: int = 0) -> dict:
    arg_keys = jax.random.split(jax.random.key(seed), 9)
    return {
        "model_dir": normal_values(arg_keys[0], (NCELL, NV), 1.0, 6.0, ((0, 16),), jnp.float32),
        "sens_blocks": normal_values(arg_keys[1], (N_ROWS, N_COLS * KB, BLK, BLK), (BLK * KB * N_COLS // (3 * RB_DEV)) ** -0.5, 0.0625, ((0, 8), (1, 16))),
        "blk_row": draw_blk_row(jax.random.fold_in(arg_keys[8], 71), 0),
        "blk_col": draw_blk_col(jax.random.fold_in(arg_keys[8], 71), 0),
        "blk_count": draw_blk_count(jax.random.fold_in(arg_keys[8], 71), 0),
        "send_order": jax.vmap(lambda own: jax.random.permutation(own, NB_DEV))(jax.random.split(arg_keys[5], N_COLS)).reshape((N_COLS, NB_DEV)).astype(jnp.int32),
        "neighbors": draw_neighbors(jax.random.fold_in(arg_keys[8], 71), 0),
        "face_weight": jnp.clip(jnp.exp(math.log(0.5) - 2.3025851 * jax.random.uniform(arg_keys[7], (4, NCELL), jnp.float32) ** block_scale(arg_keys[7], (4, NCELL), ((1, 16),), -0.2, 0.2)), 0.05, 0.5),
    }


def haar_matrix(order_n):
    matrix = jnp.ones((1, 1), jnp.float32)
    factor = 1.0 / math.sqrt(2.0)
    while matrix.shape[0] < order_n:
        length = matrix.shape[0]
        upper_half = jnp.kron(matrix, jnp.array([[1.0, 1.0]], jnp.float32))
        lower_half = jnp.kron(jnp.eye(length, dtype=jnp.float32), jnp.array([[1.0, -1.0]], jnp.float32))
        matrix = jnp.concatenate([upper_half, lower_half], axis=0) * factor
    return matrix

def reference(model_dir, sens_blocks, blk_row, blk_col, blk_count, send_order, neighbors, face_weight):
    highest = lax.Precision.HIGHEST
    haar_basis = jnp.asarray(haar_matrix(BLK), jnp.float32)
    cell_blocks = model_dir.reshape(N_COLS, NB_DEV, BLK, NV)
    coeffs = jnp.einsum('ij,sbjn->sbin', haar_basis, cell_blocks, precision=highest).astype(jnp.bfloat16)
    ordered = jnp.take_along_axis(coeffs, send_order[:, :, None, None], axis=1)
    wavelet = ordered.reshape(N_COLS, N_COLS, PER, BLK, NV).transpose(1, 0, 2, 3, 4).reshape(CB, BLK, NV)
    slot_index = jnp.arange(KB).astype(jnp.int32)
    group_index = jnp.arange(N_COLS).astype(jnp.int32)
    adjoint_wave = jnp.zeros((CB, BLK, NV), jnp.float32)
    image_rows = []
    for row_group in range(N_ROWS):
        group_sens = sens_blocks[row_group]
        group_rows = blk_row[row_group]
        group_cols = blk_col[row_group]
        group_count = blk_count[row_group]

        def lists_of(col_group):
            first_slot = (col_group * KB).astype(jnp.int32)
            blocks_here = lax.dynamic_slice_in_dim(group_sens, first_slot, KB, 0).astype(jnp.float32)
            rows_here = lax.dynamic_slice_in_dim(group_rows, first_slot, KB, 0)
            cols_here = lax.dynamic_slice_in_dim(group_cols, first_slot, KB, 0)
            live_slot = slot_index < group_count[col_group]
            return (blocks_here, rows_here, cols_here, live_slot)

        def forward(col_group):
            blocks_here, rows_here, cols_here, live_slot = lists_of(col_group)
            picked = wavelet[cols_here + col_group * NB_DEV].astype(jnp.float32)
            terms = jnp.einsum('kij,kjn->kin', blocks_here, picked)
            terms = jnp.where(live_slot[:, None, None], terms, 0.0)
            return jax.ops.segment_sum(terms, rows_here, num_segments=RB_DEV)
        image_group = lax.optimization_barrier(jnp.sum(lax.map(forward, group_index), axis=0))
        image_half = image_group.astype(jnp.bfloat16)

        def adjoint(col_group):
            blocks_here, rows_here, cols_here, live_slot = lists_of(col_group)
            chosen = image_half[rows_here].astype(jnp.float32)
            terms = jnp.einsum('kij,kin->kjn', blocks_here, chosen)
            terms = jnp.where(live_slot[:, None, None], terms, 0.0)
            return jax.ops.segment_sum(terms, cols_here, num_segments=NB_DEV)
        adjoint_parts = lax.map(adjoint, group_index)
        adjoint_wave = adjoint_wave + adjoint_parts.reshape(CB, BLK, NV)
        image_rows.append(image_group)
    data_image = jnp.concatenate(image_rows, axis=0).reshape(ND, NV)
    by_source = adjoint_wave.reshape(N_COLS, N_COLS, PER, BLK, NV).transpose(1, 0, 2, 3, 4).reshape(N_COLS, NB_DEV, BLK, NV)
    inverse = jnp.argsort(send_order, axis=1).astype(jnp.int32)
    cell_side = jnp.take_along_axis(by_source, inverse[:, :, None, None], axis=1)
    adjoint_cells = jnp.einsum('ji,sbjn->sbin', haar_basis, cell_side, precision=highest).reshape(NCELL, NV)
    beside_all = model_dir[neighbors]
    smooth_term = lax.optimization_barrier(jnp.sum(face_weight[:, :, None] * (model_dir[None, :, :] - beside_all), axis=0))
    normal_product = adjoint_cells + smooth_term
    return (data_image, normal_product)
```

```python
import math

import jax
import jax.numpy as jnp
import numpy as np
from jax import lax
from jax.experimental import pallas as pl
from jax.experimental.pallas import tpu as pltpu
from jax.sharding import PartitionSpec as P

BLK = 128
HALF = 64
RIM = 64
NROWS = 8
NCOLS = 16
NZ = 4
ROW_BLOCKS = 32
COL_BLOCKS = 64
SLOTS = 384
CHUNK = 32
UNROLL = 4
VMEM_LIMIT = 56 << 20
MESH = pl.DeviceIdType.MESH
F32 = jnp.float32
BF16 = jnp.bfloat16


def haar_parts():
    matrix = np.ones((1, 1))
    while matrix.shape[0] < BLK:
        length = matrix.shape[0]
        upper = np.kron(matrix, np.array([[1.0, 1.0]]))
        lower = np.kron(np.eye(length), np.array([[1.0, -1.0]]))
        matrix = np.concatenate([upper, lower], axis=0) / math.sqrt(2.0)
    scale = np.abs(matrix).max(axis=1)
    signs = np.round(matrix / scale[:, None])
    return signs, scale


SIGNS, SCALE = haar_parts()


def split(value):
    high = value.astype(BF16)
    low = (value - high.astype(F32)).astype(BF16)
    return high, low


def dot(a, b):
    return jnp.dot(a, b, preferred_element_type=F32)


def remote(src, dst, send_sem, recv_sem, device):
    return pltpu.make_async_remote_copy(
        src_ref=src,
        dst_ref=dst,
        send_sem=send_sem,
        recv_sem=recv_sem,
        device_id=device,
        device_id_type=MESH,
    )


def place():
    row = lax.axis_index("rows")
    col = lax.axis_index("cols")
    return row, col, lax.div(row, 2), lax.rem(row, 2)


def z_device(z, step, core, col):
    return (lax.rem(z + step, NZ) * 2 + core, col)


def greet(devices, loop_devices=None):
    barrier = pltpu.get_barrier_semaphore()
    for device in devices:
        pl.semaphore_signal(barrier, inc=1, device_id=device, device_id_type=MESH)
    count = len(devices)
    if loop_devices is not None:
        row, col = loop_devices

        def signal(i, carry):
            pl.semaphore_signal(
                barrier,
                inc=1,
                device_id=(row, lax.rem(col + i, NCOLS)),
                device_id_type=MESH,
            )
            return carry

        lax.fori_loop(1, NCOLS, signal, 0)
        count += NCOLS - 1
    pl.semaphore_wait(barrier, count)


def spread_copy(stage, out, sems, where, i):
    row, col, z, core = where
    target = lax.rem(col + i, NCOLS)
    return remote(
        stage.at[target],
        out.at[z, col, pl.ds(core * HALF, HALF)],
        sems["a_send"].at[i],
        sems["a_recv"].at[col],
        (row, target),
    )


def gather_rows(stage, out, sems, where):
    row, col, z, core = where
    own_rows = pl.ds(core * HALF, HALF)
    plus, minus = z_device(z, 1, core, col), z_device(z, NZ - 1, core, col)
    partner = (z * 2 + 1 - core, col)
    z_before, z_after, z_far = lax.rem(z + 3, NZ), lax.rem(z + 1, NZ), lax.rem(z + 2, NZ)
    group = NCOLS // 2
    sends = []

    def piece(q, p):
        return out.at[q, pl.ds(p * group, group), own_rows]

    def send(q, p, device, recv_sem):
        copy = remote(piece(q, p), piece(q, p), sems["g_send"].at[len(sends)], recv_sem, device)
        copy.start()
        sends.append(copy)

    def arrived(q, p, recv_sem, rows=None):
        ref = piece(q, p) if rows is None else out.at[q, pl.ds(p * group, group), rows]
        remote(ref, ref, sems["g_send"].at[0], recv_sem, partner).wait_recv()

    for p in range(2):

        def wait_part(s, carry):
            @pl.when(s != col)
            def _():
                ref = out.at[z, s, own_rows]
                remote(ref, ref, sems["a_send"].at[0], sems["a_recv"].at[s], partner).wait_recv()

            return carry

        lax.fori_loop(p * group, (p + 1) * group, wait_part, 0)
        send(z, p, plus, sems["minus"].at[p])
        send(z, p, minus, sems["plus"].at[p])
        send(z, p, partner, sems["pair"].at[0, p])
    arrived(z_before, 0, sems["minus"].at[0])
    send(z_before, 0, plus, sems["far"].at[0])
    send(z_before, 0, partner, sems["pair"].at[1, 0])
    arrived(z_after, 1, sems["plus"].at[1])
    send(z_after, 1, minus, sems["far"].at[1])
    send(z_after, 1, partner, sems["pair"].at[2, 1])
    arrived(z_after, 0, sems["plus"].at[0])
    send(z_after, 0, partner, sems["pair"].at[2, 0])
    arrived(z_before, 1, sems["minus"].at[1])
    send(z_before, 1, partner, sems["pair"].at[1, 1])
    for p in range(2):
        arrived(z_far, p, sems["far"].at[p])
        send(z_far, p, partner, sems["pair"].at[3, p])
    other_rows = pl.ds((1 - core) * HALF, HALF)
    for p in range(2):
        for slot, q in enumerate((z, z_before, z_after, z_far)):
            arrived(q, p, sems["pair"].at[slot, p], other_rows)

    def finish(i, carry):
        spread_copy(stage, out, sems, where, i).wait_send()
        return carry

    lax.fori_loop(1, NCOLS, finish, 0)
    for copy in sends:
        copy.wait_send()


EXCHANGE_SEMS = [
    pltpu.SemaphoreType.DMA((NCOLS,)),
    pltpu.SemaphoreType.DMA((NCOLS,)),
    pltpu.SemaphoreType.DMA((14,)),
    pltpu.SemaphoreType.DMA((2,)),
    pltpu.SemaphoreType.DMA((2,)),
    pltpu.SemaphoreType.DMA((2,)),
    pltpu.SemaphoreType.DMA((4, 2)),
]
EXCHANGE_NAMES = ("a_send", "a_recv", "g_send", "minus", "plus", "far", "pair")


def analyse_kernel(order, model, signs, scale, wavelet, halo, stage, halo_sems, *sem_refs):
    sems = dict(zip(EXCHANGE_NAMES, sem_refs))
    where = place()
    row, col, z, core = where
    greet(
        [z_device(z, 1, core, col), z_device(z, 3, core, col), (z * 2 + 1 - core, col)],
        (row, col),
    )
    below, above = lax.rem(col + NCOLS - 1, NCOLS), lax.rem(col + 1, NCOLS)
    up = remote(
        model.at[COL_BLOCKS - 1, pl.ds(BLK - RIM, RIM)],
        halo.at[0],
        halo_sems.at[0],
        halo_sems.at[2],
        (row, above),
    )
    down = remote(
        model.at[0, pl.ds(0, RIM)],
        halo.at[1],
        halo_sems.at[1],
        halo_sems.at[3],
        (row, below),
    )
    up.start()
    down.start()
    sign_rows = signs[pl.ds(core * HALF, HALF), :]
    sign_pair = jnp.concatenate([sign_rows, sign_rows], axis=1)
    row_scale = scale[pl.ds(core * HALF, HALF), :]

    def coefficients(target):
        high, low = split(model[order[target * 4 + z]])
        product = dot(sign_pair, jnp.concatenate([high, low], axis=0))
        return (product * row_scale).astype(BF16)

    def spread(i, carry):
        target = lax.rem(col + i, NCOLS)
        stage[target] = coefficients(target)
        spread_copy(stage, wavelet, sems, where, i).start()
        return carry

    lax.fori_loop(1, NCOLS, spread, 0)
    wavelet[z, col, pl.ds(core * HALF, HALF), :] = coefficients(col)
    gather_rows(stage, wavelet, sems, where)
    up.wait()
    down.wait()


def analyse(order, model_dir):
    model = model_dir.reshape(COL_BLOCKS, BLK, BLK)
    vmem = pl.BlockSpec(memory_space=pltpu.VMEM)
    return pl.pallas_call(
        analyse_kernel,
        out_shape=(
            jax.ShapeDtypeStruct((4, NCOLS, BLK, BLK), BF16),
            jax.ShapeDtypeStruct((2, RIM, BLK), F32),
        ),
        in_specs=[pl.BlockSpec(memory_space=pltpu.SMEM), vmem, vmem, vmem],
        out_specs=(vmem, vmem),
        scratch_shapes=[
            pltpu.VMEM((NCOLS, HALF, BLK), BF16),
            pltpu.SemaphoreType.DMA((4,)),
            *EXCHANGE_SEMS,
        ],
        compiler_params=pltpu.CompilerParams(
            collective_id=0, has_side_effects=True, vmem_limit_bytes=VMEM_LIMIT
        ),
        name="analyse",
    )(
        order,
        model,
        jnp.asarray(SIGNS, BF16),
        jnp.asarray(np.broadcast_to(SCALE[:, None], (BLK, BLK)), F32),
    )


def live_slots(count, step, add):
    live = jnp.clip(count[0] - step * CHUNK, 0, CHUNK)
    groups = live // UNROLL

    def group(g, carry):
        add(g * UNROLL, UNROLL)
        return carry

    def single(k, carry):
        add(k, 1)
        return carry

    lax.fori_loop(0, groups, group, 0)
    lax.fori_loop(groups * UNROLL, live, single, 0)


def forward_kernel(count, rows, cols, sens, wavelet, image):
    step = pl.program_id(0)

    @pl.when(step == 0)
    def _():
        image[...] = jnp.zeros_like(image)

    def add(first, width):
        terms = []
        for u in range(width):
            at = cols[step * CHUNK + first + u]
            terms.append(dot(sens[0, first + u], wavelet[at & 3, at >> 2]))
        for u in range(width):
            image[rows[step * CHUNK + first + u]] += terms[u]

    live_slots(count, step, add)


def sens_spec():
    def index(i, count, rows, cols):
        return 0, jnp.minimum(i, (count[0] - 1) // CHUNK), 0, 0

    return pl.BlockSpec((1, CHUNK, BLK, BLK), index)


def whole(*shape):
    return pl.BlockSpec(shape, lambda i, *refs: (0,) * len(shape))


def forward(count, rows, cols, sens, wavelet):
    return pl.pallas_call(
        forward_kernel,
        out_shape=jax.ShapeDtypeStruct((ROW_BLOCKS, BLK, BLK), F32),
        grid_spec=pltpu.PrefetchScalarGridSpec(
            num_scalar_prefetch=3,
            grid=(SLOTS // CHUNK,),
            in_specs=[sens_spec(), whole(4, NCOLS, BLK, BLK)],
            out_specs=whole(ROW_BLOCKS, BLK, BLK),
        ),
        compiler_params=pltpu.CompilerParams(vmem_limit_bytes=VMEM_LIMIT),
        name="forward",
    )(count, rows, cols, sens, wavelet)


class Ring:
    def __init__(self, me, plus, minus, send, recv):
        self.me, self.plus, self.minus = me, plus, minus
        self.send, self.recv = send, recv
        self.started = []

    def at(self, step):
        return lax.rem(self.me + step, 4)

    def copy(self, src, dst, device, slot):
        copy = remote(src, dst, self.send.at[slot], self.recv.at[slot], device)
        copy.start()
        self.started.append(copy)

    def arrived(self, ref, slot):
        remote(ref, ref, self.send.at[slot], self.recv.at[slot], self.plus).wait_recv()

    def drain(self):
        for copy in self.started:
            copy.wait_send()
        self.started = []


class Reduce:
    def __init__(self, ring, data, base, chunk, relay, landed):
        self.ring, self.data, self.base, self.chunk = ring, data, base, chunk
        self.half = chunk // 2
        self.relay, self.landed = relay, landed

    def rows(self, step, h):
        start = self.base + self.ring.at(step) * self.chunk + h * self.half
        return pl.ds(pl.multiple_of(start, self.half), self.half)

    def relay_at(self, side):
        return self.relay.at[side, pl.ds(0, self.half)]

    def landed_at(self, side, h):
        return self.landed.at[side, pl.ds(h * self.half, self.half)]

    def begin(self):
        ring, data = self.ring, self.data
        ring.copy(data.at[self.rows(2, 0)], self.relay_at(0), ring.plus, 0)
        ring.copy(data.at[self.rows(2, 1)], self.relay_at(1), ring.minus, 1)
        ring.copy(data.at[self.rows(1, 1)], self.landed_at(0, 1), ring.plus, 2)
        ring.copy(data.at[self.rows(3, 0)], self.landed_at(1, 0), ring.minus, 3)

    def pass_on(self):
        ring, data = self.ring, self.data
        ring.arrived(self.relay_at(0), 0)
        data[self.rows(1, 0), :] += self.relay[0, : self.half]
        ring.copy(data.at[self.rows(1, 0)], self.landed_at(0, 0), ring.plus, 4)
        ring.arrived(self.relay_at(1), 1)
        data[self.rows(3, 1), :] += self.relay[1, : self.half]
        ring.copy(data.at[self.rows(3, 1)], self.landed_at(1, 1), ring.minus, 5)

    def finish(self):
        ring, data = self.ring, self.data
        ring.arrived(self.landed_at(0, 1), 2)
        ring.arrived(self.landed_at(1, 0), 3)
        ring.arrived(self.landed_at(0, 0), 4)
        ring.arrived(self.landed_at(1, 1), 5)
        for h in range(2):
            part = pl.ds(h * self.half, self.half)
            data[self.rows(0, h), :] += self.landed[0, part, :] + self.landed[1, part, :]


class Gather:
    def __init__(self, ring, data, base, chunk):
        self.ring, self.data, self.base, self.chunk = ring, data, base, chunk

    def rows(self, step, h=None):
        start = self.base + self.ring.at(step) * self.chunk
        if h is None:
            return self.data.at[pl.ds(pl.multiple_of(start, self.chunk), self.chunk)]
        half = self.chunk // 2
        return self.data.at[pl.ds(pl.multiple_of(start + h * half, half), half)]

    def begin(self):
        ring = self.ring
        ring.copy(self.rows(0), self.rows(0), ring.plus, 0)
        ring.copy(self.rows(0), self.rows(0), ring.minus, 1)

    def pass_on(self):
        ring = self.ring
        ring.arrived(self.rows(3), 0)
        ring.copy(self.rows(3, 0), self.rows(3, 0), ring.plus, 2)
        ring.arrived(self.rows(1), 1)
        ring.copy(self.rows(1, 1), self.rows(1, 1), ring.minus, 3)

    def finish(self):
        ring = self.ring
        ring.arrived(self.rows(2, 0), 2)
        ring.arrived(self.rows(2, 1), 3)


HALF_ROWS = ROW_BLOCKS * BLK // 2
BIG = HALF_ROWS // 4
SMALL = BIG // 4


def combine_kernel(partial, image, data, big_relay, big_landed, small_relay, small_landed, send, recv):
    row, col, _, _ = place()
    y, x = lax.div(col, 4), lax.rem(col, 4)
    x_plus, x_minus = (row, y * 4 + lax.rem(x + 1, 4)), (row, y * 4 + lax.rem(x + 3, 4))
    y_plus, y_minus = (row, lax.rem(y + 1, 4) * 4 + x), (row, lax.rem(y + 3, 4) * 4 + x)
    greet([x_plus, x_minus, y_plus, y_minus])

    def ring(axis, slot):
        sems = send.at[slot], recv.at[slot]
        return Ring(x, x_plus, x_minus, *sems) if axis == 0 else Ring(y, y_plus, y_minus, *sems)

    def both(stages):
        for stage in stages:
            stage.begin()
        for stage in stages:
            stage.pass_on()
        for stage in stages:
            stage.finish()

    bases = [0, HALF_ROWS]
    inner = [x * BIG, HALF_ROWS + y * BIG]
    rings = [ring(a, a) for a in range(2)]
    wide = [Reduce(rings[a], partial, bases[a], BIG, big_relay.at[a], big_landed.at[a]) for a in range(2)]
    both(wide)
    cross = [ring(1 - a, 2 + a) for a in range(2)]
    narrow = [
        Reduce(cross[a], partial, inner[a], SMALL, small_relay.at[a], small_landed.at[a])
        for a in range(2)
    ]
    both(narrow)
    for a, other in ((0, y), (1, x)):
        own = pl.ds(pl.multiple_of(inner[a] + other * SMALL, SMALL), SMALL)
        image[own, :] = partial[own, :].astype(BF16)
    back = [ring(1 - a, 4 + a) for a in range(2)]
    both([Gather(back[a], image, inner[a], SMALL) for a in range(2)])
    last = [ring(a, 6 + a) for a in range(2)]
    both([Gather(last[a], image, bases[a], BIG) for a in range(2)])
    for group in (rings, cross, back, last):
        for one in group:
            one.drain()


def combine(partial):
    vmem = pl.BlockSpec(memory_space=pltpu.VMEM)
    rows = ROW_BLOCKS * BLK

    def kernel(partial_ref, image_ref, data, *rest):
        copy = pltpu.make_async_copy(partial_ref, data, rest[-1])
        copy.start()
        copy.wait()
        combine_kernel(data, image_ref, data, *rest[:-1])

    return pl.pallas_call(
        kernel,
        out_shape=jax.ShapeDtypeStruct((rows, BLK), BF16),
        in_specs=[pl.BlockSpec(memory_space=pl.ANY)],
        out_specs=vmem,
        scratch_shapes=[
            pltpu.VMEM((rows, BLK), F32),
            pltpu.VMEM((2, 2, BIG // 2, BLK), F32),
            pltpu.VMEM((2, 2, BIG, BLK), F32),
            pltpu.VMEM((2, 2, SMALL // 2, BLK), F32),
            pltpu.VMEM((2, 2, SMALL, BLK), F32),
            pltpu.SemaphoreType.DMA((8, 6)),
            pltpu.SemaphoreType.DMA((8, 6)),
            pltpu.SemaphoreType.DMA,
        ],
        compiler_params=pltpu.CompilerParams(
            collective_id=1, has_side_effects=True, vmem_limit_bytes=VMEM_LIMIT
        ),
        name="combine",
    )(partial.reshape(rows, BLK))


def adjoint_kernel(count, rows, cols, sens, image, data_image, adjoint, flipped):
    step = pl.program_id(0)

    @pl.when(step == 0)
    def _():
        adjoint[...] = jnp.zeros_like(adjoint)

        def flip(b, carry):
            block = image[b].astype(F32)
            data_image[b] = block
            flipped[b] = block.T.astype(BF16)
            return carry

        lax.fori_loop(0, ROW_BLOCKS, flip, 0)

    def add(first, width):
        terms = []
        for u in range(width):
            at = rows[step * CHUNK + first + u]
            terms.append(dot(flipped[at], sens[0, first + u]))
        for u in range(width):
            at = cols[step * CHUNK + first + u]
            adjoint[0, at & 3, at >> 2] += terms[u][:HALF]
            adjoint[1, at & 3, at >> 2] += terms[u][HALF:]

    live_slots(count, step, add)


def adjoin(count, rows, cols, sens, image):
    return pl.pallas_call(
        adjoint_kernel,
        out_shape=(
            jax.ShapeDtypeStruct((ROW_BLOCKS, BLK, BLK), F32),
            jax.ShapeDtypeStruct((2, 4, NCOLS, HALF, BLK), F32),
        ),
        grid_spec=pltpu.PrefetchScalarGridSpec(
            num_scalar_prefetch=3,
            grid=(SLOTS // CHUNK,),
            in_specs=[sens_spec(), whole(ROW_BLOCKS, BLK, BLK)],
            out_specs=(whole(ROW_BLOCKS, BLK, BLK), whole(2, 4, NCOLS, HALF, BLK)),
            scratch_shapes=[pltpu.VMEM((ROW_BLOCKS, BLK, BLK), BF16)],
        ),
        compiler_params=pltpu.CompilerParams(vmem_limit_bytes=VMEM_LIMIT),
        name="adjoin",
    )(count, rows, cols, sens, image)


GROUP = NCOLS // 2


def return_kernel(partial, scale, out, stage, pair, relay_out, relay, landed, send, recv, *sem_refs):
    sems = dict(zip(EXCHANGE_NAMES, sem_refs))
    where = place()
    row, col, z, core = where
    plus, minus = z_device(z, 1, core, col), z_device(z, NZ - 1, core, col)
    partner = (z * 2 + 1 - core, col)
    greet([plus, minus, partner], (row, col))
    ring = Ring(z, plus, minus, send, recv)
    for slot, step in ((6, 2), (7, 1), (8, 3), (9, 0)):
        ring.copy(partial.at[1 - core, ring.at(step)], pair.at[ring.at(step)], partner, slot)

    def total(step, h):
        group = pl.ds(h * GROUP, GROUP)
        return partial[core, ring.at(step), group] + pair[ring.at(step), group]

    def paired(step, slot):
        ring.arrived(pair.at[ring.at(step)], slot)

    def ship(value, slot, dst, device, sem):
        relay_out[slot] = value.astype(BF16)
        ring.copy(relay_out.at[slot], dst, device, sem)

    paired(2, 6)
    ship(total(2, 0), 0, relay.at[0], plus, 0)
    ship(total(2, 1), 1, relay.at[1], minus, 1)
    paired(1, 7)
    ship(total(1, 1), 3, landed.at[0, 1], plus, 2)
    paired(3, 8)
    ship(total(3, 0), 4, landed.at[1, 0], minus, 3)
    ring.arrived(relay.at[0], 0)
    ship(total(1, 0) + relay[0].astype(F32), 2, landed.at[0, 0], plus, 4)
    ring.arrived(relay.at[1], 1)
    ship(total(3, 1) + relay[1].astype(F32), 5, landed.at[1, 1], minus, 5)
    paired(0, 9)
    ring.arrived(landed.at[0, 1], 2)
    ring.arrived(landed.at[1, 0], 3)
    ring.arrived(landed.at[0, 0], 4)
    ring.arrived(landed.at[1, 1], 5)
    lane_scale = scale[0:1, :].reshape(1, 1, BLK)
    for h in range(2):
        value = total(0, h) + landed[0, h].astype(F32) + landed[1, h].astype(F32)
        stage[pl.ds(h * GROUP, GROUP)] = (value * lane_scale).astype(BF16)

    def spread(i, carry):
        spread_copy(stage, out, sems, where, i).start()
        return carry

    lax.fori_loop(1, NCOLS, spread, 0)
    out[z, col, pl.ds(core * HALF, HALF), :] = stage[col]
    gather_rows(stage, out, sems, where)
    ring.drain()


def give_back(partial):
    vmem = pl.BlockSpec(memory_space=pltpu.VMEM)
    return pl.pallas_call(
        return_kernel,
        out_shape=jax.ShapeDtypeStruct((4, NCOLS, BLK, BLK), BF16),
        in_specs=[vmem, vmem],
        out_specs=vmem,
        scratch_shapes=[
            pltpu.VMEM((NCOLS, HALF, BLK), BF16),
            pltpu.VMEM((4, NCOLS, HALF, BLK), F32),
            pltpu.VMEM((6, GROUP, HALF, BLK), BF16),
            pltpu.VMEM((2, GROUP, HALF, BLK), BF16),
            pltpu.VMEM((2, 2, GROUP, HALF, BLK), BF16),
            pltpu.SemaphoreType.DMA((10,)),
            pltpu.SemaphoreType.DMA((10,)),
            *EXCHANGE_SEMS,
        ],
        compiler_params=pltpu.CompilerParams(
            collective_id=2, has_side_effects=True, vmem_limit_bytes=VMEM_LIMIT
        ),
        name="give_back",
    )(partial, jnp.asarray(np.broadcast_to(SCALE[None, :], (8, BLK)), F32))


def smooth_tile(extended, neighbors, weights, tile, first_cell):
    at = pl.ds(pl.multiple_of(tile * BLK, BLK), BLK)
    local = (neighbors[:, at] - (first_cell + tile * BLK - RIM)).astype(F32)
    table = jnp.concatenate([local, weights[:, at]], axis=0).T
    span = lax.broadcasted_iota(jnp.int32, (BLK, 2 * BLK), 1).astype(F32)
    mix = jnp.zeros((BLK, 2 * BLK), F32)
    for face in range(4):
        mix += jnp.where(table[:, face : face + 1] == span, table[:, 4 + face : 5 + face], 0.0)
    mix_high, mix_low = split(mix)
    near_high, near_low = split(extended[pl.ds(pl.multiple_of(tile * BLK, BLK), 2 * BLK), :])
    mixed = dot(mix_high, near_high) + dot(mix_low, near_high) + dot(mix_high, near_low)
    total = table[:, 4:5] + table[:, 5:6] + table[:, 6:7] + table[:, 7:8]
    center = extended[pl.ds(pl.multiple_of(tile * BLK + RIM, RIM), BLK), :]
    return total * center - mixed


def smooth_kernel(model, halo, neighbors, weights, out, extended, sems):
    first_cell = lax.axis_index("cols") * (COL_BLOCKS * BLK)
    cells = COL_BLOCKS * BLK
    copies = [
        pltpu.make_async_copy(model, extended.at[pl.ds(RIM, cells)], sems.at[0]),
        pltpu.make_async_copy(halo.at[0], extended.at[pl.ds(0, RIM)], sems.at[1]),
        pltpu.make_async_copy(halo.at[1], extended.at[pl.ds(RIM + cells, RIM)], sems.at[2]),
    ]
    for copy in copies:
        copy.start()
    for copy in copies:
        copy.wait()

    def tile(t, carry):
        out[pl.ds(pl.multiple_of(t * BLK, BLK), BLK), :] = smooth_tile(
            extended, neighbors, weights, t, first_cell
        )
        return carry

    lax.fori_loop(0, COL_BLOCKS, tile, 0)


def smooth(model, halo, neighbors, weights):
    vmem = pl.BlockSpec(memory_space=pltpu.VMEM)
    anywhere = pl.BlockSpec(memory_space=pl.ANY)
    return pl.pallas_call(
        smooth_kernel,
        out_shape=jax.ShapeDtypeStruct(model.shape, F32),
        in_specs=[anywhere, anywhere, vmem, vmem],
        out_specs=vmem,
        scratch_shapes=[
            pltpu.VMEM((model.shape[0] + 2 * RIM, BLK), F32),
            pltpu.SemaphoreType.DMA((3,)),
        ],
        compiler_params=pltpu.CompilerParams(vmem_limit_bytes=VMEM_LIMIT),
        name="smooth",
    )(model, halo, neighbors, weights)


TILES = 8


def synthesise_kernel(order, signs, returned, smooth_term, out, inverse):
    step = pl.program_id(0)

    @pl.when(step == 0)
    def _():
        def note(j, carry):
            inverse[order[j]] = j
            return carry

        lax.fori_loop(0, COL_BLOCKS, note, 0)

    for t in range(TILES):
        j = inverse[step * TILES + t]
        block = returned[j & 3, j >> 2]
        cells = lax.dot_general(
            signs[...], block, (((1,), (1,)), ((), ())), preferred_element_type=F32
        )
        at = slice(t * BLK, (t + 1) * BLK)
        out[at, :] = cells + smooth_term[at, :]


def synthesise(order, returned, smooth_term):
    block = pl.BlockSpec((TILES * BLK, BLK), lambda i, order: (i, 0))
    return pl.pallas_call(
        synthesise_kernel,
        out_shape=jax.ShapeDtypeStruct(smooth_term.shape, F32),
        grid_spec=pltpu.PrefetchScalarGridSpec(
            num_scalar_prefetch=1,
            grid=(COL_BLOCKS // TILES,),
            in_specs=[whole(BLK, BLK), whole(4, NCOLS, BLK, BLK), block],
            out_specs=block,
            scratch_shapes=[pltpu.SMEM((COL_BLOCKS,), jnp.int32)],
        ),
        compiler_params=pltpu.CompilerParams(vmem_limit_bytes=VMEM_LIMIT),
        name="synthesise",
    )(order, jnp.asarray(SIGNS.T, BF16), returned, smooth_term)


def local(model_dir, sens_blocks, blk_row, blk_col, blk_count, send_order, neighbors, face_weight):
    rows, cols = blk_row.reshape(-1), blk_col.reshape(-1)
    count, order = blk_count.reshape(-1), send_order.reshape(-1)
    wavelet, halo = analyse(order, model_dir)
    partial_image = forward(count, rows, cols, sens_blocks, wavelet)
    image_half = combine(partial_image).reshape(ROW_BLOCKS, BLK, BLK)
    data_image, partial_adjoint = adjoin(count, rows, cols, sens_blocks, image_half)
    returned = give_back(partial_adjoint)
    smooth_term = smooth(model_dir, halo, neighbors, face_weight)
    normal_product = synthesise(order, returned, smooth_term)
    return data_image.reshape(ROW_BLOCKS * BLK, BLK), normal_product


def solution(mesh):
    placed = (
        P("cols", None),
        P("rows", "cols", None, None),
        P("rows", "cols"),
        P("rows", "cols"),
        P("rows", "cols"),
        P("cols", None),
        P(None, "cols"),
        P(None, "cols"),
    )
    return jax.shard_map(
        local,
        mesh=mesh,
        in_specs=placed,
        out_specs=(P("rows", None), P("cols", None)),
        check_vma=False,
    )
```

```python
import math

import jax
import jax.numpy as jnp
import numpy as np
from jax import lax
from jax.experimental import pallas as pl
from jax.experimental.pallas import tpu as pltpu
from jax.sharding import PartitionSpec as P

BLK = 128
RIM = 64
NROWS = 8
NCOLS = 16
NZ = 4
ROW_BLOCKS = 32
COL_BLOCKS = 64
SLOTS = 384
CHUNK = 128
UNROLLS = (32, 4, 1)
VMEM_LIMIT = 56 << 20
MESH = pl.DeviceIdType.MESH
F32 = jnp.float32
BF16 = jnp.bfloat16


def haar_parts():
    matrix = np.ones((1, 1))
    while matrix.shape[0] < BLK:
        length = matrix.shape[0]
        upper = np.kron(matrix, np.array([[1.0, 1.0]]))
        lower = np.kron(np.eye(length), np.array([[1.0, -1.0]]))
        matrix = np.concatenate([upper, lower], axis=0) / math.sqrt(2.0)
    scale = np.abs(matrix).max(axis=1)
    signs = np.round(matrix / scale[:, None])
    return signs, scale


SIGNS, SCALE = haar_parts()


def split(value):
    high = value.astype(BF16)
    low = (value - high.astype(F32)).astype(BF16)
    return high, low


def dot(a, b):
    return jnp.dot(a, b, preferred_element_type=F32)


def remote(src, dst, send_sem, recv_sem, device):
    return pltpu.make_async_remote_copy(
        src_ref=src,
        dst_ref=dst,
        send_sem=send_sem,
        recv_sem=recv_sem,
        device_id=device,
        device_id_type=MESH,
    )


def place():
    row = lax.axis_index("rows")
    col = lax.axis_index("cols")
    return row, col, lax.div(row, 2), lax.rem(row, 2)


def z_device(z, step, core, col):
    return (lax.rem(z + step, NZ) * 2 + core, col)


def greet(devices, extra=None):
    barrier = pltpu.get_barrier_semaphore()
    for device in devices:
        pl.semaphore_signal(barrier, inc=1, device_id=device, device_id_type=MESH)
    count = len(devices)
    if extra is not None:
        first, device_of = extra

        def signal(i, carry):
            pl.semaphore_signal(barrier, inc=1, device_id=device_of(i), device_id_type=MESH)
            return carry

        lax.fori_loop(first, PARTS, signal, 0)
        count = count + PARTS - first
    pl.semaphore_wait(barrier, count)


PARTS = NCOLS // 2


class Exchange:
    def __init__(self, stage, out, sem_refs, where):
        self.stage, self.out = stage, out
        self.a_send, self.a_recv, self.g_send, self.minus, self.plus, self.far, self.pair = sem_refs
        self.row, self.col, self.z, self.core = where
        self.first = jnp.where(self.core == lax.rem(self.col, 2), 1, 0)
        self.sends = []

    def slot(self, i):
        return lax.rem(lax.div(self.col, 2) + i, PARTS)

    def device(self, i):
        return self.z * 2 + lax.rem(self.col, 2), self.slot(i) * 2 + self.core

    def arrivals(self, landing):
        return landing.at[lax.div(self.col, 2)]

    def copy(self, i, landing):
        return remote(
            self.stage.at[self.slot(i)],
            self.arrivals(landing),
            self.a_send.at[i],
            self.a_recv.at[lax.div(self.col, 2)],
            self.device(i),
        )

    def wait_part(self, m, landing):
        @pl.when(m * 2 + self.core != self.col)
        def _():
            ref = landing.at[m]
            remote(
                ref, ref, self.a_send.at[0], self.a_recv.at[m], self.device(1)
            ).wait_recv()

    def drain_parts(self, landing):
        def finish(i, carry):
            self.copy(i, landing).wait_send()
            return carry

        lax.fori_loop(self.first, PARTS, finish, 0)

    def piece(self, step, p, core=None):
        core = self.core if core is None else core
        size = PARTS // 2
        return self.out.at[lax.rem(self.z + step, NZ), core, pl.ds(p * size, size)]

    def send(self, step, p, device, recv_sem):
        piece = self.piece(step, p)
        copy = remote(piece, piece, self.g_send.at[len(self.sends)], recv_sem, device)
        copy.start()
        self.sends.append(copy)

    def arrived(self, step, p, recv_sem, core=None):
        piece = self.piece(step, p, core)
        remote(piece, piece, self.g_send.at[0], recv_sem, self.partner()).wait_recv()

    def partner(self):
        return self.z * 2 + 1 - self.core, self.col

    def neighbour(self, step):
        return z_device(self.z, step, self.core, self.col)

    def begin(self, p):
        self.send(0, p, self.neighbour(1), self.minus.at[p])
        self.send(0, p, self.neighbour(3), self.plus.at[p])
        self.send(0, p, self.partner(), self.pair.at[0, p])

    def finish(self):
        self.arrived(3, 0, self.minus.at[0])
        self.send(3, 0, self.neighbour(1), self.far.at[0])
        self.send(3, 0, self.partner(), self.pair.at[3, 0])
        self.arrived(1, 1, self.plus.at[1])
        self.send(1, 1, self.neighbour(3), self.far.at[1])
        self.send(1, 1, self.partner(), self.pair.at[1, 1])
        self.arrived(1, 0, self.plus.at[0])
        self.send(1, 0, self.partner(), self.pair.at[1, 0])
        self.arrived(3, 1, self.minus.at[1])
        self.send(3, 1, self.partner(), self.pair.at[3, 1])
        for p in range(2):
            self.arrived(2, p, self.far.at[p])
            self.send(2, p, self.partner(), self.pair.at[2, p])
        for p in range(2):
            for step in (0, 1, 3, 2):
                self.arrived(step, p, self.pair.at[step, p], 1 - self.core)
        for copy in self.sends:
            copy.wait_send()


EXCHANGE_SEMS = [
    pltpu.SemaphoreType.DMA((PARTS,)),
    pltpu.SemaphoreType.DMA((PARTS,)),
    pltpu.SemaphoreType.DMA((14,)),
    pltpu.SemaphoreType.DMA((2,)),
    pltpu.SemaphoreType.DMA((2,)),
    pltpu.SemaphoreType.DMA((2,)),
    pltpu.SemaphoreType.DMA((4, 2)),
]
CELLS = COL_BLOCKS * BLK


def cells_of(body, block):
    return jnp.concatenate([body[2 * block], body[2 * block + 1]], axis=0)


def tabulate(neighbors, weights, tables, first_cell):
    def tile(t, carry):
        at = pl.ds(pl.multiple_of(t * BLK, BLK), BLK)
        near = (neighbors[:, at] - (first_cell + t * BLK - RIM)).astype(F32)
        tables[t] = jnp.concatenate([near, weights[:, at]], axis=0)
        return carry

    lax.fori_loop(0, COL_BLOCKS, tile, 0)


def smooth_tile(body, rims, tables, tile):
    table = tables[tile].T
    span = lax.broadcasted_iota(jnp.int32, (BLK, 2 * BLK), 1).astype(F32)
    mix = jnp.zeros((BLK, 2 * BLK), F32)
    for face in range(4):
        mix += jnp.where(table[:, face : face + 1] == span, table[:, 4 + face : 5 + face], 0.0)
    mix_high, mix_low = split(mix)
    center = cells_of(body, tile)
    last = COL_BLOCKS - 1
    low = jnp.where(tile == 0, rims[0], body[jnp.maximum(2 * tile - 1, 0)])
    high = jnp.where(tile == last, rims[1], body[jnp.minimum(2 * tile + 2, 2 * last)])
    window = jnp.concatenate([low, center, high], axis=0)
    near_high, near_low = split(window)
    mixed = dot(mix_high, near_high) + dot(mix_low, near_high) + dot(mix_high, near_low)
    total = table[:, 4:5] + table[:, 5:6] + table[:, 6:7] + table[:, 7:8]
    return total * center - mixed


def analyse_kernel(
    order, model, neighbors, weights, signs, scale, wavelet, smooth, body, rims, tables, stage, sems, *sem_refs
):
    where = place()
    row, col, z, core = where
    fill = pltpu.make_async_copy(model, body, sems.at[4])
    fill.start()
    exchange = Exchange(stage, wavelet, sem_refs, where)
    below, above = (row, lax.rem(col + NCOLS - 1, NCOLS)), (row, lax.rem(col + 1, NCOLS))
    greet(
        [exchange.neighbour(1), exchange.neighbour(3), exchange.partner(), below, above],
        (exchange.first, exchange.device),
    )
    up = remote(
        model.at[2 * COL_BLOCKS - 1],
        rims.at[0],
        sems.at[0],
        sems.at[2],
        above,
    )
    down = remote(
        model.at[0],
        rims.at[1],
        sems.at[1],
        sems.at[3],
        below,
    )
    up.start()
    down.start()
    fill.wait()
    sign_pair = jnp.concatenate([signs[...], signs[...]], axis=1)
    landing = wavelet.at[z, core]
    target = wavelet.at[z, lax.rem(col, 2)]

    def block_of(m):
        return order[0, (m * 2 + core) * 4 + z]

    def coefficients(m):
        high, low = split(cells_of(body, block_of(m)))
        product = dot(sign_pair, jnp.concatenate([high, low], axis=0))
        return (product * scale[...]).astype(BF16)

    @pl.when(exchange.first == 1)
    def _():
        wavelet[z, core, lax.div(col, 2)] = coefficients(lax.div(col, 2))

    def spread(i, carry):
        stage[exchange.slot(i)] = coefficients(exchange.slot(i))
        exchange.copy(i, target).start()
        return carry

    lax.fori_loop(exchange.first, PARTS, spread, 0)
    tabulate(neighbors, weights, tables, col * CELLS)

    def smooth_one(m, carry):
        smooth[m] = smooth_tile(body, rims, tables, block_of(m))
        return carry

    up.wait_recv()
    down.wait_recv()
    lax.fori_loop(0, 3, smooth_one, 0)

    def wait_part(m, carry):
        exchange.wait_part(m, landing)
        return carry

    for p in range(2):
        lax.fori_loop(p * PARTS // 2, (p + 1) * PARTS // 2, wait_part, 0)
        exchange.begin(p)
    lax.fori_loop(3, PARTS, smooth_one, 0)
    exchange.finish()
    exchange.drain_parts(target)
    up.wait_send()
    down.wait_send()


def analyse(order, model, neighbors, weights):
    vmem = pl.BlockSpec(memory_space=pltpu.VMEM)
    return pl.pallas_call(
        analyse_kernel,
        out_shape=(
            jax.ShapeDtypeStruct((NZ, 2, PARTS, BLK, BLK), BF16),
            jax.ShapeDtypeStruct((PARTS, BLK, BLK), F32),
        ),
        in_specs=[
            pl.BlockSpec(memory_space=pltpu.SMEM),
            pl.BlockSpec(memory_space=pl.ANY),
            vmem,
            vmem,
            vmem,
            vmem,
        ],
        out_specs=(vmem, vmem),
        scratch_shapes=[
            pltpu.VMEM((2 * COL_BLOCKS, RIM, BLK), F32),
            pltpu.VMEM((2, RIM, BLK), F32),
            pltpu.VMEM((COL_BLOCKS, 8, BLK), F32),
            pltpu.VMEM((PARTS, BLK, BLK), BF16),
            pltpu.SemaphoreType.DMA((5,)),
            *EXCHANGE_SEMS,
        ],
        compiler_params=pltpu.CompilerParams(
            collective_id=0, has_side_effects=True, vmem_limit_bytes=VMEM_LIMIT
        ),
        name="analyse",
    )(
        order,
        model.reshape(2 * COL_BLOCKS, RIM, BLK),
        neighbors,
        weights,
        jnp.asarray(SIGNS, BF16),
        jnp.asarray(np.broadcast_to(SCALE[:, None], (BLK, BLK)), F32),
    )


def live_slots(count, step, add):
    live = jnp.clip(count[0, 0] - step * CHUNK, 0, CHUNK)
    done = 0
    for width in UNROLLS:

        def group(g, carry, width=width, done=done):
            add(done + g * width, width)
            return carry

        groups = (live - done) // width
        lax.fori_loop(0, groups, group, 0)
        done = done + groups * width


def forward_kernel(count, rows, cols, sens, wavelet, image):
    step = pl.program_id(0)

    @pl.when(step == 0)
    def _():
        image[...] = jnp.zeros_like(image)

    def add(first, width):
        terms = []
        for u in range(width):
            at = cols[0, step * CHUNK + first + u]
            terms.append(dot(sens[0, first + u], wavelet[at & 3, (at >> 2) & 1, at >> 3]))
        for u in range(width):
            image[rows[0, step * CHUNK + first + u]] += terms[u]

    live_slots(count, step, add)


def sens_spec():
    def index(i, count, rows, cols):
        return 0, jnp.minimum(i, (count[0, 0] - 1) // CHUNK), 0, 0

    return pl.BlockSpec((1, CHUNK, BLK, BLK), index)


def whole(*shape):
    return pl.BlockSpec(shape, lambda i, *refs: (0,) * len(shape))


def forward(count, rows, cols, sens, wavelet):
    return pl.pallas_call(
        forward_kernel,
        out_shape=jax.ShapeDtypeStruct((ROW_BLOCKS, BLK, BLK), F32),
        grid_spec=pltpu.PrefetchScalarGridSpec(
            num_scalar_prefetch=3,
            grid=(SLOTS // CHUNK,),
            in_specs=[sens_spec(), whole(NZ, 2, PARTS, BLK, BLK)],
            out_specs=whole(ROW_BLOCKS, BLK, BLK),
        ),
        compiler_params=pltpu.CompilerParams(vmem_limit_bytes=VMEM_LIMIT),
        name="forward",
    )(count, rows, cols, sens, wavelet)


class Ring:
    def __init__(self, me, plus, minus, send, recv):
        self.me, self.plus, self.minus = me, plus, minus
        self.send, self.recv = send, recv
        self.started = []

    def at(self, step):
        return lax.rem(self.me + step, 4)

    def copy(self, src, dst, device, slot):
        copy = remote(src, dst, self.send.at[slot], self.recv.at[slot], device)
        copy.start()
        self.started.append(copy)

    def arrived(self, ref, slot):
        remote(ref, ref, self.send.at[slot], self.recv.at[slot], self.plus).wait_recv()

    def drain(self):
        for copy in self.started:
            copy.wait_send()
        self.started = []


class Reduce:
    def __init__(self, ring, data, base, chunk, relay, landed):
        self.ring, self.data, self.base, self.chunk = ring, data, base, chunk
        self.half = chunk // 2
        self.relay, self.landed = relay, landed

    def rows(self, step, h):
        start = self.base + self.ring.at(step) * self.chunk + h * self.half
        return pl.ds(pl.multiple_of(start, self.half), self.half)

    def relay_at(self, side):
        return self.relay.at[side, pl.ds(0, self.half)]

    def landed_at(self, side, h):
        return self.landed.at[side, pl.ds(h * self.half, self.half)]

    def begin(self):
        ring, data = self.ring, self.data
        ring.copy(data.at[self.rows(2, 0)], self.relay_at(0), ring.plus, 0)
        ring.copy(data.at[self.rows(2, 1)], self.relay_at(1), ring.minus, 1)
        ring.copy(data.at[self.rows(1, 1)], self.landed_at(0, 1), ring.plus, 2)
        ring.copy(data.at[self.rows(3, 0)], self.landed_at(1, 0), ring.minus, 3)

    def pass_on(self):
        ring, data = self.ring, self.data
        ring.arrived(self.relay_at(0), 0)
        data[self.rows(1, 0), :] += self.relay[0, : self.half]
        ring.copy(data.at[self.rows(1, 0)], self.landed_at(0, 0), ring.plus, 4)
        ring.arrived(self.relay_at(1), 1)
        data[self.rows(3, 1), :] += self.relay[1, : self.half]
        ring.copy(data.at[self.rows(3, 1)], self.landed_at(1, 1), ring.minus, 5)

    def finish(self):
        ring, data = self.ring, self.data
        ring.arrived(self.landed_at(0, 1), 2)
        ring.arrived(self.landed_at(1, 0), 3)
        ring.arrived(self.landed_at(0, 0), 4)
        ring.arrived(self.landed_at(1, 1), 5)
        for h in range(2):
            part = pl.ds(h * self.half, self.half)
            data[self.rows(0, h), :] += self.landed[0, part, :] + self.landed[1, part, :]


class Gather:
    def __init__(self, ring, data, base, chunk):
        self.ring, self.data, self.base, self.chunk = ring, data, base, chunk

    def rows(self, step, h=None):
        start = self.base + self.ring.at(step) * self.chunk
        if h is None:
            return self.data.at[pl.ds(pl.multiple_of(start, self.chunk), self.chunk)]
        half = self.chunk // 2
        return self.data.at[pl.ds(pl.multiple_of(start + h * half, half), half)]

    def begin(self):
        ring = self.ring
        ring.copy(self.rows(0), self.rows(0), ring.plus, 0)
        ring.copy(self.rows(0), self.rows(0), ring.minus, 1)

    def pass_on(self):
        ring = self.ring
        ring.arrived(self.rows(3), 0)
        ring.copy(self.rows(3, 0), self.rows(3, 0), ring.plus, 2)
        ring.arrived(self.rows(1), 1)
        ring.copy(self.rows(1, 1), self.rows(1, 1), ring.minus, 3)

    def finish(self):
        ring = self.ring
        ring.arrived(self.rows(2, 0), 2)
        ring.arrived(self.rows(2, 1), 3)


HALF_ROWS = ROW_BLOCKS * BLK // 2
BIG = HALF_ROWS // 4
SMALL = BIG // 4


def combine_kernel(partial, image, fill, big_relay, big_landed, small_relay, small_landed, send, recv):
    row, col, _, _ = place()
    y, x = lax.div(col, 4), lax.rem(col, 4)
    x_plus, x_minus = (row, y * 4 + lax.rem(x + 1, 4)), (row, y * 4 + lax.rem(x + 3, 4))
    y_plus, y_minus = (row, lax.rem(y + 1, 4) * 4 + x), (row, lax.rem(y + 3, 4) * 4 + x)
    greet([x_plus, x_minus, y_plus, y_minus])
    fill.wait()

    def ring(axis, slot):
        sems = send.at[slot], recv.at[slot]
        return Ring(x, x_plus, x_minus, *sems) if axis == 0 else Ring(y, y_plus, y_minus, *sems)

    def both(stages):
        for stage in stages:
            stage.begin()
        for stage in stages:
            stage.pass_on()
        for stage in stages:
            stage.finish()

    bases = [0, HALF_ROWS]
    inner = [x * BIG, HALF_ROWS + y * BIG]
    rings = [ring(a, a) for a in range(2)]
    wide = [Reduce(rings[a], partial, bases[a], BIG, big_relay.at[a], big_landed.at[a]) for a in range(2)]
    both(wide)
    cross = [ring(1 - a, 2 + a) for a in range(2)]
    narrow = [
        Reduce(cross[a], partial, inner[a], SMALL, small_relay.at[a], small_landed.at[a])
        for a in range(2)
    ]
    both(narrow)
    for a, other in ((0, y), (1, x)):
        own = pl.ds(pl.multiple_of(inner[a] + other * SMALL, SMALL), SMALL)
        image[own, :] = partial[own, :].astype(BF16)
    back = [ring(1 - a, 4 + a) for a in range(2)]
    both([Gather(back[a], image, inner[a], SMALL) for a in range(2)])
    last = [ring(a, 6 + a) for a in range(2)]
    both([Gather(last[a], image, bases[a], BIG) for a in range(2)])
    for group in (rings, cross, back, last):
        for one in group:
            one.drain()


def combine(partial):
    vmem = pl.BlockSpec(memory_space=pltpu.VMEM)
    rows = ROW_BLOCKS * BLK

    def kernel(partial_ref, image_ref, data, *rest):
        copy = pltpu.make_async_copy(partial_ref, data, rest[-1])
        copy.start()
        combine_kernel(data, image_ref, copy, *rest[:-1])

    return pl.pallas_call(
        kernel,
        out_shape=jax.ShapeDtypeStruct((rows, BLK), BF16),
        in_specs=[pl.BlockSpec(memory_space=pl.ANY)],
        out_specs=vmem,
        scratch_shapes=[
            pltpu.VMEM((rows, BLK), F32),
            pltpu.VMEM((2, 2, BIG // 2, BLK), F32),
            pltpu.VMEM((2, 2, BIG, BLK), F32),
            pltpu.VMEM((2, 2, SMALL // 2, BLK), F32),
            pltpu.VMEM((2, 2, SMALL, BLK), F32),
            pltpu.SemaphoreType.DMA((8, 6)),
            pltpu.SemaphoreType.DMA((8, 6)),
            pltpu.SemaphoreType.DMA,
        ],
        compiler_params=pltpu.CompilerParams(
            collective_id=1, has_side_effects=True, vmem_limit_bytes=VMEM_LIMIT
        ),
        name="combine",
    )(partial.reshape(rows, BLK))


def adjoint_kernel(count, rows, cols, sens, image, data_image, adjoint, flipped):
    step = pl.program_id(0)

    @pl.when(step == 0)
    def _():
        adjoint[...] = jnp.zeros_like(adjoint)

        def flip(b, carry):
            block = image[b].astype(F32)
            data_image[b] = block
            flipped[b] = block.T.astype(BF16)
            return carry

        lax.fori_loop(0, ROW_BLOCKS, flip, 0)

    def add(first, width):
        terms = []
        for u in range(width):
            at = rows[0, step * CHUNK + first + u]
            terms.append(dot(flipped[at], sens[0, first + u]))
        for u in range(width):
            at = cols[0, step * CHUNK + first + u]
            adjoint[(at >> 2) & 1, at & 3, at >> 3] += terms[u]

    live_slots(count, step, add)


def adjoin(count, rows, cols, sens, image):
    return pl.pallas_call(
        adjoint_kernel,
        out_shape=(
            jax.ShapeDtypeStruct((ROW_BLOCKS, BLK, BLK), F32),
            jax.ShapeDtypeStruct((2, NZ, PARTS, BLK, BLK), F32),
        ),
        grid_spec=pltpu.PrefetchScalarGridSpec(
            num_scalar_prefetch=3,
            grid=(SLOTS // CHUNK,),
            in_specs=[sens_spec(), whole(ROW_BLOCKS, BLK, BLK)],
            out_specs=(whole(ROW_BLOCKS, BLK, BLK), whole(2, NZ, PARTS, BLK, BLK)),
            scratch_shapes=[pltpu.VMEM((ROW_BLOCKS, BLK, BLK), BF16)],
        ),
        compiler_params=pltpu.CompilerParams(vmem_limit_bytes=VMEM_LIMIT),
        name="adjoin",
    )(count, rows, cols, sens, image)


GROUP = PARTS // 2


def return_kernel(
    partial, smooth, scale, signs, out, own, stage, pair, relay_out, relay, landed, gathered, sem, send, recv, *sem_refs
):
    where = place()
    row, col, z, core = where
    fill = pltpu.make_async_copy(partial.at[core], own, sem)
    fill.start()
    exchange = Exchange(stage, out, sem_refs, where)
    plus, minus, partner = exchange.neighbour(1), exchange.neighbour(3), exchange.partner()
    greet([plus, minus, partner], (exchange.first, exchange.device))
    ring = Ring(z, plus, minus, send, recv)
    for slot, step in ((6, 2), (7, 1), (8, 3), (9, 0)):
        ring.copy(partial.at[1 - core, ring.at(step)], pair.at[ring.at(step)], partner, slot)
    fill.wait()

    def total(step, h):
        group = pl.ds(h * GROUP, GROUP)
        return own[ring.at(step), group] + pair[ring.at(step), group]

    def paired(step, slot):
        ring.arrived(pair.at[ring.at(step)], slot)

    def ship(value, slot, dst, device, sem):
        relay_out[slot] = value.astype(BF16)
        ring.copy(relay_out.at[slot], dst, device, sem)

    paired(2, 6)
    ship(total(2, 0), 0, relay.at[0], plus, 0)
    ship(total(2, 1), 1, relay.at[1], minus, 1)
    paired(1, 7)
    ship(total(1, 1), 3, landed.at[0, 1], plus, 2)
    paired(3, 8)
    ship(total(3, 0), 4, landed.at[1, 0], minus, 3)
    ring.arrived(relay.at[0], 0)
    ship(total(1, 0) + relay[0].astype(F32), 2, landed.at[0, 0], plus, 4)
    ring.arrived(relay.at[1], 1)
    ship(total(3, 1) + relay[1].astype(F32), 5, landed.at[1, 1], minus, 5)
    paired(0, 9)
    ring.arrived(landed.at[0, 1], 2)
    ring.arrived(landed.at[1, 0], 3)
    ring.arrived(landed.at[0, 0], 4)
    ring.arrived(landed.at[1, 1], 5)
    lane_scale = scale[0:1, :].reshape(1, 1, BLK)
    for h in range(2):
        value = total(0, h) + landed[0, h].astype(F32) + landed[1, h].astype(F32)
        stage[pl.ds(h * GROUP, GROUP)] = (value * lane_scale).astype(BF16)

    @pl.when(exchange.first == 1)
    def _():
        gathered[lax.div(col, 2)] = stage[lax.div(col, 2)]

    def spread(i, carry):
        exchange.copy(i, gathered).start()
        return carry

    lax.fori_loop(exchange.first, PARTS, spread, 0)

    def synthesise(m, carry):
        exchange.wait_part(m, gathered)
        cells = lax.dot_general(
            signs[...], gathered[m], (((1,), (1,)), ((), ())), preferred_element_type=F32
        )
        out[z, core, m] = (cells + smooth[m]).astype(BF16)
        return carry

    for p in range(2):
        lax.fori_loop(p * GROUP, (p + 1) * GROUP, synthesise, 0)
        exchange.begin(p)
    exchange.finish()
    exchange.drain_parts(gathered)
    ring.drain()


def give_back(partial, smooth):
    vmem = pl.BlockSpec(memory_space=pltpu.VMEM)
    return pl.pallas_call(
        return_kernel,
        out_shape=jax.ShapeDtypeStruct((NZ, 2, PARTS, BLK, BLK), BF16),
        in_specs=[pl.BlockSpec(memory_space=pl.ANY), vmem, vmem, vmem],
        out_specs=vmem,
        scratch_shapes=[
            pltpu.VMEM((NZ, PARTS, BLK, BLK), F32),
            pltpu.VMEM((PARTS, BLK, BLK), BF16),
            pltpu.VMEM((NZ, PARTS, BLK, BLK), F32),
            pltpu.VMEM((6, GROUP, BLK, BLK), BF16),
            pltpu.VMEM((2, GROUP, BLK, BLK), BF16),
            pltpu.VMEM((2, 2, GROUP, BLK, BLK), BF16),
            pltpu.VMEM((PARTS, BLK, BLK), BF16),
            pltpu.SemaphoreType.DMA,
            pltpu.SemaphoreType.DMA((10,)),
            pltpu.SemaphoreType.DMA((10,)),
            *EXCHANGE_SEMS,
        ],
        compiler_params=pltpu.CompilerParams(
            collective_id=2, has_side_effects=True, vmem_limit_bytes=VMEM_LIMIT
        ),
        name="give_back",
    )(
        partial,
        smooth,
        jnp.asarray(np.broadcast_to(SCALE[None, :], (8, BLK)), F32),
        jnp.asarray(SIGNS.T, BF16),
    )


TILES = 8


def place_kernel(order, product, out, inverse):
    step = pl.program_id(0)

    @pl.when(step == 0)
    def _():
        def note(j, carry):
            inverse[order[0, j]] = j
            return carry

        lax.fori_loop(0, COL_BLOCKS, note, 0)

    for t in range(TILES):
        j = inverse[step * TILES + t]
        out[t * BLK : (t + 1) * BLK, :] = product[j & 3, (j >> 2) & 1, j >> 3].astype(F32)


def place_cells(order, product):
    return pl.pallas_call(
        place_kernel,
        out_shape=jax.ShapeDtypeStruct((CELLS, BLK), F32),
        grid_spec=pltpu.PrefetchScalarGridSpec(
            num_scalar_prefetch=1,
            grid=(COL_BLOCKS // TILES,),
            in_specs=[whole(NZ, 2, PARTS, BLK, BLK)],
            out_specs=pl.BlockSpec((TILES * BLK, BLK), lambda i, order: (i, 0)),
            scratch_shapes=[pltpu.SMEM((COL_BLOCKS,), jnp.int32)],
        ),
        compiler_params=pltpu.CompilerParams(vmem_limit_bytes=VMEM_LIMIT),
        name="place_cells",
    )(order, product)


def local(model_dir, sens_blocks, blk_row, blk_col, blk_count, send_order, neighbors, face_weight):
    wavelet, smooth = analyse(send_order, model_dir, neighbors, face_weight)
    partial_image = forward(blk_count, blk_row, blk_col, sens_blocks, wavelet)
    image_half = combine(partial_image).reshape(ROW_BLOCKS, BLK, BLK)
    data_image, partial_adjoint = adjoin(blk_count, blk_row, blk_col, sens_blocks, image_half)
    normal_product = place_cells(send_order, give_back(partial_adjoint, smooth))
    return data_image.reshape(ROW_BLOCKS * BLK, BLK), normal_product


def solution(mesh):
    placed = (
        P("cols", None),
        P("rows", "cols", None, None),
        P("rows", "cols"),
        P("rows", "cols"),
        P("rows", "cols"),
        P("cols", None),
        P(None, "cols"),
        P(None, "cols"),
    )
    return jax.shard_map(
        local,
        mesh=mesh,
        in_specs=placed,
        out_specs=(P("rows", None), P("cols", None)),
        check_vma=False,
    )
```

```python
import math

import jax
import jax.numpy as jnp
import numpy as np
from jax import lax
from jax.experimental import pallas as pl
from jax.experimental.pallas import tpu as pltpu
from jax.sharding import PartitionSpec as P

BLK = 128
RIM = 64
NROWS = 8
NCOLS = 16
NZ = 4
ROW_BLOCKS = 32
COL_BLOCKS = 64
SLOTS = 384
CHUNK = 32
VMEM_LIMIT = 56 << 20
MESH = pl.DeviceIdType.MESH
F32 = jnp.float32
BF16 = jnp.bfloat16


VMEM = pl.BlockSpec(memory_space=pltpu.VMEM)
SMEM = pl.BlockSpec(memory_space=pltpu.SMEM)
ANY = pl.BlockSpec(memory_space=pl.ANY)


def cost(flops, moved):
    return pl.CostEstimate(flops=flops, bytes_accessed=moved, transcendentals=0)


def haar_parts():
    matrix = np.ones((1, 1))
    while matrix.shape[0] < BLK:
        length = matrix.shape[0]
        upper = np.kron(matrix, np.array([[1.0, 1.0]]))
        lower = np.kron(np.eye(length), np.array([[1.0, -1.0]]))
        matrix = np.concatenate([upper, lower], axis=0) / math.sqrt(2.0)
    scale = np.abs(matrix).max(axis=1)
    signs = np.round(matrix / scale[:, None])
    return signs, scale


SIGNS, SCALE = haar_parts()


def split(value):
    high = value.astype(BF16)
    low = (value - high.astype(F32)).astype(BF16)
    return high, low


def dot(a, b):
    return jnp.dot(a, b, preferred_element_type=F32)


def remote(src, dst, send_sem, recv_sem, device):
    return pltpu.make_async_remote_copy(
        src_ref=src,
        dst_ref=dst,
        send_sem=send_sem,
        recv_sem=recv_sem,
        device_id=device,
        device_id_type=MESH,
    )


def place():
    row = lax.axis_index("rows")
    col = lax.axis_index("cols")
    return row, col, lax.div(row, 2), lax.rem(row, 2)


def z_device(z, step, core, col):
    return (lax.rem(z + step, NZ) * 2 + core, col)


def greet(devices, extra=None):
    barrier = pltpu.get_barrier_semaphore()
    for device in devices:
        pl.semaphore_signal(barrier, inc=1, device_id=device, device_id_type=MESH)
    count = len(devices)
    if extra is not None:
        first, device_of = extra

        def signal(i, carry):
            pl.semaphore_signal(barrier, inc=1, device_id=device_of(i), device_id_type=MESH)
            return carry

        lax.fori_loop(first, PARTS, signal, 0)
        count = count + PARTS - first
    pl.semaphore_wait(barrier, count)


PARTS = NCOLS // 2


class Exchange:
    def __init__(self, stage, out, sem_refs, where):
        self.stage, self.out = stage, out
        self.a_send, self.a_recv, self.g_send, self.minus, self.plus, self.far, self.pair = sem_refs
        self.row, self.col, self.z, self.core = where
        self.first = jnp.where(self.core == lax.rem(self.col, 2), 1, 0)
        self.sends = []

    def slot(self, i):
        return lax.rem(lax.div(self.col, 2) + i, PARTS)

    def device(self, i):
        return self.z * 2 + lax.rem(self.col, 2), self.slot(i) * 2 + self.core

    def arrivals(self, landing):
        return landing.at[lax.div(self.col, 2)]

    def copy(self, i, landing):
        return remote(
            self.stage.at[self.slot(i)],
            self.arrivals(landing),
            self.a_send.at[i],
            self.a_recv.at[lax.div(self.col, 2)],
            self.device(i),
        )

    def wait_part(self, m, landing):
        @pl.when(m * 2 + self.core != self.col)
        def _():
            ref = landing.at[m]
            remote(
                ref, ref, self.a_send.at[0], self.a_recv.at[m], self.device(1)
            ).wait_recv()

    def drain_parts(self, landing):
        def finish(i, carry):
            self.copy(i, landing).wait_send()
            return carry

        lax.fori_loop(self.first, PARTS, finish, 0)

    def piece(self, step, p, core=None):
        core = self.core if core is None else core
        size = PARTS // 2
        return self.out.at[lax.rem(self.z + step, NZ), core, pl.ds(p * size, size)]

    def send(self, step, p, device, recv_sem):
        piece = self.piece(step, p)
        copy = remote(piece, piece, self.g_send.at[len(self.sends)], recv_sem, device)
        copy.start()
        self.sends.append(copy)

    def arrived(self, step, p, recv_sem, core=None):
        piece = self.piece(step, p, core)
        remote(piece, piece, self.g_send.at[0], recv_sem, self.partner()).wait_recv()

    def partner(self):
        return self.z * 2 + 1 - self.core, self.col

    def neighbour(self, step):
        return z_device(self.z, step, self.core, self.col)

    def begin(self, p):
        self.send(0, p, self.neighbour(1), self.minus.at[p])
        self.send(0, p, self.neighbour(3), self.plus.at[p])
        self.send(0, p, self.partner(), self.pair.at[0, p])

    def finish(self):
        self.arrived(3, 0, self.minus.at[0])
        self.send(3, 0, self.neighbour(1), self.far.at[0])
        self.send(3, 0, self.partner(), self.pair.at[3, 0])
        self.arrived(1, 1, self.plus.at[1])
        self.send(1, 1, self.neighbour(3), self.far.at[1])
        self.send(1, 1, self.partner(), self.pair.at[1, 1])
        self.arrived(1, 0, self.plus.at[0])
        self.send(1, 0, self.partner(), self.pair.at[1, 0])
        self.arrived(3, 1, self.minus.at[1])
        self.send(3, 1, self.partner(), self.pair.at[3, 1])
        for p in range(2):
            self.arrived(2, p, self.far.at[p])
            self.send(2, p, self.partner(), self.pair.at[2, p])
        for p in range(2):
            for step in (0, 1, 3, 2):
                self.arrived(step, p, self.pair.at[step, p], 1 - self.core)
        for copy in self.sends:
            copy.wait_send()


EXCHANGE_SEMS = [
    pltpu.SemaphoreType.DMA((PARTS,)),
    pltpu.SemaphoreType.DMA((PARTS,)),
    pltpu.SemaphoreType.DMA((14,)),
    pltpu.SemaphoreType.DMA((2,)),
    pltpu.SemaphoreType.DMA((2,)),
    pltpu.SemaphoreType.DMA((2,)),
    pltpu.SemaphoreType.DMA((4, 2)),
]
CELLS = COL_BLOCKS * BLK


def cells_of(body, block):
    return jnp.concatenate([body[2 * block], body[2 * block + 1]], axis=0)


def tabulate(neighbors, weights, tables, first_cell):
    def tile(t, carry):
        at = pl.ds(pl.multiple_of(t * BLK, BLK), BLK)
        near = (neighbors[:, at] - (first_cell + t * BLK - RIM)).astype(F32)
        tables[t] = jnp.concatenate([near, weights[:, at]], axis=0)
        return carry

    lax.fori_loop(0, COL_BLOCKS, tile, 0)


def smooth_tile(body, rims, tables, tile):
    table = tables[tile].T
    span = lax.broadcasted_iota(jnp.int32, (BLK, 2 * BLK), 1).astype(F32)
    mix = jnp.zeros((BLK, 2 * BLK), F32)
    for face in range(4):
        mix += jnp.where(table[:, face : face + 1] == span, table[:, 4 + face : 5 + face], 0.0)
    mix_high, mix_low = split(mix)
    center = cells_of(body, tile)
    last = COL_BLOCKS - 1
    low = jnp.where(tile == 0, rims[0], body[jnp.maximum(2 * tile - 1, 0)])
    high = jnp.where(tile == last, rims[1], body[jnp.minimum(2 * tile + 2, 2 * last)])
    window = jnp.concatenate([low, center, high], axis=0)
    near_high, near_low = split(window)
    mixed = dot(mix_high, near_high) + dot(mix_low, near_high) + dot(mix_high, near_low)
    total = table[:, 4:5] + table[:, 5:6] + table[:, 6:7] + table[:, 7:8]
    return total * center - mixed


def analyse_kernel(
    order,
    model,
    neighbors_hbm,
    weights_hbm,
    signs_hbm,
    scale_hbm,
    wavelet,
    smooth,
    body,
    neighbors,
    weights,
    signs,
    scale,
    rims,
    tables,
    stage,
    sems,
    *sem_refs,
):
    where = place()
    row, col, z, core = where
    fills = [
        pltpu.make_async_copy(src, dst, sems.at[4 + i])
        for i, (src, dst) in enumerate(
            (
                (model, body),
                (signs_hbm, signs),
                (scale_hbm, scale),
                (neighbors_hbm, neighbors),
                (weights_hbm, weights),
            )
        )
    ]
    for fill in fills:
        fill.start()
    exchange = Exchange(stage, wavelet, sem_refs, where)
    below, above = (row, lax.rem(col + NCOLS - 1, NCOLS)), (row, lax.rem(col + 1, NCOLS))
    greet(
        [exchange.neighbour(1), exchange.neighbour(3), exchange.partner(), below, above],
        (exchange.first, exchange.device),
    )
    up = remote(
        model.at[2 * COL_BLOCKS - 1],
        rims.at[0],
        sems.at[0],
        sems.at[2],
        above,
    )
    down = remote(
        model.at[0],
        rims.at[1],
        sems.at[1],
        sems.at[3],
        below,
    )
    up.start()
    down.start()
    for fill in fills:
        fill.wait()
    sign_pair = jnp.concatenate([signs[...], signs[...]], axis=1)
    landing = wavelet.at[z, core]
    target = wavelet.at[z, lax.rem(col, 2)]

    def block_of(m):
        return order[0, (m * 2 + core) * 4 + z]

    def coefficients(m):
        high, low = split(cells_of(body, block_of(m)))
        product = dot(sign_pair, jnp.concatenate([high, low], axis=0))
        return (product * scale[...]).astype(BF16)

    @pl.when(exchange.first == 1)
    def _():
        wavelet[z, core, lax.div(col, 2)] = coefficients(lax.div(col, 2))

    def spread(i, carry):
        stage[exchange.slot(i)] = coefficients(exchange.slot(i))
        exchange.copy(i, target).start()
        return carry

    lax.fori_loop(exchange.first, PARTS, spread, 0)
    tabulate(neighbors, weights, tables, col * CELLS)

    def smooth_one(m, carry):
        smooth[m] = smooth_tile(body, rims, tables, block_of(m))
        return carry

    up.wait_recv()
    down.wait_recv()
    lax.fori_loop(0, 3, smooth_one, 0)

    def wait_part(m, carry):
        exchange.wait_part(m, landing)
        return carry

    for p in range(2):
        lax.fori_loop(p * PARTS // 2, (p + 1) * PARTS // 2, wait_part, 0)
        exchange.begin(p)
    lax.fori_loop(3, PARTS, smooth_one, 0)
    exchange.finish()
    exchange.drain_parts(target)
    up.wait_send()
    down.wait_send()


def analyse(order, model, neighbors, weights):
    return pl.pallas_call(
        analyse_kernel,
        out_shape=(
            jax.ShapeDtypeStruct((NZ, 2, PARTS, BLK, BLK), BF16),
            jax.ShapeDtypeStruct((PARTS, BLK, BLK), F32),
        ),
        in_specs=[SMEM, *[ANY] * 5],
        out_specs=(VMEM, VMEM),
        scratch_shapes=[
            pltpu.VMEM((2 * COL_BLOCKS, RIM, BLK), F32),
            pltpu.VMEM((4, CELLS), jnp.int32),
            pltpu.VMEM((4, CELLS), F32),
            pltpu.VMEM((BLK, BLK), BF16),
            pltpu.VMEM((BLK, BLK), F32),
            pltpu.VMEM((2, RIM, BLK), F32),
            pltpu.VMEM((COL_BLOCKS, 8, BLK), F32),
            pltpu.VMEM((PARTS, BLK, BLK), BF16),
            pltpu.SemaphoreType.DMA((9,)),
            *EXCHANGE_SEMS,
        ],
        compiler_params=pltpu.CompilerParams(
            collective_id=0, has_side_effects=True, vmem_limit_bytes=VMEM_LIMIT
        ),
        cost_estimate=cost(1 << 30, 60 << 20),
        name="analyse",
    )(
        order,
        model.reshape(2 * COL_BLOCKS, RIM, BLK),
        neighbors,
        weights,
        jnp.asarray(SIGNS, BF16),
        jnp.asarray(np.broadcast_to(SCALE[:, None], (BLK, BLK)), F32),
    )


class Sensors:
    def __init__(self, count, source, held, sems):
        self.live, self.source, self.held, self.sems = count[0, 0], source, held, sems

    def copy(self, g):
        part = pl.ds(g * CHUNK, CHUNK)
        return pltpu.make_async_copy(self.source.at[0, part], self.held.at[part], self.sems.at[g])

    def start(self):
        def begin(g, carry):
            self.copy(g).start()
            return carry

        lax.fori_loop(0, pl.cdiv(self.live, CHUNK), begin, 0)

    def run(self, add):
        full = self.live // CHUNK

        def group(g, carry):
            self.copy(g).wait()
            add(g * CHUNK, CHUNK)
            return carry

        lax.fori_loop(0, full, group, 0)
        done = full * CHUNK

        @pl.when(done < self.live)
        def _():
            self.copy(full).wait()

        for width in (4, 1):

            def few(g, carry, width=width, done=done):
                add(done + g * width, width)
                return carry

            groups = (self.live - done) // width
            lax.fori_loop(0, groups, few, 0)
            done = done + groups * width


def forward_kernel(count, rows, cols, source, wavelet_hbm, image, held, wavelet, sem, sems):
    load = pltpu.make_async_copy(wavelet_hbm, wavelet, sem)
    load.start()
    sensors = Sensors(count, source, held, sems)
    sensors.start()
    image[...] = jnp.zeros_like(image)
    load.wait()

    def add(first, width):
        terms = []
        for u in range(width):
            at = cols[0, first + u]
            terms.append(dot(held[first + u], wavelet[at & 3, (at >> 2) & 1, at >> 3]))
        for u in range(width):
            image[rows[0, first + u]] += terms[u]

    sensors.run(add)


SENSOR_SCRATCH = (
    pltpu.VMEM((SLOTS, BLK, BLK), BF16),
    pltpu.SemaphoreType.DMA((SLOTS // CHUNK,)),
)


def forward(count, rows, cols, sens, wavelet):
    held, sems = SENSOR_SCRATCH
    return pl.pallas_call(
        forward_kernel,
        out_shape=jax.ShapeDtypeStruct((ROW_BLOCKS, BLK, BLK), F32),
        in_specs=[SMEM, SMEM, SMEM, ANY, ANY],
        out_specs=VMEM,
        scratch_shapes=[
            held,
            pltpu.VMEM(wavelet.shape, BF16),
            pltpu.SemaphoreType.DMA,
            sems,
        ],
        compiler_params=pltpu.CompilerParams(vmem_limit_bytes=VMEM_LIMIT),
        name="forward",
    )(count, rows, cols, sens, wavelet)


class Ring:
    def __init__(self, me, plus, minus, send, recv, far=None):
        self.me, self.plus, self.minus = me, plus, minus
        self.others = ((2, far), (1, plus), (3, minus))
        self.send, self.recv = send, recv
        self.started = []

    def at(self, step):
        return lax.rem(self.me + step, 4)

    def copy(self, src, dst, device, slot):
        copy = remote(src, dst, self.send.at[slot], self.recv.at[slot], device)
        copy.start()
        self.started.append(copy)

    def arrived(self, ref, slot):
        remote(ref, ref, self.send.at[slot], self.recv.at[slot], self.plus).wait_recv()

    def drain(self):
        for copy in self.started:
            copy.wait_send()
        self.started = []


class Reduce:
    def __init__(self, ring, data, base, chunk, relay, landed):
        self.ring, self.data, self.base, self.chunk = ring, data, base, chunk
        self.half = chunk // 2
        self.relay, self.landed = relay, landed

    def rows(self, step, h):
        start = self.base + self.ring.at(step) * self.chunk + h * self.half
        return pl.ds(pl.multiple_of(start, self.half), self.half)

    def relay_at(self, side):
        return self.relay.at[side, pl.ds(0, self.half)]

    def landed_at(self, side, h):
        return self.landed.at[side, pl.ds(h * self.half, self.half)]

    def begin(self):
        ring, data = self.ring, self.data
        ring.copy(data.at[self.rows(2, 0)], self.relay_at(0), ring.plus, 0)
        ring.copy(data.at[self.rows(2, 1)], self.relay_at(1), ring.minus, 1)
        ring.copy(data.at[self.rows(1, 1)], self.landed_at(0, 1), ring.plus, 2)
        ring.copy(data.at[self.rows(3, 0)], self.landed_at(1, 0), ring.minus, 3)

    def pass_on(self):
        ring, data = self.ring, self.data
        ring.arrived(self.relay_at(0), 0)
        data[self.rows(1, 0), :] += self.relay[0, : self.half]
        ring.copy(data.at[self.rows(1, 0)], self.landed_at(0, 0), ring.plus, 4)
        ring.arrived(self.relay_at(1), 1)
        data[self.rows(3, 1), :] += self.relay[1, : self.half]
        ring.copy(data.at[self.rows(3, 1)], self.landed_at(1, 1), ring.minus, 5)

    def finish(self):
        ring, data = self.ring, self.data
        ring.arrived(self.landed_at(0, 1), 2)
        ring.arrived(self.landed_at(1, 0), 3)
        ring.arrived(self.landed_at(0, 0), 4)
        ring.arrived(self.landed_at(1, 1), 5)
        for h in range(2):
            part = pl.ds(h * self.half, self.half)
            data[self.rows(0, h), :] += self.landed[0, part, :] + self.landed[1, part, :]


class DirectReduce:
    def __init__(self, ring, data, base, chunk, landed):
        self.ring, self.data, self.base, self.chunk = ring, data, base, chunk
        self.landed = landed

    def rows(self, step):
        start = self.base + self.ring.at(step) * self.chunk
        return pl.ds(pl.multiple_of(start, self.chunk), self.chunk)

    def begin(self):
        for step, device in self.ring.others:
            self.ring.copy(
                self.data.at[self.rows(step)], self.landed.at[step - 1], device, step - 1
            )

    def pass_on(self):
        for step in range(3):
            self.ring.arrived(self.landed.at[step], step)

    def finish(self):
        own = self.rows(0)
        total = self.data[own, :] + self.landed[0]
        self.data[own, :] = total + (self.landed[1] + self.landed[2])


class DirectGather:
    def __init__(self, ring, data, base, chunk):
        self.ring, self.data, self.base, self.chunk = ring, data, base, chunk

    def rows(self, step):
        start = self.base + self.ring.at(step) * self.chunk
        return self.data.at[pl.ds(pl.multiple_of(start, self.chunk), self.chunk)]

    def begin(self):
        for step, device in self.ring.others:
            self.ring.copy(self.rows(0), self.rows(0), device, step - 1)

    def pass_on(self):
        pass

    def finish(self):
        for step in (1, 3, 2):
            self.ring.arrived(self.rows(4 - step), step - 1)


HALF_ROWS = ROW_BLOCKS * BLK // 2
BIG = HALF_ROWS // 4
SMALL = BIG // 4


def combine_kernel(partial, image, fill, big_relay, big_landed, small_landed, send, recv):
    row, col, _, _ = place()
    y, x = lax.div(col, 4), lax.rem(col, 4)
    x_ring = [(row, y * 4 + lax.rem(x + step, 4)) for step in range(4)]
    y_ring = [(row, lax.rem(y + step, 4) * 4 + x) for step in range(4)]
    greet(x_ring[1:] + y_ring[1:])
    fill.wait()

    def ring(axis, slot):
        me, devices = ((x, x_ring), (y, y_ring))[axis]
        return Ring(me, devices[1], devices[3], send.at[slot], recv.at[slot], devices[2])

    def both(stages):
        for stage in stages:
            stage.begin()
        for stage in stages:
            stage.pass_on()
        for stage in stages:
            stage.finish()

    bases = [0, HALF_ROWS]
    inner = [x * BIG, HALF_ROWS + y * BIG]
    rings = [ring(a, a) for a in range(2)]
    wide = [Reduce(rings[a], partial, bases[a], BIG, big_relay.at[a], big_landed.at[a]) for a in range(2)]
    both(wide)
    cross = [ring(1 - a, 2 + a) for a in range(2)]
    both([DirectReduce(cross[a], partial, inner[a], SMALL, small_landed.at[a]) for a in range(2)])
    for a, other in ((0, y), (1, x)):
        own = pl.ds(pl.multiple_of(inner[a] + other * SMALL, SMALL), SMALL)
        image[own, :] = partial[own, :].astype(BF16)
    back = [ring(1 - a, 4 + a) for a in range(2)]
    both([DirectGather(back[a], image, inner[a], SMALL) for a in range(2)])
    last = [ring(a, 6 + a) for a in range(2)]
    both([DirectGather(last[a], image, bases[a], BIG) for a in range(2)])
    for group in (rings, cross, back, last):
        for one in group:
            one.drain()


def combine(partial):
    vmem = pl.BlockSpec(memory_space=pltpu.VMEM)
    rows = ROW_BLOCKS * BLK

    def kernel(partial_ref, image_ref, data, *rest):
        copy = pltpu.make_async_copy(partial_ref, data, rest[-1])
        copy.start()
        combine_kernel(data, image_ref, copy, *rest[:-1])

    return pl.pallas_call(
        kernel,
        out_shape=jax.ShapeDtypeStruct((rows, BLK), BF16),
        in_specs=[pl.BlockSpec(memory_space=pl.ANY)],
        out_specs=vmem,
        scratch_shapes=[
            pltpu.VMEM((rows, BLK), F32),
            pltpu.VMEM((2, 2, BIG // 2, BLK), F32),
            pltpu.VMEM((2, 2, BIG, BLK), F32),
            pltpu.VMEM((2, 3, SMALL, BLK), F32),
            pltpu.SemaphoreType.DMA((8, 6)),
            pltpu.SemaphoreType.DMA((8, 6)),
            pltpu.SemaphoreType.DMA,
        ],
        compiler_params=pltpu.CompilerParams(
            collective_id=1, has_side_effects=True, vmem_limit_bytes=VMEM_LIMIT
        ),
        cost_estimate=cost(1 << 20, 80 << 20),
        name="combine",
    )(partial.reshape(rows, BLK))


def adjoint_kernel(
    count, rows, cols, source, image_hbm, data_image, adjoint, held, image, flipped, plain, sem, sems
):
    load = pltpu.make_async_copy(image_hbm, image, sem.at[0])
    load.start()
    sensors = Sensors(count, source, held, sems)
    sensors.start()
    adjoint[...] = jnp.zeros_like(adjoint)
    load.wait()

    def flip(b, carry):
        block = image[b].astype(F32)
        plain[b] = block
        flipped[b] = block.T.astype(BF16)
        return carry

    lax.fori_loop(0, ROW_BLOCKS, flip, 0, unroll=2)
    store = pltpu.make_async_copy(plain, data_image, sem.at[1])
    store.start()

    def add(first, width):
        terms = []
        for u in range(width):
            terms.append(dot(flipped[rows[0, first + u]], held[first + u]))
        for u in range(width):
            at = cols[0, first + u]
            adjoint[(at >> 2) & 1, at & 3, at >> 3] += terms[u]

    sensors.run(add)
    store.wait()


def adjoin(count, rows, cols, sens, image):
    held, sems = SENSOR_SCRATCH
    return pl.pallas_call(
        adjoint_kernel,
        out_shape=(
            jax.ShapeDtypeStruct((ROW_BLOCKS, BLK, BLK), F32),
            jax.ShapeDtypeStruct((2, NZ, PARTS, BLK, BLK), F32),
        ),
        in_specs=[SMEM, SMEM, SMEM, ANY, ANY],
        out_specs=(ANY, VMEM),
        scratch_shapes=[
            held,
            pltpu.VMEM((ROW_BLOCKS, BLK, BLK), BF16),
            pltpu.VMEM((ROW_BLOCKS, BLK, BLK), BF16),
            pltpu.VMEM((ROW_BLOCKS, BLK, BLK), F32),
            pltpu.SemaphoreType.DMA((2,)),
            sems,
        ],
        compiler_params=pltpu.CompilerParams(vmem_limit_bytes=VMEM_LIMIT),
        name="adjoin",
    )(count, rows, cols, sens, image)


GROUP = PARTS // 2


def return_kernel(
    partial, smooth, scale, signs, out, own, stage, pair, relay_out, relay, landed, gathered, sem, send, recv, *sem_refs
):
    where = place()
    row, col, z, core = where
    fill = pltpu.make_async_copy(partial.at[core], own, sem)
    fill.start()
    exchange = Exchange(stage, out, sem_refs, where)
    plus, minus, partner = exchange.neighbour(1), exchange.neighbour(3), exchange.partner()
    greet([plus, minus, partner], (exchange.first, exchange.device))
    ring = Ring(z, plus, minus, send, recv)
    for slot, step in ((6, 2), (7, 1), (8, 3), (9, 0)):
        ring.copy(partial.at[1 - core, ring.at(step)], pair.at[ring.at(step)], partner, slot)
    fill.wait()

    def total(step, h):
        group = pl.ds(h * GROUP, GROUP)
        return own[ring.at(step), group] + pair[ring.at(step), group]

    def paired(step, slot):
        ring.arrived(pair.at[ring.at(step)], slot)

    def ship(value, slot, dst, device, sem):
        relay_out[slot] = value.astype(BF16)
        ring.copy(relay_out.at[slot], dst, device, sem)

    paired(2, 6)
    ship(total(2, 0), 0, relay.at[0], plus, 0)
    ship(total(2, 1), 1, relay.at[1], minus, 1)
    paired(1, 7)
    ship(total(1, 1), 3, landed.at[0, 1], plus, 2)
    paired(3, 8)
    ship(total(3, 0), 4, landed.at[1, 0], minus, 3)
    ring.arrived(relay.at[0], 0)
    ship(total(1, 0) + relay[0].astype(F32), 2, landed.at[0, 0], plus, 4)
    ring.arrived(relay.at[1], 1)
    ship(total(3, 1) + relay[1].astype(F32), 5, landed.at[1, 1], minus, 5)
    paired(0, 9)
    ring.arrived(landed.at[0, 1], 2)
    ring.arrived(landed.at[1, 0], 3)
    ring.arrived(landed.at[0, 0], 4)
    ring.arrived(landed.at[1, 1], 5)
    lane_scale = scale[0:1, :].reshape(1, 1, BLK)
    for h in range(2):
        value = total(0, h) + landed[0, h].astype(F32) + landed[1, h].astype(F32)
        stage[pl.ds(h * GROUP, GROUP)] = (value * lane_scale).astype(BF16)

    @pl.when(exchange.first == 1)
    def _():
        gathered[lax.div(col, 2)] = stage[lax.div(col, 2)]

    def spread(i, carry):
        exchange.copy(i, gathered).start()
        return carry

    lax.fori_loop(exchange.first, PARTS, spread, 0)

    def synthesise(m, carry):
        exchange.wait_part(m, gathered)
        cells = lax.dot_general(
            signs[...], gathered[m], (((1,), (1,)), ((), ())), preferred_element_type=F32
        )
        out[z, core, m] = (cells + smooth[m]).astype(BF16)
        return carry

    for p in range(2):
        lax.fori_loop(p * GROUP, (p + 1) * GROUP, synthesise, 0)
        exchange.begin(p)
    exchange.finish()
    exchange.drain_parts(gathered)
    ring.drain()


def give_back(partial, smooth):
    vmem = pl.BlockSpec(memory_space=pltpu.VMEM)
    return pl.pallas_call(
        return_kernel,
        out_shape=jax.ShapeDtypeStruct((NZ, 2, PARTS, BLK, BLK), BF16),
        in_specs=[ANY, vmem, vmem, vmem],
        out_specs=vmem,
        scratch_shapes=[
            pltpu.VMEM((NZ, PARTS, BLK, BLK), F32),
            pltpu.VMEM((PARTS, BLK, BLK), BF16),
            pltpu.VMEM((NZ, PARTS, BLK, BLK), F32),
            pltpu.VMEM((6, GROUP, BLK, BLK), BF16),
            pltpu.VMEM((2, GROUP, BLK, BLK), BF16),
            pltpu.VMEM((2, 2, GROUP, BLK, BLK), BF16),
            pltpu.VMEM((PARTS, BLK, BLK), BF16),
            pltpu.SemaphoreType.DMA,
            pltpu.SemaphoreType.DMA((10,)),
            pltpu.SemaphoreType.DMA((10,)),
            *EXCHANGE_SEMS,
        ],
        compiler_params=pltpu.CompilerParams(
            collective_id=2, has_side_effects=True, vmem_limit_bytes=VMEM_LIMIT
        ),
        cost_estimate=cost(1 << 30, 80 << 20),
        name="give_back",
    )(
        partial,
        smooth,
        jnp.asarray(np.broadcast_to(SCALE[None, :], (8, BLK)), F32),
        jnp.asarray(SIGNS.T, BF16),
    )


def place_kernel(order, product_hbm, out, product, cells, in_sems, out_sems):
    def load(i):
        at = lax.div(i, 2), lax.rem(i, 2)
        return pltpu.make_async_copy(product_hbm.at[at], product.at[at], in_sems.at[i])

    def store(i, block):
        return pltpu.make_async_copy(cells.at[i], out.at[block], out_sems.at[i])

    for i in range(2 * NZ):
        load(i).start()
    for i in range(2 * NZ):
        load(i).wait()
        for m in range(PARTS):
            q, core = i // 2, i % 2
            at = i * PARTS + m
            cells[at] = product[q, core, m].astype(F32)
            store(at, order[0, (m * 2 + core) * 4 + q]).start()

    def finish(i, carry):
        store(i, 0).wait()
        return carry

    lax.fori_loop(0, COL_BLOCKS, finish, 0)


def place_cells(order, product):
    return pl.pallas_call(
        place_kernel,
        out_shape=jax.ShapeDtypeStruct((COL_BLOCKS, BLK, BLK), F32),
        in_specs=[SMEM, ANY],
        out_specs=ANY,
        scratch_shapes=[
            pltpu.VMEM(product.shape, BF16),
            pltpu.VMEM((COL_BLOCKS, BLK, BLK), F32),
            pltpu.SemaphoreType.DMA((2 * NZ,)),
            pltpu.SemaphoreType.DMA((COL_BLOCKS,)),
        ],
        compiler_params=pltpu.CompilerParams(vmem_limit_bytes=VMEM_LIMIT),
        name="place_cells",
    )(order, product)


def local(model_dir, sens_blocks, blk_row, blk_col, blk_count, send_order, neighbors, face_weight):
    wavelet, smooth = analyse(send_order, model_dir, neighbors, face_weight)
    partial_image = forward(blk_count, blk_row, blk_col, sens_blocks, wavelet)
    image_half = combine(partial_image).reshape(ROW_BLOCKS, BLK, BLK)
    data_image, partial_adjoint = adjoin(blk_count, blk_row, blk_col, sens_blocks, image_half)
    normal_product = place_cells(send_order, give_back(partial_adjoint, smooth))
    return data_image.reshape(ROW_BLOCKS * BLK, BLK), normal_product.reshape(CELLS, BLK)


def solution(mesh):
    placed = (
        P("cols", None),
        P("rows", "cols", None, None),
        P("rows", "cols"),
        P("rows", "cols"),
        P("rows", "cols"),
        P("cols", None),
        P(None, "cols"),
        P(None, "cols"),
    )
    return jax.shard_map(
        local,
        mesh=mesh,
        in_specs=placed,
        out_specs=(P("rows", None), P("cols", None)),
        check_vma=False,
    )
```

```python
import math

import jax
import jax.numpy as jnp
import numpy as np
from jax import lax
from jax.experimental import pallas as pl
from jax.experimental.pallas import tpu as pltpu
from jax.sharding import PartitionSpec as P

BLK = 128
RIM = 64
NROWS = 8
NCOLS = 16
NZ = 4
ROW_BLOCKS = 32
COL_BLOCKS = 64
SLOTS = 384
CHUNK = 32
VMEM_LIMIT = 56 << 20
MESH = pl.DeviceIdType.MESH
F32 = jnp.float32
BF16 = jnp.bfloat16


VMEM = pl.BlockSpec(memory_space=pltpu.VMEM)
SMEM = pl.BlockSpec(memory_space=pltpu.SMEM)
ANY = pl.BlockSpec(memory_space=pl.ANY)


def cost(flops, moved):
    return pl.CostEstimate(flops=flops, bytes_accessed=moved, transcendentals=0)


def haar_parts():
    matrix = np.ones((1, 1))
    while matrix.shape[0] < BLK:
        length = matrix.shape[0]
        upper = np.kron(matrix, np.array([[1.0, 1.0]]))
        lower = np.kron(np.eye(length), np.array([[1.0, -1.0]]))
        matrix = np.concatenate([upper, lower], axis=0) / math.sqrt(2.0)
    scale = np.abs(matrix).max(axis=1)
    signs = np.round(matrix / scale[:, None])
    return signs, scale


SIGNS, SCALE = haar_parts()


def split(value):
    high = value.astype(BF16)
    low = (value - high.astype(F32)).astype(BF16)
    return high, low


def dot(a, b):
    return jnp.dot(a, b, preferred_element_type=F32)


def remote(src, dst, send_sem, recv_sem, device):
    return pltpu.make_async_remote_copy(
        src_ref=src,
        dst_ref=dst,
        send_sem=send_sem,
        recv_sem=recv_sem,
        device_id=device,
        device_id_type=MESH,
    )


def place():
    row = lax.axis_index("rows")
    col = lax.axis_index("cols")
    return row, col, lax.div(row, 2), lax.rem(row, 2)


def z_device(z, step, core, col):
    return (lax.rem(z + step, NZ) * 2 + core, col)


def greet(devices, extra=None):
    barrier = pltpu.get_barrier_semaphore()
    for device in devices:
        pl.semaphore_signal(barrier, inc=1, device_id=device, device_id_type=MESH)
    count = len(devices)
    if extra is not None:
        first, device_of = extra

        def signal(i, carry):
            pl.semaphore_signal(barrier, inc=1, device_id=device_of(i), device_id_type=MESH)
            return carry

        lax.fori_loop(first, PARTS, signal, 0)
        count = count + PARTS - first
    pl.semaphore_wait(barrier, count)


PARTS = NCOLS // 2
GROUP = PARTS // 2


class Exchange:
    def __init__(self, stage, out, sem_refs, where):
        self.stage, self.out = stage, out
        self.a_send, self.a_recv, self.g_send, self.minus, self.plus, self.far, self.pair = sem_refs
        self.row, self.col, self.z, self.core = where
        self.first = jnp.where(self.core == lax.rem(self.col, 2), 1, 0)
        self.sends = []

    def slot(self, i):
        return lax.rem(lax.div(self.col, 2) + i, PARTS)

    def device(self, i):
        return self.z * 2 + lax.rem(self.col, 2), self.slot(i) * 2 + self.core

    def arrivals(self, landing):
        return landing.at[lax.div(self.col, 2)]

    def copy(self, i, landing):
        return remote(
            self.stage.at[self.slot(i)],
            self.arrivals(landing),
            self.a_send.at[i],
            self.a_recv.at[lax.div(self.col, 2)],
            self.device(i),
        )

    def wait_part(self, m, landing):
        @pl.when(m * 2 + self.core != self.col)
        def _():
            ref = landing.at[m]
            remote(
                ref, ref, self.a_send.at[0], self.a_recv.at[m], self.device(1)
            ).wait_recv()

    def drain_parts(self, landing):
        def finish(i, carry):
            self.copy(i, landing).wait_send()
            return carry

        lax.fori_loop(self.first, PARTS, finish, 0)

    def piece(self, step, p, core=None):
        core = self.core if core is None else core
        size = PARTS // 2
        return self.out.at[lax.rem(self.z + step, NZ), core, pl.ds(p * size, size)]

    def send(self, step, p, device, recv_sem):
        piece = self.piece(step, p)
        copy = remote(piece, piece, self.g_send.at[len(self.sends)], recv_sem, device)
        copy.start()
        self.sends.append(copy)

    def arrived(self, step, p, recv_sem, core=None):
        piece = self.piece(step, p, core)
        remote(piece, piece, self.g_send.at[0], recv_sem, self.partner()).wait_recv()

    def partner(self):
        return self.z * 2 + 1 - self.core, self.col

    def neighbour(self, step):
        return z_device(self.z, step, self.core, self.col)

    def begin(self, p):
        self.send(0, p, self.neighbour(1), self.minus.at[p])
        self.send(0, p, self.neighbour(3), self.plus.at[p])
        self.send(0, p, self.partner(), self.pair.at[0, p])

    def finish(self):
        self.arrived(3, 0, self.minus.at[0])
        self.send(3, 0, self.neighbour(1), self.far.at[0])
        self.send(3, 0, self.partner(), self.pair.at[3, 0])
        self.arrived(1, 1, self.plus.at[1])
        self.send(1, 1, self.neighbour(3), self.far.at[1])
        self.send(1, 1, self.partner(), self.pair.at[1, 1])
        self.arrived(1, 0, self.plus.at[0])
        self.send(1, 0, self.partner(), self.pair.at[1, 0])
        self.arrived(3, 1, self.minus.at[1])
        self.send(3, 1, self.partner(), self.pair.at[3, 1])
        for p in range(2):
            self.arrived(2, p, self.far.at[p])
            self.send(2, p, self.partner(), self.pair.at[2, p])
        for p in range(2):
            for step in (0, 1, 3, 2):
                self.arrived(step, p, self.pair.at[step, p], 1 - self.core)
        for copy in self.sends:
            copy.wait_send()


EXCHANGE_SEMS = [
    pltpu.SemaphoreType.DMA((PARTS,)),
    pltpu.SemaphoreType.DMA((PARTS,)),
    pltpu.SemaphoreType.DMA((14,)),
    pltpu.SemaphoreType.DMA((2,)),
    pltpu.SemaphoreType.DMA((2,)),
    pltpu.SemaphoreType.DMA((2,)),
    pltpu.SemaphoreType.DMA((4, 2)),
]
CELLS = COL_BLOCKS * BLK


def cells_of(body, block):
    return jnp.concatenate([body[2 * block], body[2 * block + 1]], axis=0)


def tabulate(neighbors, weights, tables, first_cell):
    def tile(t, carry):
        at = pl.ds(pl.multiple_of(t * BLK, BLK), BLK)
        near = (neighbors[:, at] - (first_cell + t * BLK - RIM)).astype(F32)
        tables[t] = jnp.concatenate([near, weights[:, at]], axis=0)
        return carry

    lax.fori_loop(0, COL_BLOCKS, tile, 0)


def smooth_tile(body, rims, tables, tile):
    table = tables[tile].T
    span = lax.broadcasted_iota(jnp.int32, (BLK, 2 * BLK), 1).astype(F32)
    mix = jnp.zeros((BLK, 2 * BLK), F32)
    for face in range(4):
        mix += jnp.where(table[:, face : face + 1] == span, table[:, 4 + face : 5 + face], 0.0)
    mix_high, mix_low = split(mix)
    center = cells_of(body, tile)
    last = COL_BLOCKS - 1
    low = jnp.where(tile == 0, rims[0], body[jnp.maximum(2 * tile - 1, 0)])
    high = jnp.where(tile == last, rims[1], body[jnp.minimum(2 * tile + 2, 2 * last)])
    window = jnp.concatenate([low, center, high], axis=0)
    near_high, near_low = split(window)
    mixed = dot(mix_high, near_high) + dot(mix_low, near_high) + dot(mix_high, near_low)
    total = table[:, 4:5] + table[:, 5:6] + table[:, 6:7] + table[:, 7:8]
    return total * center - mixed


def analyse_kernel(
    order,
    model,
    neighbors_hbm,
    weights_hbm,
    signs_hbm,
    scale_hbm,
    wavelet,
    smooth,
    body,
    neighbors,
    weights,
    signs,
    scale,
    rims,
    tables,
    stage,
    sems,
    *sem_refs,
):
    where = place()
    row, col, z, core = where
    fills = [
        pltpu.make_async_copy(src, dst, sems.at[4 + i])
        for i, (src, dst) in enumerate(
            (
                (model, body),
                (signs_hbm, signs),
                (scale_hbm, scale),
                (neighbors_hbm, neighbors),
                (weights_hbm, weights),
            )
        )
    ]
    for fill in fills:
        fill.start()
    exchange = Exchange(stage, wavelet, sem_refs, where)
    below, above = (row, lax.rem(col + NCOLS - 1, NCOLS)), (row, lax.rem(col + 1, NCOLS))
    greet(
        [exchange.neighbour(1), exchange.neighbour(3), exchange.partner(), below, above],
        (exchange.first, exchange.device),
    )
    up = remote(
        model.at[2 * COL_BLOCKS - 1],
        rims.at[0],
        sems.at[0],
        sems.at[2],
        above,
    )
    down = remote(
        model.at[0],
        rims.at[1],
        sems.at[1],
        sems.at[3],
        below,
    )
    up.start()
    down.start()
    for fill in fills:
        fill.wait()
    sign_pair = jnp.concatenate([signs[...], signs[...]], axis=1)
    landing = wavelet.at[z, core]
    target = wavelet.at[z, lax.rem(col, 2)]

    def block_of(m):
        return order[0, (m * 2 + core) * 4 + z]

    def coefficients(m):
        high, low = split(cells_of(body, block_of(m)))
        product = dot(sign_pair, jnp.concatenate([high, low], axis=0))
        return (product * scale[...]).astype(BF16)

    @pl.when(exchange.first == 1)
    def _():
        wavelet[z, core, lax.div(col, 2)] = coefficients(lax.div(col, 2))

    def spread(i, carry):
        stage[exchange.slot(i)] = coefficients(exchange.slot(i))
        exchange.copy(i, target).start()
        return carry

    lax.fori_loop(exchange.first, PARTS, spread, 0)
    tabulate(neighbors, weights, tables, col * CELLS)

    def smooth_one(m, carry):
        smooth[m] = smooth_tile(body, rims, tables, block_of(m))
        return carry

    up.wait_recv()
    down.wait_recv()
    lax.fori_loop(0, 3, smooth_one, 0)

    def wait_part(m, carry):
        exchange.wait_part(m, landing)
        return carry

    for p in range(2):
        lax.fori_loop(p * PARTS // 2, (p + 1) * PARTS // 2, wait_part, 0)
        exchange.begin(p)
    lax.fori_loop(3, PARTS, smooth_one, 0)
    exchange.finish()
    exchange.drain_parts(target)
    up.wait_send()
    down.wait_send()


def analyse(order, model, neighbors, weights):
    return pl.pallas_call(
        analyse_kernel,
        out_shape=(
            jax.ShapeDtypeStruct((NZ, 2, PARTS, BLK, BLK), BF16),
            jax.ShapeDtypeStruct((PARTS, BLK, BLK), F32),
        ),
        in_specs=[SMEM, *[ANY] * 5],
        out_specs=(VMEM, VMEM),
        scratch_shapes=[
            pltpu.VMEM((2 * COL_BLOCKS, RIM, BLK), F32),
            pltpu.VMEM((4, CELLS), jnp.int32),
            pltpu.VMEM((4, CELLS), F32),
            pltpu.VMEM((BLK, BLK), BF16),
            pltpu.VMEM((BLK, BLK), F32),
            pltpu.VMEM((2, RIM, BLK), F32),
            pltpu.VMEM((COL_BLOCKS, 8, BLK), F32),
            pltpu.VMEM((PARTS, BLK, BLK), BF16),
            pltpu.SemaphoreType.DMA((9,)),
            *EXCHANGE_SEMS,
        ],
        compiler_params=pltpu.CompilerParams(
            collective_id=0, has_side_effects=True, vmem_limit_bytes=VMEM_LIMIT
        ),
        cost_estimate=cost(1 << 30, 60 << 20),
        name="analyse",
    )(
        order,
        model.reshape(2 * COL_BLOCKS, RIM, BLK),
        neighbors,
        weights,
        jnp.asarray(SIGNS, BF16),
        jnp.asarray(np.broadcast_to(SCALE[:, None], (BLK, BLK)), F32),
    )


class Sensors:
    def __init__(self, count, source, held, sems):
        self.live, self.source, self.held, self.sems = count[0, 0], source, held, sems

    def copy(self, g):
        part = pl.ds(g * CHUNK, CHUNK)
        return pltpu.make_async_copy(self.source.at[0, part], self.held.at[part], self.sems.at[g])

    def start(self):
        def begin(g, carry):
            self.copy(g).start()
            return carry

        lax.fori_loop(0, pl.cdiv(self.live, CHUNK), begin, 0)

    def run(self, add):
        full = self.live // CHUNK

        def group(g, carry):
            self.copy(g).wait()
            add(g * CHUNK, CHUNK)
            return carry

        lax.fori_loop(0, full, group, 0)
        done = full * CHUNK

        @pl.when(done < self.live)
        def _():
            self.copy(full).wait()

        for width in (4, 1):

            def few(g, carry, width=width, done=done):
                add(done + g * width, width)
                return carry

            groups = (self.live - done) // width
            lax.fori_loop(0, groups, few, 0)
            done = done + groups * width


def forward_kernel(count, rows, cols, source, wavelet_hbm, image, held, wavelet, sem, sems):
    load = pltpu.make_async_copy(wavelet_hbm, wavelet, sem)
    load.start()
    sensors = Sensors(count, source, held, sems)
    sensors.start()
    image[...] = jnp.zeros_like(image)
    load.wait()

    def add(first, width):
        terms = []
        for u in range(width):
            at = cols[0, first + u]
            terms.append(dot(held[first + u], wavelet[at & 3, (at >> 2) & 1, at >> 3]))
        for u in range(width):
            image[rows[0, first + u]] += terms[u]

    sensors.run(add)


SENSOR_SCRATCH = (
    pltpu.VMEM((SLOTS, BLK, BLK), BF16),
    pltpu.SemaphoreType.DMA((SLOTS // CHUNK,)),
)


def forward(count, rows, cols, sens, wavelet):
    held, sems = SENSOR_SCRATCH
    return pl.pallas_call(
        forward_kernel,
        out_shape=jax.ShapeDtypeStruct((ROW_BLOCKS, BLK, BLK), F32),
        in_specs=[SMEM, SMEM, SMEM, ANY, ANY],
        out_specs=VMEM,
        scratch_shapes=[
            held,
            pltpu.VMEM(wavelet.shape, BF16),
            pltpu.SemaphoreType.DMA,
            sems,
        ],
        compiler_params=pltpu.CompilerParams(vmem_limit_bytes=VMEM_LIMIT),
        name="forward",
    )(count, rows, cols, sens, wavelet)


class Ring:
    def __init__(self, me, plus, minus, send, recv, far=None):
        self.me, self.plus, self.minus = me, plus, minus
        self.others = ((2, far), (1, plus), (3, minus))
        self.send, self.recv = send, recv
        self.started = []

    def at(self, step):
        return lax.rem(self.me + step, 4)

    def copy(self, src, dst, device, slot):
        copy = remote(src, dst, self.send.at[slot], self.recv.at[slot], device)
        copy.start()
        self.started.append(copy)

    def arrived(self, ref, slot):
        remote(ref, ref, self.send.at[slot], self.recv.at[slot], self.plus).wait_recv()

    def drain(self):
        for copy in self.started:
            copy.wait_send()
        self.started = []


class Reduce:
    def __init__(self, ring, data, base, chunk, relay, landed):
        self.ring, self.data, self.base, self.chunk = ring, data, base, chunk
        self.half = chunk // 2
        self.relay, self.landed = relay, landed

    def rows(self, step, h):
        start = self.base + self.ring.at(step) * self.chunk + h * self.half
        return pl.ds(pl.multiple_of(start, self.half), self.half)

    def relay_at(self, side):
        return self.relay.at[side, pl.ds(0, self.half)]

    def landed_at(self, side, h):
        return self.landed.at[side, pl.ds(h * self.half, self.half)]

    def begin(self):
        ring, data = self.ring, self.data
        ring.copy(data.at[self.rows(2, 0)], self.relay_at(0), ring.plus, 0)
        ring.copy(data.at[self.rows(2, 1)], self.relay_at(1), ring.minus, 1)
        ring.copy(data.at[self.rows(1, 1)], self.landed_at(0, 1), ring.plus, 2)
        ring.copy(data.at[self.rows(3, 0)], self.landed_at(1, 0), ring.minus, 3)

    def pass_on(self):
        ring, data = self.ring, self.data
        ring.arrived(self.relay_at(0), 0)
        data[self.rows(1, 0), :] += self.relay[0, : self.half]
        ring.copy(data.at[self.rows(1, 0)], self.landed_at(0, 0), ring.plus, 4)
        ring.arrived(self.relay_at(1), 1)
        data[self.rows(3, 1), :] += self.relay[1, : self.half]
        ring.copy(data.at[self.rows(3, 1)], self.landed_at(1, 1), ring.minus, 5)

    def finish(self):
        ring, data = self.ring, self.data
        ring.arrived(self.landed_at(0, 1), 2)
        ring.arrived(self.landed_at(1, 0), 3)
        ring.arrived(self.landed_at(0, 0), 4)
        ring.arrived(self.landed_at(1, 1), 5)
        for h in range(2):
            part = pl.ds(h * self.half, self.half)
            data[self.rows(0, h), :] += self.landed[0, part, :] + self.landed[1, part, :]


class DirectReduce:
    def __init__(self, ring, data, base, chunk, landed):
        self.ring, self.data, self.base, self.chunk = ring, data, base, chunk
        self.landed = landed

    def rows(self, step):
        start = self.base + self.ring.at(step) * self.chunk
        return pl.ds(pl.multiple_of(start, self.chunk), self.chunk)

    def begin(self):
        for step, device in self.ring.others:
            self.ring.copy(
                self.data.at[self.rows(step)], self.landed.at[step - 1], device, step - 1
            )

    def pass_on(self):
        for step in range(3):
            self.ring.arrived(self.landed.at[step], step)

    def finish(self):
        own = self.rows(0)
        total = self.data[own, :] + self.landed[0]
        self.data[own, :] = total + (self.landed[1] + self.landed[2])


class DirectGather:
    def __init__(self, ring, data, base, chunk):
        self.ring, self.data, self.base, self.chunk = ring, data, base, chunk

    def rows(self, step):
        start = self.base + self.ring.at(step) * self.chunk
        return self.data.at[pl.ds(pl.multiple_of(start, self.chunk), self.chunk)]

    def begin(self):
        for step, device in self.ring.others:
            self.ring.copy(self.rows(0), self.rows(0), device, step - 1)

    def pass_on(self):
        pass

    def finish(self):
        for step in (1, 3, 2):
            self.ring.arrived(self.rows(4 - step), step - 1)


STREAMS = 4
STREAM = ROW_BLOCKS * BLK // STREAMS
BIG = STREAM // 4
SMALL = BIG // 4


def combine_kernel(partial, image, fill, big_relay, big_landed, small_landed, send, recv):
    row, col, _, _ = place()
    y, x = lax.div(col, 4), lax.rem(col, 4)
    x_ring = [(row, y * 4 + lax.rem(x + step, 4)) for step in range(4)]
    y_ring = [(row, lax.rem(y + step, 4) * 4 + x) for step in range(4)]
    greet(x_ring[1:] + y_ring[1:])
    fill.wait()

    def ring(axis, slot):
        me, devices = ((x, x_ring), (y, y_ring))[axis]
        return Ring(me, devices[1], devices[3], send.at[slot], recv.at[slot], devices[2])

    streams = range(STREAMS)
    axis = [a % 2 for a in streams]
    bases = [a * STREAM for a in streams]
    inner = [bases[a] + (x, y)[axis[a]] * BIG for a in streams]
    wide_rings = [ring(axis[a], a) for a in streams]
    cross_rings = [ring(1 - axis[a], STREAMS + a) for a in streams]
    back_rings = [ring(1 - axis[a], 2 * STREAMS + a) for a in streams]
    last_rings = [ring(axis[a], 3 * STREAMS + a) for a in streams]
    wide = [Reduce(wide_rings[a], partial, bases[a], BIG, big_relay.at[a], big_landed.at[a]) for a in streams]
    cross = [DirectReduce(cross_rings[a], partial, inner[a], SMALL, small_landed.at[a]) for a in streams]
    back = [DirectGather(back_rings[a], image, inner[a], SMALL) for a in streams]
    last = [DirectGather(last_rings[a], image, bases[a], BIG) for a in streams]

    def cast(a):
        start = inner[a] + (y, x)[axis[a]] * SMALL
        own = pl.ds(pl.multiple_of(start, SMALL), SMALL)
        image[own, :] = partial[own, :].astype(BF16)

    pairs = [(a, a + 1) for a in range(0, STREAMS, 2)]
    for a in streams:
        wide[a].begin()
    for a in streams:
        wide[a].pass_on()
    for pair in pairs:
        for a in pair:
            wide[a].finish()
            cross[a].begin()
    for pair in pairs:
        for a in pair:
            cross[a].pass_on()
            cross[a].finish()
            cast(a)
            back[a].begin()
    for pair in pairs:
        for a in pair:
            back[a].finish()
            last[a].begin()
    for a in streams:
        last[a].finish()
    for group in (wide_rings, cross_rings, back_rings, last_rings):
        for one in group:
            one.drain()


def combine(partial):
    vmem = pl.BlockSpec(memory_space=pltpu.VMEM)
    rows = ROW_BLOCKS * BLK

    def kernel(partial_ref, image_ref, data, *rest):
        copy = pltpu.make_async_copy(partial_ref, data, rest[-1])
        copy.start()
        combine_kernel(data, image_ref, copy, *rest[:-1])

    return pl.pallas_call(
        kernel,
        out_shape=jax.ShapeDtypeStruct((rows, BLK), BF16),
        in_specs=[pl.BlockSpec(memory_space=pl.ANY)],
        out_specs=vmem,
        scratch_shapes=[
            pltpu.VMEM((rows, BLK), F32),
            pltpu.VMEM((STREAMS, 2, BIG // 2, BLK), F32),
            pltpu.VMEM((STREAMS, 2, BIG, BLK), F32),
            pltpu.VMEM((STREAMS, 3, SMALL, BLK), F32),
            pltpu.SemaphoreType.DMA((4 * STREAMS, 6)),
            pltpu.SemaphoreType.DMA((4 * STREAMS, 6)),
            pltpu.SemaphoreType.DMA,
        ],
        compiler_params=pltpu.CompilerParams(
            collective_id=1, has_side_effects=True, vmem_limit_bytes=VMEM_LIMIT
        ),
        cost_estimate=cost(1 << 20, 80 << 20),
        name="combine",
    )(partial.reshape(rows, BLK))


def adjoint_kernel(
    count, rows, cols, source, image_hbm, data_image, adjoint, held, image, flipped, plain, sem, sems
):
    load = pltpu.make_async_copy(image_hbm, image, sem.at[0])
    load.start()
    sensors = Sensors(count, source, held, sems)
    sensors.start()
    adjoint[...] = jnp.zeros_like(adjoint)
    load.wait()

    def flip(b, carry):
        block = image[b].astype(F32)
        plain[b] = block
        flipped[b] = block.T.astype(BF16)
        return carry

    lax.fori_loop(0, ROW_BLOCKS, flip, 0, unroll=2)
    store = pltpu.make_async_copy(plain, data_image, sem.at[1])
    store.start()
    shift = lax.axis_index("cols") >> 1

    def add(first, width):
        terms = []
        for u in range(width):
            terms.append(dot(flipped[rows[0, first + u]], held[first + u]))
        for u in range(width):
            at = cols[0, first + u]
            part = at >> 3
            adjoint[(at >> 2) & 1, at & 3, (part + shift) & 1, part >> 1] += terms[u]

    sensors.run(add)
    store.wait()


def adjoin(count, rows, cols, sens, image):
    held, sems = SENSOR_SCRATCH
    return pl.pallas_call(
        adjoint_kernel,
        out_shape=(
            jax.ShapeDtypeStruct((ROW_BLOCKS, BLK, BLK), F32),
            jax.ShapeDtypeStruct((2, NZ, 2, GROUP, BLK, BLK), F32),
        ),
        in_specs=[SMEM, SMEM, SMEM, ANY, ANY],
        out_specs=(ANY, VMEM),
        scratch_shapes=[
            held,
            pltpu.VMEM((ROW_BLOCKS, BLK, BLK), BF16),
            pltpu.VMEM((ROW_BLOCKS, BLK, BLK), BF16),
            pltpu.VMEM((ROW_BLOCKS, BLK, BLK), F32),
            pltpu.SemaphoreType.DMA((2,)),
            sems,
        ],
        compiler_params=pltpu.CompilerParams(vmem_limit_bytes=VMEM_LIMIT),
        name="adjoin",
    )(count, rows, cols, sens, image)


def return_kernel(
    partial, smooth, scale, signs, out, own, stage, pair, relay_out, relay, landed, gathered, sem, send, recv, *sem_refs
):
    where = place()
    row, col, z, core = where
    fill = pltpu.make_async_copy(partial.at[core], own, sem)
    fill.start()
    exchange = Exchange(stage, out, sem_refs, where)
    plus, minus, partner = exchange.neighbour(1), exchange.neighbour(3), exchange.partner()
    greet([plus, minus, partner], (exchange.first, exchange.device))
    rings = [Ring(z, plus, minus, send.at[p], recv.at[p]) for p in range(2)]
    half = GROUP // 2
    for p in range(2):
        ring = rings[p]
        for slot, step in ((6, 2), (7, 1), (8, 3), (9, 0)):
            q = ring.at(step)
            ring.copy(partial.at[1 - core, q, p], pair.at[q, p], partner, slot)
    fill.wait()

    def total(p, step, h):
        group = pl.ds(h * half, half)
        q = rings[p].at(step)
        return own[q, p, group] + pair[q, p, group]

    def paired(p, step, slot):
        rings[p].arrived(pair.at[rings[p].at(step), p], slot)

    def ship(p, value, slot, dst, device, sem):
        relay_out[p, slot] = value.astype(BF16)
        rings[p].copy(relay_out.at[p, slot], dst, device, sem)

    for p in range(2):
        paired(p, 2, 6)
        ship(p, total(p, 2, 0), 0, relay.at[p, 0], plus, 0)
        ship(p, total(p, 2, 1), 1, relay.at[p, 1], minus, 1)
        paired(p, 1, 7)
        ship(p, total(p, 1, 1), 3, landed.at[p, 0, 1], plus, 2)
        paired(p, 3, 8)
        ship(p, total(p, 3, 0), 4, landed.at[p, 1, 0], minus, 3)
    for p in range(2):
        ring = rings[p]
        ring.arrived(relay.at[p, 0], 0)
        ship(p, total(p, 1, 0) + relay[p, 0].astype(F32), 2, landed.at[p, 0, 0], plus, 4)
        ring.arrived(relay.at[p, 1], 1)
        ship(p, total(p, 3, 1) + relay[p, 1].astype(F32), 5, landed.at[p, 1, 1], minus, 5)
    lane_scale = scale[0:1, :]
    mine = lax.div(col, 2)

    def member(p, i):
        return i * 2 + lax.rem(mine + p, 2)

    for p in range(2):
        ring = rings[p]
        paired(p, 0, 9)
        for slot, ref in ((2, landed.at[p, 0, 1]), (3, landed.at[p, 1, 0]), (4, landed.at[p, 0, 0]), (5, landed.at[p, 1, 1])):
            ring.arrived(ref, slot)
        for i in range(GROUP):
            h, j = i // half, i % half
            value = own[z, p, i] + pair[z, p, i]
            value = value + landed[p, 0, h, j].astype(F32) + landed[p, 1, h, j].astype(F32)
            stage[member(p, i)] = (value * lane_scale).astype(BF16)

        def spread(i, carry, p=p):
            exchange.copy(2 * i + p, gathered).start()
            return carry

        if p == 0:

            @pl.when(exchange.first == 1)
            def _():
                gathered[mine] = stage[mine]

        lax.fori_loop(exchange.first if p == 0 else 0, GROUP, spread, 0)

    for p in range(2):

        def synthesise(i, carry, p=p):
            m = member(p, i)
            exchange.wait_part(m, gathered)
            cells = lax.dot_general(
                signs[...], gathered[m], (((1,), (1,)), ((), ())), preferred_element_type=F32
            )
            out[z, core, p * GROUP + i] = (cells + smooth[m]).astype(BF16)
            return carry

        lax.fori_loop(0, GROUP, synthesise, 0)
        exchange.begin(p)
    exchange.finish()
    exchange.drain_parts(gathered)
    for ring in rings:
        ring.drain()


def give_back(partial, smooth):
    vmem = pl.BlockSpec(memory_space=pltpu.VMEM)
    half = GROUP // 2
    return pl.pallas_call(
        return_kernel,
        out_shape=jax.ShapeDtypeStruct((NZ, 2, PARTS, BLK, BLK), BF16),
        in_specs=[ANY, vmem, vmem, vmem],
        out_specs=vmem,
        scratch_shapes=[
            pltpu.VMEM((NZ, 2, GROUP, BLK, BLK), F32),
            pltpu.VMEM((PARTS, BLK, BLK), BF16),
            pltpu.VMEM((NZ, 2, GROUP, BLK, BLK), F32),
            pltpu.VMEM((2, 6, half, BLK, BLK), BF16),
            pltpu.VMEM((2, 2, half, BLK, BLK), BF16),
            pltpu.VMEM((2, 2, 2, half, BLK, BLK), BF16),
            pltpu.VMEM((PARTS, BLK, BLK), BF16),
            pltpu.SemaphoreType.DMA,
            pltpu.SemaphoreType.DMA((2, 10)),
            pltpu.SemaphoreType.DMA((2, 10)),
            *EXCHANGE_SEMS,
        ],
        compiler_params=pltpu.CompilerParams(
            collective_id=2, has_side_effects=True, vmem_limit_bytes=VMEM_LIMIT
        ),
        cost_estimate=cost(1 << 30, 80 << 20),
        name="give_back",
    )(
        partial,
        smooth,
        jnp.asarray(np.broadcast_to(SCALE[None, :], (8, BLK)), F32),
        jnp.asarray(SIGNS.T, BF16),
    )


def place_kernel(order, product_hbm, out, product, cells, in_sems, out_sems):
    def load(i):
        at = lax.div(i, 2), lax.rem(i, 2)
        return pltpu.make_async_copy(product_hbm.at[at], product.at[at], in_sems.at[i])

    def store(i, block):
        return pltpu.make_async_copy(cells.at[i], out.at[block], out_sems.at[i])

    for i in range(2 * NZ):
        load(i).start()
    shift = lax.axis_index("cols") >> 1
    for i in range(2 * NZ):
        load(i).wait()
        for n in range(PARTS):
            q, core, p = i // 2, i % 2, n // GROUP
            at = i * PARTS + n
            cells[at] = product[q, core, n].astype(F32)
            m = (n % GROUP) * 2 + ((shift + p) & 1)
            store(at, order[0, (m * 2 + core) * 4 + q]).start()

    def finish(i, carry):
        store(i, 0).wait()
        return carry

    lax.fori_loop(0, COL_BLOCKS, finish, 0)


def place_cells(order, product):
    return pl.pallas_call(
        place_kernel,
        out_shape=jax.ShapeDtypeStruct((COL_BLOCKS, BLK, BLK), F32),
        in_specs=[SMEM, ANY],
        out_specs=ANY,
        scratch_shapes=[
            pltpu.VMEM(product.shape, BF16),
            pltpu.VMEM((COL_BLOCKS, BLK, BLK), F32),
            pltpu.SemaphoreType.DMA((2 * NZ,)),
            pltpu.SemaphoreType.DMA((COL_BLOCKS,)),
        ],
        compiler_params=pltpu.CompilerParams(vmem_limit_bytes=VMEM_LIMIT),
        name="place_cells",
    )(order, product)


def local(model_dir, sens_blocks, blk_row, blk_col, blk_count, send_order, neighbors, face_weight):
    wavelet, smooth = analyse(send_order, model_dir, neighbors, face_weight)
    partial_image = forward(blk_count, blk_row, blk_col, sens_blocks, wavelet)
    image_half = combine(partial_image).reshape(ROW_BLOCKS, BLK, BLK)
    data_image, partial_adjoint = adjoin(blk_count, blk_row, blk_col, sens_blocks, image_half)
    normal_product = place_cells(send_order, give_back(partial_adjoint, smooth))
    return data_image.reshape(ROW_BLOCKS * BLK, BLK), normal_product.reshape(CELLS, BLK)


def solution(mesh):
    placed = (
        P("cols", None),
        P("rows", "cols", None, None),
        P("rows", "cols"),
        P("rows", "cols"),
        P("rows", "cols"),
        P("cols", None),
        P(None, "cols"),
        P(None, "cols"),
    )
    return jax.shard_map(
        local,
        mesh=mesh,
        in_specs=placed,
        out_specs=(P("rows", None), P("cols", None)),
        check_vma=False,
    )
```

```python
import math

import jax
import jax.numpy as jnp
import numpy as np
from jax import lax
from jax.experimental import pallas as pl
from jax.experimental.pallas import tpu as pltpu
from jax.sharding import PartitionSpec as P

BLK = 128
RIM = 64
NROWS = 8
NCOLS = 16
NZ = 4
ROW_BLOCKS = 32
COL_BLOCKS = 64
SLOTS = 384
CHUNK = 32
VMEM_LIMIT = 56 << 20
MESH = pl.DeviceIdType.MESH
F32 = jnp.float32
BF16 = jnp.bfloat16


VMEM = pl.BlockSpec(memory_space=pltpu.VMEM)
SMEM = pl.BlockSpec(memory_space=pltpu.SMEM)
ANY = pl.BlockSpec(memory_space=pl.ANY)


def cost(flops, moved):
    return pl.CostEstimate(flops=flops, bytes_accessed=moved, transcendentals=0)


def haar_parts():
    matrix = np.ones((1, 1))
    while matrix.shape[0] < BLK:
        length = matrix.shape[0]
        upper = np.kron(matrix, np.array([[1.0, 1.0]]))
        lower = np.kron(np.eye(length), np.array([[1.0, -1.0]]))
        matrix = np.concatenate([upper, lower], axis=0) / math.sqrt(2.0)
    scale = np.abs(matrix).max(axis=1)
    signs = np.round(matrix / scale[:, None])
    return signs, scale


SIGNS, SCALE = haar_parts()


def split(value):
    high = value.astype(BF16)
    low = (value - high.astype(F32)).astype(BF16)
    return high, low


def dot(a, b):
    return jnp.dot(a, b, preferred_element_type=F32)


def remote(src, dst, send_sem, recv_sem, device):
    return pltpu.make_async_remote_copy(
        src_ref=src,
        dst_ref=dst,
        send_sem=send_sem,
        recv_sem=recv_sem,
        device_id=device,
        device_id_type=MESH,
    )


def place():
    row = lax.axis_index("rows")
    col = lax.axis_index("cols")
    return row, col, lax.div(row, 2), lax.rem(row, 2)


def z_device(z, step, core, col):
    return (lax.rem(z + step, NZ) * 2 + core, col)


def greet(devices, extra=None):
    barrier = pltpu.get_barrier_semaphore()
    for device in devices:
        pl.semaphore_signal(barrier, inc=1, device_id=device, device_id_type=MESH)
    count = len(devices)
    if extra is not None:
        first, device_of = extra

        def signal(i, carry):
            pl.semaphore_signal(barrier, inc=1, device_id=device_of(i), device_id_type=MESH)
            return carry

        lax.fori_loop(first, PARTS, signal, 0)
        count = count + PARTS - first

    def wait_for_all():
        pl.semaphore_wait(barrier, count)

    return wait_for_all


PARTS = NCOLS // 2
GROUP = PARTS // 2


class RowGather:
    def __init__(self, piece, sem_refs, where):
        self.piece_of = piece
        self.g_send, self.minus, self.plus, self.far, self.pair = sem_refs
        self.row, self.col, self.z, self.core = where
        self.sends = []

    def piece(self, step, p, core=None):
        return self.piece_of(lax.rem(self.z + step, NZ), self.core if core is None else core, p)

    def send(self, step, p, device, recv_sem):
        piece = self.piece(step, p)
        copy = remote(piece, piece, self.g_send.at[len(self.sends)], recv_sem, device)
        copy.start()
        self.sends.append(copy)

    def arrived(self, step, p, recv_sem, core=None):
        piece = self.piece(step, p, core)
        remote(piece, piece, self.g_send.at[0], recv_sem, self.partner()).wait_recv()

    def partner(self):
        return self.z * 2 + 1 - self.core, self.col

    def neighbour(self, step):
        return z_device(self.z, step, self.core, self.col)

    def begin(self, p):
        self.send(0, p, self.neighbour(1), self.minus.at[p])
        self.send(0, p, self.neighbour(3), self.plus.at[p])
        self.send(0, p, self.partner(), self.pair.at[0, p])

    def pass_on(self):
        self.arrived(3, 0, self.minus.at[0])
        self.send(3, 0, self.neighbour(1), self.far.at[0])
        self.send(3, 0, self.partner(), self.pair.at[3, 0])
        self.arrived(1, 1, self.plus.at[1])
        self.send(1, 1, self.neighbour(3), self.far.at[1])
        self.send(1, 1, self.partner(), self.pair.at[1, 1])
        self.arrived(1, 0, self.plus.at[0])
        self.send(1, 0, self.partner(), self.pair.at[1, 0])
        self.arrived(3, 1, self.minus.at[1])
        self.send(3, 1, self.partner(), self.pair.at[3, 1])

    def finish(self):
        for p in range(2):
            self.arrived(2, p, self.far.at[p])
            self.send(2, p, self.partner(), self.pair.at[2, p])
        for p in range(2):
            for step in (0, 1, 3, 2):
                self.arrived(step, p, self.pair.at[step, p], 1 - self.core)
        for copy in self.sends:
            copy.wait_send()


GATHER_SEMS = [
    pltpu.SemaphoreType.DMA((14,)),
    pltpu.SemaphoreType.DMA((2,)),
    pltpu.SemaphoreType.DMA((2,)),
    pltpu.SemaphoreType.DMA((2,)),
    pltpu.SemaphoreType.DMA((4, 2)),
]


class Parts:
    def __init__(self, where):
        self.row, self.col, self.z, self.core = where
        self.mine = lax.div(self.col, 2)
        self.first = jnp.where(self.core == lax.rem(self.col, 2), 1, 0)

    def slot(self, i):
        return lax.rem(self.mine + i, PARTS)

    def device_at(self, m):
        return self.z * 2 + lax.rem(self.col, 2), m * 2 + self.core

    def device(self, i):
        return self.device_at(self.slot(i))

    def own(self, m):
        return m * 2 + self.core == self.col


CELLS = COL_BLOCKS * BLK


def cells_of(body, block):
    return jnp.concatenate([body[2 * block], body[2 * block + 1]], axis=0)


def tabulate(neighbors, weights, tables, first_cell):
    def tile(t, carry):
        at = pl.ds(pl.multiple_of(t * BLK, BLK), BLK)
        near = (neighbors[:, at] - (first_cell + t * BLK - RIM)).astype(F32)
        tables[t] = jnp.concatenate([near, weights[:, at]], axis=0)
        return carry

    lax.fori_loop(0, COL_BLOCKS, tile, 0)


def smooth_tile(body, rims, tables, tile):
    table = tables[tile].T
    span = lax.broadcasted_iota(jnp.int32, (BLK, 2 * BLK), 1).astype(F32)
    mix = jnp.zeros((BLK, 2 * BLK), F32)
    for face in range(4):
        mix += jnp.where(table[:, face : face + 1] == span, table[:, 4 + face : 5 + face], 0.0)
    mix_high, mix_low = split(mix)
    center = cells_of(body, tile)
    last = COL_BLOCKS - 1
    low = jnp.where(tile == 0, rims[0], body[jnp.maximum(2 * tile - 1, 0)])
    high = jnp.where(tile == last, rims[1], body[jnp.minimum(2 * tile + 2, 2 * last)])
    window = jnp.concatenate([low, center, high], axis=0)
    near_high, near_low = split(window)
    mixed = dot(mix_high, near_high) + dot(mix_low, near_high) + dot(mix_high, near_low)
    total = table[:, 4:5] + table[:, 5:6] + table[:, 6:7] + table[:, 7:8]
    return total * center - mixed


RING_BLOCKS = COL_BLOCKS // 2


def ring_place(z, core, part):
    return (z * 2 + core) * GROUP + part


def plane_place(core, part):
    return RING_BLOCKS + (core * PARTS + part) * 2


def analyse_kernel(
    order,
    model,
    neighbors_hbm,
    weights_hbm,
    signs_hbm,
    scale_hbm,
    wavelet,
    smooth,
    body,
    neighbors,
    weights,
    signs,
    scale,
    rims,
    tables,
    ring_stage,
    plane_stage,
    sems,
    ring_send,
    ring_recv,
    plane_send,
    plane_recv,
    plane_pair,
    *gather_sems,
):
    where = place()
    row, col, z, core = where
    fills = [
        pltpu.make_async_copy(src, dst, sems.at[4 + i])
        for i, (src, dst) in enumerate(
            (
                (model, body),
                (signs_hbm, signs),
                (scale_hbm, scale),
                (neighbors_hbm, neighbors),
                (weights_hbm, weights),
            )
        )
    ]
    for fill in fills:
        fill.start()
    parts = Parts(where)
    mine, lane = parts.mine, lax.div(z, 2)

    def ring_piece(at, k, p):
        return wavelet.at[pl.ds(ring_place(at, k, p * 2), 2)]

    gather = RowGather(ring_piece, gather_sems, where)
    below, above = (row, lax.rem(col + NCOLS - 1, NCOLS)), (row, lax.rem(col + 1, NCOLS))
    wait_for_all = greet(
        [gather.neighbour(1), gather.neighbour(3), gather.partner(), below, above],
        (parts.first, parts.device),
    )
    up = remote(
        model.at[2 * COL_BLOCKS - 1],
        rims.at[0],
        sems.at[0],
        sems.at[2],
        above,
    )
    down = remote(
        model.at[0],
        rims.at[1],
        sems.at[1],
        sems.at[3],
        below,
    )
    for fill in fills:
        fill.wait()
    sign_pair = jnp.concatenate([signs[...], signs[...]], axis=1)

    def block_of(m, q):
        return order[0, (m * 2 + core) * 4 + q]

    def coefficients(m, q):
        high, low = split(cells_of(body, block_of(m, q)))
        product = dot(sign_pair, jnp.concatenate([high, low], axis=0))
        return (product * scale[...]).astype(BF16)

    def ring_part(i):
        return i * 2 + lax.rem(lane + mine, 2)

    def make_ring(i, carry):
        ring_stage[i] = coefficients(ring_part(i), 2 + lax.rem(z, 2))
        return carry

    lax.fori_loop(0, GROUP, make_ring, 0)
    wait_for_all()

    def ring_copy(i):
        return remote(
            ring_stage.at[i],
            wavelet.at[ring_place(z, lax.rem(col, 2), lax.div(mine, 2))],
            ring_send.at[i],
            ring_recv.at[lax.div(mine, 2)],
            parts.device_at(ring_part(i)),
        )

    def spread_ring(i, carry):
        @pl.when(parts.own(ring_part(i)))
        def _():
            wavelet[ring_place(z, core, lax.div(mine, 2))] = ring_stage[i]

        @pl.when(jnp.logical_not(parts.own(ring_part(i))))
        def _():
            ring_copy(i).start()

        return carry

    lax.fori_loop(0, GROUP, spread_ring, 0)
    up.start()
    down.start()

    def plane_copy(i):
        return remote(
            plane_stage.at[i],
            wavelet.at[pl.ds(plane_place(lax.rem(col, 2), mine), 2)],
            plane_send.at[i],
            plane_recv.at[mine],
            parts.device(i),
        )

    def spread_plane(i, carry):
        for q in range(2):
            plane_stage[i, q] = coefficients(parts.slot(i), q)
        plane_copy(i).start()
        return carry

    lax.fori_loop(parts.first, PARTS, spread_plane, 0)

    @pl.when(parts.first == 1)
    def _():
        for q in range(2):
            wavelet[plane_place(core, mine) + q] = coefficients(mine, q)

    def wait_ring(i, carry):
        @pl.when(jnp.logical_not(parts.own(ring_part(i))))
        def _():
            ref = wavelet.at[ring_place(z, core, i)]
            remote(ref, ref, ring_send.at[0], ring_recv.at[i], gather.partner()).wait_recv()

        return carry

    def wait_plane(m, carry):
        @pl.when(jnp.logical_not(parts.own(m)))
        def _():
            ref = wavelet.at[pl.ds(plane_place(core, m), 2)]
            remote(ref, ref, plane_send.at[0], plane_recv.at[m], gather.partner()).wait_recv()

        return carry

    def half_plane(core_of, h):
        return wavelet.at[pl.ds(plane_place(core_of, h * GROUP), PARTS)]

    def swap(h):
        ref = half_plane(core, h)
        return remote(ref, ref, plane_pair.at[h], plane_pair.at[2 + h], gather.partner())

    def smooth_one(m, carry):
        smooth[m] = smooth_tile(body, rims, tables, block_of(m, z))
        return carry

    for p in range(2):
        lax.fori_loop(2 * p, 2 * p + 2, wait_ring, 0)
        gather.begin(p)
    tabulate(neighbors, weights, tables, col * CELLS)
    up.wait_recv()
    down.wait_recv()
    lax.fori_loop(0, 2, smooth_one, 0)
    gather.pass_on()
    lax.fori_loop(2, PARTS, smooth_one, 0)
    for h in range(2):
        lax.fori_loop(h * GROUP, (h + 1) * GROUP, wait_plane, 0)
        swap(h).start()
    gather.finish()
    for h in range(2):
        ref = half_plane(1 - core, h)
        remote(ref, ref, plane_pair.at[h], plane_pair.at[2 + h], gather.partner()).wait_recv()
        swap(h).wait_send()

    def drain_ring(i, carry):
        @pl.when(jnp.logical_not(parts.own(ring_part(i))))
        def _():
            ring_copy(i).wait_send()

        return carry

    def drain_plane(i, carry):
        plane_copy(i).wait_send()
        return carry

    lax.fori_loop(0, GROUP, drain_ring, 0)
    lax.fori_loop(parts.first, PARTS, drain_plane, 0)
    up.wait_send()
    down.wait_send()


def analyse(order, model, neighbors, weights):
    return pl.pallas_call(
        analyse_kernel,
        out_shape=(
            jax.ShapeDtypeStruct((COL_BLOCKS, BLK, BLK), BF16),
            jax.ShapeDtypeStruct((PARTS, BLK, BLK), F32),
        ),
        in_specs=[SMEM, *[ANY] * 5],
        out_specs=(VMEM, VMEM),
        scratch_shapes=[
            pltpu.VMEM((2 * COL_BLOCKS, RIM, BLK), F32),
            pltpu.VMEM((4, CELLS), jnp.int32),
            pltpu.VMEM((4, CELLS), F32),
            pltpu.VMEM((BLK, BLK), BF16),
            pltpu.VMEM((BLK, BLK), F32),
            pltpu.VMEM((2, RIM, BLK), F32),
            pltpu.VMEM((COL_BLOCKS, 8, BLK), F32),
            pltpu.VMEM((GROUP, BLK, BLK), BF16),
            pltpu.VMEM((PARTS, 2, BLK, BLK), BF16),
            pltpu.SemaphoreType.DMA((9,)),
            pltpu.SemaphoreType.DMA((GROUP,)),
            pltpu.SemaphoreType.DMA((GROUP,)),
            pltpu.SemaphoreType.DMA((PARTS,)),
            pltpu.SemaphoreType.DMA((PARTS,)),
            pltpu.SemaphoreType.DMA((4,)),
            *GATHER_SEMS,
        ],
        compiler_params=pltpu.CompilerParams(
            collective_id=0, has_side_effects=True, vmem_limit_bytes=VMEM_LIMIT
        ),
        cost_estimate=cost(1 << 30, 60 << 20),
        name="analyse",
    )(
        order,
        model.reshape(2 * COL_BLOCKS, RIM, BLK),
        neighbors,
        weights,
        jnp.asarray(SIGNS, BF16),
        jnp.asarray(np.broadcast_to(SCALE[:, None], (BLK, BLK)), F32),
    )


class Sensors:
    def __init__(self, count, source, held, sems):
        self.live, self.source, self.held, self.sems = count[0, 0], source, held, sems

    def copy(self, g):
        part = pl.ds(g * CHUNK, CHUNK)
        return pltpu.make_async_copy(self.source.at[0, part], self.held.at[part], self.sems.at[g])

    def start(self):
        def begin(g, carry):
            self.copy(g).start()
            return carry

        lax.fori_loop(0, pl.cdiv(self.live, CHUNK), begin, 0)

    def run(self, add):
        full = self.live // CHUNK

        def group(g, carry):
            self.copy(g).wait()
            add(g * CHUNK, CHUNK)
            return carry

        lax.fori_loop(0, full, group, 0)
        done = full * CHUNK

        @pl.when(done < self.live)
        def _():
            self.copy(full).wait()

        for width in (4, 1):

            def few(g, carry, width=width, done=done):
                add(done + g * width, width)
                return carry

            groups = (self.live - done) // width
            lax.fori_loop(0, groups, few, 0)
            done = done + groups * width


def forward_kernel(count, rows, cols, source, wavelet_hbm, image, held, wavelet, places, sem, sems):
    load = pltpu.make_async_copy(wavelet_hbm, wavelet, sem)
    load.start()
    sensors = Sensors(count, source, held, sems)
    sensors.start()
    image[...] = jnp.zeros_like(image)
    mine = lax.axis_index("cols") >> 1

    def note(at, carry):
        q, core, part = at & 3, (at >> 2) & 1, at >> 3
        by_ring = ring_place(2 * ((part + mine) & 1) + (q & 1), core, part >> 1)
        places[at] = jnp.where(q >= 2, by_ring, plane_place(core, part) + q)
        return carry

    lax.fori_loop(0, COL_BLOCKS, note, 0)
    load.wait()

    def add(first, width):
        terms = []
        for u in range(width):
            terms.append(dot(held[first + u], wavelet[places[cols[0, first + u]]]))
        for u in range(width):
            image[rows[0, first + u]] += terms[u]

    sensors.run(add)


SENSOR_SCRATCH = (
    pltpu.VMEM((SLOTS, BLK, BLK), BF16),
    pltpu.SemaphoreType.DMA((SLOTS // CHUNK,)),
)


def forward(count, rows, cols, sens, wavelet):
    held, sems = SENSOR_SCRATCH
    return pl.pallas_call(
        forward_kernel,
        out_shape=jax.ShapeDtypeStruct((ROW_BLOCKS, BLK, BLK), F32),
        in_specs=[SMEM, SMEM, SMEM, ANY, ANY],
        out_specs=VMEM,
        scratch_shapes=[
            held,
            pltpu.VMEM(wavelet.shape, BF16),
            pltpu.SMEM((COL_BLOCKS,), jnp.int32),
            pltpu.SemaphoreType.DMA,
            sems,
        ],
        compiler_params=pltpu.CompilerParams(vmem_limit_bytes=VMEM_LIMIT),
        name="forward",
    )(count, rows, cols, sens, wavelet)


class Ring:
    def __init__(self, me, plus, minus, send, recv, far=None):
        self.me, self.plus, self.minus = me, plus, minus
        self.others = ((2, far), (1, plus), (3, minus))
        self.send, self.recv = send, recv
        self.started = []

    def at(self, step):
        return lax.rem(self.me + step, 4)

    def copy(self, src, dst, device, slot):
        copy = remote(src, dst, self.send.at[slot], self.recv.at[slot], device)
        copy.start()
        self.started.append(copy)

    def arrived(self, ref, slot):
        remote(ref, ref, self.send.at[slot], self.recv.at[slot], self.plus).wait_recv()

    def drain(self):
        for copy in self.started:
            copy.wait_send()
        self.started = []


class Reduce:
    def __init__(self, ring, data, base, chunk, relay, landed):
        self.ring, self.data, self.base, self.chunk = ring, data, base, chunk
        self.half = chunk // 2
        self.relay, self.landed = relay, landed

    def rows(self, step, h):
        start = self.base + self.ring.at(step) * self.chunk + h * self.half
        return pl.ds(pl.multiple_of(start, self.half), self.half)

    def relay_at(self, side):
        return self.relay.at[side, pl.ds(0, self.half)]

    def landed_at(self, side, h):
        return self.landed.at[side, pl.ds(h * self.half, self.half)]

    def begin(self):
        ring, data = self.ring, self.data
        ring.copy(data.at[self.rows(2, 0)], self.relay_at(0), ring.plus, 0)
        ring.copy(data.at[self.rows(2, 1)], self.relay_at(1), ring.minus, 1)
        ring.copy(data.at[self.rows(1, 1)], self.landed_at(0, 1), ring.plus, 2)
        ring.copy(data.at[self.rows(3, 0)], self.landed_at(1, 0), ring.minus, 3)

    def pass_on(self):
        ring, data = self.ring, self.data
        ring.arrived(self.relay_at(0), 0)
        data[self.rows(1, 0), :] += self.relay[0, : self.half]
        ring.copy(data.at[self.rows(1, 0)], self.landed_at(0, 0), ring.plus, 4)
        ring.arrived(self.relay_at(1), 1)
        data[self.rows(3, 1), :] += self.relay[1, : self.half]
        ring.copy(data.at[self.rows(3, 1)], self.landed_at(1, 1), ring.minus, 5)

    def finish(self):
        ring, data = self.ring, self.data
        ring.arrived(self.landed_at(0, 1), 2)
        ring.arrived(self.landed_at(1, 0), 3)
        ring.arrived(self.landed_at(0, 0), 4)
        ring.arrived(self.landed_at(1, 1), 5)
        for h in range(2):
            part = pl.ds(h * self.half, self.half)
            data[self.rows(0, h), :] += self.landed[0, part, :] + self.landed[1, part, :]


class DirectReduce:
    def __init__(self, ring, data, base, chunk, landed):
        self.ring, self.data, self.base, self.chunk = ring, data, base, chunk
        self.landed = landed

    def rows(self, step):
        start = self.base + self.ring.at(step) * self.chunk
        return pl.ds(pl.multiple_of(start, self.chunk), self.chunk)

    def begin(self):
        for step, device in self.ring.others:
            self.ring.copy(
                self.data.at[self.rows(step)], self.landed.at[step - 1], device, step - 1
            )

    def pass_on(self):
        for step in range(3):
            self.ring.arrived(self.landed.at[step], step)

    def finish(self):
        own = self.rows(0)
        total = self.data[own, :] + self.landed[0]
        self.data[own, :] = total + (self.landed[1] + self.landed[2])


class DirectGather:
    def __init__(self, ring, data, base, chunk):
        self.ring, self.data, self.base, self.chunk = ring, data, base, chunk

    def rows(self, step):
        start = self.base + self.ring.at(step) * self.chunk
        return self.data.at[pl.ds(pl.multiple_of(start, self.chunk), self.chunk)]

    def begin(self):
        for step, device in self.ring.others:
            self.ring.copy(self.rows(0), self.rows(0), device, step - 1)

    def pass_on(self):
        pass

    def finish(self):
        for step in (1, 3, 2):
            self.ring.arrived(self.rows(4 - step), step - 1)


STREAMS = 4
STREAM = ROW_BLOCKS * BLK // STREAMS
BIG = STREAM // 4
SMALL = BIG // 4


def combine_kernel(partial, image, fill, big_relay, big_landed, small_landed, send, recv):
    row, col, _, _ = place()
    y, x = lax.div(col, 4), lax.rem(col, 4)
    x_ring = [(row, y * 4 + lax.rem(x + step, 4)) for step in range(4)]
    y_ring = [(row, lax.rem(y + step, 4) * 4 + x) for step in range(4)]
    greet(x_ring[1:] + y_ring[1:])()
    fill.wait()

    def ring(axis, slot):
        me, devices = ((x, x_ring), (y, y_ring))[axis]
        return Ring(me, devices[1], devices[3], send.at[slot], recv.at[slot], devices[2])

    streams = range(STREAMS)
    axis = [a % 2 for a in streams]
    bases = [a * STREAM for a in streams]
    inner = [bases[a] + (x, y)[axis[a]] * BIG for a in streams]
    wide_rings = [ring(axis[a], a) for a in streams]
    cross_rings = [ring(1 - axis[a], STREAMS + a) for a in streams]
    back_rings = [ring(1 - axis[a], 2 * STREAMS + a) for a in streams]
    last_rings = [ring(axis[a], 3 * STREAMS + a) for a in streams]
    wide = [Reduce(wide_rings[a], partial, bases[a], BIG, big_relay.at[a], big_landed.at[a]) for a in streams]
    cross = [DirectReduce(cross_rings[a], partial, inner[a], SMALL, small_landed.at[a]) for a in streams]
    back = [DirectGather(back_rings[a], image, inner[a], SMALL) for a in streams]
    last = [DirectGather(last_rings[a], image, bases[a], BIG) for a in streams]

    def cast(a):
        start = inner[a] + (y, x)[axis[a]] * SMALL
        own = pl.ds(pl.multiple_of(start, SMALL), SMALL)
        image[own, :] = partial[own, :].astype(BF16)

    pairs = [(a, a + 1) for a in range(0, STREAMS, 2)]
    for a in streams:
        wide[a].begin()
    for a in streams:
        wide[a].pass_on()
    for pair in pairs:
        for a in pair:
            wide[a].finish()
            cross[a].begin()
    for pair in pairs:
        for a in pair:
            cross[a].pass_on()
            cross[a].finish()
            cast(a)
            back[a].begin()
    for pair in pairs:
        for a in pair:
            back[a].finish()
            last[a].begin()
    for a in streams:
        last[a].finish()
    for group in (wide_rings, cross_rings, back_rings, last_rings):
        for one in group:
            one.drain()


def combine(partial):
    vmem = pl.BlockSpec(memory_space=pltpu.VMEM)
    rows = ROW_BLOCKS * BLK

    def kernel(partial_ref, image_ref, data, *rest):
        copy = pltpu.make_async_copy(partial_ref, data, rest[-1])
        copy.start()
        combine_kernel(data, image_ref, copy, *rest[:-1])

    return pl.pallas_call(
        kernel,
        out_shape=jax.ShapeDtypeStruct((rows, BLK), BF16),
        in_specs=[pl.BlockSpec(memory_space=pl.ANY)],
        out_specs=vmem,
        scratch_shapes=[
            pltpu.VMEM((rows, BLK), F32),
            pltpu.VMEM((STREAMS, 2, BIG // 2, BLK), F32),
            pltpu.VMEM((STREAMS, 2, BIG, BLK), F32),
            pltpu.VMEM((STREAMS, 3, SMALL, BLK), F32),
            pltpu.SemaphoreType.DMA((4 * STREAMS, 6)),
            pltpu.SemaphoreType.DMA((4 * STREAMS, 6)),
            pltpu.SemaphoreType.DMA,
        ],
        compiler_params=pltpu.CompilerParams(
            collective_id=1, has_side_effects=True, vmem_limit_bytes=VMEM_LIMIT
        ),
        cost_estimate=cost(1 << 20, 80 << 20),
        name="combine",
    )(partial.reshape(rows, BLK))


def adjoint_kernel(
    count, rows, cols, source, image_hbm, data_image, adjoint, held, image, flipped, plain, sem, sems
):
    load = pltpu.make_async_copy(image_hbm, image, sem.at[0])
    load.start()
    sensors = Sensors(count, source, held, sems)
    sensors.start()
    adjoint[...] = jnp.zeros_like(adjoint)
    load.wait()

    def flip(b, carry):
        block = image[b].astype(F32)
        plain[b] = block
        flipped[b] = block.T.astype(BF16)
        return carry

    lax.fori_loop(0, ROW_BLOCKS, flip, 0, unroll=2)
    store = pltpu.make_async_copy(plain, data_image, sem.at[1])
    store.start()
    shift = lax.axis_index("cols") >> 1

    def add(first, width):
        terms = []
        for u in range(width):
            terms.append(dot(flipped[rows[0, first + u]], held[first + u]))
        for u in range(width):
            at = cols[0, first + u]
            part = at >> 3
            adjoint[(at >> 2) & 1, at & 3, (part + shift) & 1, part >> 1] += terms[u]

    sensors.run(add)
    store.wait()


def adjoin(count, rows, cols, sens, image):
    held, sems = SENSOR_SCRATCH
    return pl.pallas_call(
        adjoint_kernel,
        out_shape=(
            jax.ShapeDtypeStruct((ROW_BLOCKS, BLK, BLK), F32),
            jax.ShapeDtypeStruct((2, NZ, 2, GROUP, BLK, BLK), F32),
        ),
        in_specs=[SMEM, SMEM, SMEM, ANY, ANY],
        out_specs=(ANY, VMEM),
        scratch_shapes=[
            held,
            pltpu.VMEM((ROW_BLOCKS, BLK, BLK), BF16),
            pltpu.VMEM((ROW_BLOCKS, BLK, BLK), BF16),
            pltpu.VMEM((ROW_BLOCKS, BLK, BLK), F32),
            pltpu.SemaphoreType.DMA((2,)),
            sems,
        ],
        compiler_params=pltpu.CompilerParams(vmem_limit_bytes=VMEM_LIMIT),
        name="adjoin",
    )(count, rows, cols, sens, image)


def return_kernel(
    partial, smooth, scale, signs, out, own, stage, pair, relay_out, relay, landed, gathered, sem, send, recv, part_send, part_recv, *sem_refs
):
    where = place()
    row, col, z, core = where
    fill = pltpu.make_async_copy(partial.at[core], own, sem)
    fill.start()
    parts = Parts(where)
    mine = parts.mine

    def out_piece(at, k, p):
        return out.at[at, k, pl.ds(p * GROUP, GROUP)]

    gather = RowGather(out_piece, sem_refs, where)
    plus, minus, partner = gather.neighbour(1), gather.neighbour(3), gather.partner()
    greet([plus, minus, partner], (parts.first, parts.device))()
    rings = [Ring(z, plus, minus, send.at[p], recv.at[p]) for p in range(2)]
    half = GROUP // 2
    for p in range(2):
        ring = rings[p]
        for slot, step in ((6, 2), (7, 1), (8, 3), (9, 0)):
            q = ring.at(step)
            ring.copy(partial.at[1 - core, q, p], pair.at[q, p], partner, slot)
    fill.wait()

    def total(p, step, h):
        group = pl.ds(h * half, half)
        q = rings[p].at(step)
        return own[q, p, group] + pair[q, p, group]

    def paired(p, step, slot):
        rings[p].arrived(pair.at[rings[p].at(step), p], slot)

    def ship(p, value, slot, dst, device, sem):
        relay_out[p, slot] = value.astype(BF16)
        rings[p].copy(relay_out.at[p, slot], dst, device, sem)

    for p in range(2):
        paired(p, 2, 6)
        ship(p, total(p, 2, 0), 0, relay.at[p, 0], plus, 0)
        ship(p, total(p, 2, 1), 1, relay.at[p, 1], minus, 1)
        paired(p, 1, 7)
        ship(p, total(p, 1, 1), 3, landed.at[p, 0, 1], plus, 2)
        paired(p, 3, 8)
        ship(p, total(p, 3, 0), 4, landed.at[p, 1, 0], minus, 3)
    for p in range(2):
        ring = rings[p]
        ring.arrived(relay.at[p, 0], 0)
        ship(p, total(p, 1, 0) + relay[p, 0].astype(F32), 2, landed.at[p, 0, 0], plus, 4)
        ring.arrived(relay.at[p, 1], 1)
        ship(p, total(p, 3, 1) + relay[p, 1].astype(F32), 5, landed.at[p, 1, 1], minus, 5)
    lane_scale = scale[0:1, :]

    def part_copy(i):
        return remote(
            stage.at[parts.slot(i)],
            gathered.at[mine],
            part_send.at[i],
            part_recv.at[mine],
            parts.device(i),
        )

    def member(p, i):
        return i * 2 + lax.rem(mine + p, 2)

    for p in range(2):
        ring = rings[p]
        paired(p, 0, 9)
        for slot, ref in ((2, landed.at[p, 0, 1]), (3, landed.at[p, 1, 0]), (4, landed.at[p, 0, 0]), (5, landed.at[p, 1, 1])):
            ring.arrived(ref, slot)
        for i in range(GROUP):
            h, j = i // half, i % half
            value = own[z, p, i] + pair[z, p, i]
            value = value + landed[p, 0, h, j].astype(F32) + landed[p, 1, h, j].astype(F32)
            stage[member(p, i)] = (value * lane_scale).astype(BF16)

        def spread(i, carry, p=p):
            part_copy(2 * i + p).start()
            return carry

        if p == 0:

            @pl.when(parts.first == 1)
            def _():
                gathered[mine] = stage[mine]

        lax.fori_loop(parts.first if p == 0 else 0, GROUP, spread, 0)

    for p in range(2):

        def synthesise(i, carry, p=p):
            m = member(p, i)

            @pl.when(jnp.logical_not(parts.own(m)))
            def _():
                ref = gathered.at[m]
                remote(ref, ref, part_send.at[0], part_recv.at[m], partner).wait_recv()

            cells = lax.dot_general(
                signs[...], gathered[m], (((1,), (1,)), ((), ())), preferred_element_type=F32
            )
            out[z, core, p * GROUP + i] = (cells + smooth[m]).astype(BF16)
            return carry

        lax.fori_loop(0, GROUP, synthesise, 0)
        gather.begin(p)
    gather.pass_on()
    gather.finish()

    def drain(i, carry):
        part_copy(i).wait_send()
        return carry

    lax.fori_loop(parts.first, PARTS, drain, 0)
    for ring in rings:
        ring.drain()


def give_back(partial, smooth):
    vmem = pl.BlockSpec(memory_space=pltpu.VMEM)
    half = GROUP // 2
    return pl.pallas_call(
        return_kernel,
        out_shape=jax.ShapeDtypeStruct((NZ, 2, PARTS, BLK, BLK), BF16),
        in_specs=[ANY, vmem, vmem, vmem],
        out_specs=vmem,
        scratch_shapes=[
            pltpu.VMEM((NZ, 2, GROUP, BLK, BLK), F32),
            pltpu.VMEM((PARTS, BLK, BLK), BF16),
            pltpu.VMEM((NZ, 2, GROUP, BLK, BLK), F32),
            pltpu.VMEM((2, 6, half, BLK, BLK), BF16),
            pltpu.VMEM((2, 2, half, BLK, BLK), BF16),
            pltpu.VMEM((2, 2, 2, half, BLK, BLK), BF16),
            pltpu.VMEM((PARTS, BLK, BLK), BF16),
            pltpu.SemaphoreType.DMA,
            pltpu.SemaphoreType.DMA((2, 10)),
            pltpu.SemaphoreType.DMA((2, 10)),
            pltpu.SemaphoreType.DMA((PARTS,)),
            pltpu.SemaphoreType.DMA((PARTS,)),
            *GATHER_SEMS,
        ],
        compiler_params=pltpu.CompilerParams(
            collective_id=2, has_side_effects=True, vmem_limit_bytes=VMEM_LIMIT
        ),
        cost_estimate=cost(1 << 30, 80 << 20),
        name="give_back",
    )(
        partial,
        smooth,
        jnp.asarray(np.broadcast_to(SCALE[None, :], (8, BLK)), F32),
        jnp.asarray(SIGNS.T, BF16),
    )


def place_kernel(order, product_hbm, out, product, cells, in_sems, out_sems):
    def load(i):
        at = lax.div(i, 2), lax.rem(i, 2)
        return pltpu.make_async_copy(product_hbm.at[at], product.at[at], in_sems.at[i])

    def store(i, block):
        return pltpu.make_async_copy(cells.at[i], out.at[block], out_sems.at[i])

    for i in range(2 * NZ):
        load(i).start()
    shift = lax.axis_index("cols") >> 1
    for i in range(2 * NZ):
        load(i).wait()
        for n in range(PARTS):
            q, core, p = i // 2, i % 2, n // GROUP
            at = i * PARTS + n
            cells[at] = product[q, core, n].astype(F32)
            m = (n % GROUP) * 2 + ((shift + p) & 1)
            store(at, order[0, (m * 2 + core) * 4 + q]).start()

    def finish(i, carry):
        store(i, 0).wait()
        return carry

    lax.fori_loop(0, COL_BLOCKS, finish, 0)


def place_cells(order, product):
    return pl.pallas_call(
        place_kernel,
        out_shape=jax.ShapeDtypeStruct((COL_BLOCKS, BLK, BLK), F32),
        in_specs=[SMEM, ANY],
        out_specs=ANY,
        scratch_shapes=[
            pltpu.VMEM(product.shape, BF16),
            pltpu.VMEM((COL_BLOCKS, BLK, BLK), F32),
            pltpu.SemaphoreType.DMA((2 * NZ,)),
            pltpu.SemaphoreType.DMA((COL_BLOCKS,)),
        ],
        compiler_params=pltpu.CompilerParams(vmem_limit_bytes=VMEM_LIMIT),
        name="place_cells",
    )(order, product)


def local(model_dir, sens_blocks, blk_row, blk_col, blk_count, send_order, neighbors, face_weight):
    wavelet, smooth = analyse(send_order, model_dir, neighbors, face_weight)
    partial_image = forward(blk_count, blk_row, blk_col, sens_blocks, wavelet)
    image_half = combine(partial_image).reshape(ROW_BLOCKS, BLK, BLK)
    data_image, partial_adjoint = adjoin(blk_count, blk_row, blk_col, sens_blocks, image_half)
    normal_product = place_cells(send_order, give_back(partial_adjoint, smooth))
    return data_image.reshape(ROW_BLOCKS * BLK, BLK), normal_product.reshape(CELLS, BLK)


def solution(mesh):
    placed = (
        P("cols", None),
        P("rows", "cols", None, None),
        P("rows", "cols"),
        P("rows", "cols"),
        P("rows", "cols"),
        P("cols", None),
        P(None, "cols"),
        P(None, "cols"),
    )
    return jax.shard_map(
        local,
        mesh=mesh,
        in_specs=placed,
        out_specs=(P("rows", None), P("cols", None)),
        check_vma=False,
    )
```

```python
import math

import jax
import jax.numpy as jnp
import numpy as np
from jax import lax
from jax.experimental import pallas as pl
from jax.experimental.pallas import tpu as pltpu
from jax.sharding import PartitionSpec as P

BLK = 128
RIM = 64
NROWS = 8
NCOLS = 16
NZ = 4
ROW_BLOCKS = 32
COL_BLOCKS = 64
SLOTS = 384
CHUNK = 32
VMEM_LIMIT = 56 << 20
MESH = pl.DeviceIdType.MESH
F32 = jnp.float32
BF16 = jnp.bfloat16


VMEM = pl.BlockSpec(memory_space=pltpu.VMEM)
SMEM = pl.BlockSpec(memory_space=pltpu.SMEM)
ANY = pl.BlockSpec(memory_space=pl.ANY)


def cost(flops, moved):
    return pl.CostEstimate(flops=flops, bytes_accessed=moved, transcendentals=0)


def haar_parts():
    matrix = np.ones((1, 1))
    while matrix.shape[0] < BLK:
        length = matrix.shape[0]
        upper = np.kron(matrix, np.array([[1.0, 1.0]]))
        lower = np.kron(np.eye(length), np.array([[1.0, -1.0]]))
        matrix = np.concatenate([upper, lower], axis=0) / math.sqrt(2.0)
    scale = np.abs(matrix).max(axis=1)
    signs = np.round(matrix / scale[:, None])
    return signs, scale


SIGNS, SCALE = haar_parts()


def split(value):
    high = value.astype(BF16)
    low = (value - high.astype(F32)).astype(BF16)
    return high, low


def dot(a, b):
    return jnp.dot(a, b, preferred_element_type=F32)


def remote(src, dst, send_sem, recv_sem, device):
    return pltpu.make_async_remote_copy(
        src_ref=src,
        dst_ref=dst,
        send_sem=send_sem,
        recv_sem=recv_sem,
        device_id=device,
        device_id_type=MESH,
    )


def place():
    row = lax.axis_index("rows")
    col = lax.axis_index("cols")
    return row, col, lax.div(row, 2), lax.rem(row, 2)


def z_device(z, step, core, col):
    return (lax.rem(z + step, NZ) * 2 + core, col)


def greet(devices, extra=None):
    barrier = pltpu.get_barrier_semaphore()
    for device in devices:
        pl.semaphore_signal(barrier, inc=1, device_id=device, device_id_type=MESH)
    count = len(devices)
    if extra is not None:
        first, device_of = extra

        def signal(i, carry):
            pl.semaphore_signal(barrier, inc=1, device_id=device_of(i), device_id_type=MESH)
            return carry

        lax.fori_loop(first, PARTS, signal, 0)
        count = count + PARTS - first

    def wait_for_all():
        pl.semaphore_wait(barrier, count)

    return wait_for_all


PARTS = NCOLS // 2
GROUP = PARTS // 2
LANES = 4
EACH = PARTS // LANES


class RowGather:
    def __init__(self, piece, sem_refs, where):
        self.piece = piece
        self.g_send, self.minus, self.plus, self.far, self.pair = sem_refs
        self.row, self.col, self.z, self.core = where
        self.sends = []

    def ref(self, step, p, h=None, core=None):
        return self.piece(
            lax.rem(self.z + step, NZ), self.core if core is None else core, p, h
        )

    def send(self, ref, device, recv_sem):
        copy = remote(ref, ref, self.g_send.at[len(self.sends)], recv_sem, device)
        copy.start()
        self.sends.append(copy)

    def arrived(self, ref, recv_sem):
        remote(ref, ref, self.g_send.at[0], recv_sem, self.partner()).wait_recv()

    def partner(self):
        return self.z * 2 + 1 - self.core, self.col

    def neighbour(self, step):
        return z_device(self.z, step, self.core, self.col)

    def begin(self, p):
        own = self.ref(0, p)
        self.send(own, self.neighbour(1), self.minus.at[p])
        self.send(own, self.neighbour(3), self.plus.at[p])
        self.send(own, self.partner(), self.pair.at[0, p])

    def pass_on(self, p):
        self.arrived(self.ref(3, p), self.minus.at[p])
        self.send(self.ref(3, p, 0), self.neighbour(1), self.far.at[0, p])
        self.arrived(self.ref(1, p), self.plus.at[p])
        self.send(self.ref(1, p, 1), self.neighbour(3), self.far.at[1, p])
        self.send(self.ref(3, p), self.partner(), self.pair.at[3, p])
        self.send(self.ref(1, p), self.partner(), self.pair.at[1, p])

    def finish(self, p):
        for h in range(2):
            half = self.ref(2, p, h)
            self.arrived(half, self.far.at[h, p])
            self.send(half, self.partner(), self.pair.at[2 + 2 * h, p])

    def close(self, pieces):
        other = 1 - self.core
        for p in range(pieces):
            for step in (0, 1, 3):
                self.arrived(self.ref(step, p, None, other), self.pair.at[step, p])
            for h in range(2):
                self.arrived(self.ref(2, p, h, other), self.pair.at[2 + 2 * h, p])
        for copy in self.sends:
            copy.wait_send()


def gather_sems(pieces):
    return [
        pltpu.SemaphoreType.DMA((9 * pieces,)),
        pltpu.SemaphoreType.DMA((pieces,)),
        pltpu.SemaphoreType.DMA((pieces,)),
        pltpu.SemaphoreType.DMA((2, pieces)),
        pltpu.SemaphoreType.DMA((5, pieces)),
    ]


class Parts:
    def __init__(self, where):
        self.row, self.col, self.z, self.core = where
        self.mine = lax.div(self.col, 2)
        self.first = jnp.where(self.core == lax.rem(self.col, 2), 1, 0)

    def slot(self, i):
        return lax.rem(self.mine + i, PARTS)

    def device_at(self, m):
        return self.z * 2 + lax.rem(self.col, 2), m * 2 + self.core

    def device(self, i):
        return self.device_at(self.slot(i))

    def own(self, m):
        return m * 2 + self.core == self.col


CELLS = COL_BLOCKS * BLK


def cells_of(body, block):
    return jnp.concatenate([body[2 * block], body[2 * block + 1]], axis=0)


def tabulate(neighbors, weights, tables, first_cell):
    def tile(t, carry):
        at = pl.ds(pl.multiple_of(t * BLK, BLK), BLK)
        near = (neighbors[:, at] - (first_cell + t * BLK - RIM)).astype(F32)
        tables[t] = jnp.concatenate([near, weights[:, at]], axis=0)
        return carry

    lax.fori_loop(0, COL_BLOCKS, tile, 0)


def smooth_tile(body, rims, tables, tile):
    table = tables[tile].T
    span = lax.broadcasted_iota(jnp.int32, (BLK, 2 * BLK), 1).astype(F32)
    mix = jnp.zeros((BLK, 2 * BLK), F32)
    for face in range(4):
        mix += jnp.where(table[:, face : face + 1] == span, table[:, 4 + face : 5 + face], 0.0)
    mix_high, mix_low = split(mix)
    center = cells_of(body, tile)
    last = COL_BLOCKS - 1
    low = jnp.where(tile == 0, rims[0], body[jnp.maximum(2 * tile - 1, 0)])
    high = jnp.where(tile == last, rims[1], body[jnp.minimum(2 * tile + 2, 2 * last)])
    window = jnp.concatenate([low, center, high], axis=0)
    near_high, near_low = split(window)
    mixed = dot(mix_high, near_high) + dot(mix_low, near_high) + dot(mix_high, near_low)
    total = table[:, 4:5] + table[:, 5:6] + table[:, 6:7] + table[:, 7:8]
    return total * center - mixed


RING_BLOCKS = COL_BLOCKS // 2


def ring_place(z, core, part):
    return (z * 2 + core) * GROUP + part


def plane_place(core, part):
    return RING_BLOCKS + (core * PARTS + part) * 2


def analyse_kernel(
    order,
    model,
    neighbors_hbm,
    weights_hbm,
    signs_hbm,
    scale_hbm,
    wavelet,
    smooth,
    body,
    neighbors,
    weights,
    signs,
    scale,
    rims,
    tables,
    ring_stage,
    plane_stage,
    sems,
    ring_send,
    ring_recv,
    plane_send,
    plane_recv,
    plane_pair,
    *sem_refs,
):
    where = place()
    row, col, z, core = where
    fills = [
        pltpu.make_async_copy(src, dst, sems.at[4 + i])
        for i, (src, dst) in enumerate(
            (
                (model, body),
                (signs_hbm, signs),
                (scale_hbm, scale),
                (neighbors_hbm, neighbors),
                (weights_hbm, weights),
            )
        )
    ]
    for fill in fills:
        fill.start()
    parts = Parts(where)
    mine, lane = parts.mine, lax.div(z, 2)

    def ring_piece(at, k, p, h):
        first = ring_place(at, k, p * 2)
        return wavelet.at[pl.ds(first, 2) if h is None else pl.ds(first + h, 1)]

    gather = RowGather(ring_piece, sem_refs, where)
    below, above = (row, lax.rem(col + NCOLS - 1, NCOLS)), (row, lax.rem(col + 1, NCOLS))
    wait_for_all = greet(
        [gather.neighbour(1), gather.neighbour(3), gather.partner(), below, above],
        (parts.first, parts.device),
    )
    up = remote(
        model.at[2 * COL_BLOCKS - 1],
        rims.at[0],
        sems.at[0],
        sems.at[2],
        above,
    )
    down = remote(
        model.at[0],
        rims.at[1],
        sems.at[1],
        sems.at[3],
        below,
    )
    for fill in fills:
        fill.wait()
    sign_pair = jnp.concatenate([signs[...], signs[...]], axis=1)

    def block_of(m, q):
        return order[0, (m * 2 + core) * 4 + q]

    def coefficients(m, q):
        high, low = split(cells_of(body, block_of(m, q)))
        product = dot(sign_pair, jnp.concatenate([high, low], axis=0))
        return (product * scale[...]).astype(BF16)

    def ring_part(i):
        return i * 2 + lax.rem(lane + mine, 2)

    def make_ring(i, carry):
        ring_stage[i] = coefficients(ring_part(i), 2 + lax.rem(z, 2))
        return carry

    lax.fori_loop(0, GROUP, make_ring, 0)
    wait_for_all()

    def ring_copy(i):
        return remote(
            ring_stage.at[i],
            wavelet.at[ring_place(z, lax.rem(col, 2), lax.div(mine, 2))],
            ring_send.at[i],
            ring_recv.at[lax.div(mine, 2)],
            parts.device_at(ring_part(i)),
        )

    def spread_ring(i, carry):
        @pl.when(parts.own(ring_part(i)))
        def _():
            wavelet[ring_place(z, core, lax.div(mine, 2))] = ring_stage[i]

        @pl.when(jnp.logical_not(parts.own(ring_part(i))))
        def _():
            ring_copy(i).start()

        return carry

    lax.fori_loop(0, GROUP, spread_ring, 0)
    up.start()
    down.start()

    def plane_copy(i):
        return remote(
            plane_stage.at[i],
            wavelet.at[pl.ds(plane_place(lax.rem(col, 2), mine), 2)],
            plane_send.at[i],
            plane_recv.at[mine],
            parts.device(i),
        )

    def spread_plane(i, carry):
        for q in range(2):
            plane_stage[i, q] = coefficients(parts.slot(i), q)
        plane_copy(i).start()
        return carry

    lax.fori_loop(parts.first, PARTS, spread_plane, 0)

    @pl.when(parts.first == 1)
    def _():
        for q in range(2):
            wavelet[plane_place(core, mine) + q] = coefficients(mine, q)

    def wait_ring(i, carry):
        @pl.when(jnp.logical_not(parts.own(ring_part(i))))
        def _():
            ref = wavelet.at[ring_place(z, core, i)]
            remote(ref, ref, ring_send.at[0], ring_recv.at[i], gather.partner()).wait_recv()

        return carry

    def wait_plane(m, carry):
        @pl.when(jnp.logical_not(parts.own(m)))
        def _():
            ref = wavelet.at[pl.ds(plane_place(core, m), 2)]
            remote(ref, ref, plane_send.at[0], plane_recv.at[m], gather.partner()).wait_recv()

        return carry

    def half_plane(core_of, h):
        return wavelet.at[pl.ds(plane_place(core_of, h * GROUP), PARTS)]

    def swap(h):
        ref = half_plane(core, h)
        return remote(ref, ref, plane_pair.at[h], plane_pair.at[2 + h], gather.partner())

    def smooth_one(m, carry):
        smooth[m] = smooth_tile(body, rims, tables, block_of(m, z))
        return carry

    for p in range(2):
        lax.fori_loop(2 * p, 2 * p + 2, wait_ring, 0)
        gather.begin(p)
    tabulate(neighbors, weights, tables, col * CELLS)
    up.wait_recv()
    down.wait_recv()
    lax.fori_loop(0, 2, smooth_one, 0)
    for p in range(2):
        gather.pass_on(p)
    lax.fori_loop(2, PARTS, smooth_one, 0)
    for h in range(2):
        lax.fori_loop(h * GROUP, (h + 1) * GROUP, wait_plane, 0)
        swap(h).start()
    for p in range(2):
        gather.finish(p)
    gather.close(2)
    for h in range(2):
        ref = half_plane(1 - core, h)
        remote(ref, ref, plane_pair.at[h], plane_pair.at[2 + h], gather.partner()).wait_recv()
        swap(h).wait_send()

    def drain_ring(i, carry):
        @pl.when(jnp.logical_not(parts.own(ring_part(i))))
        def _():
            ring_copy(i).wait_send()

        return carry

    def drain_plane(i, carry):
        plane_copy(i).wait_send()
        return carry

    lax.fori_loop(0, GROUP, drain_ring, 0)
    lax.fori_loop(parts.first, PARTS, drain_plane, 0)
    up.wait_send()
    down.wait_send()


def analyse(order, model, neighbors, weights):
    return pl.pallas_call(
        analyse_kernel,
        out_shape=(
            jax.ShapeDtypeStruct((COL_BLOCKS, BLK, BLK), BF16),
            jax.ShapeDtypeStruct((PARTS, BLK, BLK), F32),
        ),
        in_specs=[SMEM, *[ANY] * 5],
        out_specs=(VMEM, VMEM),
        scratch_shapes=[
            pltpu.VMEM((2 * COL_BLOCKS, RIM, BLK), F32),
            pltpu.VMEM((4, CELLS), jnp.int32),
            pltpu.VMEM((4, CELLS), F32),
            pltpu.VMEM((BLK, BLK), BF16),
            pltpu.VMEM((BLK, BLK), F32),
            pltpu.VMEM((2, RIM, BLK), F32),
            pltpu.VMEM((COL_BLOCKS, 8, BLK), F32),
            pltpu.VMEM((GROUP, BLK, BLK), BF16),
            pltpu.VMEM((PARTS, 2, BLK, BLK), BF16),
            pltpu.SemaphoreType.DMA((9,)),
            pltpu.SemaphoreType.DMA((GROUP,)),
            pltpu.SemaphoreType.DMA((GROUP,)),
            pltpu.SemaphoreType.DMA((PARTS,)),
            pltpu.SemaphoreType.DMA((PARTS,)),
            pltpu.SemaphoreType.DMA((4,)),
            *gather_sems(2),
        ],
        compiler_params=pltpu.CompilerParams(
            collective_id=0, has_side_effects=True, vmem_limit_bytes=VMEM_LIMIT
        ),
        cost_estimate=cost(1 << 30, 60 << 20),
        name="analyse",
    )(
        order,
        model.reshape(2 * COL_BLOCKS, RIM, BLK),
        neighbors,
        weights,
        jnp.asarray(SIGNS, BF16),
        jnp.asarray(np.broadcast_to(SCALE[:, None], (BLK, BLK)), F32),
    )


class Sensors:
    def __init__(self, count, source, held, sems):
        self.live, self.source, self.held, self.sems = count[0, 0], source, held, sems

    def copy(self, g):
        part = pl.ds(g * CHUNK, CHUNK)
        return pltpu.make_async_copy(self.source.at[0, part], self.held.at[part], self.sems.at[g])

    def start(self):
        def begin(g, carry):
            self.copy(g).start()
            return carry

        lax.fori_loop(0, pl.cdiv(self.live, CHUNK), begin, 0)

    def run(self, add):
        full = self.live // CHUNK

        def group(g, carry):
            self.copy(g).wait()
            add(g * CHUNK, CHUNK)
            return carry

        lax.fori_loop(0, full, group, 0)
        done = full * CHUNK

        @pl.when(done < self.live)
        def _():
            self.copy(full).wait()

        for width in (4, 1):

            def few(g, carry, width=width, done=done):
                add(done + g * width, width)
                return carry

            groups = (self.live - done) // width
            lax.fori_loop(0, groups, few, 0)
            done = done + groups * width


def forward_kernel(count, rows, cols, source, wavelet_hbm, image, held, wavelet, places, sem, sems):
    load = pltpu.make_async_copy(wavelet_hbm, wavelet, sem)
    load.start()
    sensors = Sensors(count, source, held, sems)
    sensors.start()
    image[...] = jnp.zeros_like(image)
    mine = lax.axis_index("cols") >> 1

    def note(at, carry):
        q, core, part = at & 3, (at >> 2) & 1, at >> 3
        by_ring = ring_place(2 * ((part + mine) & 1) + (q & 1), core, part >> 1)
        places[at] = jnp.where(q >= 2, by_ring, plane_place(core, part) + q)
        return carry

    lax.fori_loop(0, COL_BLOCKS, note, 0)
    load.wait()

    def add(first, width):
        terms = []
        for u in range(width):
            terms.append(dot(held[first + u], wavelet[places[cols[0, first + u]]]))
        for u in range(width):
            image[rows[0, first + u]] += terms[u]

    sensors.run(add)


SENSOR_SCRATCH = (
    pltpu.VMEM((SLOTS, BLK, BLK), BF16),
    pltpu.SemaphoreType.DMA((SLOTS // CHUNK,)),
)


def forward(count, rows, cols, sens, wavelet):
    held, sems = SENSOR_SCRATCH
    return pl.pallas_call(
        forward_kernel,
        out_shape=jax.ShapeDtypeStruct((ROW_BLOCKS, BLK, BLK), F32),
        in_specs=[SMEM, SMEM, SMEM, ANY, ANY],
        out_specs=VMEM,
        scratch_shapes=[
            held,
            pltpu.VMEM(wavelet.shape, BF16),
            pltpu.SMEM((COL_BLOCKS,), jnp.int32),
            pltpu.SemaphoreType.DMA,
            sems,
        ],
        compiler_params=pltpu.CompilerParams(vmem_limit_bytes=VMEM_LIMIT),
        name="forward",
    )(count, rows, cols, sens, wavelet)


class Ring:
    def __init__(self, me, plus, minus, send, recv, far=None):
        self.me, self.plus, self.minus = me, plus, minus
        self.others = ((2, far), (1, plus), (3, minus))
        self.send, self.recv = send, recv
        self.started = []

    def at(self, step):
        return lax.rem(self.me + step, 4)

    def copy(self, src, dst, device, slot):
        copy = remote(src, dst, self.send.at[slot], self.recv.at[slot], device)
        copy.start()
        self.started.append(copy)

    def arrived(self, ref, slot):
        remote(ref, ref, self.send.at[slot], self.recv.at[slot], self.plus).wait_recv()

    def drain(self):
        for copy in self.started:
            copy.wait_send()
        self.started = []


class Reduce:
    def __init__(self, ring, data, base, chunk, relay, landed):
        self.ring, self.data, self.base, self.chunk = ring, data, base, chunk
        self.half = chunk // 2
        self.relay, self.landed = relay, landed

    def rows(self, step, h):
        start = self.base + self.ring.at(step) * self.chunk + h * self.half
        return pl.ds(pl.multiple_of(start, self.half), self.half)

    def relay_at(self, side):
        return self.relay.at[side, pl.ds(0, self.half)]

    def landed_at(self, side, h):
        return self.landed.at[side, pl.ds(h * self.half, self.half)]

    def begin(self):
        ring, data = self.ring, self.data
        ring.copy(data.at[self.rows(2, 0)], self.relay_at(0), ring.plus, 0)
        ring.copy(data.at[self.rows(2, 1)], self.relay_at(1), ring.minus, 1)
        ring.copy(data.at[self.rows(1, 1)], self.landed_at(0, 1), ring.plus, 2)
        ring.copy(data.at[self.rows(3, 0)], self.landed_at(1, 0), ring.minus, 3)

    def pass_on(self):
        ring, data = self.ring, self.data
        ring.arrived(self.relay_at(0), 0)
        data[self.rows(1, 0), :] += self.relay[0, : self.half]
        ring.copy(data.at[self.rows(1, 0)], self.landed_at(0, 0), ring.plus, 4)
        ring.arrived(self.relay_at(1), 1)
        data[self.rows(3, 1), :] += self.relay[1, : self.half]
        ring.copy(data.at[self.rows(3, 1)], self.landed_at(1, 1), ring.minus, 5)

    def finish(self):
        ring, data = self.ring, self.data
        ring.arrived(self.landed_at(0, 1), 2)
        ring.arrived(self.landed_at(1, 0), 3)
        ring.arrived(self.landed_at(0, 0), 4)
        ring.arrived(self.landed_at(1, 1), 5)
        for h in range(2):
            part = pl.ds(h * self.half, self.half)
            data[self.rows(0, h), :] += self.landed[0, part, :] + self.landed[1, part, :]


class DirectReduce:
    def __init__(self, ring, data, base, chunk, landed):
        self.ring, self.data, self.base, self.chunk = ring, data, base, chunk
        self.landed = landed

    def rows(self, step):
        start = self.base + self.ring.at(step) * self.chunk
        return pl.ds(pl.multiple_of(start, self.chunk), self.chunk)

    def begin(self):
        for step, device in self.ring.others:
            self.ring.copy(
                self.data.at[self.rows(step)], self.landed.at[step - 1], device, step - 1
            )

    def pass_on(self):
        for step in range(3):
            self.ring.arrived(self.landed.at[step], step)

    def finish(self):
        own = self.rows(0)
        total = self.data[own, :] + self.landed[0]
        self.data[own, :] = total + (self.landed[1] + self.landed[2])


class DirectGather:
    def __init__(self, ring, data, base, chunk):
        self.ring, self.data, self.base, self.chunk = ring, data, base, chunk

    def rows(self, step):
        start = self.base + self.ring.at(step) * self.chunk
        return self.data.at[pl.ds(pl.multiple_of(start, self.chunk), self.chunk)]

    def begin(self):
        for step, device in self.ring.others:
            self.ring.copy(self.rows(0), self.rows(0), device, step - 1)

    def pass_on(self):
        pass

    def finish(self):
        for step in (1, 3, 2):
            self.ring.arrived(self.rows(4 - step), step - 1)


STREAMS = 4
STREAM = ROW_BLOCKS * BLK // STREAMS
BIG = STREAM // 4
SMALL = BIG // 4


def combine_kernel(partial, image, fill, big_relay, big_landed, small_landed, send, recv):
    row, col, _, _ = place()
    y, x = lax.div(col, 4), lax.rem(col, 4)
    x_ring = [(row, y * 4 + lax.rem(x + step, 4)) for step in range(4)]
    y_ring = [(row, lax.rem(y + step, 4) * 4 + x) for step in range(4)]
    greet(x_ring[1:] + y_ring[1:])()
    fill.wait()

    def ring(axis, slot):
        me, devices = ((x, x_ring), (y, y_ring))[axis]
        return Ring(me, devices[1], devices[3], send.at[slot], recv.at[slot], devices[2])

    streams = range(STREAMS)
    axis = [a % 2 for a in streams]
    bases = [a * STREAM for a in streams]
    inner = [bases[a] + (x, y)[axis[a]] * BIG for a in streams]
    wide_rings = [ring(axis[a], a) for a in streams]
    cross_rings = [ring(1 - axis[a], STREAMS + a) for a in streams]
    back_rings = [ring(1 - axis[a], 2 * STREAMS + a) for a in streams]
    last_rings = [ring(axis[a], 3 * STREAMS + a) for a in streams]
    wide = [Reduce(wide_rings[a], partial, bases[a], BIG, big_relay.at[a], big_landed.at[a]) for a in streams]
    cross = [DirectReduce(cross_rings[a], partial, inner[a], SMALL, small_landed.at[a]) for a in streams]
    back = [DirectGather(back_rings[a], image, inner[a], SMALL) for a in streams]
    last = [DirectGather(last_rings[a], image, bases[a], BIG) for a in streams]

    def cast(a):
        start = inner[a] + (y, x)[axis[a]] * SMALL
        own = pl.ds(pl.multiple_of(start, SMALL), SMALL)
        image[own, :] = partial[own, :].astype(BF16)

    pairs = [(a, a + 1) for a in range(0, STREAMS, 2)]
    for a in streams:
        wide[a].begin()
    for a in streams:
        wide[a].pass_on()
    for pair in pairs:
        for a in pair:
            wide[a].finish()
            cross[a].begin()
    for pair in pairs:
        for a in pair:
            cross[a].pass_on()
            cross[a].finish()
            cast(a)
            back[a].begin()
    for pair in pairs:
        for a in pair:
            back[a].finish()
            last[a].begin()
    for a in streams:
        last[a].finish()
    for group in (wide_rings, cross_rings, back_rings, last_rings):
        for one in group:
            one.drain()


def combine(partial):
    vmem = pl.BlockSpec(memory_space=pltpu.VMEM)
    rows = ROW_BLOCKS * BLK

    def kernel(partial_ref, image_ref, data, *rest):
        copy = pltpu.make_async_copy(partial_ref, data, rest[-1])
        copy.start()
        combine_kernel(data, image_ref, copy, *rest[:-1])

    return pl.pallas_call(
        kernel,
        out_shape=jax.ShapeDtypeStruct((rows, BLK), BF16),
        in_specs=[pl.BlockSpec(memory_space=pl.ANY)],
        out_specs=vmem,
        scratch_shapes=[
            pltpu.VMEM((rows, BLK), F32),
            pltpu.VMEM((STREAMS, 2, BIG // 2, BLK), F32),
            pltpu.VMEM((STREAMS, 2, BIG, BLK), F32),
            pltpu.VMEM((STREAMS, 3, SMALL, BLK), F32),
            pltpu.SemaphoreType.DMA((4 * STREAMS, 6)),
            pltpu.SemaphoreType.DMA((4 * STREAMS, 6)),
            pltpu.SemaphoreType.DMA,
        ],
        compiler_params=pltpu.CompilerParams(
            collective_id=1, has_side_effects=True, vmem_limit_bytes=VMEM_LIMIT
        ),
        cost_estimate=cost(1 << 20, 80 << 20),
        name="combine",
    )(partial.reshape(rows, BLK))


def adjoint_kernel(
    count, rows, cols, source, image_hbm, data_image, adjoint, held, image, flipped, plain, sem, sems
):
    load = pltpu.make_async_copy(image_hbm, image, sem.at[0])
    load.start()
    sensors = Sensors(count, source, held, sems)
    sensors.start()
    adjoint[...] = jnp.zeros_like(adjoint)
    load.wait()

    def flip(b, carry):
        block = image[b].astype(F32)
        plain[b] = block
        flipped[b] = block.T.astype(BF16)
        return carry

    lax.fori_loop(0, ROW_BLOCKS, flip, 0, unroll=2)
    store = pltpu.make_async_copy(plain, data_image, sem.at[1])
    store.start()
    shift = lax.axis_index("cols") >> 1

    def add(first, width):
        terms = []
        for u in range(width):
            terms.append(dot(flipped[rows[0, first + u]], held[first + u]))
        for u in range(width):
            at = cols[0, first + u]
            part = at >> 3
            adjoint[(at >> 2) & 1, at & 3, (part + shift) & 3, part >> 2] += terms[u]

    sensors.run(add)
    store.wait()


def adjoin(count, rows, cols, sens, image):
    held, sems = SENSOR_SCRATCH
    return pl.pallas_call(
        adjoint_kernel,
        out_shape=(
            jax.ShapeDtypeStruct((ROW_BLOCKS, BLK, BLK), F32),
            jax.ShapeDtypeStruct((2, NZ, LANES, EACH, BLK, BLK), F32),
        ),
        in_specs=[SMEM, SMEM, SMEM, ANY, ANY],
        out_specs=(ANY, VMEM),
        scratch_shapes=[
            held,
            pltpu.VMEM((ROW_BLOCKS, BLK, BLK), BF16),
            pltpu.VMEM((ROW_BLOCKS, BLK, BLK), BF16),
            pltpu.VMEM((ROW_BLOCKS, BLK, BLK), F32),
            pltpu.SemaphoreType.DMA((2,)),
            sems,
        ],
        compiler_params=pltpu.CompilerParams(vmem_limit_bytes=VMEM_LIMIT),
        name="adjoin",
    )(count, rows, cols, sens, image)


def return_kernel(
    partial, smooth, scale, signs, out, own, stage, pair, relay_out, relay, landed, gathered, sem, send, recv, part_send, part_recv, *sem_refs
):
    where = place()
    row, col, z, core = where
    fill = pltpu.make_async_copy(partial.at[core], own, sem)
    fill.start()
    parts = Parts(where)
    mine = parts.mine

    def out_piece(at, k, p, h):
        first = p * EACH
        return out.at[at, k, pl.ds(first, EACH) if h is None else pl.ds(first + h, 1)]

    gather = RowGather(out_piece, sem_refs, where)
    plus, minus, partner = gather.neighbour(1), gather.neighbour(3), gather.partner()
    greet([plus, minus, partner], (parts.first, parts.device))()
    rings = [Ring(z, plus, minus, send.at[p], recv.at[p]) for p in range(LANES)]
    for p in range(LANES):
        ring = rings[p]
        for slot, step in ((6, 2), (7, 1), (8, 3), (9, 0)):
            q = ring.at(step)
            ring.copy(partial.at[1 - core, q, p], pair.at[q, p], partner, slot)
    fill.wait()

    def total(p, step, h):
        q = rings[p].at(step)
        return own[q, p, h] + pair[q, p, h]

    def paired(p, step, slot):
        rings[p].arrived(pair.at[rings[p].at(step), p], slot)

    def ship(p, value, slot, dst, device, sem):
        relay_out[p, slot] = value.astype(BF16)
        rings[p].copy(relay_out.at[p, slot], dst, device, sem)

    def launch(p):
        paired(p, 2, 6)
        ship(p, total(p, 2, 0), 0, relay.at[p, 0], plus, 0)
        ship(p, total(p, 2, 1), 1, relay.at[p, 1], minus, 1)
        paired(p, 1, 7)
        ship(p, total(p, 1, 1), 3, landed.at[p, 0, 1], plus, 2)
        paired(p, 3, 8)
        ship(p, total(p, 3, 0), 4, landed.at[p, 1, 0], minus, 3)

    def pass_on(p):
        ring = rings[p]
        ring.arrived(relay.at[p, 0], 0)
        ship(p, total(p, 1, 0) + relay[p, 0].astype(F32), 2, landed.at[p, 0, 0], plus, 4)
        ring.arrived(relay.at[p, 1], 1)
        ship(p, total(p, 3, 1) + relay[p, 1].astype(F32), 5, landed.at[p, 1, 1], minus, 5)

    lane_scale = scale[0:1, :]

    def member(p, i):
        return i * LANES + lax.rem(p + PARTS - mine, LANES)

    def part_copy(m):
        return remote(
            stage.at[m], gathered.at[mine], part_send.at[m], part_recv.at[mine], parts.device_at(m)
        )

    def hand_over(p):
        ring = rings[p]
        paired(p, 0, 9)
        for slot, (side, h) in ((2, (0, 1)), (3, (1, 0)), (4, (0, 0)), (5, (1, 1))):
            ring.arrived(landed.at[p, side, h], slot)
        for h in range(EACH):
            m = member(p, h)
            value = total(p, 0, h) + (landed[p, 0, h].astype(F32) + landed[p, 1, h].astype(F32))
            value = (value * lane_scale).astype(BF16)
            stage[m] = value

            @pl.when(parts.own(m))
            def _(m=m):
                gathered[m] = stage[m]

            @pl.when(jnp.logical_not(parts.own(m)))
            def _(m=m):
                part_copy(m).start()

    def synthesise(p):
        for h in range(EACH):
            m = member(p, h)

            @pl.when(jnp.logical_not(parts.own(m)))
            def _(m=m):
                ref = gathered.at[m]
                remote(ref, ref, part_send.at[0], part_recv.at[m], partner).wait_recv()

            cells = lax.dot_general(
                signs[...], gathered[m], (((1,), (1,)), ((), ())), preferred_element_type=F32
            )
            out[z, core, p * EACH + h] = (cells + smooth[m]).astype(BF16)
        gather.begin(p)

    for p in range(LANES):
        launch(p)
    pass_on(0)
    pass_on(1)
    hand_over(0)
    pass_on(2)
    hand_over(1)
    pass_on(3)
    hand_over(2)
    synthesise(0)
    hand_over(3)
    synthesise(1)
    synthesise(2)
    gather.pass_on(0)
    synthesise(3)
    for p in range(1, LANES):
        gather.pass_on(p)
        gather.finish(p - 1)
    gather.finish(LANES - 1)
    gather.close(LANES)

    def drain(m, carry):
        @pl.when(jnp.logical_not(parts.own(m)))
        def _():
            part_copy(m).wait_send()

        return carry

    lax.fori_loop(0, PARTS, drain, 0)
    for ring in rings:
        ring.drain()


def give_back(partial, smooth):
    return pl.pallas_call(
        return_kernel,
        out_shape=jax.ShapeDtypeStruct((NZ, 2, PARTS, BLK, BLK), BF16),
        in_specs=[ANY, VMEM, VMEM, VMEM],
        out_specs=VMEM,
        scratch_shapes=[
            pltpu.VMEM((NZ, LANES, EACH, BLK, BLK), F32),
            pltpu.VMEM((PARTS, BLK, BLK), BF16),
            pltpu.VMEM((NZ, LANES, EACH, BLK, BLK), F32),
            pltpu.VMEM((LANES, 6, BLK, BLK), BF16),
            pltpu.VMEM((LANES, 2, BLK, BLK), BF16),
            pltpu.VMEM((LANES, 2, 2, BLK, BLK), BF16),
            pltpu.VMEM((PARTS, BLK, BLK), BF16),
            pltpu.SemaphoreType.DMA,
            pltpu.SemaphoreType.DMA((LANES, 10)),
            pltpu.SemaphoreType.DMA((LANES, 10)),
            pltpu.SemaphoreType.DMA((PARTS,)),
            pltpu.SemaphoreType.DMA((PARTS,)),
            *gather_sems(LANES),
        ],
        compiler_params=pltpu.CompilerParams(
            collective_id=2, has_side_effects=True, vmem_limit_bytes=VMEM_LIMIT
        ),
        cost_estimate=cost(1 << 30, 80 << 20),
        name="give_back",
    )(
        partial,
        smooth,
        jnp.asarray(np.broadcast_to(SCALE[None, :], (8, BLK)), F32),
        jnp.asarray(SIGNS.T, BF16),
    )


def place_kernel(order, product_hbm, out, product, cells, in_sems, out_sems):
    def load(i):
        at = lax.div(i, 2), lax.rem(i, 2)
        return pltpu.make_async_copy(product_hbm.at[at], product.at[at], in_sems.at[i])

    def store(i, block):
        return pltpu.make_async_copy(cells.at[i], out.at[block], out_sems.at[i])

    for i in range(2 * NZ):
        load(i).start()
    shift = lax.axis_index("cols") >> 1
    for i in range(2 * NZ):
        load(i).wait()
        for n in range(PARTS):
            q, core, p = i // 2, i % 2, n // EACH
            at = i * PARTS + n
            cells[at] = product[q, core, n].astype(F32)
            m = (n % EACH) * LANES + ((p + PARTS - shift) & (LANES - 1))
            store(at, order[0, (m * 2 + core) * 4 + q]).start()

    def finish(i, carry):
        store(i, 0).wait()
        return carry

    lax.fori_loop(0, COL_BLOCKS, finish, 0)


def place_cells(order, product):
    return pl.pallas_call(
        place_kernel,
        out_shape=jax.ShapeDtypeStruct((COL_BLOCKS, BLK, BLK), F32),
        in_specs=[SMEM, ANY],
        out_specs=ANY,
        scratch_shapes=[
            pltpu.VMEM(product.shape, BF16),
            pltpu.VMEM((COL_BLOCKS, BLK, BLK), F32),
            pltpu.SemaphoreType.DMA((2 * NZ,)),
            pltpu.SemaphoreType.DMA((COL_BLOCKS,)),
        ],
        compiler_params=pltpu.CompilerParams(vmem_limit_bytes=VMEM_LIMIT),
        name="place_cells",
    )(order, product)


def local(model_dir, sens_blocks, blk_row, blk_col, blk_count, send_order, neighbors, face_weight):
    wavelet, smooth = analyse(send_order, model_dir, neighbors, face_weight)
    partial_image = forward(blk_count, blk_row, blk_col, sens_blocks, wavelet)
    image_half = combine(partial_image).reshape(ROW_BLOCKS, BLK, BLK)
    data_image, partial_adjoint = adjoin(blk_count, blk_row, blk_col, sens_blocks, image_half)
    normal_product = place_cells(send_order, give_back(partial_adjoint, smooth))
    return data_image.reshape(ROW_BLOCKS * BLK, BLK), normal_product.reshape(CELLS, BLK)


def solution(mesh):
    placed = (
        P("cols", None),
        P("rows", "cols", None, None),
        P("rows", "cols"),
        P("rows", "cols"),
        P("rows", "cols"),
        P("cols", None),
        P(None, "cols"),
        P(None, "cols"),
    )
    return jax.shard_map(
        local,
        mesh=mesh,
        in_specs=placed,
        out_specs=(P("rows", None), P("cols", None)),
        check_vma=False,
    )
```

```python
import math

import jax
import jax.numpy as jnp
import numpy as np
from jax import lax
from jax.experimental import pallas as pl
from jax.experimental.pallas import tpu as pltpu
from jax.sharding import PartitionSpec as P

BLK = 128
RIM = 64
NROWS = 8
NCOLS = 16
NZ = 4
ROW_BLOCKS = 32
COL_BLOCKS = 64
SLOTS = 384
CHUNK = 32
VMEM_LIMIT = 56 << 20
MIDDLE_LIMIT = 42 << 20
MESH = pl.DeviceIdType.MESH
F32 = jnp.float32
BF16 = jnp.bfloat16


VMEM = pl.BlockSpec(memory_space=pltpu.VMEM)
SMEM = pl.BlockSpec(memory_space=pltpu.SMEM)
ANY = pl.BlockSpec(memory_space=pl.ANY)


def cost(flops, moved):
    return pl.CostEstimate(flops=flops, bytes_accessed=moved, transcendentals=0)


def haar_parts():
    matrix = np.ones((1, 1))
    while matrix.shape[0] < BLK:
        length = matrix.shape[0]
        upper = np.kron(matrix, np.array([[1.0, 1.0]]))
        lower = np.kron(np.eye(length), np.array([[1.0, -1.0]]))
        matrix = np.concatenate([upper, lower], axis=0) / math.sqrt(2.0)
    scale = np.abs(matrix).max(axis=1)
    signs = np.round(matrix / scale[:, None])
    return signs, scale


SIGNS, SCALE = haar_parts()


def split(value):
    high = value.astype(BF16)
    low = (value - high.astype(F32)).astype(BF16)
    return high, low


def dot(a, b):
    return jnp.dot(a, b, preferred_element_type=F32)


def remote(src, dst, send_sem, recv_sem, device):
    return pltpu.make_async_remote_copy(
        src_ref=src,
        dst_ref=dst,
        send_sem=send_sem,
        recv_sem=recv_sem,
        device_id=device,
        device_id_type=MESH,
    )


def place():
    row = lax.axis_index("rows")
    col = lax.axis_index("cols")
    return row, col, lax.div(row, 2), lax.rem(row, 2)


def z_device(z, step, core, col):
    return (lax.rem(z + step, NZ) * 2 + core, col)


def greet(devices, extra=None):
    barrier = pltpu.get_barrier_semaphore()
    for device in devices:
        pl.semaphore_signal(barrier, inc=1, device_id=device, device_id_type=MESH)
    count = len(devices)
    if extra is not None:
        first, device_of = extra

        def signal(i, carry):
            pl.semaphore_signal(barrier, inc=1, device_id=device_of(i), device_id_type=MESH)
            return carry

        lax.fori_loop(first, PARTS, signal, 0)
        count = count + PARTS - first

    def wait_for_all():
        pl.semaphore_wait(barrier, count)

    return wait_for_all


PARTS = NCOLS // 2
GROUP = PARTS // 2
LANES = 4
EACH = PARTS // LANES


class RowGather:
    def __init__(self, piece, sem_refs, where):
        self.piece = piece
        self.g_send, self.minus, self.plus, self.far, self.pair = sem_refs
        self.row, self.col, self.z, self.core = where
        self.sends = []

    def ref(self, step, p, h=None, core=None):
        return self.piece(
            lax.rem(self.z + step, NZ), self.core if core is None else core, p, h
        )

    def send(self, ref, device, recv_sem):
        copy = remote(ref, ref, self.g_send.at[len(self.sends)], recv_sem, device)
        copy.start()
        self.sends.append(copy)

    def arrived(self, ref, recv_sem):
        remote(ref, ref, self.g_send.at[0], recv_sem, self.partner()).wait_recv()

    def partner(self):
        return self.z * 2 + 1 - self.core, self.col

    def neighbour(self, step):
        return z_device(self.z, step, self.core, self.col)

    def begin(self, p):
        own = self.ref(0, p)
        self.send(own, self.neighbour(1), self.minus.at[p])
        self.send(own, self.neighbour(3), self.plus.at[p])
        self.send(own, self.partner(), self.pair.at[0, p])

    def pass_on(self, p):
        self.arrived(self.ref(3, p), self.minus.at[p])
        self.send(self.ref(3, p, 0), self.neighbour(1), self.far.at[0, p])
        self.arrived(self.ref(1, p), self.plus.at[p])
        self.send(self.ref(1, p, 1), self.neighbour(3), self.far.at[1, p])
        self.send(self.ref(3, p), self.partner(), self.pair.at[3, p])
        self.send(self.ref(1, p), self.partner(), self.pair.at[1, p])

    def finish(self, p):
        for h in range(2):
            half = self.ref(2, p, h)
            self.arrived(half, self.far.at[h, p])
            self.send(half, self.partner(), self.pair.at[2 + 2 * h, p])

    def close(self, pieces):
        other = 1 - self.core
        for p in range(pieces):
            for step in (0, 1, 3):
                self.arrived(self.ref(step, p, None, other), self.pair.at[step, p])
            for h in range(2):
                self.arrived(self.ref(2, p, h, other), self.pair.at[2 + 2 * h, p])
        for copy in self.sends:
            copy.wait_send()


def gather_sems(pieces):
    return [
        pltpu.SemaphoreType.DMA((9 * pieces,)),
        pltpu.SemaphoreType.DMA((pieces,)),
        pltpu.SemaphoreType.DMA((pieces,)),
        pltpu.SemaphoreType.DMA((2, pieces)),
        pltpu.SemaphoreType.DMA((5, pieces)),
    ]


class Parts:
    def __init__(self, where):
        self.row, self.col, self.z, self.core = where
        self.mine = lax.div(self.col, 2)
        self.first = jnp.where(self.core == lax.rem(self.col, 2), 1, 0)

    def slot(self, i):
        return lax.rem(self.mine + i, PARTS)

    def device_at(self, m):
        return self.z * 2 + lax.rem(self.col, 2), m * 2 + self.core

    def device(self, i):
        return self.device_at(self.slot(i))

    def own(self, m):
        return m * 2 + self.core == self.col


CELLS = COL_BLOCKS * BLK


def cells_of(body, block):
    return jnp.concatenate([body[2 * block], body[2 * block + 1]], axis=0)


def tabulate(neighbors, weights, tables, first_cell):
    def tile(t, carry):
        at = pl.ds(pl.multiple_of(t * BLK, BLK), BLK)
        near = (neighbors[:, at] - (first_cell + t * BLK - RIM)).astype(F32)
        tables[t] = jnp.concatenate([near, weights[:, at]], axis=0)
        return carry

    lax.fori_loop(0, COL_BLOCKS, tile, 0)


def smooth_tile(body, rims, tables, tile):
    table = tables[tile].T
    span = lax.broadcasted_iota(jnp.int32, (BLK, 2 * BLK), 1).astype(F32)
    mix = jnp.zeros((BLK, 2 * BLK), F32)
    for face in range(4):
        mix += jnp.where(table[:, face : face + 1] == span, table[:, 4 + face : 5 + face], 0.0)
    mix_high, mix_low = split(mix)
    center = cells_of(body, tile)
    last = COL_BLOCKS - 1
    low = jnp.where(tile == 0, rims[0], body[jnp.maximum(2 * tile - 1, 0)])
    high = jnp.where(tile == last, rims[1], body[jnp.minimum(2 * tile + 2, 2 * last)])
    window = jnp.concatenate([low, center, high], axis=0)
    near_high, near_low = split(window)
    mixed = dot(mix_high, near_high) + dot(mix_low, near_high) + dot(mix_high, near_low)
    total = table[:, 4:5] + table[:, 5:6] + table[:, 6:7] + table[:, 7:8]
    return total * center - mixed


RING_BLOCKS = COL_BLOCKS // 2


def ring_place(z, core, part):
    return (z * 2 + core) * GROUP + part


def plane_place(core, part):
    return RING_BLOCKS + (core * PARTS + part) * 2


def analyse_kernel(
    order,
    model,
    neighbors_hbm,
    weights_hbm,
    signs_hbm,
    scale_hbm,
    wavelet,
    smooth,
    body,
    neighbors,
    weights,
    signs,
    scale,
    rims,
    tables,
    ring_stage,
    plane_stage,
    sems,
    ring_send,
    ring_recv,
    plane_send,
    plane_recv,
    plane_pair,
    *sem_refs,
):
    where = place()
    row, col, z, core = where
    fills = [
        pltpu.make_async_copy(src, dst, sems.at[4 + i])
        for i, (src, dst) in enumerate(
            (
                (model, body),
                (signs_hbm, signs),
                (scale_hbm, scale),
                (neighbors_hbm, neighbors),
                (weights_hbm, weights),
            )
        )
    ]
    for fill in fills:
        fill.start()
    parts = Parts(where)
    mine, lane = parts.mine, lax.div(z, 2)

    def ring_piece(at, k, p, h):
        first = ring_place(at, k, p * 2)
        return wavelet.at[pl.ds(first, 2) if h is None else pl.ds(first + h, 1)]

    gather = RowGather(ring_piece, sem_refs, where)
    below, above = (row, lax.rem(col + NCOLS - 1, NCOLS)), (row, lax.rem(col + 1, NCOLS))
    wait_for_all = greet(
        [gather.neighbour(1), gather.neighbour(3), gather.partner(), below, above],
        (parts.first, parts.device),
    )
    up = remote(
        model.at[2 * COL_BLOCKS - 1],
        rims.at[0],
        sems.at[0],
        sems.at[2],
        above,
    )
    down = remote(
        model.at[0],
        rims.at[1],
        sems.at[1],
        sems.at[3],
        below,
    )
    for fill in fills:
        fill.wait()
    sign_pair = jnp.concatenate([signs[...], signs[...]], axis=1)

    def block_of(m, q):
        return order[0, (m * 2 + core) * 4 + q]

    def coefficients(m, q):
        high, low = split(cells_of(body, block_of(m, q)))
        product = dot(sign_pair, jnp.concatenate([high, low], axis=0))
        return (product * scale[...]).astype(BF16)

    def ring_part(i):
        return i * 2 + lax.rem(lane + mine, 2)

    def make_ring(i, carry):
        ring_stage[i] = coefficients(ring_part(i), 2 + lax.rem(z, 2))
        return carry

    lax.fori_loop(0, GROUP, make_ring, 0)
    wait_for_all()

    def ring_copy(i):
        return remote(
            ring_stage.at[i],
            wavelet.at[ring_place(z, lax.rem(col, 2), lax.div(mine, 2))],
            ring_send.at[i],
            ring_recv.at[lax.div(mine, 2)],
            parts.device_at(ring_part(i)),
        )

    def spread_ring(i, carry):
        @pl.when(parts.own(ring_part(i)))
        def _():
            wavelet[ring_place(z, core, lax.div(mine, 2))] = ring_stage[i]

        @pl.when(jnp.logical_not(parts.own(ring_part(i))))
        def _():
            ring_copy(i).start()

        return carry

    lax.fori_loop(0, GROUP, spread_ring, 0)
    up.start()
    down.start()

    def plane_copy(i):
        return remote(
            plane_stage.at[i],
            wavelet.at[pl.ds(plane_place(lax.rem(col, 2), mine), 2)],
            plane_send.at[i],
            plane_recv.at[mine],
            parts.device(i),
        )

    def spread_plane(i, carry):
        for q in range(2):
            plane_stage[i, q] = coefficients(parts.slot(i), q)
        plane_copy(i).start()
        return carry

    lax.fori_loop(parts.first, PARTS, spread_plane, 0)

    @pl.when(parts.first == 1)
    def _():
        for q in range(2):
            wavelet[plane_place(core, mine) + q] = coefficients(mine, q)

    def wait_ring(i, carry):
        @pl.when(jnp.logical_not(parts.own(ring_part(i))))
        def _():
            ref = wavelet.at[ring_place(z, core, i)]
            remote(ref, ref, ring_send.at[0], ring_recv.at[i], gather.partner()).wait_recv()

        return carry

    def wait_plane(m, carry):
        @pl.when(jnp.logical_not(parts.own(m)))
        def _():
            ref = wavelet.at[pl.ds(plane_place(core, m), 2)]
            remote(ref, ref, plane_send.at[0], plane_recv.at[m], gather.partner()).wait_recv()

        return carry

    def half_plane(core_of, h):
        return wavelet.at[pl.ds(plane_place(core_of, h * GROUP), PARTS)]

    def swap(h):
        ref = half_plane(core, h)
        return remote(ref, ref, plane_pair.at[h], plane_pair.at[2 + h], gather.partner())

    def smooth_one(m, carry):
        smooth[m] = smooth_tile(body, rims, tables, block_of(m, z))
        return carry

    for p in range(2):
        lax.fori_loop(2 * p, 2 * p + 2, wait_ring, 0)
        gather.begin(p)
    tabulate(neighbors, weights, tables, col * CELLS)
    up.wait_recv()
    down.wait_recv()
    lax.fori_loop(0, 2, smooth_one, 0)
    for p in range(2):
        gather.pass_on(p)
    lax.fori_loop(2, PARTS, smooth_one, 0)
    for h in range(2):
        lax.fori_loop(h * GROUP, (h + 1) * GROUP, wait_plane, 0)
        swap(h).start()
    for p in range(2):
        gather.finish(p)
    gather.close(2)
    for h in range(2):
        ref = half_plane(1 - core, h)
        remote(ref, ref, plane_pair.at[h], plane_pair.at[2 + h], gather.partner()).wait_recv()
        swap(h).wait_send()

    def drain_ring(i, carry):
        @pl.when(jnp.logical_not(parts.own(ring_part(i))))
        def _():
            ring_copy(i).wait_send()

        return carry

    def drain_plane(i, carry):
        plane_copy(i).wait_send()
        return carry

    lax.fori_loop(0, GROUP, drain_ring, 0)
    lax.fori_loop(parts.first, PARTS, drain_plane, 0)
    up.wait_send()
    down.wait_send()


def analyse(order, model, neighbors, weights):
    return pl.pallas_call(
        analyse_kernel,
        out_shape=(
            jax.ShapeDtypeStruct((COL_BLOCKS, BLK, BLK), BF16),
            jax.ShapeDtypeStruct((PARTS, BLK, BLK), F32),
        ),
        in_specs=[SMEM, *[ANY] * 5],
        out_specs=(VMEM, VMEM),
        scratch_shapes=[
            pltpu.VMEM((2 * COL_BLOCKS, RIM, BLK), F32),
            pltpu.VMEM((4, CELLS), jnp.int32),
            pltpu.VMEM((4, CELLS), F32),
            pltpu.VMEM((BLK, BLK), BF16),
            pltpu.VMEM((BLK, BLK), F32),
            pltpu.VMEM((2, RIM, BLK), F32),
            pltpu.VMEM((COL_BLOCKS, 8, BLK), F32),
            pltpu.VMEM((GROUP, BLK, BLK), BF16),
            pltpu.VMEM((PARTS, 2, BLK, BLK), BF16),
            pltpu.SemaphoreType.DMA((9,)),
            pltpu.SemaphoreType.DMA((GROUP,)),
            pltpu.SemaphoreType.DMA((GROUP,)),
            pltpu.SemaphoreType.DMA((PARTS,)),
            pltpu.SemaphoreType.DMA((PARTS,)),
            pltpu.SemaphoreType.DMA((4,)),
            *gather_sems(2),
        ],
        compiler_params=pltpu.CompilerParams(
            collective_id=0, has_side_effects=True, vmem_limit_bytes=VMEM_LIMIT
        ),
        cost_estimate=cost(1 << 30, 60 << 20),
        name="analyse",
    )(
        order,
        model.reshape(2 * COL_BLOCKS, RIM, BLK),
        neighbors,
        weights,
        jnp.asarray(SIGNS, BF16),
        jnp.asarray(np.broadcast_to(SCALE[:, None], (BLK, BLK)), F32),
    )


class Sensors:
    def __init__(self, count, source, held, sems):
        self.live, self.source, self.held, self.sems = count[0, 0], source, held, sems

    def copy(self, g):
        part = pl.ds(g * CHUNK, CHUNK)
        return pltpu.make_async_copy(self.source.at[0, part], self.held.at[part], self.sems.at[g])

    def start(self):
        def begin(g, carry):
            self.copy(g).start()
            return carry

        lax.fori_loop(0, pl.cdiv(self.live, CHUNK), begin, 0)

    def run(self, add):
        full = self.live // CHUNK

        def group(g, carry):
            self.copy(g).wait()
            add(g * CHUNK, CHUNK)
            return carry

        lax.fori_loop(0, full, group, 0)
        done = full * CHUNK

        @pl.when(done < self.live)
        def _():
            self.copy(full).wait()

        for width in (4, 1):

            def few(g, carry, width=width, done=done):
                add(done + g * width, width)
                return carry

            groups = (self.live - done) // width
            lax.fori_loop(0, groups, few, 0)
            done = done + groups * width


def forward_kernel(count, rows, cols, source, wavelet, image, held, places, sems):
    sensors = Sensors(count, source, held, sems)
    sensors.start()
    image[...] = jnp.zeros_like(image)
    mine = lax.axis_index("cols") >> 1

    def note(at, carry):
        q, core, part = at & 3, (at >> 2) & 1, at >> 3
        by_ring = ring_place(2 * ((part + mine) & 1) + (q & 1), core, part >> 1)
        places[at] = jnp.where(q >= 2, by_ring, plane_place(core, part) + q)
        return carry

    lax.fori_loop(0, COL_BLOCKS, note, 0)

    def add(first, width):
        terms = []
        for u in range(width):
            terms.append(dot(held[first + u], wavelet[places[cols[0, first + u]]]))
        for u in range(width):
            image[rows[0, first + u]] += terms[u]

    sensors.run(add)


SENSOR_SCRATCH = (
    pltpu.VMEM((SLOTS, BLK, BLK), BF16),
    pltpu.SemaphoreType.DMA((SLOTS // CHUNK,)),
)


def forward(count, rows, cols, sens, wavelet):
    held, sems = SENSOR_SCRATCH
    return pl.pallas_call(
        forward_kernel,
        out_shape=jax.ShapeDtypeStruct((ROW_BLOCKS, BLK, BLK), F32),
        in_specs=[SMEM, SMEM, SMEM, ANY, VMEM],
        out_specs=VMEM,
        scratch_shapes=[
            held,
            pltpu.SMEM((COL_BLOCKS,), jnp.int32),
            sems,
        ],
        compiler_params=pltpu.CompilerParams(vmem_limit_bytes=MIDDLE_LIMIT),
        name="forward",
    )(count, rows, cols, sens, wavelet)


class Ring:
    def __init__(self, me, plus, minus, send, recv, far=None):
        self.me, self.plus, self.minus = me, plus, minus
        self.others = ((2, far), (1, plus), (3, minus))
        self.send, self.recv = send, recv
        self.started = []

    def at(self, step):
        return lax.rem(self.me + step, 4)

    def copy(self, src, dst, device, slot):
        copy = remote(src, dst, self.send.at[slot], self.recv.at[slot], device)
        copy.start()
        self.started.append(copy)

    def arrived(self, ref, slot):
        remote(ref, ref, self.send.at[slot], self.recv.at[slot], self.plus).wait_recv()

    def drain(self):
        for copy in self.started:
            copy.wait_send()
        self.started = []


class Reduce:
    def __init__(self, ring, data, base, chunk, relay, landed):
        self.ring, self.data, self.base, self.chunk = ring, data, base, chunk
        self.half = chunk // 2
        self.relay, self.landed = relay, landed

    def rows(self, step, h):
        start = self.base + self.ring.at(step) * self.chunk + h * self.half
        return pl.ds(pl.multiple_of(start, self.half), self.half)

    def relay_at(self, side):
        return self.relay.at[side, pl.ds(0, self.half)]

    def landed_at(self, side, h):
        return self.landed.at[side, pl.ds(h * self.half, self.half)]

    def begin(self):
        ring, data = self.ring, self.data
        ring.copy(data.at[self.rows(2, 0)], self.relay_at(0), ring.plus, 0)
        ring.copy(data.at[self.rows(2, 1)], self.relay_at(1), ring.minus, 1)
        ring.copy(data.at[self.rows(1, 1)], self.landed_at(0, 1), ring.plus, 2)
        ring.copy(data.at[self.rows(3, 0)], self.landed_at(1, 0), ring.minus, 3)

    def pass_on(self):
        ring, data = self.ring, self.data
        ring.arrived(self.relay_at(0), 0)
        data[self.rows(1, 0), :] += self.relay[0, : self.half]
        ring.copy(data.at[self.rows(1, 0)], self.landed_at(0, 0), ring.plus, 4)
        ring.arrived(self.relay_at(1), 1)
        data[self.rows(3, 1), :] += self.relay[1, : self.half]
        ring.copy(data.at[self.rows(3, 1)], self.landed_at(1, 1), ring.minus, 5)

    def finish(self):
        ring, data = self.ring, self.data
        ring.arrived(self.landed_at(0, 1), 2)
        ring.arrived(self.landed_at(1, 0), 3)
        ring.arrived(self.landed_at(0, 0), 4)
        ring.arrived(self.landed_at(1, 1), 5)
        for h in range(2):
            part = pl.ds(h * self.half, self.half)
            data[self.rows(0, h), :] += self.landed[0, part, :] + self.landed[1, part, :]


class DirectReduce:
    def __init__(self, ring, data, base, chunk, landed):
        self.ring, self.data, self.base, self.chunk = ring, data, base, chunk
        self.landed = landed

    def rows(self, step):
        start = self.base + self.ring.at(step) * self.chunk
        return pl.ds(pl.multiple_of(start, self.chunk), self.chunk)

    def begin(self):
        for step, device in self.ring.others:
            self.ring.copy(
                self.data.at[self.rows(step)], self.landed.at[step - 1], device, step - 1
            )

    def pass_on(self):
        for step in range(3):
            self.ring.arrived(self.landed.at[step], step)

    def finish(self):
        own = self.rows(0)
        total = self.data[own, :] + self.landed[0]
        self.data[own, :] = total + (self.landed[1] + self.landed[2])


class DirectGather:
    def __init__(self, ring, data, base, chunk):
        self.ring, self.data, self.base, self.chunk = ring, data, base, chunk

    def rows(self, step):
        start = self.base + self.ring.at(step) * self.chunk
        return self.data.at[pl.ds(pl.multiple_of(start, self.chunk), self.chunk)]

    def begin(self):
        for step, device in self.ring.others:
            self.ring.copy(self.rows(0), self.rows(0), device, step - 1)

    def pass_on(self):
        pass

    def finish(self):
        for step in (1, 3, 2):
            self.ring.arrived(self.rows(4 - step), step - 1)


STREAMS = 4
STREAM = ROW_BLOCKS * BLK // STREAMS
BIG = STREAM // 4
SMALL = BIG // 4


def combine_kernel(partial, image, fill, big_relay, big_landed, small_landed, send, recv):
    row, col, _, _ = place()
    y, x = lax.div(col, 4), lax.rem(col, 4)
    x_ring = [(row, y * 4 + lax.rem(x + step, 4)) for step in range(4)]
    y_ring = [(row, lax.rem(y + step, 4) * 4 + x) for step in range(4)]
    greet(x_ring[1:] + y_ring[1:])()
    fill.wait()

    def ring(axis, slot):
        me, devices = ((x, x_ring), (y, y_ring))[axis]
        return Ring(me, devices[1], devices[3], send.at[slot], recv.at[slot], devices[2])

    streams = range(STREAMS)
    axis = [a % 2 for a in streams]
    bases = [a * STREAM for a in streams]
    inner = [bases[a] + (x, y)[axis[a]] * BIG for a in streams]
    wide_rings = [ring(axis[a], a) for a in streams]
    cross_rings = [ring(1 - axis[a], STREAMS + a) for a in streams]
    back_rings = [ring(1 - axis[a], 2 * STREAMS + a) for a in streams]
    last_rings = [ring(axis[a], 3 * STREAMS + a) for a in streams]
    wide = [Reduce(wide_rings[a], partial, bases[a], BIG, big_relay.at[a], big_landed.at[a]) for a in streams]
    cross = [DirectReduce(cross_rings[a], partial, inner[a], SMALL, small_landed.at[a]) for a in streams]
    back = [DirectGather(back_rings[a], image, inner[a], SMALL) for a in streams]
    last = [DirectGather(last_rings[a], image, bases[a], BIG) for a in streams]

    def cast(a):
        start = inner[a] + (y, x)[axis[a]] * SMALL
        own = pl.ds(pl.multiple_of(start, SMALL), SMALL)
        image[own, :] = partial[own, :].astype(BF16)

    pairs = [(a, a + 1) for a in range(0, STREAMS, 2)]
    for a in streams:
        wide[a].begin()
    for a in streams:
        wide[a].pass_on()
    for pair in pairs:
        for a in pair:
            wide[a].finish()
            cross[a].begin()
    for pair in pairs:
        for a in pair:
            cross[a].pass_on()
            cross[a].finish()
            cast(a)
            back[a].begin()
    for pair in pairs:
        for a in pair:
            back[a].finish()
            last[a].begin()
    for a in streams:
        last[a].finish()
    for group in (wide_rings, cross_rings, back_rings, last_rings):
        for one in group:
            one.drain()


def combine(partial):
    vmem = pl.BlockSpec(memory_space=pltpu.VMEM)
    rows = ROW_BLOCKS * BLK

    def kernel(partial_ref, image_ref, data, *rest):
        copy = pltpu.make_async_copy(partial_ref, data, rest[-1])
        copy.start()
        combine_kernel(data, image_ref, copy, *rest[:-1])

    return pl.pallas_call(
        kernel,
        out_shape=jax.ShapeDtypeStruct((rows, BLK), BF16),
        in_specs=[pl.BlockSpec(memory_space=pl.ANY)],
        out_specs=vmem,
        scratch_shapes=[
            pltpu.VMEM((rows, BLK), F32),
            pltpu.VMEM((STREAMS, 2, BIG // 2, BLK), F32),
            pltpu.VMEM((STREAMS, 2, BIG, BLK), F32),
            pltpu.VMEM((STREAMS, 3, SMALL, BLK), F32),
            pltpu.SemaphoreType.DMA((4 * STREAMS, 6)),
            pltpu.SemaphoreType.DMA((4 * STREAMS, 6)),
            pltpu.SemaphoreType.DMA,
        ],
        compiler_params=pltpu.CompilerParams(
            collective_id=1, has_side_effects=True, vmem_limit_bytes=MIDDLE_LIMIT
        ),
        cost_estimate=cost(1 << 20, 80 << 20),
        name="combine",
    )(partial.reshape(rows, BLK))


def adjoint_kernel(
    count, rows, cols, source, image, data_image, adjoint, held, flipped, plain, sem, sems
):
    sensors = Sensors(count, source, held, sems)
    sensors.start()
    adjoint[...] = jnp.zeros_like(adjoint)

    def flip(b, carry):
        block = image[b].astype(F32)
        plain[b] = block
        flipped[b] = block.T.astype(BF16)
        return carry

    lax.fori_loop(0, ROW_BLOCKS, flip, 0, unroll=2)
    store = pltpu.make_async_copy(plain, data_image, sem)
    store.start()
    shift = lax.axis_index("cols") >> 1

    def add(first, width):
        terms = []
        for u in range(width):
            terms.append(dot(flipped[rows[0, first + u]], held[first + u]))
        for u in range(width):
            at = cols[0, first + u]
            part = at >> 3
            adjoint[(at >> 2) & 1, at & 3, (part + shift) & 3, part >> 2] += terms[u]

    sensors.run(add)
    store.wait()


def adjoin(count, rows, cols, sens, image):
    held, sems = SENSOR_SCRATCH
    return pl.pallas_call(
        adjoint_kernel,
        out_shape=(
            jax.ShapeDtypeStruct((ROW_BLOCKS, BLK, BLK), F32),
            jax.ShapeDtypeStruct((2, NZ, LANES, EACH, BLK, BLK), F32),
        ),
        in_specs=[SMEM, SMEM, SMEM, ANY, VMEM],
        out_specs=(ANY, VMEM),
        scratch_shapes=[
            held,
            pltpu.VMEM((ROW_BLOCKS, BLK, BLK), BF16),
            pltpu.VMEM((ROW_BLOCKS, BLK, BLK), F32),
            pltpu.SemaphoreType.DMA,
            sems,
        ],
        compiler_params=pltpu.CompilerParams(vmem_limit_bytes=MIDDLE_LIMIT),
        name="adjoin",
    )(count, rows, cols, sens, image)


def return_kernel(
    partial, smooth, scale, signs, out, own, stage, pair, relay_out, relay, landed, gathered, sem, send, recv, part_send, part_recv, *sem_refs
):
    where = place()
    row, col, z, core = where
    fill = pltpu.make_async_copy(partial.at[core], own, sem)
    fill.start()
    parts = Parts(where)
    mine = parts.mine

    def out_piece(at, k, p, h):
        first = p * EACH
        return out.at[at, k, pl.ds(first, EACH) if h is None else pl.ds(first + h, 1)]

    gather = RowGather(out_piece, sem_refs, where)
    plus, minus, partner = gather.neighbour(1), gather.neighbour(3), gather.partner()
    greet([plus, minus, partner], (parts.first, parts.device))()
    rings = [Ring(z, plus, minus, send.at[p], recv.at[p]) for p in range(LANES)]
    for p in range(LANES):
        ring = rings[p]
        for slot, step in ((6, 2), (7, 1), (8, 3), (9, 0)):
            q = ring.at(step)
            ring.copy(partial.at[1 - core, q, p], pair.at[q, p], partner, slot)
    fill.wait()

    def total(p, step, h):
        q = rings[p].at(step)
        return own[q, p, h] + pair[q, p, h]

    def paired(p, step, slot):
        rings[p].arrived(pair.at[rings[p].at(step), p], slot)

    def ship(p, value, slot, dst, device, sem):
        relay_out[p, slot] = value.astype(BF16)
        rings[p].copy(relay_out.at[p, slot], dst, device, sem)

    def launch(p):
        paired(p, 2, 6)
        ship(p, total(p, 2, 0), 0, relay.at[p, 0], plus, 0)
        ship(p, total(p, 2, 1), 1, relay.at[p, 1], minus, 1)
        paired(p, 1, 7)
        ship(p, total(p, 1, 1), 3, landed.at[p, 0, 1], plus, 2)
        paired(p, 3, 8)
        ship(p, total(p, 3, 0), 4, landed.at[p, 1, 0], minus, 3)

    def pass_on(p):
        ring = rings[p]
        ring.arrived(relay.at[p, 0], 0)
        ship(p, total(p, 1, 0) + relay[p, 0].astype(F32), 2, landed.at[p, 0, 0], plus, 4)
        ring.arrived(relay.at[p, 1], 1)
        ship(p, total(p, 3, 1) + relay[p, 1].astype(F32), 5, landed.at[p, 1, 1], minus, 5)

    lane_scale = scale[0:1, :]

    def member(p, i):
        return i * LANES + lax.rem(p + PARTS - mine, LANES)

    def part_copy(m):
        return remote(
            stage.at[m], gathered.at[mine], part_send.at[m], part_recv.at[mine], parts.device_at(m)
        )

    def hand_over(p):
        ring = rings[p]
        paired(p, 0, 9)
        for slot, (side, h) in ((2, (0, 1)), (3, (1, 0)), (4, (0, 0)), (5, (1, 1))):
            ring.arrived(landed.at[p, side, h], slot)
        for h in range(EACH):
            m = member(p, h)
            value = total(p, 0, h) + (landed[p, 0, h].astype(F32) + landed[p, 1, h].astype(F32))
            value = (value * lane_scale).astype(BF16)
            stage[m] = value

            @pl.when(parts.own(m))
            def _(m=m):
                gathered[m] = stage[m]

            @pl.when(jnp.logical_not(parts.own(m)))
            def _(m=m):
                part_copy(m).start()

    def synthesise(p):
        for h in range(EACH):
            m = member(p, h)

            @pl.when(jnp.logical_not(parts.own(m)))
            def _(m=m):
                ref = gathered.at[m]
                remote(ref, ref, part_send.at[0], part_recv.at[m], partner).wait_recv()

            cells = lax.dot_general(
                signs[...], gathered[m], (((1,), (1,)), ((), ())), preferred_element_type=F32
            )
            out[z, core, p * EACH + h] = (cells + smooth[m]).astype(BF16)
        gather.begin(p)

    for p in range(LANES):
        launch(p)
    pass_on(0)
    pass_on(1)
    hand_over(0)
    pass_on(2)
    hand_over(1)
    pass_on(3)
    hand_over(2)
    synthesise(0)
    hand_over(3)
    synthesise(1)
    synthesise(2)
    gather.pass_on(0)
    synthesise(3)
    for p in range(1, LANES):
        gather.pass_on(p)
        gather.finish(p - 1)
    gather.finish(LANES - 1)
    gather.close(LANES)

    def drain(m, carry):
        @pl.when(jnp.logical_not(parts.own(m)))
        def _():
            part_copy(m).wait_send()

        return carry

    lax.fori_loop(0, PARTS, drain, 0)
    for ring in rings:
        ring.drain()


def give_back(partial, smooth):
    return pl.pallas_call(
        return_kernel,
        out_shape=jax.ShapeDtypeStruct((NZ, 2, PARTS, BLK, BLK), BF16),
        in_specs=[ANY, VMEM, VMEM, VMEM],
        out_specs=VMEM,
        scratch_shapes=[
            pltpu.VMEM((NZ, LANES, EACH, BLK, BLK), F32),
            pltpu.VMEM((PARTS, BLK, BLK), BF16),
            pltpu.VMEM((NZ, LANES, EACH, BLK, BLK), F32),
            pltpu.VMEM((LANES, 6, BLK, BLK), BF16),
            pltpu.VMEM((LANES, 2, BLK, BLK), BF16),
            pltpu.VMEM((LANES, 2, 2, BLK, BLK), BF16),
            pltpu.VMEM((PARTS, BLK, BLK), BF16),
            pltpu.SemaphoreType.DMA,
            pltpu.SemaphoreType.DMA((LANES, 10)),
            pltpu.SemaphoreType.DMA((LANES, 10)),
            pltpu.SemaphoreType.DMA((PARTS,)),
            pltpu.SemaphoreType.DMA((PARTS,)),
            *gather_sems(LANES),
        ],
        compiler_params=pltpu.CompilerParams(
            collective_id=2, has_side_effects=True, vmem_limit_bytes=MIDDLE_LIMIT
        ),
        cost_estimate=cost(1 << 30, 80 << 20),
        name="give_back",
    )(
        partial,
        smooth,
        jnp.asarray(np.broadcast_to(SCALE[None, :], (8, BLK)), F32),
        jnp.asarray(SIGNS.T, BF16),
    )


def place_kernel(order, product, out, cells, out_sems):
    def store(i, block):
        return pltpu.make_async_copy(cells.at[i], out.at[block], out_sems.at[i])

    shift = lax.axis_index("cols") >> 1
    for i in range(2 * NZ):
        for n in range(PARTS):
            q, core, p = i // 2, i % 2, n // EACH
            at = i * PARTS + n
            cells[at] = product[q, core, n].astype(F32)
            m = (n % EACH) * LANES + ((p + PARTS - shift) & (LANES - 1))
            store(at, order[0, (m * 2 + core) * 4 + q]).start()

    def finish(i, carry):
        store(i, 0).wait()
        return carry

    lax.fori_loop(0, COL_BLOCKS, finish, 0)


def place_cells(order, product):
    return pl.pallas_call(
        place_kernel,
        out_shape=jax.ShapeDtypeStruct((COL_BLOCKS, BLK, BLK), F32),
        in_specs=[SMEM, VMEM],
        out_specs=ANY,
        scratch_shapes=[
            pltpu.VMEM((COL_BLOCKS, BLK, BLK), F32),
            pltpu.SemaphoreType.DMA((COL_BLOCKS,)),
        ],
        compiler_params=pltpu.CompilerParams(vmem_limit_bytes=MIDDLE_LIMIT),
        name="place_cells",
    )(order, product)


def local(model_dir, sens_blocks, blk_row, blk_col, blk_count, send_order, neighbors, face_weight):
    wavelet, smooth = analyse(send_order, model_dir, neighbors, face_weight)
    partial_image = forward(blk_count, blk_row, blk_col, sens_blocks, wavelet)
    image_half = combine(partial_image).reshape(ROW_BLOCKS, BLK, BLK)
    data_image, partial_adjoint = adjoin(blk_count, blk_row, blk_col, sens_blocks, image_half)
    normal_product = place_cells(send_order, give_back(partial_adjoint, smooth))
    return data_image.reshape(ROW_BLOCKS * BLK, BLK), normal_product.reshape(CELLS, BLK)


def solution(mesh):
    placed = (
        P("cols", None),
        P("rows", "cols", None, None),
        P("rows", "cols"),
        P("rows", "cols"),
        P("rows", "cols"),
        P("cols", None),
        P(None, "cols"),
        P(None, "cols"),
    )
    return jax.shard_map(
        local,
        mesh=mesh,
        in_specs=placed,
        out_specs=(P("rows", None), P("cols", None)),
        check_vma=False,
    )
```

```python
import math

import jax
import jax.numpy as jnp
import numpy as np
from jax import lax
from jax.experimental import pallas as pl
from jax.experimental.pallas import tpu as pltpu
from jax.sharding import PartitionSpec as P

BLK = 128
RIM = 64
NROWS = 8
NCOLS = 16
NZ = 4
ROW_BLOCKS = 32
COL_BLOCKS = 64
SLOTS = 384
CHUNK = 32
VMEM_LIMIT = 51 << 20
MIDDLE_LIMIT = 42 << 20
ADJOIN_LIMIT = 38 << 20
LATE_LIMIT = 32 << 20
MESH = pl.DeviceIdType.MESH
F32 = jnp.float32
BF16 = jnp.bfloat16


VMEM = pl.BlockSpec(memory_space=pltpu.VMEM)
SMEM = pl.BlockSpec(memory_space=pltpu.SMEM)
ANY = pl.BlockSpec(memory_space=pl.ANY)


def cost(flops, moved):
    return pl.CostEstimate(flops=flops, bytes_accessed=moved, transcendentals=0)


def haar_parts():
    matrix = np.ones((1, 1))
    while matrix.shape[0] < BLK:
        length = matrix.shape[0]
        upper = np.kron(matrix, np.array([[1.0, 1.0]]))
        lower = np.kron(np.eye(length), np.array([[1.0, -1.0]]))
        matrix = np.concatenate([upper, lower], axis=0) / math.sqrt(2.0)
    scale = np.abs(matrix).max(axis=1)
    signs = np.round(matrix / scale[:, None])
    return signs, scale


SIGNS, SCALE = haar_parts()


def haar_tiles():
    row = lax.broadcasted_iota(jnp.int32, (BLK, BLK), 0)
    col = lax.broadcasted_iota(jnp.int32, (BLK, BLK), 1)
    width = jnp.full((BLK, BLK), BLK, jnp.int32)
    start = jnp.zeros((BLK, BLK), jnp.int32)
    scale = jnp.full((BLK, BLK), SCALE[0], F32)
    for level in range(7):
        first, long = 1 << level, BLK >> level
        inside = row >= first
        width = jnp.where(inside, long, width)
        start = jnp.where(inside, (row - first) * long, start)
        scale = jnp.where(inside, np.float32(SCALE[first]), scale)
    at = col - start
    middle = jnp.where(row == 0, width, jnp.where(width > 0, width >> 1, 0))
    signs = jnp.where(at < middle, 1.0, -1.0)
    signs = jnp.where((at >= 0) & (at < width), signs, 0.0)
    return signs.astype(BF16), scale


def split(value):
    high = value.astype(BF16)
    low = (value - high.astype(F32)).astype(BF16)
    return high, low


def dot(a, b):
    return jnp.dot(a, b, preferred_element_type=F32)


def remote(src, dst, send_sem, recv_sem, device):
    return pltpu.make_async_remote_copy(
        src_ref=src,
        dst_ref=dst,
        send_sem=send_sem,
        recv_sem=recv_sem,
        device_id=device,
        device_id_type=MESH,
    )


def place():
    row = lax.axis_index("rows")
    col = lax.axis_index("cols")
    return row, col, lax.div(row, 2), lax.rem(row, 2)


def z_device(z, step, core, col):
    return (lax.rem(z + step, NZ) * 2 + core, col)


def greet(devices, extra=None):
    barrier = pltpu.get_barrier_semaphore()
    for device in devices:
        pl.semaphore_signal(barrier, inc=1, device_id=device, device_id_type=MESH)
    count = len(devices)
    if extra is not None:
        first, device_of = extra

        def signal(i, carry):
            pl.semaphore_signal(barrier, inc=1, device_id=device_of(i), device_id_type=MESH)
            return carry

        lax.fori_loop(first, PARTS, signal, 0)
        count = count + PARTS - first

    def wait_for_all():
        pl.semaphore_wait(barrier, count)

    return wait_for_all


PARTS = NCOLS // 2
GROUP = PARTS // 2
LANES = 4
EACH = PARTS // LANES


class RowGather:
    def __init__(self, piece, sem_refs, where):
        self.piece = piece
        self.g_send, self.minus, self.plus, self.far, self.pair = sem_refs
        self.row, self.col, self.z, self.core = where
        self.sends = []

    def ref(self, step, p, h=None, core=None):
        return self.piece(
            lax.rem(self.z + step, NZ), self.core if core is None else core, p, h
        )

    def send(self, ref, device, recv_sem):
        copy = remote(ref, ref, self.g_send.at[len(self.sends)], recv_sem, device)
        copy.start()
        self.sends.append(copy)

    def arrived(self, ref, recv_sem):
        remote(ref, ref, self.g_send.at[0], recv_sem, self.partner()).wait_recv()

    def partner(self):
        return self.z * 2 + 1 - self.core, self.col

    def neighbour(self, step):
        return z_device(self.z, step, self.core, self.col)

    def begin(self, p):
        own = self.ref(0, p)
        self.send(own, self.neighbour(1), self.minus.at[p])
        self.send(own, self.neighbour(3), self.plus.at[p])
        self.send(own, self.partner(), self.pair.at[0, p])

    def pass_on(self, p):
        self.arrived(self.ref(3, p), self.minus.at[p])
        self.send(self.ref(3, p, 0), self.neighbour(1), self.far.at[0, p])
        self.arrived(self.ref(1, p), self.plus.at[p])
        self.send(self.ref(1, p, 1), self.neighbour(3), self.far.at[1, p])
        self.send(self.ref(3, p), self.partner(), self.pair.at[3, p])
        self.send(self.ref(1, p), self.partner(), self.pair.at[1, p])

    def finish(self, p):
        for h in range(2):
            half = self.ref(2, p, h)
            self.arrived(half, self.far.at[h, p])
            self.send(half, self.partner(), self.pair.at[2 + 2 * h, p])

    def close(self, pieces):
        other = 1 - self.core
        for p in range(pieces):
            for step in (0, 1, 3):
                self.arrived(self.ref(step, p, None, other), self.pair.at[step, p])
            for h in range(2):
                self.arrived(self.ref(2, p, h, other), self.pair.at[2 + 2 * h, p])
        for copy in self.sends:
            copy.wait_send()


def gather_sems(pieces):
    return [
        pltpu.SemaphoreType.DMA((9 * pieces,)),
        pltpu.SemaphoreType.DMA((pieces,)),
        pltpu.SemaphoreType.DMA((pieces,)),
        pltpu.SemaphoreType.DMA((2, pieces)),
        pltpu.SemaphoreType.DMA((5, pieces)),
    ]


class Parts:
    def __init__(self, where):
        self.row, self.col, self.z, self.core = where
        self.mine = lax.div(self.col, 2)
        self.first = jnp.where(self.core == lax.rem(self.col, 2), 1, 0)

    def slot(self, i):
        return lax.rem(self.mine + i, PARTS)

    def device_at(self, m):
        return self.z * 2 + lax.rem(self.col, 2), m * 2 + self.core

    def device(self, i):
        return self.device_at(self.slot(i))

    def own(self, m):
        return m * 2 + self.core == self.col


CELLS = COL_BLOCKS * BLK


def cells_of(body, block):
    return jnp.concatenate([body[2 * block], body[2 * block + 1]], axis=0)


def tabulate(neighbors, weights, tables, first_cell):
    def tile(t, carry):
        at = pl.ds(pl.multiple_of(t * BLK, BLK), BLK)
        near = (neighbors[:, at] - (first_cell + t * BLK - RIM)).astype(F32)
        tables[t] = jnp.concatenate([near, weights[:, at]], axis=0)
        return carry

    lax.fori_loop(0, COL_BLOCKS, tile, 0)


def smooth_tile(body, rims, tables, tile):
    table = tables[tile].T
    span = lax.broadcasted_iota(jnp.int32, (BLK, 2 * BLK), 1).astype(F32)
    mix = jnp.zeros((BLK, 2 * BLK), F32)
    for face in range(4):
        mix += jnp.where(table[:, face : face + 1] == span, table[:, 4 + face : 5 + face], 0.0)
    mix_high, mix_low = split(mix)
    center = cells_of(body, tile)
    last = COL_BLOCKS - 1
    low = jnp.where(tile == 0, rims[0], body[jnp.maximum(2 * tile - 1, 0)])
    high = jnp.where(tile == last, rims[1], body[jnp.minimum(2 * tile + 2, 2 * last)])
    window = jnp.concatenate([low, center, high], axis=0)
    near_high, near_low = split(window)
    mixed = dot(mix_high, near_high) + dot(mix_low, near_high) + dot(mix_high, near_low)
    total = table[:, 4:5] + table[:, 5:6] + table[:, 6:7] + table[:, 7:8]
    return total * center - mixed


RING_BLOCKS = COL_BLOCKS // 2


def ring_place(z, core, part):
    return (z * 2 + core) * GROUP + part


def plane_place(core, part):
    return RING_BLOCKS + (core * PARTS + part) * 2


def analyse_kernel(
    order,
    model,
    wavelet,
    rims,
    body,
    ring_stage,
    plane_stage,
    sems,
    ring_send,
    ring_recv,
    plane_send,
    plane_recv,
    plane_pair,
    *sem_refs,
):
    where = place()
    row, col, z, core = where
    fill = pltpu.make_async_copy(model, body, sems.at[4])
    fill.start()
    parts = Parts(where)
    mine, lane = parts.mine, lax.div(z, 2)

    def ring_piece(at, k, p, h):
        first = ring_place(at, k, p * 2)
        return wavelet.at[pl.ds(first, 2) if h is None else pl.ds(first + h, 1)]

    gather = RowGather(ring_piece, sem_refs, where)
    below, above = (row, lax.rem(col + NCOLS - 1, NCOLS)), (row, lax.rem(col + 1, NCOLS))
    wait_for_all = greet(
        [gather.neighbour(1), gather.neighbour(3), gather.partner(), below, above],
        (parts.first, parts.device),
    )
    up = remote(
        model.at[2 * COL_BLOCKS - 1],
        rims.at[0],
        sems.at[0],
        sems.at[2],
        above,
    )
    down = remote(
        model.at[0],
        rims.at[1],
        sems.at[1],
        sems.at[3],
        below,
    )
    signs, scale = haar_tiles()
    sign_pair = jnp.concatenate([signs, signs], axis=1)
    fill.wait()

    def block_of(m, q):
        return order[0, (m * 2 + core) * 4 + q]

    def coefficients(m, q):
        high, low = split(cells_of(body, block_of(m, q)))
        product = dot(sign_pair, jnp.concatenate([high, low], axis=0))
        return (product * scale).astype(BF16)

    def ring_part(i):
        return i * 2 + lax.rem(lane + mine, 2)

    def make_ring(i, carry):
        ring_stage[i] = coefficients(ring_part(i), 2 + lax.rem(z, 2))
        return carry

    lax.fori_loop(0, GROUP, make_ring, 0)
    wait_for_all()

    def ring_copy(i):
        return remote(
            ring_stage.at[i],
            wavelet.at[ring_place(z, lax.rem(col, 2), lax.div(mine, 2))],
            ring_send.at[i],
            ring_recv.at[lax.div(mine, 2)],
            parts.device_at(ring_part(i)),
        )

    def spread_ring(i, carry):
        @pl.when(parts.own(ring_part(i)))
        def _():
            wavelet[ring_place(z, core, lax.div(mine, 2))] = ring_stage[i]

        @pl.when(jnp.logical_not(parts.own(ring_part(i))))
        def _():
            ring_copy(i).start()

        return carry

    lax.fori_loop(0, GROUP, spread_ring, 0)
    up.start()
    down.start()

    def plane_copy(i):
        return remote(
            plane_stage.at[i],
            wavelet.at[pl.ds(plane_place(lax.rem(col, 2), mine), 2)],
            plane_send.at[i],
            plane_recv.at[mine],
            parts.device(i),
        )

    def spread_plane(i, carry):
        for q in range(2):
            plane_stage[i, q] = coefficients(parts.slot(i), q)
        plane_copy(i).start()
        return carry

    lax.fori_loop(parts.first, PARTS, spread_plane, 0)

    @pl.when(parts.first == 1)
    def _():
        for q in range(2):
            wavelet[plane_place(core, mine) + q] = coefficients(mine, q)

    def wait_ring(i, carry):
        @pl.when(jnp.logical_not(parts.own(ring_part(i))))
        def _():
            ref = wavelet.at[ring_place(z, core, i)]
            remote(ref, ref, ring_send.at[0], ring_recv.at[i], gather.partner()).wait_recv()

        return carry

    def wait_plane(m, carry):
        @pl.when(jnp.logical_not(parts.own(m)))
        def _():
            ref = wavelet.at[pl.ds(plane_place(core, m), 2)]
            remote(ref, ref, plane_send.at[0], plane_recv.at[m], gather.partner()).wait_recv()

        return carry

    def half_plane(core_of, h):
        return wavelet.at[pl.ds(plane_place(core_of, h * GROUP), PARTS)]

    def swap(h):
        ref = half_plane(core, h)
        return remote(ref, ref, plane_pair.at[h], plane_pair.at[2 + h], gather.partner())

    for p in range(2):
        lax.fori_loop(2 * p, 2 * p + 2, wait_ring, 0)
        gather.begin(p)
    for p in range(2):
        gather.pass_on(p)
    for h in range(2):
        lax.fori_loop(h * GROUP, (h + 1) * GROUP, wait_plane, 0)
        swap(h).start()
    for p in range(2):
        gather.finish(p)
    gather.close(2)
    for h in range(2):
        ref = half_plane(1 - core, h)
        remote(ref, ref, plane_pair.at[h], plane_pair.at[2 + h], gather.partner()).wait_recv()
        swap(h).wait_send()

    def drain_ring(i, carry):
        @pl.when(jnp.logical_not(parts.own(ring_part(i))))
        def _():
            ring_copy(i).wait_send()

        return carry

    def drain_plane(i, carry):
        plane_copy(i).wait_send()
        return carry

    lax.fori_loop(0, GROUP, drain_ring, 0)
    lax.fori_loop(parts.first, PARTS, drain_plane, 0)
    up.wait()
    down.wait()


def analyse(order, model):
    return pl.pallas_call(
        analyse_kernel,
        out_shape=(
            jax.ShapeDtypeStruct((COL_BLOCKS, BLK, BLK), BF16),
            jax.ShapeDtypeStruct((2, RIM, BLK), F32),
        ),
        in_specs=[SMEM, ANY],
        out_specs=(VMEM, VMEM),
        scratch_shapes=[
            pltpu.VMEM((2 * COL_BLOCKS, RIM, BLK), F32),
            pltpu.VMEM((GROUP, BLK, BLK), BF16),
            pltpu.VMEM((PARTS, 2, BLK, BLK), BF16),
            pltpu.SemaphoreType.DMA((5,)),
            pltpu.SemaphoreType.DMA((GROUP,)),
            pltpu.SemaphoreType.DMA((GROUP,)),
            pltpu.SemaphoreType.DMA((PARTS,)),
            pltpu.SemaphoreType.DMA((PARTS,)),
            pltpu.SemaphoreType.DMA((4,)),
            *gather_sems(2),
        ],
        compiler_params=pltpu.CompilerParams(
            collective_id=0, has_side_effects=True, vmem_limit_bytes=VMEM_LIMIT
        ),
        cost_estimate=cost(1 << 30, 60 << 20),
        name="analyse",
    )(order, model)


class Sensors:
    def __init__(self, count, source, held, sems):
        self.live, self.source, self.held, self.sems = count[0, 0], source, held, sems

    def copy(self, g):
        part = pl.ds(g * CHUNK, CHUNK)
        return pltpu.make_async_copy(self.source.at[0, part], self.held.at[part], self.sems.at[g])

    def start(self):
        def begin(g, carry):
            self.copy(g).start()
            return carry

        lax.fori_loop(0, pl.cdiv(self.live, CHUNK), begin, 0)

    def run(self, add):
        full = self.live // CHUNK

        def group(g, carry):
            self.copy(g).wait()
            add(g * CHUNK, CHUNK)
            return carry

        lax.fori_loop(0, full, group, 0)
        done = full * CHUNK

        @pl.when(done < self.live)
        def _():
            self.copy(full).wait()

        for width in (4, 1):

            def few(g, carry, width=width, done=done):
                add(done + g * width, width)
                return carry

            groups = (self.live - done) // width
            lax.fori_loop(0, groups, few, 0)
            done = done + groups * width


def forward_kernel(count, rows, cols, source, wavelet, image, held, places, sems):
    sensors = Sensors(count, source, held, sems)
    sensors.start()
    image[...] = jnp.zeros_like(image)
    mine = lax.axis_index("cols") >> 1

    def note(at, carry):
        q, core, part = at & 3, (at >> 2) & 1, at >> 3
        by_ring = ring_place(2 * ((part + mine) & 1) + (q & 1), core, part >> 1)
        places[at] = jnp.where(q >= 2, by_ring, plane_place(core, part) + q)
        return carry

    lax.fori_loop(0, COL_BLOCKS, note, 0)

    def add(first, width):
        terms = []
        for u in range(width):
            terms.append(dot(held[first + u], wavelet[places[cols[0, first + u]]]))
        for u in range(width):
            image[rows[0, first + u]] += terms[u]

    sensors.run(add)


SENSOR_SCRATCH = (
    pltpu.VMEM((SLOTS, BLK, BLK), BF16),
    pltpu.SemaphoreType.DMA((SLOTS // CHUNK,)),
)


def forward(count, rows, cols, sens, wavelet):
    held, sems = SENSOR_SCRATCH
    return pl.pallas_call(
        forward_kernel,
        out_shape=jax.ShapeDtypeStruct((ROW_BLOCKS, BLK, BLK), F32),
        in_specs=[SMEM, SMEM, SMEM, ANY, VMEM],
        out_specs=VMEM,
        scratch_shapes=[
            held,
            pltpu.SMEM((COL_BLOCKS,), jnp.int32),
            sems,
        ],
        compiler_params=pltpu.CompilerParams(vmem_limit_bytes=MIDDLE_LIMIT),
        name="forward",
    )(count, rows, cols, sens, wavelet)


class Ring:
    def __init__(self, me, plus, minus, send, recv, far=None):
        self.me, self.plus, self.minus = me, plus, minus
        self.others = ((2, far), (1, plus), (3, minus))
        self.send, self.recv = send, recv
        self.started = []

    def at(self, step):
        return lax.rem(self.me + step, 4)

    def copy(self, src, dst, device, slot):
        copy = remote(src, dst, self.send.at[slot], self.recv.at[slot], device)
        copy.start()
        self.started.append(copy)

    def arrived(self, ref, slot):
        remote(ref, ref, self.send.at[slot], self.recv.at[slot], self.plus).wait_recv()

    def drain(self):
        for copy in self.started:
            copy.wait_send()
        self.started = []


class Reduce:
    def __init__(self, ring, data, base, chunk, relay, landed):
        self.ring, self.data, self.base, self.chunk = ring, data, base, chunk
        self.half = chunk // 2
        self.relay, self.landed = relay, landed

    def rows(self, step, h):
        start = self.base + self.ring.at(step) * self.chunk + h * self.half
        return pl.ds(pl.multiple_of(start, self.half), self.half)

    def relay_at(self, side):
        return self.relay.at[side, pl.ds(0, self.half)]

    def landed_at(self, side, h):
        return self.landed.at[side, pl.ds(h * self.half, self.half)]

    def begin(self):
        ring, data = self.ring, self.data
        ring.copy(data.at[self.rows(2, 0)], self.relay_at(0), ring.plus, 0)
        ring.copy(data.at[self.rows(2, 1)], self.relay_at(1), ring.minus, 1)
        ring.copy(data.at[self.rows(1, 1)], self.landed_at(0, 1), ring.plus, 2)
        ring.copy(data.at[self.rows(3, 0)], self.landed_at(1, 0), ring.minus, 3)

    def pass_on(self):
        ring, data = self.ring, self.data
        ring.arrived(self.relay_at(0), 0)
        data[self.rows(1, 0), :] += self.relay[0, : self.half]
        ring.copy(data.at[self.rows(1, 0)], self.landed_at(0, 0), ring.plus, 4)
        ring.arrived(self.relay_at(1), 1)
        data[self.rows(3, 1), :] += self.relay[1, : self.half]
        ring.copy(data.at[self.rows(3, 1)], self.landed_at(1, 1), ring.minus, 5)

    def finish(self):
        ring, data = self.ring, self.data
        ring.arrived(self.landed_at(0, 1), 2)
        ring.arrived(self.landed_at(1, 0), 3)
        ring.arrived(self.landed_at(0, 0), 4)
        ring.arrived(self.landed_at(1, 1), 5)
        for h in range(2):
            part = pl.ds(h * self.half, self.half)
            data[self.rows(0, h), :] += self.landed[0, part, :] + self.landed[1, part, :]


class DirectReduce:
    def __init__(self, ring, data, base, chunk, landed):
        self.ring, self.data, self.base, self.chunk = ring, data, base, chunk
        self.landed = landed

    def rows(self, step):
        start = self.base + self.ring.at(step) * self.chunk
        return pl.ds(pl.multiple_of(start, self.chunk), self.chunk)

    def begin(self):
        for step, device in self.ring.others:
            self.ring.copy(
                self.data.at[self.rows(step)], self.landed.at[step - 1], device, step - 1
            )

    def pass_on(self):
        for step in range(3):
            self.ring.arrived(self.landed.at[step], step)

    def finish(self):
        own = self.rows(0)
        total = self.data[own, :] + self.landed[0]
        self.data[own, :] = total + (self.landed[1] + self.landed[2])


class DirectGather:
    def __init__(self, ring, data, base, chunk):
        self.ring, self.data, self.base, self.chunk = ring, data, base, chunk

    def rows(self, step):
        start = self.base + self.ring.at(step) * self.chunk
        return self.data.at[pl.ds(pl.multiple_of(start, self.chunk), self.chunk)]

    def begin(self):
        for step, device in self.ring.others:
            self.ring.copy(self.rows(0), self.rows(0), device, step - 1)

    def pass_on(self):
        pass

    def finish(self):
        for step in (1, 3, 2):
            self.ring.arrived(self.rows(4 - step), step - 1)


STREAMS = 4
STREAM = ROW_BLOCKS * BLK // STREAMS
BIG = STREAM // 4
SMALL = BIG // 4


def combine_kernel(partial, flipped, plain, image, fill, big_relay, big_landed, small_landed, send, recv):
    row, col, _, _ = place()
    y, x = lax.div(col, 4), lax.rem(col, 4)
    x_ring = [(row, y * 4 + lax.rem(x + step, 4)) for step in range(4)]
    y_ring = [(row, lax.rem(y + step, 4) * 4 + x) for step in range(4)]
    greet(x_ring[1:] + y_ring[1:])()
    fill.wait()

    def ring(axis, slot):
        me, devices = ((x, x_ring), (y, y_ring))[axis]
        return Ring(me, devices[1], devices[3], send.at[slot], recv.at[slot], devices[2])

    streams = range(STREAMS)
    axis = [a % 2 for a in streams]
    bases = [a * STREAM for a in streams]
    inner = [bases[a] + (x, y)[axis[a]] * BIG for a in streams]
    wide_rings = [ring(axis[a], a) for a in streams]
    cross_rings = [ring(1 - axis[a], STREAMS + a) for a in streams]
    back_rings = [ring(1 - axis[a], 2 * STREAMS + a) for a in streams]
    last_rings = [ring(axis[a], 3 * STREAMS + a) for a in streams]
    wide = [Reduce(wide_rings[a], partial, bases[a], BIG, big_relay.at[a], big_landed.at[a]) for a in streams]
    cross = [DirectReduce(cross_rings[a], partial, inner[a], SMALL, small_landed.at[a]) for a in streams]
    back = [DirectGather(back_rings[a], image, inner[a], SMALL) for a in streams]
    last = [DirectGather(last_rings[a], image, bases[a], BIG) for a in streams]

    def cast(a):
        start = inner[a] + (y, x)[axis[a]] * SMALL
        own = pl.ds(pl.multiple_of(start, SMALL), SMALL)
        image[own, :] = partial[own, :].astype(BF16)

    pairs = [(a, a + 1) for a in range(0, STREAMS, 2)]
    for a in streams:
        wide[a].begin()
    for a in streams:
        wide[a].pass_on()
    for pair in pairs:
        for a in pair:
            wide[a].finish()
            cross[a].begin()
    for pair in pairs:
        for a in pair:
            cross[a].pass_on()
            cross[a].finish()
            cast(a)
            back[a].begin()
    for pair in pairs:
        for a in pair:
            back[a].finish()
            last[a].begin()
    for a in streams:
        last[a].finish()

        def turn(b, carry):
            block = image[pl.ds(pl.multiple_of(b * BLK, BLK), BLK), :].astype(F32)
            plain[b] = block
            flipped[b] = block.T.astype(BF16)
            return carry

        blocks = STREAM // BLK
        lax.fori_loop(a * blocks, (a + 1) * blocks, turn, 0, unroll=2)
    for group in (wide_rings, cross_rings, back_rings, last_rings):
        for one in group:
            one.drain()


def combine(partial):
    vmem = pl.BlockSpec(memory_space=pltpu.VMEM)
    rows = ROW_BLOCKS * BLK

    def kernel(partial_ref, flipped, plain, data, image, *rest):
        copy = pltpu.make_async_copy(partial_ref, data, rest[-1])
        copy.start()
        combine_kernel(data, flipped, plain, image, copy, *rest[:-1])

    return pl.pallas_call(
        kernel,
        out_shape=(
            jax.ShapeDtypeStruct((ROW_BLOCKS, BLK, BLK), BF16),
            jax.ShapeDtypeStruct((ROW_BLOCKS, BLK, BLK), F32),
        ),
        in_specs=[ANY],
        out_specs=(VMEM, VMEM),
        scratch_shapes=[
            pltpu.VMEM((rows, BLK), F32),
            pltpu.VMEM((rows, BLK), BF16),
            pltpu.VMEM((STREAMS, 2, BIG // 2, BLK), F32),
            pltpu.VMEM((STREAMS, 2, BIG, BLK), F32),
            pltpu.VMEM((STREAMS, 3, SMALL, BLK), F32),
            pltpu.SemaphoreType.DMA((4 * STREAMS, 6)),
            pltpu.SemaphoreType.DMA((4 * STREAMS, 6)),
            pltpu.SemaphoreType.DMA,
        ],
        compiler_params=pltpu.CompilerParams(
            collective_id=1, has_side_effects=True, vmem_limit_bytes=MIDDLE_LIMIT
        ),
        cost_estimate=cost(1 << 20, 80 << 20),
        name="combine",
    )(partial.reshape(rows, BLK))


def adjoint_kernel(
    count, rows, cols, source, flipped, plain, data_image, adjoint, held, sem, sems
):
    sensors = Sensors(count, source, held, sems)
    sensors.start()
    store = pltpu.make_async_copy(plain, data_image, sem)
    store.start()
    adjoint[...] = jnp.zeros_like(adjoint)
    shift = lax.axis_index("cols") >> 1

    def add(first, width):
        terms = []
        for u in range(width):
            terms.append(dot(flipped[rows[0, first + u]], held[first + u]))
        for u in range(width):
            at = cols[0, first + u]
            part = at >> 3
            adjoint[(at >> 2) & 1, at & 3, (part + shift) & 3, part >> 2] += terms[u]

    sensors.run(add)
    store.wait()


def adjoin(count, rows, cols, sens, flipped, plain):
    held, sems = SENSOR_SCRATCH
    return pl.pallas_call(
        adjoint_kernel,
        out_shape=(
            jax.ShapeDtypeStruct((ROW_BLOCKS, BLK, BLK), F32),
            jax.ShapeDtypeStruct((2, NZ, LANES, EACH, BLK, BLK), F32),
        ),
        in_specs=[SMEM, SMEM, SMEM, ANY, VMEM, ANY],
        out_specs=(ANY, VMEM),
        scratch_shapes=[held, pltpu.SemaphoreType.DMA, sems],
        compiler_params=pltpu.CompilerParams(vmem_limit_bytes=ADJOIN_LIMIT),
        name="adjoin",
    )(count, rows, cols, sens, flipped, plain)


def return_kernel(
    order, partial, body, rims, neighbors, weights, scale, signs, out, smooth, tables, own, stage, pair, relay_out, relay, landed, gathered, sem, send, recv, part_send, part_recv, *sem_refs
):
    where = place()
    row, col, z, core = where
    fill = pltpu.make_async_copy(partial.at[core], own, sem)
    fill.start()
    parts = Parts(where)
    mine = parts.mine

    def out_piece(at, k, p, h):
        first = p * EACH
        return out.at[at, k, pl.ds(first, EACH) if h is None else pl.ds(first + h, 1)]

    gather = RowGather(out_piece, sem_refs, where)
    plus, minus, partner = gather.neighbour(1), gather.neighbour(3), gather.partner()
    greet([plus, minus, partner], (parts.first, parts.device))()
    rings = [Ring(z, plus, minus, send.at[p], recv.at[p]) for p in range(LANES)]
    for p in range(LANES):
        ring = rings[p]
        for slot, step in ((6, 2), (7, 1), (8, 3), (9, 0)):
            q = ring.at(step)
            ring.copy(partial.at[1 - core, q, p], pair.at[q, p], partner, slot)
    fill.wait()

    def total(p, step, h):
        q = rings[p].at(step)
        return own[q, p, h] + pair[q, p, h]

    def paired(p, step, slot):
        rings[p].arrived(pair.at[rings[p].at(step), p], slot)

    def ship(p, value, slot, dst, device, sem):
        relay_out[p, slot] = value.astype(BF16)
        rings[p].copy(relay_out.at[p, slot], dst, device, sem)

    def launch(p):
        paired(p, 2, 6)
        ship(p, total(p, 2, 0), 0, relay.at[p, 0], plus, 0)
        ship(p, total(p, 2, 1), 1, relay.at[p, 1], minus, 1)
        paired(p, 1, 7)
        ship(p, total(p, 1, 1), 3, landed.at[p, 0, 1], plus, 2)
        paired(p, 3, 8)
        ship(p, total(p, 3, 0), 4, landed.at[p, 1, 0], minus, 3)

    def pass_on(p):
        ring = rings[p]
        ring.arrived(relay.at[p, 0], 0)
        ship(p, total(p, 1, 0) + relay[p, 0].astype(F32), 2, landed.at[p, 0, 0], plus, 4)
        ring.arrived(relay.at[p, 1], 1)
        ship(p, total(p, 3, 1) + relay[p, 1].astype(F32), 5, landed.at[p, 1, 1], minus, 5)

    lane_scale = scale[0:1, :]

    def member(p, i):
        return i * LANES + lax.rem(p + PARTS - mine, LANES)

    def part_copy(m):
        return remote(
            stage.at[m], gathered.at[mine], part_send.at[m], part_recv.at[mine], parts.device_at(m)
        )

    def hand_over(p):
        ring = rings[p]
        paired(p, 0, 9)
        for slot, (side, h) in ((2, (0, 1)), (3, (1, 0)), (4, (0, 0)), (5, (1, 1))):
            ring.arrived(landed.at[p, side, h], slot)
        for h in range(EACH):
            m = member(p, h)
            value = total(p, 0, h) + (landed[p, 0, h].astype(F32) + landed[p, 1, h].astype(F32))
            value = (value * lane_scale).astype(BF16)
            stage[m] = value

            @pl.when(parts.own(m))
            def _(m=m):
                gathered[m] = stage[m]

            @pl.when(jnp.logical_not(parts.own(m)))
            def _(m=m):
                part_copy(m).start()

    def synthesise(p):
        for h in range(EACH):
            m = member(p, h)

            @pl.when(jnp.logical_not(parts.own(m)))
            def _(m=m):
                ref = gathered.at[m]
                remote(ref, ref, part_send.at[0], part_recv.at[m], partner).wait_recv()

            cells = lax.dot_general(
                signs[...], gathered[m], (((1,), (1,)), ((), ())), preferred_element_type=F32
            )
            out[z, core, p * EACH + h] = (cells + smooth[m]).astype(BF16)
        gather.begin(p)

    def smooth_one(m, carry):
        block = order[0, (m * 2 + core) * 4 + z]
        smooth[m] = smooth_tile(body, rims, tables, block)
        return carry

    for p in range(LANES):
        launch(p)
        if p == 0:
            tabulate(neighbors, weights, tables, col * CELLS)
    lax.fori_loop(0, 2, smooth_one, 0)
    pass_on(0)
    pass_on(1)
    hand_over(0)
    pass_on(2)
    hand_over(1)
    pass_on(3)
    lax.fori_loop(2, 4, smooth_one, 0)
    hand_over(2)
    hand_over(3)
    lax.fori_loop(4, PARTS, smooth_one, 0)
    synthesise(0)
    synthesise(1)
    synthesise(2)
    gather.pass_on(0)
    synthesise(3)
    for p in range(1, LANES):
        gather.pass_on(p)
        gather.finish(p - 1)
    gather.finish(LANES - 1)
    gather.close(LANES)

    def drain(m, carry):
        @pl.when(jnp.logical_not(parts.own(m)))
        def _():
            part_copy(m).wait_send()

        return carry

    lax.fori_loop(0, PARTS, drain, 0)
    for ring in rings:
        ring.drain()


def give_back(order, partial, model, rims, neighbors, weights):
    return pl.pallas_call(
        return_kernel,
        out_shape=jax.ShapeDtypeStruct((NZ, 2, PARTS, BLK, BLK), BF16),
        in_specs=[SMEM, ANY, *[VMEM] * 6],
        out_specs=VMEM,
        scratch_shapes=[
            pltpu.VMEM((PARTS, BLK, BLK), F32),
            pltpu.VMEM((COL_BLOCKS, 8, BLK), F32),
            pltpu.VMEM((NZ, LANES, EACH, BLK, BLK), F32),
            pltpu.VMEM((PARTS, BLK, BLK), BF16),
            pltpu.VMEM((NZ, LANES, EACH, BLK, BLK), F32),
            pltpu.VMEM((LANES, 6, BLK, BLK), BF16),
            pltpu.VMEM((LANES, 2, BLK, BLK), BF16),
            pltpu.VMEM((LANES, 2, 2, BLK, BLK), BF16),
            pltpu.VMEM((PARTS, BLK, BLK), BF16),
            pltpu.SemaphoreType.DMA,
            pltpu.SemaphoreType.DMA((LANES, 10)),
            pltpu.SemaphoreType.DMA((LANES, 10)),
            pltpu.SemaphoreType.DMA((PARTS,)),
            pltpu.SemaphoreType.DMA((PARTS,)),
            *gather_sems(LANES),
        ],
        compiler_params=pltpu.CompilerParams(
            collective_id=2, has_side_effects=True, vmem_limit_bytes=LATE_LIMIT
        ),
        cost_estimate=cost(1 << 30, 80 << 20),
        name="give_back",
    )(
        order,
        partial,
        model,
        rims,
        neighbors,
        weights,
        jnp.asarray(np.broadcast_to(SCALE[None, :], (8, BLK)), F32),
        jnp.asarray(SIGNS.T, BF16),
    )


def place_kernel(order, product, out, cells, out_sems):
    def store(i, block):
        return pltpu.make_async_copy(cells.at[i], out.at[block], out_sems.at[i])

    shift = lax.axis_index("cols") >> 1
    for i in range(2 * NZ):
        for n in range(PARTS):
            q, core, p = i // 2, i % 2, n // EACH
            at = i * PARTS + n
            cells[at] = product[q, core, n].astype(F32)
            m = (n % EACH) * LANES + ((p + PARTS - shift) & (LANES - 1))
            store(at, order[0, (m * 2 + core) * 4 + q]).start()

    def finish(i, carry):
        store(i, 0).wait()
        return carry

    lax.fori_loop(0, COL_BLOCKS, finish, 0)


def place_cells(order, product):
    return pl.pallas_call(
        place_kernel,
        out_shape=jax.ShapeDtypeStruct((COL_BLOCKS, BLK, BLK), F32),
        in_specs=[SMEM, VMEM],
        out_specs=ANY,
        scratch_shapes=[
            pltpu.VMEM((COL_BLOCKS, BLK, BLK), F32),
            pltpu.SemaphoreType.DMA((COL_BLOCKS,)),
        ],
        compiler_params=pltpu.CompilerParams(vmem_limit_bytes=MIDDLE_LIMIT),
        name="place_cells",
    )(order, product)


def local(model_dir, sens_blocks, blk_row, blk_col, blk_count, send_order, neighbors, face_weight):
    model = model_dir.reshape(2 * COL_BLOCKS, RIM, BLK)
    wavelet, rims = analyse(send_order, model)
    partial_image = forward(blk_count, blk_row, blk_col, sens_blocks, wavelet)
    flipped, plain = combine(partial_image)
    data_image, partial_adjoint = adjoin(blk_count, blk_row, blk_col, sens_blocks, flipped, plain)
    product = give_back(send_order, partial_adjoint, model, rims, neighbors, face_weight)
    normal_product = place_cells(send_order, product)
    return data_image.reshape(ROW_BLOCKS * BLK, BLK), normal_product.reshape(CELLS, BLK)


def solution(mesh):
    placed = (
        P("cols", None),
        P("rows", "cols", None, None),
        P("rows", "cols"),
        P("rows", "cols"),
        P("rows", "cols"),
        P("cols", None),
        P(None, "cols"),
        P(None, "cols"),
    )
    return jax.shard_map(
        local,
        mesh=mesh,
        in_specs=placed,
        out_specs=(P("rows", None), P("cols", None)),
        check_vma=False,
    )
```

```python
import math

import jax
import jax.numpy as jnp
import numpy as np
from jax import lax
from jax.experimental import pallas as pl
from jax.experimental.pallas import tpu as pltpu
from jax.sharding import PartitionSpec as P

BLK = 128
RIM = 64
NROWS = 8
NCOLS = 16
NZ = 4
ROW_BLOCKS = 32
COL_BLOCKS = 64
SLOTS = 384
CHUNK = 32
VMEM_LIMIT = 101 << 19
MIDDLE_LIMIT = 42 << 20
ADJOIN_LIMIT = 38 << 20
LATE_LIMIT = 32 << 20
MESH = pl.DeviceIdType.MESH
F32 = jnp.float32
BF16 = jnp.bfloat16


VMEM = pl.BlockSpec(memory_space=pltpu.VMEM)
SMEM = pl.BlockSpec(memory_space=pltpu.SMEM)
ANY = pl.BlockSpec(memory_space=pl.ANY)


def cost(flops, moved):
    return pl.CostEstimate(flops=flops, bytes_accessed=moved, transcendentals=0)


def haar_parts():
    matrix = np.ones((1, 1))
    while matrix.shape[0] < BLK:
        length = matrix.shape[0]
        upper = np.kron(matrix, np.array([[1.0, 1.0]]))
        lower = np.kron(np.eye(length), np.array([[1.0, -1.0]]))
        matrix = np.concatenate([upper, lower], axis=0) / math.sqrt(2.0)
    scale = np.abs(matrix).max(axis=1)
    signs = np.round(matrix / scale[:, None])
    return signs, scale


SIGNS, SCALE = haar_parts()


def haar_tiles():
    row = lax.broadcasted_iota(jnp.int32, (BLK, BLK), 0)
    col = lax.broadcasted_iota(jnp.int32, (BLK, BLK), 1)
    width = jnp.full((BLK, BLK), BLK, jnp.int32)
    start = jnp.zeros((BLK, BLK), jnp.int32)
    scale = jnp.full((BLK, BLK), SCALE[0], F32)
    for level in range(7):
        first, long = 1 << level, BLK >> level
        inside = row >= first
        width = jnp.where(inside, long, width)
        start = jnp.where(inside, (row - first) * long, start)
        scale = jnp.where(inside, np.float32(SCALE[first]), scale)
    at = col - start
    middle = jnp.where(row == 0, width, jnp.where(width > 0, width >> 1, 0))
    signs = jnp.where(at < middle, 1.0, -1.0)
    signs = jnp.where((at >= 0) & (at < width), signs, 0.0)
    return signs.astype(BF16), scale


def split(value):
    high = value.astype(BF16)
    low = (value - high.astype(F32)).astype(BF16)
    return high, low


def dot(a, b):
    return jnp.dot(a, b, preferred_element_type=F32)


def remote(src, dst, send_sem, recv_sem, device):
    return pltpu.make_async_remote_copy(
        src_ref=src,
        dst_ref=dst,
        send_sem=send_sem,
        recv_sem=recv_sem,
        device_id=device,
        device_id_type=MESH,
    )


def place():
    row = lax.axis_index("rows")
    col = lax.axis_index("cols")
    return row, col, lax.div(row, 2), lax.rem(row, 2)


def z_device(z, step, core, col):
    return (lax.rem(z + step, NZ) * 2 + core, col)


def greet(devices, extra=None):
    barrier = pltpu.get_barrier_semaphore()
    for device in devices:
        pl.semaphore_signal(barrier, inc=1, device_id=device, device_id_type=MESH)
    count = len(devices)
    if extra is not None:
        first, device_of = extra

        def signal(i, carry):
            pl.semaphore_signal(barrier, inc=1, device_id=device_of(i), device_id_type=MESH)
            return carry

        lax.fori_loop(first, PARTS, signal, 0)
        count = count + PARTS - first

    def wait_for_all():
        pl.semaphore_wait(barrier, count)

    return wait_for_all


PARTS = NCOLS // 2
GROUP = PARTS // 2
LANES = 4
EACH = PARTS // LANES


class RowGather:
    def __init__(self, piece, sem_refs, where):
        self.piece = piece
        self.g_send, self.minus, self.plus, self.far, self.pair = sem_refs
        self.row, self.col, self.z, self.core = where
        self.sends = []

    def ref(self, step, p, h=None, core=None):
        return self.piece(
            lax.rem(self.z + step, NZ), self.core if core is None else core, p, h
        )

    def send(self, ref, device, recv_sem):
        copy = remote(ref, ref, self.g_send.at[len(self.sends)], recv_sem, device)
        copy.start()
        self.sends.append(copy)

    def arrived(self, ref, recv_sem):
        remote(ref, ref, self.g_send.at[0], recv_sem, self.partner()).wait_recv()

    def partner(self):
        return self.z * 2 + 1 - self.core, self.col

    def neighbour(self, step):
        return z_device(self.z, step, self.core, self.col)

    def begin(self, p):
        own = self.ref(0, p)
        self.send(own, self.neighbour(1), self.minus.at[p])
        self.send(own, self.neighbour(3), self.plus.at[p])
        self.send(own, self.partner(), self.pair.at[0, p])

    def pass_on(self, p):
        self.arrived(self.ref(3, p), self.minus.at[p])
        self.send(self.ref(3, p, 0), self.neighbour(1), self.far.at[0, p])
        self.arrived(self.ref(1, p), self.plus.at[p])
        self.send(self.ref(1, p, 1), self.neighbour(3), self.far.at[1, p])
        self.send(self.ref(3, p), self.partner(), self.pair.at[3, p])
        self.send(self.ref(1, p), self.partner(), self.pair.at[1, p])

    def finish(self, p):
        for h in range(2):
            half = self.ref(2, p, h)
            self.arrived(half, self.far.at[h, p])
            self.send(half, self.partner(), self.pair.at[2 + 2 * h, p])

    def close(self, pieces):
        other = 1 - self.core
        for p in range(pieces):
            for step in (0, 1, 3):
                self.arrived(self.ref(step, p, None, other), self.pair.at[step, p])
            for h in range(2):
                self.arrived(self.ref(2, p, h, other), self.pair.at[2 + 2 * h, p])
        for copy in self.sends:
            copy.wait_send()


def gather_sems(pieces):
    return [
        pltpu.SemaphoreType.DMA((9 * pieces,)),
        pltpu.SemaphoreType.DMA((pieces,)),
        pltpu.SemaphoreType.DMA((pieces,)),
        pltpu.SemaphoreType.DMA((2, pieces)),
        pltpu.SemaphoreType.DMA((5, pieces)),
    ]


class Parts:
    def __init__(self, where):
        self.row, self.col, self.z, self.core = where
        self.mine = lax.div(self.col, 2)
        self.first = jnp.where(self.core == lax.rem(self.col, 2), 1, 0)

    def slot(self, i):
        return lax.rem(self.mine + i, PARTS)

    def device_at(self, m):
        return self.z * 2 + lax.rem(self.col, 2), m * 2 + self.core

    def device(self, i):
        return self.device_at(self.slot(i))

    def own(self, m):
        return m * 2 + self.core == self.col


CELLS = COL_BLOCKS * BLK


def cells_of(body, block):
    return jnp.concatenate([body[2 * block], body[2 * block + 1]], axis=0)


def tabulate(neighbors, weights, tables, first_cell):
    def tile(t, carry):
        at = pl.ds(pl.multiple_of(t * BLK, BLK), BLK)
        near = (neighbors[:, at] - (first_cell + t * BLK - RIM)).astype(F32)
        tables[t] = jnp.concatenate([near, weights[:, at]], axis=0)
        return carry

    lax.fori_loop(0, COL_BLOCKS, tile, 0)


def window_of(body, rims, tile):
    last = COL_BLOCKS - 1
    low = jnp.where(tile == 0, rims[0], body[jnp.maximum(2 * tile - 1, 0)])
    high = jnp.where(tile == last, rims[1], body[jnp.minimum(2 * tile + 2, 2 * last)])
    return jnp.concatenate([low, cells_of(body, tile), high], axis=0)


def smooth_tile(window, table):
    table = table.T
    span = lax.broadcasted_iota(jnp.int32, (BLK, 2 * BLK), 1).astype(F32)
    mix = jnp.zeros((BLK, 2 * BLK), F32)
    for face in range(4):
        mix += jnp.where(table[:, face : face + 1] == span, table[:, 4 + face : 5 + face], 0.0)
    mix_high, mix_low = split(mix)
    center = window[RIM : RIM + BLK]
    near_high, near_low = split(window)
    mixed = dot(mix_high, near_high) + dot(mix_low, near_high) + dot(mix_high, near_low)
    total = table[:, 4:5] + table[:, 5:6] + table[:, 6:7] + table[:, 7:8]
    return total * center - mixed


RING_BLOCKS = COL_BLOCKS // 2


def ring_place(z, core, part):
    return (z * 2 + core) * GROUP + part


def plane_place(core, part):
    return RING_BLOCKS + (core * PARTS + part) * 2


def analyse_kernel(
    order,
    model,
    wavelet,
    windows,
    body,
    rims,
    ring_stage,
    plane_stage,
    sems,
    ring_send,
    ring_recv,
    plane_send,
    plane_recv,
    plane_pair,
    *sem_refs,
):
    where = place()
    row, col, z, core = where
    fill = pltpu.make_async_copy(model, body, sems.at[4])
    fill.start()
    parts = Parts(where)
    mine, lane = parts.mine, lax.div(z, 2)

    def ring_piece(at, k, p, h):
        first = ring_place(at, k, p * 2)
        return wavelet.at[pl.ds(first, 2) if h is None else pl.ds(first + h, 1)]

    gather = RowGather(ring_piece, sem_refs, where)
    below, above = (row, lax.rem(col + NCOLS - 1, NCOLS)), (row, lax.rem(col + 1, NCOLS))
    wait_for_all = greet(
        [gather.neighbour(1), gather.neighbour(3), gather.partner(), below, above],
        (parts.first, parts.device),
    )
    up = remote(
        model.at[2 * COL_BLOCKS - 1],
        rims.at[0],
        sems.at[0],
        sems.at[2],
        above,
    )
    down = remote(
        model.at[0],
        rims.at[1],
        sems.at[1],
        sems.at[3],
        below,
    )
    signs, scale = haar_tiles()
    sign_pair = jnp.concatenate([signs, signs], axis=1)
    fill.wait()

    def block_of(m, q):
        return order[0, (m * 2 + core) * 4 + q]

    def coefficients(m, q):
        high, low = split(cells_of(body, block_of(m, q)))
        product = dot(sign_pair, jnp.concatenate([high, low], axis=0))
        return (product * scale).astype(BF16)

    def ring_part(i):
        return i * 2 + lax.rem(lane + mine, 2)

    def make_ring(i, carry):
        ring_stage[i] = coefficients(ring_part(i), 2 + lax.rem(z, 2))
        return carry

    lax.fori_loop(0, GROUP, make_ring, 0)
    wait_for_all()

    def ring_copy(i):
        return remote(
            ring_stage.at[i],
            wavelet.at[ring_place(z, lax.rem(col, 2), lax.div(mine, 2))],
            ring_send.at[i],
            ring_recv.at[lax.div(mine, 2)],
            parts.device_at(ring_part(i)),
        )

    def spread_ring(i, carry):
        @pl.when(parts.own(ring_part(i)))
        def _():
            wavelet[ring_place(z, core, lax.div(mine, 2))] = ring_stage[i]

        @pl.when(jnp.logical_not(parts.own(ring_part(i))))
        def _():
            ring_copy(i).start()

        return carry

    lax.fori_loop(0, GROUP, spread_ring, 0)
    up.start()
    down.start()

    def plane_copy(i):
        return remote(
            plane_stage.at[i],
            wavelet.at[pl.ds(plane_place(lax.rem(col, 2), mine), 2)],
            plane_send.at[i],
            plane_recv.at[mine],
            parts.device(i),
        )

    def spread_plane(i, carry):
        for q in range(2):
            plane_stage[i, q] = coefficients(parts.slot(i), q)
        plane_copy(i).start()
        return carry

    lax.fori_loop(parts.first, PARTS, spread_plane, 0)

    @pl.when(parts.first == 1)
    def _():
        for q in range(2):
            wavelet[plane_place(core, mine) + q] = coefficients(mine, q)

    def wait_ring(i, carry):
        @pl.when(jnp.logical_not(parts.own(ring_part(i))))
        def _():
            ref = wavelet.at[ring_place(z, core, i)]
            remote(ref, ref, ring_send.at[0], ring_recv.at[i], gather.partner()).wait_recv()

        return carry

    def wait_plane(m, carry):
        @pl.when(jnp.logical_not(parts.own(m)))
        def _():
            ref = wavelet.at[pl.ds(plane_place(core, m), 2)]
            remote(ref, ref, plane_send.at[0], plane_recv.at[m], gather.partner()).wait_recv()

        return carry

    def half_plane(core_of, h):
        return wavelet.at[pl.ds(plane_place(core_of, h * GROUP), PARTS)]

    def swap(h):
        ref = half_plane(core, h)
        return remote(ref, ref, plane_pair.at[h], plane_pair.at[2 + h], gather.partner())

    for p in range(2):
        lax.fori_loop(2 * p, 2 * p + 2, wait_ring, 0)
        gather.begin(p)
    up.wait_recv()
    down.wait_recv()

    def keep_window(m, carry):
        windows[m] = window_of(body, rims, block_of(m, z))
        return carry

    lax.fori_loop(0, PARTS, keep_window, 0)
    for p in range(2):
        gather.pass_on(p)
    for h in range(2):
        lax.fori_loop(h * GROUP, (h + 1) * GROUP, wait_plane, 0)
        swap(h).start()
    for p in range(2):
        gather.finish(p)
    gather.close(2)
    for h in range(2):
        ref = half_plane(1 - core, h)
        remote(ref, ref, plane_pair.at[h], plane_pair.at[2 + h], gather.partner()).wait_recv()
        swap(h).wait_send()

    def drain_ring(i, carry):
        @pl.when(jnp.logical_not(parts.own(ring_part(i))))
        def _():
            ring_copy(i).wait_send()

        return carry

    def drain_plane(i, carry):
        plane_copy(i).wait_send()
        return carry

    lax.fori_loop(0, GROUP, drain_ring, 0)
    lax.fori_loop(parts.first, PARTS, drain_plane, 0)
    up.wait_send()
    down.wait_send()


def analyse(order, model):
    return pl.pallas_call(
        analyse_kernel,
        out_shape=(
            jax.ShapeDtypeStruct((COL_BLOCKS, BLK, BLK), BF16),
            jax.ShapeDtypeStruct((PARTS, 2 * BLK, BLK), F32),
        ),
        in_specs=[SMEM, ANY],
        out_specs=(VMEM, VMEM),
        scratch_shapes=[
            pltpu.VMEM((2 * COL_BLOCKS, RIM, BLK), F32),
            pltpu.VMEM((2, RIM, BLK), F32),
            pltpu.VMEM((GROUP, BLK, BLK), BF16),
            pltpu.VMEM((PARTS, 2, BLK, BLK), BF16),
            pltpu.SemaphoreType.DMA((5,)),
            pltpu.SemaphoreType.DMA((GROUP,)),
            pltpu.SemaphoreType.DMA((GROUP,)),
            pltpu.SemaphoreType.DMA((PARTS,)),
            pltpu.SemaphoreType.DMA((PARTS,)),
            pltpu.SemaphoreType.DMA((4,)),
            *gather_sems(2),
        ],
        compiler_params=pltpu.CompilerParams(
            collective_id=0, has_side_effects=True, vmem_limit_bytes=VMEM_LIMIT
        ),
        cost_estimate=cost(1 << 30, 60 << 20),
        name="analyse",
    )(order, model)


class Sensors:
    def __init__(self, count, source, held, sems):
        self.live, self.source, self.held, self.sems = count[0, 0], source, held, sems

    def copy(self, g):
        part = pl.ds(g * CHUNK, CHUNK)
        return pltpu.make_async_copy(self.source.at[0, part], self.held.at[part], self.sems.at[g])

    def start(self):
        def begin(g, carry):
            self.copy(g).start()
            return carry

        lax.fori_loop(0, pl.cdiv(self.live, CHUNK), begin, 0)

    def run(self, add):
        full = self.live // CHUNK

        def group(g, carry):
            self.copy(g).wait()
            add(g * CHUNK, CHUNK)
            return carry

        lax.fori_loop(0, full, group, 0)
        done = full * CHUNK

        @pl.when(done < self.live)
        def _():
            self.copy(full).wait()

        for width in (4, 1):

            def few(g, carry, width=width, done=done):
                add(done + g * width, width)
                return carry

            groups = (self.live - done) // width
            lax.fori_loop(0, groups, few, 0)
            done = done + groups * width


def forward_kernel(count, rows, cols, source, wavelet, image, held, places, sems):
    sensors = Sensors(count, source, held, sems)
    sensors.start()
    image[...] = jnp.zeros_like(image)
    mine = lax.axis_index("cols") >> 1

    def note(at, carry):
        q, core, part = at & 3, (at >> 2) & 1, at >> 3
        by_ring = ring_place(2 * ((part + mine) & 1) + (q & 1), core, part >> 1)
        places[at] = jnp.where(q >= 2, by_ring, plane_place(core, part) + q)
        return carry

    lax.fori_loop(0, COL_BLOCKS, note, 0)

    def add(first, width):
        terms = []
        for u in range(width):
            terms.append(dot(held[first + u], wavelet[places[cols[0, first + u]]]))
        for u in range(width):
            image[rows[0, first + u]] += terms[u]

    sensors.run(add)


SENSOR_SCRATCH = (
    pltpu.VMEM((SLOTS, BLK, BLK), BF16),
    pltpu.SemaphoreType.DMA((SLOTS // CHUNK,)),
)


def forward(count, rows, cols, sens, wavelet):
    held, sems = SENSOR_SCRATCH
    return pl.pallas_call(
        forward_kernel,
        out_shape=jax.ShapeDtypeStruct((ROW_BLOCKS, BLK, BLK), F32),
        in_specs=[SMEM, SMEM, SMEM, ANY, VMEM],
        out_specs=VMEM,
        scratch_shapes=[
            held,
            pltpu.SMEM((COL_BLOCKS,), jnp.int32),
            sems,
        ],
        compiler_params=pltpu.CompilerParams(vmem_limit_bytes=MIDDLE_LIMIT),
        name="forward",
    )(count, rows, cols, sens, wavelet)


class Ring:
    def __init__(self, me, plus, minus, send, recv, far=None):
        self.me, self.plus, self.minus = me, plus, minus
        self.others = ((2, far), (1, plus), (3, minus))
        self.send, self.recv = send, recv
        self.started = []

    def at(self, step):
        return lax.rem(self.me + step, 4)

    def copy(self, src, dst, device, slot):
        copy = remote(src, dst, self.send.at[slot], self.recv.at[slot], device)
        copy.start()
        self.started.append(copy)

    def arrived(self, ref, slot):
        remote(ref, ref, self.send.at[slot], self.recv.at[slot], self.plus).wait_recv()

    def drain(self):
        for copy in self.started:
            copy.wait_send()
        self.started = []


class Reduce:
    def __init__(self, ring, data, base, chunk, relay, landed):
        self.ring, self.data, self.base, self.chunk = ring, data, base, chunk
        self.half = chunk // 2
        self.relay, self.landed = relay, landed

    def rows(self, step, h):
        start = self.base + self.ring.at(step) * self.chunk + h * self.half
        return pl.ds(pl.multiple_of(start, self.half), self.half)

    def relay_at(self, side):
        return self.relay.at[side, pl.ds(0, self.half)]

    def landed_at(self, side, h):
        return self.landed.at[side, pl.ds(h * self.half, self.half)]

    def begin(self):
        ring, data = self.ring, self.data
        ring.copy(data.at[self.rows(2, 0)], self.relay_at(0), ring.plus, 0)
        ring.copy(data.at[self.rows(2, 1)], self.relay_at(1), ring.minus, 1)
        ring.copy(data.at[self.rows(1, 1)], self.landed_at(0, 1), ring.plus, 2)
        ring.copy(data.at[self.rows(3, 0)], self.landed_at(1, 0), ring.minus, 3)

    def pass_on(self):
        ring, data = self.ring, self.data
        ring.arrived(self.relay_at(0), 0)
        data[self.rows(1, 0), :] += self.relay[0, : self.half]
        ring.copy(data.at[self.rows(1, 0)], self.landed_at(0, 0), ring.plus, 4)
        ring.arrived(self.relay_at(1), 1)
        data[self.rows(3, 1), :] += self.relay[1, : self.half]
        ring.copy(data.at[self.rows(3, 1)], self.landed_at(1, 1), ring.minus, 5)

    def finish(self):
        ring, data = self.ring, self.data
        ring.arrived(self.landed_at(0, 1), 2)
        ring.arrived(self.landed_at(1, 0), 3)
        ring.arrived(self.landed_at(0, 0), 4)
        ring.arrived(self.landed_at(1, 1), 5)
        for h in range(2):
            part = pl.ds(h * self.half, self.half)
            data[self.rows(0, h), :] += self.landed[0, part, :] + self.landed[1, part, :]


class DirectReduce:
    def __init__(self, ring, data, base, chunk, landed):
        self.ring, self.data, self.base, self.chunk = ring, data, base, chunk
        self.landed = landed

    def rows(self, step):
        start = self.base + self.ring.at(step) * self.chunk
        return pl.ds(pl.multiple_of(start, self.chunk), self.chunk)

    def begin(self):
        for step, device in self.ring.others:
            self.ring.copy(
                self.data.at[self.rows(step)], self.landed.at[step - 1], device, step - 1
            )

    def pass_on(self):
        for step in range(3):
            self.ring.arrived(self.landed.at[step], step)

    def finish(self):
        own = self.rows(0)
        total = self.data[own, :] + self.landed[0]
        self.data[own, :] = total + (self.landed[1] + self.landed[2])


class DirectGather:
    def __init__(self, ring, data, base, chunk):
        self.ring, self.data, self.base, self.chunk = ring, data, base, chunk

    def rows(self, step):
        start = self.base + self.ring.at(step) * self.chunk
        return self.data.at[pl.ds(pl.multiple_of(start, self.chunk), self.chunk)]

    def begin(self):
        for step, device in self.ring.others:
            self.ring.copy(self.rows(0), self.rows(0), device, step - 1)

    def pass_on(self):
        pass

    def finish(self):
        for step in (1, 3, 2):
            self.ring.arrived(self.rows(4 - step), step - 1)


STREAMS = 4
STREAM = ROW_BLOCKS * BLK // STREAMS
BIG = STREAM // 4
SMALL = BIG // 4


def combine_kernel(partial, image, fill, big_relay, big_landed, small_landed, send, recv):
    row, col, _, _ = place()
    y, x = lax.div(col, 4), lax.rem(col, 4)
    x_ring = [(row, y * 4 + lax.rem(x + step, 4)) for step in range(4)]
    y_ring = [(row, lax.rem(y + step, 4) * 4 + x) for step in range(4)]
    greet(x_ring[1:] + y_ring[1:])()
    fill.wait()

    def ring(axis, slot):
        me, devices = ((x, x_ring), (y, y_ring))[axis]
        return Ring(me, devices[1], devices[3], send.at[slot], recv.at[slot], devices[2])

    streams = range(STREAMS)
    axis = [a % 2 for a in streams]
    bases = [a * STREAM for a in streams]
    inner = [bases[a] + (x, y)[axis[a]] * BIG for a in streams]
    wide_rings = [ring(axis[a], a) for a in streams]
    cross_rings = [ring(1 - axis[a], STREAMS + a) for a in streams]
    back_rings = [ring(1 - axis[a], 2 * STREAMS + a) for a in streams]
    last_rings = [ring(axis[a], 3 * STREAMS + a) for a in streams]
    wide = [Reduce(wide_rings[a], partial, bases[a], BIG, big_relay.at[a], big_landed.at[a]) for a in streams]
    cross = [DirectReduce(cross_rings[a], partial, inner[a], SMALL, small_landed.at[a]) for a in streams]
    back = [DirectGather(back_rings[a], image, inner[a], SMALL) for a in streams]
    last = [DirectGather(last_rings[a], image, bases[a], BIG) for a in streams]

    def cast(a):
        start = inner[a] + (y, x)[axis[a]] * SMALL
        own = pl.ds(pl.multiple_of(start, SMALL), SMALL)
        image[own, :] = partial[own, :].astype(BF16)

    pairs = [(a, a + 1) for a in range(0, STREAMS, 2)]
    for a in streams:
        wide[a].begin()
    for a in streams:
        wide[a].pass_on()
    for pair in pairs:
        for a in pair:
            wide[a].finish()
            cross[a].begin()
    for pair in pairs:
        for a in pair:
            cross[a].pass_on()
            cross[a].finish()
            cast(a)
            back[a].begin()
    for pair in pairs:
        for a in pair:
            back[a].finish()
            last[a].begin()
    for a in streams:
        last[a].finish()
    for group in (wide_rings, cross_rings, back_rings, last_rings):
        for one in group:
            one.drain()


def combine(partial):
    vmem = pl.BlockSpec(memory_space=pltpu.VMEM)
    rows = ROW_BLOCKS * BLK

    def kernel(partial_ref, image_ref, data, *rest):
        copy = pltpu.make_async_copy(partial_ref, data, rest[-1])
        copy.start()
        combine_kernel(data, image_ref, copy, *rest[:-1])

    return pl.pallas_call(
        kernel,
        out_shape=jax.ShapeDtypeStruct((rows, BLK), BF16),
        in_specs=[pl.BlockSpec(memory_space=pl.ANY)],
        out_specs=vmem,
        scratch_shapes=[
            pltpu.VMEM((rows, BLK), F32),
            pltpu.VMEM((STREAMS, 2, BIG // 2, BLK), F32),
            pltpu.VMEM((STREAMS, 2, BIG, BLK), F32),
            pltpu.VMEM((STREAMS, 3, SMALL, BLK), F32),
            pltpu.SemaphoreType.DMA((4 * STREAMS, 6)),
            pltpu.SemaphoreType.DMA((4 * STREAMS, 6)),
            pltpu.SemaphoreType.DMA,
        ],
        compiler_params=pltpu.CompilerParams(
            collective_id=1, has_side_effects=True, vmem_limit_bytes=MIDDLE_LIMIT
        ),
        cost_estimate=cost(1 << 20, 80 << 20),
        name="combine",
    )(partial.reshape(rows, BLK))


def adjoint_kernel(
    count, rows, cols, source, image, data_image, adjoint, held, flipped, plain, sem, sems
):
    sensors = Sensors(count, source, held, sems)
    sensors.start()
    adjoint[...] = jnp.zeros_like(adjoint)

    def flip(b, carry):
        block = image[b].astype(F32)
        plain[b] = block
        flipped[b] = block.T.astype(BF16)
        return carry

    lax.fori_loop(0, ROW_BLOCKS, flip, 0, unroll=2)
    store = pltpu.make_async_copy(plain, data_image, sem)
    store.start()
    shift = lax.axis_index("cols") >> 1

    def add(first, width):
        terms = []
        for u in range(width):
            terms.append(dot(flipped[rows[0, first + u]], held[first + u]))
        for u in range(width):
            at = cols[0, first + u]
            part = at >> 3
            adjoint[(at >> 2) & 1, at & 3, (part + shift) & 3, part >> 2] += terms[u]

    sensors.run(add)
    store.wait()


def adjoin(count, rows, cols, sens, image):
    held, sems = SENSOR_SCRATCH
    return pl.pallas_call(
        adjoint_kernel,
        out_shape=(
            jax.ShapeDtypeStruct((ROW_BLOCKS, BLK, BLK), F32),
            jax.ShapeDtypeStruct((2, NZ, LANES, EACH, BLK, BLK), F32),
        ),
        in_specs=[SMEM, SMEM, SMEM, ANY, VMEM],
        out_specs=(ANY, VMEM),
        scratch_shapes=[
            held,
            pltpu.VMEM((ROW_BLOCKS, BLK, BLK), BF16),
            pltpu.VMEM((ROW_BLOCKS, BLK, BLK), F32),
            pltpu.SemaphoreType.DMA,
            sems,
        ],
        compiler_params=pltpu.CompilerParams(vmem_limit_bytes=ADJOIN_LIMIT),
        name="adjoin",
    )(count, rows, cols, sens, image)


def return_kernel(
    order, partial, windows, neighbors, weights, scale, signs, out, tables, own, stage, pair, relay_out, relay, landed, gathered, sem, send, recv, part_send, part_recv, *sem_refs
):
    where = place()
    row, col, z, core = where
    fill = pltpu.make_async_copy(partial.at[core], own, sem)
    fill.start()
    parts = Parts(where)
    mine = parts.mine

    def out_piece(at, k, p, h):
        first = p * EACH
        return out.at[at, k, pl.ds(first, EACH) if h is None else pl.ds(first + h, 1)]

    gather = RowGather(out_piece, sem_refs, where)
    plus, minus, partner = gather.neighbour(1), gather.neighbour(3), gather.partner()
    greet([plus, minus, partner], (parts.first, parts.device))()
    rings = [Ring(z, plus, minus, send.at[p], recv.at[p]) for p in range(LANES)]
    for p in range(LANES):
        ring = rings[p]
        for slot, step in ((6, 2), (7, 1), (8, 3), (9, 0)):
            q = ring.at(step)
            ring.copy(partial.at[1 - core, q, p], pair.at[q, p], partner, slot)
    fill.wait()

    def total(p, step, h):
        q = rings[p].at(step)
        return own[q, p, h] + pair[q, p, h]

    def paired(p, step, slot):
        rings[p].arrived(pair.at[rings[p].at(step), p], slot)

    def ship(p, value, slot, dst, device, sem):
        relay_out[p, slot] = value.astype(BF16)
        rings[p].copy(relay_out.at[p, slot], dst, device, sem)

    def launch(p):
        paired(p, 2, 6)
        ship(p, total(p, 2, 0), 0, relay.at[p, 0], plus, 0)
        ship(p, total(p, 2, 1), 1, relay.at[p, 1], minus, 1)
        paired(p, 1, 7)
        ship(p, total(p, 1, 1), 3, landed.at[p, 0, 1], plus, 2)
        paired(p, 3, 8)
        ship(p, total(p, 3, 0), 4, landed.at[p, 1, 0], minus, 3)

    def pass_on(p):
        ring = rings[p]
        ring.arrived(relay.at[p, 0], 0)
        ship(p, total(p, 1, 0) + relay[p, 0].astype(F32), 2, landed.at[p, 0, 0], plus, 4)
        ring.arrived(relay.at[p, 1], 1)
        ship(p, total(p, 3, 1) + relay[p, 1].astype(F32), 5, landed.at[p, 1, 1], minus, 5)

    lane_scale = scale[0:1, :]

    def member(p, i):
        return i * LANES + lax.rem(p + PARTS - mine, LANES)

    def part_copy(m):
        return remote(
            stage.at[m], gathered.at[mine], part_send.at[m], part_recv.at[mine], parts.device_at(m)
        )

    def hand_over(p):
        ring = rings[p]
        paired(p, 0, 9)
        for slot, (side, h) in ((2, (0, 1)), (3, (1, 0)), (4, (0, 0)), (5, (1, 1))):
            ring.arrived(landed.at[p, side, h], slot)
        for h in range(EACH):
            m = member(p, h)
            value = total(p, 0, h) + (landed[p, 0, h].astype(F32) + landed[p, 1, h].astype(F32))
            value = (value * lane_scale).astype(BF16)
            stage[m] = value

            @pl.when(parts.own(m))
            def _(m=m):
                gathered[m] = stage[m]

            @pl.when(jnp.logical_not(parts.own(m)))
            def _(m=m):
                part_copy(m).start()

    def synthesise(p):
        members = [member(p, h) for h in range(EACH)]
        smooth = [
            smooth_tile(windows[m], tables[order[0, (m * 2 + core) * 4 + z]]) for m in members
        ]
        for m in members:

            @pl.when(jnp.logical_not(parts.own(m)))
            def _(m=m):
                ref = gathered.at[m]
                remote(ref, ref, part_send.at[0], part_recv.at[m], partner).wait_recv()

        for h, m in enumerate(members):
            cells = lax.dot_general(
                signs[...], gathered[m], (((1,), (1,)), ((), ())), preferred_element_type=F32
            )
            out[z, core, p * EACH + h] = (cells + smooth[h]).astype(BF16)
        gather.begin(p)

    for p in range(LANES):
        launch(p)
    pass_on(0)
    pass_on(1)
    hand_over(0)
    pass_on(2)
    hand_over(1)
    pass_on(3)
    hand_over(2)
    hand_over(3)
    tabulate(neighbors, weights, tables, col * CELLS)
    synthesise(0)
    synthesise(1)
    synthesise(2)
    gather.pass_on(0)
    synthesise(3)
    for p in range(1, LANES):
        gather.pass_on(p)
        gather.finish(p - 1)
    gather.finish(LANES - 1)
    gather.close(LANES)

    def drain(m, carry):
        @pl.when(jnp.logical_not(parts.own(m)))
        def _():
            part_copy(m).wait_send()

        return carry

    lax.fori_loop(0, PARTS, drain, 0)
    for ring in rings:
        ring.drain()


def give_back(order, partial, windows, neighbors, weights):
    return pl.pallas_call(
        return_kernel,
        out_shape=jax.ShapeDtypeStruct((NZ, 2, PARTS, BLK, BLK), BF16),
        in_specs=[SMEM, ANY, *[VMEM] * 5],
        out_specs=VMEM,
        scratch_shapes=[
            pltpu.VMEM((COL_BLOCKS, 8, BLK), F32),
            pltpu.VMEM((NZ, LANES, EACH, BLK, BLK), F32),
            pltpu.VMEM((PARTS, BLK, BLK), BF16),
            pltpu.VMEM((NZ, LANES, EACH, BLK, BLK), F32),
            pltpu.VMEM((LANES, 6, BLK, BLK), BF16),
            pltpu.VMEM((LANES, 2, BLK, BLK), BF16),
            pltpu.VMEM((LANES, 2, 2, BLK, BLK), BF16),
            pltpu.VMEM((PARTS, BLK, BLK), BF16),
            pltpu.SemaphoreType.DMA,
            pltpu.SemaphoreType.DMA((LANES, 10)),
            pltpu.SemaphoreType.DMA((LANES, 10)),
            pltpu.SemaphoreType.DMA((PARTS,)),
            pltpu.SemaphoreType.DMA((PARTS,)),
            *gather_sems(LANES),
        ],
        compiler_params=pltpu.CompilerParams(
            collective_id=2, has_side_effects=True, vmem_limit_bytes=LATE_LIMIT
        ),
        cost_estimate=cost(1 << 30, 80 << 20),
        name="give_back",
    )(
        order,
        partial,
        windows,
        neighbors,
        weights,
        jnp.asarray(np.broadcast_to(SCALE[None, :], (8, BLK)), F32),
        jnp.asarray(SIGNS.T, BF16),
    )


def place_kernel(order, product, out, cells, out_sems):
    def store(i, block):
        return pltpu.make_async_copy(cells.at[i], out.at[block], out_sems.at[i])

    shift = lax.axis_index("cols") >> 1
    for i in range(2 * NZ):
        for n in range(PARTS):
            q, core, p = i // 2, i % 2, n // EACH
            at = i * PARTS + n
            cells[at] = product[q, core, n].astype(F32)
            m = (n % EACH) * LANES + ((p + PARTS - shift) & (LANES - 1))
            store(at, order[0, (m * 2 + core) * 4 + q]).start()

    def finish(i, carry):
        store(i, 0).wait()
        return carry

    lax.fori_loop(0, COL_BLOCKS, finish, 0)


def place_cells(order, product):
    return pl.pallas_call(
        place_kernel,
        out_shape=jax.ShapeDtypeStruct((COL_BLOCKS, BLK, BLK), F32),
        in_specs=[SMEM, VMEM],
        out_specs=ANY,
        scratch_shapes=[
            pltpu.VMEM((COL_BLOCKS, BLK, BLK), F32),
            pltpu.SemaphoreType.DMA((COL_BLOCKS,)),
        ],
        compiler_params=pltpu.CompilerParams(vmem_limit_bytes=MIDDLE_LIMIT),
        name="place_cells",
    )(order, product)


def local(model_dir, sens_blocks, blk_row, blk_col, blk_count, send_order, neighbors, face_weight):
    model = model_dir.reshape(2 * COL_BLOCKS, RIM, BLK)
    wavelet, windows = analyse(send_order, model)
    partial_image = forward(blk_count, blk_row, blk_col, sens_blocks, wavelet)
    image_half = combine(partial_image).reshape(ROW_BLOCKS, BLK, BLK)
    data_image, partial_adjoint = adjoin(blk_count, blk_row, blk_col, sens_blocks, image_half)
    product = give_back(send_order, partial_adjoint, windows, neighbors, face_weight)
    normal_product = place_cells(send_order, product)
    return data_image.reshape(ROW_BLOCKS * BLK, BLK), normal_product.reshape(CELLS, BLK)


def solution(mesh):
    placed = (
        P("cols", None),
        P("rows", "cols", None, None),
        P("rows", "cols"),
        P("rows", "cols"),
        P("rows", "cols"),
        P("cols", None),
        P(None, "cols"),
        P(None, "cols"),
    )
    return jax.shard_map(
        local,
        mesh=mesh,
        in_specs=placed,
        out_specs=(P("rows", None), P("cols", None)),
        check_vma=False,
    )
```

```python
import math

import jax
import jax.numpy as jnp
import numpy as np
from jax import lax
from jax.experimental import pallas as pl
from jax.experimental.pallas import tpu as pltpu
from jax.sharding import PartitionSpec as P

BLK = 128
RIM = 64
NROWS = 8
NCOLS = 16
NZ = 4
ROW_BLOCKS = 32
COL_BLOCKS = 64
SLOTS = 384
CHUNK = 32
VMEM_LIMIT = 101 << 19
MIDDLE_LIMIT = 42 << 20
ADJOIN_LIMIT = 38 << 20
LATE_LIMIT = 32 << 20
MESH = pl.DeviceIdType.MESH
F32 = jnp.float32
BF16 = jnp.bfloat16


VMEM = pl.BlockSpec(memory_space=pltpu.VMEM)
SMEM = pl.BlockSpec(memory_space=pltpu.SMEM)
ANY = pl.BlockSpec(memory_space=pl.ANY)


def cost(flops, moved):
    return pl.CostEstimate(flops=flops, bytes_accessed=moved, transcendentals=0)


def haar_parts():
    matrix = np.ones((1, 1))
    while matrix.shape[0] < BLK:
        length = matrix.shape[0]
        upper = np.kron(matrix, np.array([[1.0, 1.0]]))
        lower = np.kron(np.eye(length), np.array([[1.0, -1.0]]))
        matrix = np.concatenate([upper, lower], axis=0) / math.sqrt(2.0)
    scale = np.abs(matrix).max(axis=1)
    signs = np.round(matrix / scale[:, None])
    return signs, scale


SIGNS, SCALE = haar_parts()


def haar_tiles():
    row = lax.broadcasted_iota(jnp.int32, (BLK, BLK), 0)
    col = lax.broadcasted_iota(jnp.int32, (BLK, BLK), 1)
    width = jnp.full((BLK, BLK), BLK, jnp.int32)
    start = jnp.zeros((BLK, BLK), jnp.int32)
    scale = jnp.full((BLK, BLK), SCALE[0], F32)
    for level in range(7):
        first, long = 1 << level, BLK >> level
        inside = row >= first
        width = jnp.where(inside, long, width)
        start = jnp.where(inside, (row - first) * long, start)
        scale = jnp.where(inside, np.float32(SCALE[first]), scale)
    at = col - start
    middle = jnp.where(row == 0, width, jnp.where(width > 0, width >> 1, 0))
    signs = jnp.where(at < middle, 1.0, -1.0)
    signs = jnp.where((at >= 0) & (at < width), signs, 0.0)
    return signs.astype(BF16), scale


def split(value):
    high = value.astype(BF16)
    low = (value - high.astype(F32)).astype(BF16)
    return high, low


def dot(a, b):
    return jnp.dot(a, b, preferred_element_type=F32)


def remote(src, dst, send_sem, recv_sem, device):
    return pltpu.make_async_remote_copy(
        src_ref=src,
        dst_ref=dst,
        send_sem=send_sem,
        recv_sem=recv_sem,
        device_id=device,
        device_id_type=MESH,
    )


def place():
    row = lax.axis_index("rows")
    col = lax.axis_index("cols")
    return row, col, lax.div(row, 2), lax.rem(row, 2)


def z_device(z, step, core, col):
    return (lax.rem(z + step, NZ) * 2 + core, col)


def greet(devices, extra=None):
    barrier = pltpu.get_barrier_semaphore()
    for device in devices:
        pl.semaphore_signal(barrier, inc=1, device_id=device, device_id_type=MESH)
    count = len(devices)
    if extra is not None:
        first, device_of = extra

        def signal(i, carry):
            pl.semaphore_signal(barrier, inc=1, device_id=device_of(i), device_id_type=MESH)
            return carry

        lax.fori_loop(first, PARTS, signal, 0)
        count = count + PARTS - first

    def wait_for_all():
        pl.semaphore_wait(barrier, count)

    return wait_for_all


PARTS = NCOLS // 2
GROUP = PARTS // 2
LANES = 4
EACH = PARTS // LANES


class RowGather:
    def __init__(self, piece, sem_refs, where):
        self.piece = piece
        self.g_send, self.minus, self.plus, self.far, self.pair = sem_refs
        self.row, self.col, self.z, self.core = where
        self.sends = []

    def ref(self, step, p, h=None, core=None):
        return self.piece(
            lax.rem(self.z + step, NZ), self.core if core is None else core, p, h
        )

    def send(self, ref, device, recv_sem):
        copy = remote(ref, ref, self.g_send.at[len(self.sends)], recv_sem, device)
        copy.start()
        self.sends.append(copy)

    def arrived(self, ref, recv_sem):
        remote(ref, ref, self.g_send.at[0], recv_sem, self.partner()).wait_recv()

    def partner(self):
        return self.z * 2 + 1 - self.core, self.col

    def neighbour(self, step):
        return z_device(self.z, step, self.core, self.col)

    def begin(self, p):
        own = self.ref(0, p)
        self.send(own, self.neighbour(1), self.minus.at[p])
        self.send(own, self.neighbour(3), self.plus.at[p])
        self.send(own, self.partner(), self.pair.at[0, p])

    def pass_on(self, p):
        self.arrived(self.ref(3, p), self.minus.at[p])
        self.send(self.ref(3, p, 0), self.neighbour(1), self.far.at[0, p])
        self.arrived(self.ref(1, p), self.plus.at[p])
        self.send(self.ref(1, p, 1), self.neighbour(3), self.far.at[1, p])
        self.send(self.ref(3, p), self.partner(), self.pair.at[3, p])
        self.send(self.ref(1, p), self.partner(), self.pair.at[1, p])

    def finish(self, p):
        for h in range(2):
            half = self.ref(2, p, h)
            self.arrived(half, self.far.at[h, p])
            self.send(half, self.partner(), self.pair.at[2 + 2 * h, p])

    def close(self, pieces):
        other = 1 - self.core
        for p in range(pieces):
            for step in (0, 1, 3):
                self.arrived(self.ref(step, p, None, other), self.pair.at[step, p])
            for h in range(2):
                self.arrived(self.ref(2, p, h, other), self.pair.at[2 + 2 * h, p])
        for copy in self.sends:
            copy.wait_send()


def gather_sems(pieces):
    return [
        pltpu.SemaphoreType.DMA((9 * pieces,)),
        pltpu.SemaphoreType.DMA((pieces,)),
        pltpu.SemaphoreType.DMA((pieces,)),
        pltpu.SemaphoreType.DMA((2, pieces)),
        pltpu.SemaphoreType.DMA((5, pieces)),
    ]


class Parts:
    def __init__(self, where):
        self.row, self.col, self.z, self.core = where
        self.mine = lax.div(self.col, 2)
        self.first = jnp.where(self.core == lax.rem(self.col, 2), 1, 0)

    def slot(self, i):
        return lax.rem(self.mine + i, PARTS)

    def device_at(self, m):
        return self.z * 2 + lax.rem(self.col, 2), m * 2 + self.core

    def device(self, i):
        return self.device_at(self.slot(i))

    def own(self, m):
        return m * 2 + self.core == self.col


CELLS = COL_BLOCKS * BLK


def cells_of(body, block):
    return jnp.concatenate([body[2 * block], body[2 * block + 1]], axis=0)


def tabulate(neighbors, weights, tables, first_cell):
    def tile(t, carry):
        at = pl.ds(pl.multiple_of(t * BLK, BLK), BLK)
        near = (neighbors[:, at] - (first_cell + t * BLK - RIM)).astype(F32)
        tables[t] = jnp.concatenate([near, weights[:, at]], axis=0)
        return carry

    lax.fori_loop(0, COL_BLOCKS, tile, 0, unroll=4)


def window_of(body, rims, tile):
    last = COL_BLOCKS - 1
    low = jnp.where(tile == 0, rims[0], body[jnp.maximum(2 * tile - 1, 0)])
    high = jnp.where(tile == last, rims[1], body[jnp.minimum(2 * tile + 2, 2 * last)])
    return jnp.concatenate([low, cells_of(body, tile), high], axis=0)


def smooth_tile(window, table):
    table = table.T
    span = lax.broadcasted_iota(jnp.int32, (BLK, 2 * BLK), 1).astype(F32)
    mix = jnp.zeros((BLK, 2 * BLK), F32)
    for face in range(4):
        mix += jnp.where(table[:, face : face + 1] == span, table[:, 4 + face : 5 + face], 0.0)
    mix_high, mix_low = split(mix)
    center = window[RIM : RIM + BLK]
    near_high, near_low = split(window)
    mixed = dot(mix_high, near_high) + dot(mix_low, near_high) + dot(mix_high, near_low)
    total = table[:, 4:5] + table[:, 5:6] + table[:, 6:7] + table[:, 7:8]
    return total * center - mixed


RING_BLOCKS = COL_BLOCKS // 2


def ring_place(z, core, part):
    return (z * 2 + core) * GROUP + part


def plane_place(core, part):
    return RING_BLOCKS + (core * PARTS + part) * 2


def analyse_kernel(
    order,
    model,
    wavelet,
    windows,
    body,
    rims,
    ring_stage,
    plane_stage,
    sems,
    ring_send,
    ring_recv,
    plane_send,
    plane_recv,
    plane_pair,
    *sem_refs,
):
    where = place()
    row, col, z, core = where
    fill = pltpu.make_async_copy(model, body, sems.at[4])
    fill.start()
    parts = Parts(where)
    mine, lane = parts.mine, lax.div(z, 2)

    def ring_piece(at, k, p, h):
        first = ring_place(at, k, p * 2)
        return wavelet.at[pl.ds(first, 2) if h is None else pl.ds(first + h, 1)]

    gather = RowGather(ring_piece, sem_refs, where)
    below, above = (row, lax.rem(col + NCOLS - 1, NCOLS)), (row, lax.rem(col + 1, NCOLS))
    wait_for_all = greet(
        [gather.neighbour(1), gather.neighbour(3), gather.partner(), below, above],
        (parts.first, parts.device),
    )
    up = remote(
        model.at[2 * COL_BLOCKS - 1],
        rims.at[0],
        sems.at[0],
        sems.at[2],
        above,
    )
    down = remote(
        model.at[0],
        rims.at[1],
        sems.at[1],
        sems.at[3],
        below,
    )
    signs, scale = haar_tiles()
    sign_pair = jnp.concatenate([signs, signs], axis=1)
    fill.wait()

    def block_of(m, q):
        return order[0, (m * 2 + core) * 4 + q]

    def coefficients(m, q):
        high, low = split(cells_of(body, block_of(m, q)))
        product = dot(sign_pair, jnp.concatenate([high, low], axis=0))
        return (product * scale).astype(BF16)

    def ring_part(i):
        return i * 2 + lax.rem(lane + mine, 2)

    def make_ring(i, carry):
        ring_stage[i] = coefficients(ring_part(i), 2 + lax.rem(z, 2))
        return carry

    lax.fori_loop(0, GROUP, make_ring, 0)
    wait_for_all()

    def ring_copy(i):
        return remote(
            ring_stage.at[i],
            wavelet.at[ring_place(z, lax.rem(col, 2), lax.div(mine, 2))],
            ring_send.at[i],
            ring_recv.at[lax.div(mine, 2)],
            parts.device_at(ring_part(i)),
        )

    def spread_ring(i, carry):
        @pl.when(parts.own(ring_part(i)))
        def _():
            wavelet[ring_place(z, core, lax.div(mine, 2))] = ring_stage[i]

        @pl.when(jnp.logical_not(parts.own(ring_part(i))))
        def _():
            ring_copy(i).start()

        return carry

    lax.fori_loop(0, GROUP, spread_ring, 0)
    up.start()
    down.start()

    def plane_copy(i):
        return remote(
            plane_stage.at[i],
            wavelet.at[pl.ds(plane_place(lax.rem(col, 2), mine), 2)],
            plane_send.at[i],
            plane_recv.at[mine],
            parts.device(i),
        )

    def spread_plane(i, carry):
        for q in range(2):
            plane_stage[i, q] = coefficients(parts.slot(i), q)
        plane_copy(i).start()
        return carry

    lax.fori_loop(parts.first, PARTS, spread_plane, 0)

    @pl.when(parts.first == 1)
    def _():
        for q in range(2):
            wavelet[plane_place(core, mine) + q] = coefficients(mine, q)

    def wait_ring(i, carry):
        @pl.when(jnp.logical_not(parts.own(ring_part(i))))
        def _():
            ref = wavelet.at[ring_place(z, core, i)]
            remote(ref, ref, ring_send.at[0], ring_recv.at[i], gather.partner()).wait_recv()

        return carry

    def wait_plane(m, carry):
        @pl.when(jnp.logical_not(parts.own(m)))
        def _():
            ref = wavelet.at[pl.ds(plane_place(core, m), 2)]
            remote(ref, ref, plane_send.at[0], plane_recv.at[m], gather.partner()).wait_recv()

        return carry

    def half_plane(core_of, h):
        return wavelet.at[pl.ds(plane_place(core_of, h * GROUP), PARTS)]

    def swap(h):
        ref = half_plane(core, h)
        return remote(ref, ref, plane_pair.at[h], plane_pair.at[2 + h], gather.partner())

    for p in range(2):
        lax.fori_loop(2 * p, 2 * p + 2, wait_ring, 0)
        gather.begin(p)
    up.wait_recv()
    down.wait_recv()

    def keep_window(m, carry):
        windows[m] = window_of(body, rims, block_of(m, z))
        return carry

    lax.fori_loop(0, PARTS, keep_window, 0)
    for p in range(2):
        gather.pass_on(p)
    for h in range(2):
        lax.fori_loop(h * GROUP, (h + 1) * GROUP, wait_plane, 0)
        swap(h).start()
    for p in range(2):
        gather.finish(p)
    gather.close(2)
    for h in range(2):
        ref = half_plane(1 - core, h)
        remote(ref, ref, plane_pair.at[h], plane_pair.at[2 + h], gather.partner()).wait_recv()
        swap(h).wait_send()

    def drain_ring(i, carry):
        @pl.when(jnp.logical_not(parts.own(ring_part(i))))
        def _():
            ring_copy(i).wait_send()

        return carry

    def drain_plane(i, carry):
        plane_copy(i).wait_send()
        return carry

    lax.fori_loop(0, GROUP, drain_ring, 0)
    lax.fori_loop(parts.first, PARTS, drain_plane, 0)
    up.wait_send()
    down.wait_send()


def analyse(order, model):
    return pl.pallas_call(
        analyse_kernel,
        out_shape=(
            jax.ShapeDtypeStruct((COL_BLOCKS, BLK, BLK), BF16),
            jax.ShapeDtypeStruct((PARTS, 2 * BLK, BLK), F32),
        ),
        in_specs=[SMEM, ANY],
        out_specs=(VMEM, VMEM),
        scratch_shapes=[
            pltpu.VMEM((2 * COL_BLOCKS, RIM, BLK), F32),
            pltpu.VMEM((2, RIM, BLK), F32),
            pltpu.VMEM((GROUP, BLK, BLK), BF16),
            pltpu.VMEM((PARTS, 2, BLK, BLK), BF16),
            pltpu.SemaphoreType.DMA((5,)),
            pltpu.SemaphoreType.DMA((GROUP,)),
            pltpu.SemaphoreType.DMA((GROUP,)),
            pltpu.SemaphoreType.DMA((PARTS,)),
            pltpu.SemaphoreType.DMA((PARTS,)),
            pltpu.SemaphoreType.DMA((4,)),
            *gather_sems(2),
        ],
        compiler_params=pltpu.CompilerParams(
            collective_id=0, has_side_effects=True, vmem_limit_bytes=VMEM_LIMIT
        ),
        cost_estimate=cost(1 << 30, 60 << 20),
        name="analyse",
    )(order, model)


class Sensors:
    def __init__(self, count, source, held, sems):
        self.live, self.source, self.held, self.sems = count[0, 0], source, held, sems

    def copy(self, g):
        part = pl.ds(g * CHUNK, CHUNK)
        return pltpu.make_async_copy(self.source.at[0, part], self.held.at[part], self.sems.at[g])

    def start(self):
        def begin(g, carry):
            self.copy(g).start()
            return carry

        lax.fori_loop(0, pl.cdiv(self.live, CHUNK), begin, 0)

    def run(self, add):
        full = self.live // CHUNK

        def group(g, carry):
            self.copy(g).wait()
            add(g * CHUNK, CHUNK)
            return carry

        lax.fori_loop(0, full, group, 0)
        done = full * CHUNK

        @pl.when(done < self.live)
        def _():
            self.copy(full).wait()

        for width in (4, 1):

            def few(g, carry, width=width, done=done):
                add(done + g * width, width)
                return carry

            groups = (self.live - done) // width
            lax.fori_loop(0, groups, few, 0)
            done = done + groups * width


def forward_kernel(count, rows, cols, source, wavelet, image, held, places, sems):
    sensors = Sensors(count, source, held, sems)
    sensors.start()
    image[...] = jnp.zeros_like(image)
    mine = lax.axis_index("cols") >> 1

    def note(at, carry):
        q, core, part = at & 3, (at >> 2) & 1, at >> 3
        by_ring = ring_place(2 * ((part + mine) & 1) + (q & 1), core, part >> 1)
        places[at] = jnp.where(q >= 2, by_ring, plane_place(core, part) + q)
        return carry

    lax.fori_loop(0, COL_BLOCKS, note, 0)

    def add(first, width):
        terms = []
        for u in range(width):
            terms.append(dot(held[first + u], wavelet[places[cols[0, first + u]]]))
        for u in range(width):
            image[rows[0, first + u]] += terms[u]

    sensors.run(add)


SENSOR_SCRATCH = (
    pltpu.VMEM((SLOTS, BLK, BLK), BF16),
    pltpu.SemaphoreType.DMA((SLOTS // CHUNK,)),
)


def forward(count, rows, cols, sens, wavelet):
    held, sems = SENSOR_SCRATCH
    return pl.pallas_call(
        forward_kernel,
        out_shape=jax.ShapeDtypeStruct((ROW_BLOCKS, BLK, BLK), F32),
        in_specs=[SMEM, SMEM, SMEM, ANY, VMEM],
        out_specs=VMEM,
        scratch_shapes=[
            held,
            pltpu.SMEM((COL_BLOCKS,), jnp.int32),
            sems,
        ],
        compiler_params=pltpu.CompilerParams(vmem_limit_bytes=MIDDLE_LIMIT),
        name="forward",
    )(count, rows, cols, sens, wavelet)


class Ring:
    def __init__(self, me, plus, minus, send, recv, far=None):
        self.me, self.plus, self.minus = me, plus, minus
        self.others = ((2, far), (1, plus), (3, minus))
        self.send, self.recv = send, recv
        self.started = []

    def at(self, step):
        return lax.rem(self.me + step, 4)

    def copy(self, src, dst, device, slot):
        copy = remote(src, dst, self.send.at[slot], self.recv.at[slot], device)
        copy.start()
        self.started.append(copy)

    def arrived(self, ref, slot):
        remote(ref, ref, self.send.at[slot], self.recv.at[slot], self.plus).wait_recv()

    def drain(self):
        for copy in self.started:
            copy.wait_send()
        self.started = []


class Reduce:
    def __init__(self, ring, source, data, base, chunk, relay, landed):
        self.ring, self.source, self.data = ring, source, data
        self.base, self.chunk = base, chunk
        self.half = chunk // 2
        self.relay, self.landed = relay, landed

    def rows(self, step, h):
        start = self.base + self.ring.at(step) * self.chunk + h * self.half
        return pl.ds(pl.multiple_of(start, self.half), self.half)

    def relay_at(self, side):
        return self.relay.at[side, pl.ds(0, self.half)]

    def landed_at(self, side, h):
        return self.landed.at[side, pl.ds(h * self.half, self.half)]

    def begin(self):
        ring, source = self.ring, self.source
        ring.copy(source.at[self.rows(2, 0)], self.relay_at(0), ring.plus, 0)
        ring.copy(source.at[self.rows(2, 1)], self.relay_at(1), ring.minus, 1)
        ring.copy(source.at[self.rows(1, 1)], self.landed_at(0, 1), ring.plus, 2)
        ring.copy(source.at[self.rows(3, 0)], self.landed_at(1, 0), ring.minus, 3)

    def pass_on(self):
        ring, source, data = self.ring, self.source, self.data
        ring.arrived(self.relay_at(0), 0)
        data[self.rows(1, 0), :] = source[self.rows(1, 0), :] + self.relay[0, : self.half]
        ring.copy(data.at[self.rows(1, 0)], self.landed_at(0, 0), ring.plus, 4)
        ring.arrived(self.relay_at(1), 1)
        data[self.rows(3, 1), :] = source[self.rows(3, 1), :] + self.relay[1, : self.half]
        ring.copy(data.at[self.rows(3, 1)], self.landed_at(1, 1), ring.minus, 5)

    def finish(self):
        ring, source, data = self.ring, self.source, self.data
        ring.arrived(self.landed_at(0, 1), 2)
        ring.arrived(self.landed_at(1, 0), 3)
        ring.arrived(self.landed_at(0, 0), 4)
        ring.arrived(self.landed_at(1, 1), 5)
        for h in range(2):
            part = pl.ds(h * self.half, self.half)
            landed = self.landed[0, part, :] + self.landed[1, part, :]
            data[self.rows(0, h), :] = source[self.rows(0, h), :] + landed


class DirectReduce:
    def __init__(self, ring, data, base, chunk, landed):
        self.ring, self.data, self.base, self.chunk = ring, data, base, chunk
        self.landed = landed

    def rows(self, step):
        start = self.base + self.ring.at(step) * self.chunk
        return pl.ds(pl.multiple_of(start, self.chunk), self.chunk)

    def begin(self):
        for step, device in self.ring.others:
            self.ring.copy(
                self.data.at[self.rows(step)], self.landed.at[step - 1], device, step - 1
            )

    def pass_on(self):
        for step in range(3):
            self.ring.arrived(self.landed.at[step], step)

    def finish(self):
        own = self.rows(0)
        total = self.data[own, :] + self.landed[0]
        self.data[own, :] = total + (self.landed[1] + self.landed[2])


class DirectGather:
    def __init__(self, ring, data, base, chunk):
        self.ring, self.data, self.base, self.chunk = ring, data, base, chunk

    def rows(self, step):
        start = self.base + self.ring.at(step) * self.chunk
        return self.data.at[pl.ds(pl.multiple_of(start, self.chunk), self.chunk)]

    def begin(self):
        for step, device in self.ring.others:
            self.ring.copy(self.rows(0), self.rows(0), device, step - 1)

    def pass_on(self):
        pass

    def finish(self):
        for step in (1, 3, 2):
            self.ring.arrived(self.rows(4 - step), step - 1)


STREAMS = 4
STREAM = ROW_BLOCKS * BLK // STREAMS
BIG = STREAM // 4
SMALL = BIG // 4


def combine_kernel(source, image, partial, big_relay, big_landed, small_landed, send, recv):
    row, col, _, _ = place()
    y, x = lax.div(col, 4), lax.rem(col, 4)
    x_ring = [(row, y * 4 + lax.rem(x + step, 4)) for step in range(4)]
    y_ring = [(row, lax.rem(y + step, 4) * 4 + x) for step in range(4)]
    greet(x_ring[1:] + y_ring[1:])()

    def ring(axis, slot):
        me, devices = ((x, x_ring), (y, y_ring))[axis]
        return Ring(me, devices[1], devices[3], send.at[slot], recv.at[slot], devices[2])

    streams = range(STREAMS)
    axis = [a % 2 for a in streams]
    bases = [a * STREAM for a in streams]
    inner = [bases[a] + (x, y)[axis[a]] * BIG for a in streams]
    wide_rings = [ring(axis[a], a) for a in streams]
    cross_rings = [ring(1 - axis[a], STREAMS + a) for a in streams]
    back_rings = [ring(1 - axis[a], 2 * STREAMS + a) for a in streams]
    last_rings = [ring(axis[a], 3 * STREAMS + a) for a in streams]
    wide = [
        Reduce(wide_rings[a], source, partial, bases[a], BIG, big_relay.at[a], big_landed.at[a])
        for a in streams
    ]
    cross = [DirectReduce(cross_rings[a], partial, inner[a], SMALL, small_landed.at[a]) for a in streams]
    back = [DirectGather(back_rings[a], image, inner[a], SMALL) for a in streams]
    last = [DirectGather(last_rings[a], image, bases[a], BIG) for a in streams]

    def cast(a):
        start = inner[a] + (y, x)[axis[a]] * SMALL
        own = pl.ds(pl.multiple_of(start, SMALL), SMALL)
        image[own, :] = partial[own, :].astype(BF16)

    pairs = [(a, a + 1) for a in range(0, STREAMS, 2)]
    for a in streams:
        wide[a].begin()
    for a in streams:
        wide[a].pass_on()
    for pair in pairs:
        for a in pair:
            wide[a].finish()
            cross[a].begin()
    for pair in pairs:
        for a in pair:
            cross[a].pass_on()
            cross[a].finish()
            cast(a)
            back[a].begin()
    for pair in pairs:
        for a in pair:
            back[a].finish()
            last[a].begin()
    for a in streams:
        last[a].finish()
    for group in (wide_rings, cross_rings, back_rings, last_rings):
        for one in group:
            one.drain()


def combine(partial):
    vmem = pl.BlockSpec(memory_space=pltpu.VMEM)
    rows = ROW_BLOCKS * BLK

    return pl.pallas_call(
        combine_kernel,
        out_shape=jax.ShapeDtypeStruct((rows, BLK), BF16),
        in_specs=[vmem],
        out_specs=vmem,
        scratch_shapes=[
            pltpu.VMEM((rows, BLK), F32),
            pltpu.VMEM((STREAMS, 2, BIG // 2, BLK), F32),
            pltpu.VMEM((STREAMS, 2, BIG, BLK), F32),
            pltpu.VMEM((STREAMS, 3, SMALL, BLK), F32),
            pltpu.SemaphoreType.DMA((4 * STREAMS, 6)),
            pltpu.SemaphoreType.DMA((4 * STREAMS, 6)),
        ],
        compiler_params=pltpu.CompilerParams(
            collective_id=1, has_side_effects=True, vmem_limit_bytes=MIDDLE_LIMIT
        ),
        cost_estimate=cost(1 << 20, 80 << 20),
        name="combine",
    )(partial.reshape(rows, BLK))


def adjoint_kernel(
    count, rows, cols, source, image, data_image, adjoint, held, flipped, plain, sem, sems
):
    sensors = Sensors(count, source, held, sems)
    sensors.start()
    adjoint[...] = jnp.zeros_like(adjoint)

    def flip(b, carry):
        block = image[b].astype(F32)
        plain[b] = block
        flipped[b] = block.T.astype(BF16)
        return carry

    lax.fori_loop(0, ROW_BLOCKS, flip, 0, unroll=2)
    store = pltpu.make_async_copy(plain, data_image, sem)
    store.start()
    shift = lax.axis_index("cols") >> 1

    def add(first, width):
        terms = []
        for u in range(width):
            terms.append(dot(flipped[rows[0, first + u]], held[first + u]))
        for u in range(width):
            at = cols[0, first + u]
            part = at >> 3
            adjoint[(at >> 2) & 1, at & 3, (part + shift) & 3, part >> 2] += terms[u]

    sensors.run(add)
    store.wait()


def adjoin(count, rows, cols, sens, image):
    held, sems = SENSOR_SCRATCH
    return pl.pallas_call(
        adjoint_kernel,
        out_shape=(
            jax.ShapeDtypeStruct((ROW_BLOCKS, BLK, BLK), F32),
            jax.ShapeDtypeStruct((2, NZ, LANES, EACH, BLK, BLK), F32),
        ),
        in_specs=[SMEM, SMEM, SMEM, ANY, VMEM],
        out_specs=(ANY, VMEM),
        scratch_shapes=[
            held,
            pltpu.VMEM((ROW_BLOCKS, BLK, BLK), BF16),
            pltpu.VMEM((ROW_BLOCKS, BLK, BLK), F32),
            pltpu.SemaphoreType.DMA,
            sems,
        ],
        compiler_params=pltpu.CompilerParams(vmem_limit_bytes=ADJOIN_LIMIT),
        name="adjoin",
    )(count, rows, cols, sens, image)


def return_kernel(
    order, partial, windows, neighbors, weights, scale, signs, out, tables, stage, pair, relay_out, relay, landed, gathered, send, recv, part_send, part_recv, *sem_refs
):
    where = place()
    row, col, z, core = where
    parts = Parts(where)
    mine = parts.mine

    def out_piece(at, k, p, h):
        first = p * EACH
        return out.at[at, k, pl.ds(first, EACH) if h is None else pl.ds(first + h, 1)]

    gather = RowGather(out_piece, sem_refs, where)
    plus, minus, partner = gather.neighbour(1), gather.neighbour(3), gather.partner()
    greet([plus, minus, partner], (parts.first, parts.device))()
    rings = [Ring(z, plus, minus, send.at[p], recv.at[p]) for p in range(LANES)]
    for p in range(LANES):
        ring = rings[p]
        for slot, step in ((6, 2), (7, 1), (8, 3), (9, 0)):
            q = ring.at(step)
            ring.copy(partial.at[1 - core, q, p], pair.at[q, p], partner, slot)

    def total(p, step, h):
        q = rings[p].at(step)
        return partial[core, q, p, h] + pair[q, p, h]

    def paired(p, step, slot):
        rings[p].arrived(pair.at[rings[p].at(step), p], slot)

    def ship(p, value, slot, dst, device, sem):
        relay_out[p, slot] = value.astype(BF16)
        rings[p].copy(relay_out.at[p, slot], dst, device, sem)

    def launch(p):
        paired(p, 2, 6)
        ship(p, total(p, 2, 0), 0, relay.at[p, 0], plus, 0)
        ship(p, total(p, 2, 1), 1, relay.at[p, 1], minus, 1)
        paired(p, 1, 7)
        ship(p, total(p, 1, 1), 3, landed.at[p, 0, 1], plus, 2)
        paired(p, 3, 8)
        ship(p, total(p, 3, 0), 4, landed.at[p, 1, 0], minus, 3)

    def pass_on(p):
        ring = rings[p]
        ring.arrived(relay.at[p, 0], 0)
        ship(p, total(p, 1, 0) + relay[p, 0].astype(F32), 2, landed.at[p, 0, 0], plus, 4)
        ring.arrived(relay.at[p, 1], 1)
        ship(p, total(p, 3, 1) + relay[p, 1].astype(F32), 5, landed.at[p, 1, 1], minus, 5)

    lane_scale = scale[0:1, :]

    def member(p, i):
        return i * LANES + lax.rem(p + PARTS - mine, LANES)

    def part_copy(m):
        return remote(
            stage.at[m], gathered.at[mine], part_send.at[m], part_recv.at[mine], parts.device_at(m)
        )

    def hand_over(p):
        ring = rings[p]
        paired(p, 0, 9)
        for slot, (side, h) in ((2, (0, 1)), (3, (1, 0)), (4, (0, 0)), (5, (1, 1))):
            ring.arrived(landed.at[p, side, h], slot)
        for h in range(EACH):
            m = member(p, h)
            value = total(p, 0, h) + (landed[p, 0, h].astype(F32) + landed[p, 1, h].astype(F32))
            value = (value * lane_scale).astype(BF16)
            stage[m] = value

            @pl.when(parts.own(m))
            def _(m=m):
                gathered[m] = stage[m]

            @pl.when(jnp.logical_not(parts.own(m)))
            def _(m=m):
                part_copy(m).start()

    def synthesise(p):
        members = [member(p, h) for h in range(EACH)]
        smooth = [
            smooth_tile(windows[m], tables[order[0, (m * 2 + core) * 4 + z]]) for m in members
        ]
        for m in members:

            @pl.when(jnp.logical_not(parts.own(m)))
            def _(m=m):
                ref = gathered.at[m]
                remote(ref, ref, part_send.at[0], part_recv.at[m], partner).wait_recv()

        for h, m in enumerate(members):
            cells = lax.dot_general(
                signs[...], gathered[m], (((1,), (1,)), ((), ())), preferred_element_type=F32
            )
            out[z, core, p * EACH + h] = (cells + smooth[h]).astype(BF16)
        gather.begin(p)

    for p in range(LANES):
        launch(p)
    pass_on(0)
    pass_on(1)
    hand_over(0)
    pass_on(2)
    hand_over(1)
    pass_on(3)
    hand_over(2)
    hand_over(3)
    tabulate(neighbors, weights, tables, col * CELLS)
    synthesise(0)
    synthesise(1)
    synthesise(2)
    gather.pass_on(0)
    synthesise(3)
    for p in range(1, LANES):
        gather.pass_on(p)
        gather.finish(p - 1)
    gather.finish(LANES - 1)
    gather.close(LANES)

    def drain(m, carry):
        @pl.when(jnp.logical_not(parts.own(m)))
        def _():
            part_copy(m).wait_send()

        return carry

    lax.fori_loop(0, PARTS, drain, 0)
    for ring in rings:
        ring.drain()


def give_back(order, partial, windows, neighbors, weights):
    return pl.pallas_call(
        return_kernel,
        out_shape=jax.ShapeDtypeStruct((NZ, 2, PARTS, BLK, BLK), BF16),
        in_specs=[SMEM, *[VMEM] * 6],
        out_specs=VMEM,
        scratch_shapes=[
            pltpu.VMEM((COL_BLOCKS, 8, BLK), F32),
            pltpu.VMEM((PARTS, BLK, BLK), BF16),
            pltpu.VMEM((NZ, LANES, EACH, BLK, BLK), F32),
            pltpu.VMEM((LANES, 6, BLK, BLK), BF16),
            pltpu.VMEM((LANES, 2, BLK, BLK), BF16),
            pltpu.VMEM((LANES, 2, 2, BLK, BLK), BF16),
            pltpu.VMEM((PARTS, BLK, BLK), BF16),
            pltpu.SemaphoreType.DMA((LANES, 10)),
            pltpu.SemaphoreType.DMA((LANES, 10)),
            pltpu.SemaphoreType.DMA((PARTS,)),
            pltpu.SemaphoreType.DMA((PARTS,)),
            *gather_sems(LANES),
        ],
        compiler_params=pltpu.CompilerParams(
            collective_id=2, has_side_effects=True, vmem_limit_bytes=LATE_LIMIT
        ),
        cost_estimate=cost(1 << 30, 80 << 20),
        name="give_back",
    )(
        order,
        partial,
        windows,
        neighbors,
        weights,
        jnp.asarray(np.broadcast_to(SCALE[None, :], (8, BLK)), F32),
        jnp.asarray(SIGNS.T, BF16),
    )


def place_kernel(order, product, out, cells, out_sems):
    def store(i, block):
        return pltpu.make_async_copy(cells.at[i], out.at[block], out_sems.at[i])

    shift = lax.axis_index("cols") >> 1
    for i in range(2 * NZ):
        for n in range(PARTS):
            q, core, p = i // 2, i % 2, n // EACH
            at = i * PARTS + n
            cells[at] = product[q, core, n].astype(F32)
            m = (n % EACH) * LANES + ((p + PARTS - shift) & (LANES - 1))
            store(at, order[0, (m * 2 + core) * 4 + q]).start()

    def finish(i, carry):
        store(i, 0).wait()
        return carry

    lax.fori_loop(0, COL_BLOCKS, finish, 0)


def place_cells(order, product):
    return pl.pallas_call(
        place_kernel,
        out_shape=jax.ShapeDtypeStruct((COL_BLOCKS, BLK, BLK), F32),
        in_specs=[SMEM, VMEM],
        out_specs=ANY,
        scratch_shapes=[
            pltpu.VMEM((COL_BLOCKS, BLK, BLK), F32),
            pltpu.SemaphoreType.DMA((COL_BLOCKS,)),
        ],
        compiler_params=pltpu.CompilerParams(vmem_limit_bytes=MIDDLE_LIMIT),
        name="place_cells",
    )(order, product)


def local(model_dir, sens_blocks, blk_row, blk_col, blk_count, send_order, neighbors, face_weight):
    model = model_dir.reshape(2 * COL_BLOCKS, RIM, BLK)
    wavelet, windows = analyse(send_order, model)
    partial_image = forward(blk_count, blk_row, blk_col, sens_blocks, wavelet)
    image_half = combine(partial_image).reshape(ROW_BLOCKS, BLK, BLK)
    data_image, partial_adjoint = adjoin(blk_count, blk_row, blk_col, sens_blocks, image_half)
    product = give_back(send_order, partial_adjoint, windows, neighbors, face_weight)
    normal_product = place_cells(send_order, product)
    return data_image.reshape(ROW_BLOCKS * BLK, BLK), normal_product.reshape(CELLS, BLK)


def solution(mesh):
    placed = (
        P("cols", None),
        P("rows", "cols", None, None),
        P("rows", "cols"),
        P("rows", "cols"),
        P("rows", "cols"),
        P("cols", None),
        P(None, "cols"),
        P(None, "cols"),
    )
    return jax.shard_map(
        local,
        mesh=mesh,
        in_specs=placed,
        out_specs=(P("rows", None), P("cols", None)),
        check_vma=False,
    )
```

```python
import math

import jax
import jax.numpy as jnp
import numpy as np
from jax import lax
from jax.experimental import pallas as pl
from jax.experimental.pallas import tpu as pltpu
from jax.sharding import PartitionSpec as P

BLK = 128
RIM = 64
NROWS = 8
NCOLS = 16
NZ = 4
ROW_BLOCKS = 32
COL_BLOCKS = 64
SLOTS = 384
CHUNK = 32
VMEM_LIMIT = 101 << 19
MIDDLE_LIMIT = 42 << 20
ADJOIN_LIMIT = 38 << 20
LATE_LIMIT = 32 << 20
MESH = pl.DeviceIdType.MESH
F32 = jnp.float32
BF16 = jnp.bfloat16


VMEM = pl.BlockSpec(memory_space=pltpu.VMEM)
SMEM = pl.BlockSpec(memory_space=pltpu.SMEM)
ANY = pl.BlockSpec(memory_space=pl.ANY)


def cost(flops, moved):
    return pl.CostEstimate(flops=flops, bytes_accessed=moved, transcendentals=0)


def haar_parts():
    matrix = np.ones((1, 1))
    while matrix.shape[0] < BLK:
        length = matrix.shape[0]
        upper = np.kron(matrix, np.array([[1.0, 1.0]]))
        lower = np.kron(np.eye(length), np.array([[1.0, -1.0]]))
        matrix = np.concatenate([upper, lower], axis=0) / math.sqrt(2.0)
    scale = np.abs(matrix).max(axis=1)
    signs = np.round(matrix / scale[:, None])
    return signs, scale


SIGNS, SCALE = haar_parts()


def haar_tiles():
    row = lax.broadcasted_iota(jnp.int32, (BLK, BLK), 0)
    col = lax.broadcasted_iota(jnp.int32, (BLK, BLK), 1)
    width = jnp.full((BLK, BLK), BLK, jnp.int32)
    start = jnp.zeros((BLK, BLK), jnp.int32)
    scale = jnp.full((BLK, BLK), SCALE[0], F32)
    for level in range(7):
        first, long = 1 << level, BLK >> level
        inside = row >= first
        width = jnp.where(inside, long, width)
        start = jnp.where(inside, (row - first) * long, start)
        scale = jnp.where(inside, np.float32(SCALE[first]), scale)
    at = col - start
    middle = jnp.where(row == 0, width, jnp.where(width > 0, width >> 1, 0))
    signs = jnp.where(at < middle, 1.0, -1.0)
    signs = jnp.where((at >= 0) & (at < width), signs, 0.0)
    return signs.astype(BF16), scale


def split(value):
    high = value.astype(BF16)
    low = (value - high.astype(F32)).astype(BF16)
    return high, low


def dot(a, b):
    return jnp.dot(a, b, preferred_element_type=F32)


def remote(src, dst, send_sem, recv_sem, device):
    return pltpu.make_async_remote_copy(
        src_ref=src,
        dst_ref=dst,
        send_sem=send_sem,
        recv_sem=recv_sem,
        device_id=device,
        device_id_type=MESH,
    )


def place():
    row = lax.axis_index("rows")
    col = lax.axis_index("cols")
    return row, col, lax.div(row, 2), lax.rem(row, 2)


def z_device(z, step, core, col):
    return (lax.rem(z + step, NZ) * 2 + core, col)


def greet(devices, extra=None):
    barrier = pltpu.get_barrier_semaphore()
    for device in devices:
        pl.semaphore_signal(barrier, inc=1, device_id=device, device_id_type=MESH)
    count = len(devices)
    if extra is not None:
        first, device_of = extra

        def signal(i, carry):
            pl.semaphore_signal(barrier, inc=1, device_id=device_of(i), device_id_type=MESH)
            return carry

        lax.fori_loop(first, PARTS, signal, 0)
        count = count + PARTS - first

    def wait_for_all():
        pl.semaphore_wait(barrier, count)

    return wait_for_all


PARTS = NCOLS // 2
GROUP = PARTS // 2
LANES = 2
EACH = PARTS // LANES
PAIR = EACH // 2


class RowGather:
    def __init__(self, piece, sem_refs, where):
        self.piece = piece
        self.g_send, self.minus, self.plus, self.far, self.pair = sem_refs
        self.row, self.col, self.z, self.core = where
        self.sends = []

    def ref(self, step, p, h=None, core=None):
        return self.piece(
            lax.rem(self.z + step, NZ), self.core if core is None else core, p, h
        )

    def send(self, ref, device, recv_sem):
        copy = remote(ref, ref, self.g_send.at[len(self.sends)], recv_sem, device)
        copy.start()
        self.sends.append(copy)

    def arrived(self, ref, recv_sem):
        remote(ref, ref, self.g_send.at[0], recv_sem, self.partner()).wait_recv()

    def partner(self):
        return self.z * 2 + 1 - self.core, self.col

    def neighbour(self, step):
        return z_device(self.z, step, self.core, self.col)

    def begin(self, p):
        own = self.ref(0, p)
        self.send(own, self.neighbour(1), self.minus.at[p])
        self.send(own, self.neighbour(3), self.plus.at[p])
        self.send(own, self.partner(), self.pair.at[0, p])

    def pass_on(self, p):
        self.arrived(self.ref(3, p), self.minus.at[p])
        self.send(self.ref(3, p, 0), self.neighbour(1), self.far.at[0, p])
        self.arrived(self.ref(1, p), self.plus.at[p])
        self.send(self.ref(1, p, 1), self.neighbour(3), self.far.at[1, p])
        self.send(self.ref(3, p), self.partner(), self.pair.at[3, p])
        self.send(self.ref(1, p), self.partner(), self.pair.at[1, p])

    def finish(self, p):
        for h in range(2):
            half = self.ref(2, p, h)
            self.arrived(half, self.far.at[h, p])
            self.send(half, self.partner(), self.pair.at[2 + 2 * h, p])

    def close(self, pieces):
        other = 1 - self.core
        for p in range(pieces):
            for step in (0, 1, 3):
                self.arrived(self.ref(step, p, None, other), self.pair.at[step, p])
            for h in range(2):
                self.arrived(self.ref(2, p, h, other), self.pair.at[2 + 2 * h, p])
        for copy in self.sends:
            copy.wait_send()


def gather_sems(pieces):
    return [
        pltpu.SemaphoreType.DMA((9 * pieces,)),
        pltpu.SemaphoreType.DMA((pieces,)),
        pltpu.SemaphoreType.DMA((pieces,)),
        pltpu.SemaphoreType.DMA((2, pieces)),
        pltpu.SemaphoreType.DMA((5, pieces)),
    ]


class Parts:
    def __init__(self, where):
        self.row, self.col, self.z, self.core = where
        self.mine = lax.div(self.col, 2)
        self.first = jnp.where(self.core == lax.rem(self.col, 2), 1, 0)

    def slot(self, i):
        return lax.rem(self.mine + i, PARTS)

    def device_at(self, m):
        return self.z * 2 + lax.rem(self.col, 2), m * 2 + self.core

    def device(self, i):
        return self.device_at(self.slot(i))

    def own(self, m):
        return m * 2 + self.core == self.col


CELLS = COL_BLOCKS * BLK


def cells_of(body, block):
    return jnp.concatenate([body[2 * block], body[2 * block + 1]], axis=0)


def tabulate(neighbors, weights, tables, first_cell):
    def tile(t, carry):
        at = pl.ds(pl.multiple_of(t * BLK, BLK), BLK)
        near = (neighbors[:, at] - (first_cell + t * BLK - RIM)).astype(F32)
        tables[t] = jnp.concatenate([near, weights[:, at]], axis=0)
        return carry

    lax.fori_loop(0, COL_BLOCKS, tile, 0, unroll=4)


def window_of(body, rims, tile):
    last = COL_BLOCKS - 1
    low = jnp.where(tile == 0, rims[0], body[jnp.maximum(2 * tile - 1, 0)])
    high = jnp.where(tile == last, rims[1], body[jnp.minimum(2 * tile + 2, 2 * last)])
    return jnp.concatenate([low, cells_of(body, tile), high], axis=0)


def smooth_tile(window, table):
    table = table.T
    span = lax.broadcasted_iota(jnp.int32, (BLK, 2 * BLK), 1).astype(F32)
    mix = jnp.zeros((BLK, 2 * BLK), F32)
    for face in range(4):
        mix += jnp.where(table[:, face : face + 1] == span, table[:, 4 + face : 5 + face], 0.0)
    mix_high, mix_low = split(mix)
    center = window[RIM : RIM + BLK]
    near_high, near_low = split(window)
    mixed = dot(mix_high, near_high) + dot(mix_low, near_high) + dot(mix_high, near_low)
    total = table[:, 4:5] + table[:, 5:6] + table[:, 6:7] + table[:, 7:8]
    return total * center - mixed


RING_BLOCKS = COL_BLOCKS // 2


def ring_place(z, core, part):
    return (z * 2 + core) * GROUP + part


def plane_place(core, part):
    return RING_BLOCKS + (core * PARTS + part) * 2


def analyse_kernel(
    order,
    model,
    wavelet,
    windows,
    body,
    rims,
    ring_stage,
    plane_stage,
    sems,
    ring_send,
    ring_recv,
    plane_send,
    plane_recv,
    plane_pair,
    *sem_refs,
):
    where = place()
    row, col, z, core = where
    fill = pltpu.make_async_copy(model, body, sems.at[4])
    fill.start()
    parts = Parts(where)
    mine, lane = parts.mine, lax.div(z, 2)

    def ring_piece(at, k, p, h):
        first = ring_place(at, k, p * 2)
        return wavelet.at[pl.ds(first, 2) if h is None else pl.ds(first + h, 1)]

    gather = RowGather(ring_piece, sem_refs, where)
    below, above = (row, lax.rem(col + NCOLS - 1, NCOLS)), (row, lax.rem(col + 1, NCOLS))
    wait_for_all = greet(
        [gather.neighbour(1), gather.neighbour(3), gather.partner(), below, above],
        (parts.first, parts.device),
    )
    up = remote(
        model.at[2 * COL_BLOCKS - 1],
        rims.at[0],
        sems.at[0],
        sems.at[2],
        above,
    )
    down = remote(
        model.at[0],
        rims.at[1],
        sems.at[1],
        sems.at[3],
        below,
    )
    signs, scale = haar_tiles()
    sign_pair = jnp.concatenate([signs, signs], axis=1)
    fill.wait()

    def block_of(m, q):
        return order[0, (m * 2 + core) * 4 + q]

    def coefficients(m, q):
        high, low = split(cells_of(body, block_of(m, q)))
        product = dot(sign_pair, jnp.concatenate([high, low], axis=0))
        return (product * scale).astype(BF16)

    def ring_part(i):
        return i * 2 + lax.rem(lane + mine, 2)

    def make_ring(i, carry):
        ring_stage[i] = coefficients(ring_part(i), 2 + lax.rem(z, 2))
        return carry

    lax.fori_loop(0, GROUP, make_ring, 0)
    wait_for_all()

    def ring_copy(i):
        return remote(
            ring_stage.at[i],
            wavelet.at[ring_place(z, lax.rem(col, 2), lax.div(mine, 2))],
            ring_send.at[i],
            ring_recv.at[lax.div(mine, 2)],
            parts.device_at(ring_part(i)),
        )

    def spread_ring(i, carry):
        @pl.when(parts.own(ring_part(i)))
        def _():
            wavelet[ring_place(z, core, lax.div(mine, 2))] = ring_stage[i]

        @pl.when(jnp.logical_not(parts.own(ring_part(i))))
        def _():
            ring_copy(i).start()

        return carry

    lax.fori_loop(0, GROUP, spread_ring, 0)
    up.start()
    down.start()

    def plane_copy(i):
        return remote(
            plane_stage.at[i],
            wavelet.at[pl.ds(plane_place(lax.rem(col, 2), mine), 2)],
            plane_send.at[i],
            plane_recv.at[mine],
            parts.device(i),
        )

    def spread_plane(i, carry):
        for q in range(2):
            plane_stage[i, q] = coefficients(parts.slot(i), q)
        plane_copy(i).start()
        return carry

    lax.fori_loop(parts.first, PARTS, spread_plane, 0)

    @pl.when(parts.first == 1)
    def _():
        for q in range(2):
            wavelet[plane_place(core, mine) + q] = coefficients(mine, q)

    def wait_ring(i, carry):
        @pl.when(jnp.logical_not(parts.own(ring_part(i))))
        def _():
            ref = wavelet.at[ring_place(z, core, i)]
            remote(ref, ref, ring_send.at[0], ring_recv.at[i], gather.partner()).wait_recv()

        return carry

    def wait_plane(m, carry):
        @pl.when(jnp.logical_not(parts.own(m)))
        def _():
            ref = wavelet.at[pl.ds(plane_place(core, m), 2)]
            remote(ref, ref, plane_send.at[0], plane_recv.at[m], gather.partner()).wait_recv()

        return carry

    def half_plane(core_of, h):
        return wavelet.at[pl.ds(plane_place(core_of, h * GROUP), PARTS)]

    def swap(h):
        ref = half_plane(core, h)
        return remote(ref, ref, plane_pair.at[h], plane_pair.at[2 + h], gather.partner())

    for p in range(2):
        lax.fori_loop(2 * p, 2 * p + 2, wait_ring, 0)
        gather.begin(p)
    up.wait_recv()
    down.wait_recv()

    def keep_window(m, carry):
        windows[m] = window_of(body, rims, block_of(m, z))
        return carry

    lax.fori_loop(0, PARTS, keep_window, 0)
    for p in range(2):
        gather.pass_on(p)
    for h in range(2):
        lax.fori_loop(h * GROUP, (h + 1) * GROUP, wait_plane, 0)
        swap(h).start()
    for p in range(2):
        gather.finish(p)
    gather.close(2)
    for h in range(2):
        ref = half_plane(1 - core, h)
        remote(ref, ref, plane_pair.at[h], plane_pair.at[2 + h], gather.partner()).wait_recv()
        swap(h).wait_send()

    def drain_ring(i, carry):
        @pl.when(jnp.logical_not(parts.own(ring_part(i))))
        def _():
            ring_copy(i).wait_send()

        return carry

    def drain_plane(i, carry):
        plane_copy(i).wait_send()
        return carry

    lax.fori_loop(0, GROUP, drain_ring, 0)
    lax.fori_loop(parts.first, PARTS, drain_plane, 0)
    up.wait_send()
    down.wait_send()


def analyse(order, model):
    return pl.pallas_call(
        analyse_kernel,
        out_shape=(
            jax.ShapeDtypeStruct((COL_BLOCKS, BLK, BLK), BF16),
            jax.ShapeDtypeStruct((PARTS, 2 * BLK, BLK), F32),
        ),
        in_specs=[SMEM, ANY],
        out_specs=(VMEM, VMEM),
        scratch_shapes=[
            pltpu.VMEM((2 * COL_BLOCKS, RIM, BLK), F32),
            pltpu.VMEM((2, RIM, BLK), F32),
            pltpu.VMEM((GROUP, BLK, BLK), BF16),
            pltpu.VMEM((PARTS, 2, BLK, BLK), BF16),
            pltpu.SemaphoreType.DMA((5,)),
            pltpu.SemaphoreType.DMA((GROUP,)),
            pltpu.SemaphoreType.DMA((GROUP,)),
            pltpu.SemaphoreType.DMA((PARTS,)),
            pltpu.SemaphoreType.DMA((PARTS,)),
            pltpu.SemaphoreType.DMA((4,)),
            *gather_sems(2),
        ],
        compiler_params=pltpu.CompilerParams(
            collective_id=0, has_side_effects=True, vmem_limit_bytes=VMEM_LIMIT
        ),
        cost_estimate=cost(1 << 30, 60 << 20),
        name="analyse",
    )(order, model)


class Sensors:
    def __init__(self, count, source, held, sems):
        self.live, self.source, self.held, self.sems = count[0, 0], source, held, sems

    def copy(self, g):
        part = pl.ds(g * CHUNK, CHUNK)
        return pltpu.make_async_copy(self.source.at[0, part], self.held.at[part], self.sems.at[g])

    def start(self):
        def begin(g, carry):
            self.copy(g).start()
            return carry

        lax.fori_loop(0, pl.cdiv(self.live, CHUNK), begin, 0)

    def run(self, add):
        full = self.live // CHUNK

        def group(g, carry):
            self.copy(g).wait()
            add(g * CHUNK, CHUNK)
            return carry

        lax.fori_loop(0, full, group, 0)
        done = full * CHUNK

        @pl.when(done < self.live)
        def _():
            self.copy(full).wait()

        for width in (4, 1):

            def few(g, carry, width=width, done=done):
                add(done + g * width, width)
                return carry

            groups = (self.live - done) // width
            lax.fori_loop(0, groups, few, 0)
            done = done + groups * width


def forward_kernel(count, rows, cols, source, wavelet, image, held, places, sems):
    sensors = Sensors(count, source, held, sems)
    sensors.start()
    image[...] = jnp.zeros_like(image)
    mine = lax.axis_index("cols") >> 1

    def note(at, carry):
        q, core, part = at & 3, (at >> 2) & 1, at >> 3
        by_ring = ring_place(2 * ((part + mine) & 1) + (q & 1), core, part >> 1)
        places[at] = jnp.where(q >= 2, by_ring, plane_place(core, part) + q)
        return carry

    lax.fori_loop(0, COL_BLOCKS, note, 0)

    def add(first, width):
        terms = []
        for u in range(width):
            terms.append(dot(held[first + u], wavelet[places[cols[0, first + u]]]))
        for u in range(width):
            image[rows[0, first + u]] += terms[u]

    sensors.run(add)


SENSOR_SCRATCH = (
    pltpu.VMEM((SLOTS, BLK, BLK), BF16),
    pltpu.SemaphoreType.DMA((SLOTS // CHUNK,)),
)


def forward(count, rows, cols, sens, wavelet):
    held, sems = SENSOR_SCRATCH
    return pl.pallas_call(
        forward_kernel,
        out_shape=jax.ShapeDtypeStruct((ROW_BLOCKS, BLK, BLK), F32),
        in_specs=[SMEM, SMEM, SMEM, ANY, VMEM],
        out_specs=VMEM,
        scratch_shapes=[
            held,
            pltpu.SMEM((COL_BLOCKS,), jnp.int32),
            sems,
        ],
        compiler_params=pltpu.CompilerParams(vmem_limit_bytes=MIDDLE_LIMIT),
        name="forward",
    )(count, rows, cols, sens, wavelet)


class Ring:
    def __init__(self, me, plus, minus, send, recv, far=None):
        self.me, self.plus, self.minus = me, plus, minus
        self.others = ((2, far), (1, plus), (3, minus))
        self.send, self.recv = send, recv
        self.started = []

    def at(self, step):
        return lax.rem(self.me + step, 4)

    def copy(self, src, dst, device, slot):
        copy = remote(src, dst, self.send.at[slot], self.recv.at[slot], device)
        copy.start()
        self.started.append(copy)

    def arrived(self, ref, slot):
        remote(ref, ref, self.send.at[slot], self.recv.at[slot], self.plus).wait_recv()

    def drain(self):
        for copy in self.started:
            copy.wait_send()
        self.started = []


class Reduce:
    def __init__(self, ring, source, data, base, chunk, relay, landed):
        self.ring, self.source, self.data = ring, source, data
        self.base, self.chunk = base, chunk
        self.half = chunk // 2
        self.relay, self.landed = relay, landed

    def rows(self, step, h):
        start = self.base + self.ring.at(step) * self.chunk + h * self.half
        return pl.ds(pl.multiple_of(start, self.half), self.half)

    def relay_at(self, side):
        return self.relay.at[side, pl.ds(0, self.half)]

    def landed_at(self, side, h):
        return self.landed.at[side, pl.ds(h * self.half, self.half)]

    def begin(self):
        ring, source = self.ring, self.source
        ring.copy(source.at[self.rows(2, 0)], self.relay_at(0), ring.plus, 0)
        ring.copy(source.at[self.rows(2, 1)], self.relay_at(1), ring.minus, 1)
        ring.copy(source.at[self.rows(1, 1)], self.landed_at(0, 1), ring.plus, 2)
        ring.copy(source.at[self.rows(3, 0)], self.landed_at(1, 0), ring.minus, 3)

    def pass_on(self):
        ring, source, data = self.ring, self.source, self.data
        ring.arrived(self.relay_at(0), 0)
        data[self.rows(1, 0), :] = source[self.rows(1, 0), :] + self.relay[0, : self.half]
        ring.copy(data.at[self.rows(1, 0)], self.landed_at(0, 0), ring.plus, 4)
        ring.arrived(self.relay_at(1), 1)
        data[self.rows(3, 1), :] = source[self.rows(3, 1), :] + self.relay[1, : self.half]
        ring.copy(data.at[self.rows(3, 1)], self.landed_at(1, 1), ring.minus, 5)

    def finish(self):
        ring, source, data = self.ring, self.source, self.data
        ring.arrived(self.landed_at(0, 1), 2)
        ring.arrived(self.landed_at(1, 0), 3)
        ring.arrived(self.landed_at(0, 0), 4)
        ring.arrived(self.landed_at(1, 1), 5)
        for h in range(2):
            part = pl.ds(h * self.half, self.half)
            landed = self.landed[0, part, :] + self.landed[1, part, :]
            data[self.rows(0, h), :] = source[self.rows(0, h), :] + landed


class DirectReduce:
    def __init__(self, ring, data, base, chunk, landed):
        self.ring, self.data, self.base, self.chunk = ring, data, base, chunk
        self.landed = landed

    def rows(self, step):
        start = self.base + self.ring.at(step) * self.chunk
        return pl.ds(pl.multiple_of(start, self.chunk), self.chunk)

    def begin(self):
        for step, device in self.ring.others:
            self.ring.copy(
                self.data.at[self.rows(step)], self.landed.at[step - 1], device, step - 1
            )

    def pass_on(self):
        for step in range(3):
            self.ring.arrived(self.landed.at[step], step)

    def finish(self):
        own = self.rows(0)
        total = self.data[own, :] + self.landed[0]
        self.data[own, :] = total + (self.landed[1] + self.landed[2])


class DirectGather:
    def __init__(self, ring, data, base, chunk):
        self.ring, self.data, self.base, self.chunk = ring, data, base, chunk

    def rows(self, step):
        start = self.base + self.ring.at(step) * self.chunk
        return self.data.at[pl.ds(pl.multiple_of(start, self.chunk), self.chunk)]

    def begin(self):
        for step, device in self.ring.others:
            self.ring.copy(self.rows(0), self.rows(0), device, step - 1)

    def pass_on(self):
        pass

    def finish(self):
        for step in (1, 3, 2):
            self.ring.arrived(self.rows(4 - step), step - 1)


STREAMS = 4
STREAM = ROW_BLOCKS * BLK // STREAMS
BIG = STREAM // 4
SMALL = BIG // 4


def combine_kernel(source, image, partial, big_relay, big_landed, small_landed, send, recv):
    row, col, _, _ = place()
    y, x = lax.div(col, 4), lax.rem(col, 4)
    x_ring = [(row, y * 4 + lax.rem(x + step, 4)) for step in range(4)]
    y_ring = [(row, lax.rem(y + step, 4) * 4 + x) for step in range(4)]
    greet(x_ring[1:] + y_ring[1:])()

    def ring(axis, slot):
        me, devices = ((x, x_ring), (y, y_ring))[axis]
        return Ring(me, devices[1], devices[3], send.at[slot], recv.at[slot], devices[2])

    streams = range(STREAMS)
    axis = [a % 2 for a in streams]
    bases = [a * STREAM for a in streams]
    inner = [bases[a] + (x, y)[axis[a]] * BIG for a in streams]
    wide_rings = [ring(axis[a], a) for a in streams]
    cross_rings = [ring(1 - axis[a], STREAMS + a) for a in streams]
    back_rings = [ring(1 - axis[a], 2 * STREAMS + a) for a in streams]
    last_rings = [ring(axis[a], 3 * STREAMS + a) for a in streams]
    wide = [
        Reduce(wide_rings[a], source, partial, bases[a], BIG, big_relay.at[a], big_landed.at[a])
        for a in streams
    ]
    cross = [DirectReduce(cross_rings[a], partial, inner[a], SMALL, small_landed.at[a]) for a in streams]
    back = [DirectGather(back_rings[a], image, inner[a], SMALL) for a in streams]
    last = [DirectGather(last_rings[a], image, bases[a], BIG) for a in streams]

    def cast(a):
        start = inner[a] + (y, x)[axis[a]] * SMALL
        own = pl.ds(pl.multiple_of(start, SMALL), SMALL)
        image[own, :] = partial[own, :].astype(BF16)

    pairs = [(a, a + 1) for a in range(0, STREAMS, 2)]
    for a in streams:
        wide[a].begin()
    for a in streams:
        wide[a].pass_on()
    for pair in pairs:
        for a in pair:
            wide[a].finish()
            cross[a].begin()
    for pair in pairs:
        for a in pair:
            cross[a].pass_on()
            cross[a].finish()
            cast(a)
            back[a].begin()
    for pair in pairs:
        for a in pair:
            back[a].finish()
            last[a].begin()
    for a in streams:
        last[a].finish()
    for group in (wide_rings, cross_rings, back_rings, last_rings):
        for one in group:
            one.drain()


def combine(partial):
    vmem = pl.BlockSpec(memory_space=pltpu.VMEM)
    rows = ROW_BLOCKS * BLK

    return pl.pallas_call(
        combine_kernel,
        out_shape=jax.ShapeDtypeStruct((rows, BLK), BF16),
        in_specs=[vmem],
        out_specs=vmem,
        scratch_shapes=[
            pltpu.VMEM((rows, BLK), F32),
            pltpu.VMEM((STREAMS, 2, BIG // 2, BLK), F32),
            pltpu.VMEM((STREAMS, 2, BIG, BLK), F32),
            pltpu.VMEM((STREAMS, 3, SMALL, BLK), F32),
            pltpu.SemaphoreType.DMA((4 * STREAMS, 6)),
            pltpu.SemaphoreType.DMA((4 * STREAMS, 6)),
        ],
        compiler_params=pltpu.CompilerParams(
            collective_id=1, has_side_effects=True, vmem_limit_bytes=MIDDLE_LIMIT
        ),
        cost_estimate=cost(1 << 20, 80 << 20),
        name="combine",
    )(partial.reshape(rows, BLK))


def adjoint_kernel(
    count, rows, cols, source, image, data_image, adjoint, held, flipped, plain, sem, sems
):
    sensors = Sensors(count, source, held, sems)
    sensors.start()
    adjoint[...] = jnp.zeros_like(adjoint)

    def flip(b, carry):
        block = image[b].astype(F32)
        plain[b] = block
        flipped[b] = block.T.astype(BF16)
        return carry

    lax.fori_loop(0, ROW_BLOCKS, flip, 0, unroll=2)
    store = pltpu.make_async_copy(plain, data_image, sem)
    store.start()
    shift = lax.axis_index("cols") >> 1

    def add(first, width):
        terms = []
        for u in range(width):
            terms.append(dot(flipped[rows[0, first + u]], held[first + u]))
        for u in range(width):
            at = cols[0, first + u]
            part = at >> 3
            adjoint[(at >> 2) & 1, at & 3, (part + shift) & (LANES - 1), part >> (LANES // 2)] += terms[u]

    sensors.run(add)
    store.wait()


def adjoin(count, rows, cols, sens, image):
    held, sems = SENSOR_SCRATCH
    return pl.pallas_call(
        adjoint_kernel,
        out_shape=(
            jax.ShapeDtypeStruct((ROW_BLOCKS, BLK, BLK), F32),
            jax.ShapeDtypeStruct((2, NZ, LANES, EACH, BLK, BLK), F32),
        ),
        in_specs=[SMEM, SMEM, SMEM, ANY, VMEM],
        out_specs=(ANY, VMEM),
        scratch_shapes=[
            held,
            pltpu.VMEM((ROW_BLOCKS, BLK, BLK), BF16),
            pltpu.VMEM((ROW_BLOCKS, BLK, BLK), F32),
            pltpu.SemaphoreType.DMA,
            sems,
        ],
        compiler_params=pltpu.CompilerParams(vmem_limit_bytes=ADJOIN_LIMIT),
        name="adjoin",
    )(count, rows, cols, sens, image)


def return_kernel(
    order, partial, windows, neighbors, weights, scale, signs, out, tables, stage, pair, relay_out, relay, landed, gathered, send, recv, part_send, part_recv, *sem_refs
):
    where = place()
    row, col, z, core = where
    parts = Parts(where)
    mine = parts.mine

    def out_piece(at, k, p, h):
        first = p * EACH
        return out.at[at, k, pl.ds(first, EACH) if h is None else pl.ds(first + h * PAIR, PAIR)]

    gather = RowGather(out_piece, sem_refs, where)
    plus, minus, partner = gather.neighbour(1), gather.neighbour(3), gather.partner()
    greet([plus, minus, partner], (parts.first, parts.device))()
    rings = [Ring(z, plus, minus, send.at[p], recv.at[p]) for p in range(LANES)]
    for p in range(LANES):
        ring = rings[p]
        for slot, step in ((6, 2), (7, 1), (8, 3), (9, 0)):
            q = ring.at(step)
            ring.copy(partial.at[1 - core, q, p], pair.at[q, p], partner, slot)

    def total(p, step, h):
        q = rings[p].at(step)
        part = pl.ds(h * PAIR, PAIR)
        return partial[core, q, p, part] + pair[q, p, part]

    def paired(p, step, slot):
        rings[p].arrived(pair.at[rings[p].at(step), p], slot)

    def ship(p, value, slot, dst, device, sem):
        relay_out[p, slot] = value.astype(BF16)
        rings[p].copy(relay_out.at[p, slot], dst, device, sem)

    def launch(p):
        paired(p, 2, 6)
        ship(p, total(p, 2, 0), 0, relay.at[p, 0], plus, 0)
        ship(p, total(p, 2, 1), 1, relay.at[p, 1], minus, 1)
        paired(p, 1, 7)
        ship(p, total(p, 1, 1), 3, landed.at[p, 0, 1], plus, 2)
        paired(p, 3, 8)
        ship(p, total(p, 3, 0), 4, landed.at[p, 1, 0], minus, 3)

    def pass_on(p):
        ring = rings[p]
        ring.arrived(relay.at[p, 0], 0)
        ship(p, total(p, 1, 0) + relay[p, 0].astype(F32), 2, landed.at[p, 0, 0], plus, 4)
        ring.arrived(relay.at[p, 1], 1)
        ship(p, total(p, 3, 1) + relay[p, 1].astype(F32), 5, landed.at[p, 1, 1], minus, 5)

    lane_scale = scale[0:1, :]

    def member(p, i):
        return i * LANES + lax.rem(p + PARTS - mine, LANES)

    def part_copy(m):
        return remote(
            stage.at[m], gathered.at[mine], part_send.at[m], part_recv.at[mine], parts.device_at(m)
        )

    def hand_over(p):
        ring = rings[p]
        paired(p, 0, 9)
        for slot, (side, h) in ((2, (0, 1)), (3, (1, 0)), (4, (0, 0)), (5, (1, 1))):
            ring.arrived(landed.at[p, side, h], slot)
        for i in range(EACH):
            m, h, j = member(p, i), i // PAIR, i % PAIR
            landed_sum = landed[p, 0, h, j].astype(F32) + landed[p, 1, h, j].astype(F32)
            value = partial[core, z, p, i] + pair[z, p, i] + landed_sum
            stage[m] = (value * lane_scale).astype(BF16)

            @pl.when(parts.own(m))
            def _(m=m):
                gathered[m] = stage[m]

            @pl.when(jnp.logical_not(parts.own(m)))
            def _(m=m):
                part_copy(m).start()

    def synthesise(p):
        members = [member(p, h) for h in range(EACH)]
        smooth = [
            smooth_tile(windows[m], tables[order[0, (m * 2 + core) * 4 + z]]) for m in members
        ]
        for m in members:

            @pl.when(jnp.logical_not(parts.own(m)))
            def _(m=m):
                ref = gathered.at[m]
                remote(ref, ref, part_send.at[0], part_recv.at[m], partner).wait_recv()

        for h, m in enumerate(members):
            cells = lax.dot_general(
                signs[...], gathered[m], (((1,), (1,)), ((), ())), preferred_element_type=F32
            )
            out[z, core, p * EACH + h] = (cells + smooth[h]).astype(BF16)
        gather.begin(p)

    for p in range(LANES):
        launch(p)
    for p in range(LANES):
        pass_on(p)
    for p in range(LANES):
        hand_over(p)
    tabulate(neighbors, weights, tables, col * CELLS)
    for p in range(LANES):
        synthesise(p)
    for p in range(LANES):
        gather.pass_on(p)
    for p in range(LANES):
        gather.finish(p)
    gather.close(LANES)

    def drain(m, carry):
        @pl.when(jnp.logical_not(parts.own(m)))
        def _():
            part_copy(m).wait_send()

        return carry

    lax.fori_loop(0, PARTS, drain, 0)
    for ring in rings:
        ring.drain()


def give_back(order, partial, windows, neighbors, weights):
    return pl.pallas_call(
        return_kernel,
        out_shape=jax.ShapeDtypeStruct((NZ, 2, PARTS, BLK, BLK), BF16),
        in_specs=[SMEM, *[VMEM] * 6],
        out_specs=VMEM,
        scratch_shapes=[
            pltpu.VMEM((COL_BLOCKS, 8, BLK), F32),
            pltpu.VMEM((PARTS, BLK, BLK), BF16),
            pltpu.VMEM((NZ, LANES, EACH, BLK, BLK), F32),
            pltpu.VMEM((LANES, 6, PAIR, BLK, BLK), BF16),
            pltpu.VMEM((LANES, 2, PAIR, BLK, BLK), BF16),
            pltpu.VMEM((LANES, 2, 2, PAIR, BLK, BLK), BF16),
            pltpu.VMEM((PARTS, BLK, BLK), BF16),
            pltpu.SemaphoreType.DMA((LANES, 10)),
            pltpu.SemaphoreType.DMA((LANES, 10)),
            pltpu.SemaphoreType.DMA((PARTS,)),
            pltpu.SemaphoreType.DMA((PARTS,)),
            *gather_sems(LANES),
        ],
        compiler_params=pltpu.CompilerParams(
            collective_id=2, has_side_effects=True, vmem_limit_bytes=LATE_LIMIT
        ),
        cost_estimate=cost(1 << 30, 80 << 20),
        name="give_back",
    )(
        order,
        partial,
        windows,
        neighbors,
        weights,
        jnp.asarray(np.broadcast_to(SCALE[None, :], (8, BLK)), F32),
        jnp.asarray(SIGNS.T, BF16),
    )


def place_kernel(order, product, out, cells, out_sems):
    def store(i, block):
        return pltpu.make_async_copy(cells.at[i], out.at[block], out_sems.at[i])

    shift = lax.axis_index("cols") >> 1
    for i in range(2 * NZ):
        for n in range(PARTS):
            q, core, p = i // 2, i % 2, n // EACH
            at = i * PARTS + n
            cells[at] = product[q, core, n].astype(F32)
            m = (n % EACH) * LANES + ((p + PARTS - shift) & (LANES - 1))
            store(at, order[0, (m * 2 + core) * 4 + q]).start()

    def finish(i, carry):
        store(i, 0).wait()
        return carry

    lax.fori_loop(0, COL_BLOCKS, finish, 0)


def place_cells(order, product):
    return pl.pallas_call(
        place_kernel,
        out_shape=jax.ShapeDtypeStruct((COL_BLOCKS, BLK, BLK), F32),
        in_specs=[SMEM, VMEM],
        out_specs=ANY,
        scratch_shapes=[
            pltpu.VMEM((COL_BLOCKS, BLK, BLK), F32),
            pltpu.SemaphoreType.DMA((COL_BLOCKS,)),
        ],
        compiler_params=pltpu.CompilerParams(vmem_limit_bytes=MIDDLE_LIMIT),
        name="place_cells",
    )(order, product)


def local(model_dir, sens_blocks, blk_row, blk_col, blk_count, send_order, neighbors, face_weight):
    model = model_dir.reshape(2 * COL_BLOCKS, RIM, BLK)
    wavelet, windows = analyse(send_order, model)
    partial_image = forward(blk_count, blk_row, blk_col, sens_blocks, wavelet)
    image_half = combine(partial_image).reshape(ROW_BLOCKS, BLK, BLK)
    data_image, partial_adjoint = adjoin(blk_count, blk_row, blk_col, sens_blocks, image_half)
    product = give_back(send_order, partial_adjoint, windows, neighbors, face_weight)
    normal_product = place_cells(send_order, product)
    return data_image.reshape(ROW_BLOCKS * BLK, BLK), normal_product.reshape(CELLS, BLK)


def solution(mesh):
    placed = (
        P("cols", None),
        P("rows", "cols", None, None),
        P("rows", "cols"),
        P("rows", "cols"),
        P("rows", "cols"),
        P("cols", None),
        P(None, "cols"),
        P(None, "cols"),
    )
    return jax.shard_map(
        local,
        mesh=mesh,
        in_specs=placed,
        out_specs=(P("rows", None), P("cols", None)),
        check_vma=False,
    )
```

```python
import math

import jax
import jax.numpy as jnp
import numpy as np
from jax import lax
from jax.experimental import pallas as pl
from jax.experimental.pallas import tpu as pltpu
from jax.sharding import PartitionSpec as P

BLK = 128
RIM = 64
NROWS = 8
NCOLS = 16
NZ = 4
ROW_BLOCKS = 32
COL_BLOCKS = 64
SLOTS = 384
CHUNK = 32
VMEM_LIMIT = 101 << 19
MIDDLE_LIMIT = 42 << 20
ADJOIN_LIMIT = 38 << 20
LATE_LIMIT = 32 << 20
MESH = pl.DeviceIdType.MESH
F32 = jnp.float32
BF16 = jnp.bfloat16


VMEM = pl.BlockSpec(memory_space=pltpu.VMEM)
SMEM = pl.BlockSpec(memory_space=pltpu.SMEM)
ANY = pl.BlockSpec(memory_space=pl.ANY)


def cost(flops, moved):
    return pl.CostEstimate(flops=flops, bytes_accessed=moved, transcendentals=0)


def haar_parts():
    matrix = np.ones((1, 1))
    while matrix.shape[0] < BLK:
        length = matrix.shape[0]
        upper = np.kron(matrix, np.array([[1.0, 1.0]]))
        lower = np.kron(np.eye(length), np.array([[1.0, -1.0]]))
        matrix = np.concatenate([upper, lower], axis=0) / math.sqrt(2.0)
    scale = np.abs(matrix).max(axis=1)
    signs = np.round(matrix / scale[:, None])
    return signs, scale


SIGNS, SCALE = haar_parts()


def haar_tiles():
    row = lax.broadcasted_iota(jnp.int32, (BLK, BLK), 0)
    col = lax.broadcasted_iota(jnp.int32, (BLK, BLK), 1)
    width = jnp.full((BLK, BLK), BLK, jnp.int32)
    start = jnp.zeros((BLK, BLK), jnp.int32)
    scale = jnp.full((BLK, BLK), SCALE[0], F32)
    for level in range(7):
        first, long = 1 << level, BLK >> level
        inside = row >= first
        width = jnp.where(inside, long, width)
        start = jnp.where(inside, (row - first) * long, start)
        scale = jnp.where(inside, np.float32(SCALE[first]), scale)
    at = col - start
    middle = jnp.where(row == 0, width, jnp.where(width > 0, width >> 1, 0))
    signs = jnp.where(at < middle, 1.0, -1.0)
    signs = jnp.where((at >= 0) & (at < width), signs, 0.0)
    return signs.astype(BF16), scale


def split(value):
    high = value.astype(BF16)
    low = (value - high.astype(F32)).astype(BF16)
    return high, low


def dot(a, b):
    return jnp.dot(a, b, preferred_element_type=F32)


def remote(src, dst, send_sem, recv_sem, device):
    return pltpu.make_async_remote_copy(
        src_ref=src,
        dst_ref=dst,
        send_sem=send_sem,
        recv_sem=recv_sem,
        device_id=device,
        device_id_type=MESH,
    )


def place():
    row = lax.axis_index("rows")
    col = lax.axis_index("cols")
    return row, col, lax.div(row, 2), lax.rem(row, 2)


def z_device(z, step, core, col):
    return (lax.rem(z + step, NZ) * 2 + core, col)


def greet(devices, extra=None):
    barrier = pltpu.get_barrier_semaphore()
    for device in devices:
        pl.semaphore_signal(barrier, inc=1, device_id=device, device_id_type=MESH)
    count = len(devices)
    if extra is not None:
        first, device_of = extra

        def signal(i, carry):
            pl.semaphore_signal(barrier, inc=1, device_id=device_of(i), device_id_type=MESH)
            return carry

        lax.fori_loop(first, PARTS, signal, 0)
        count = count + PARTS - first

    def wait_for_all():
        pl.semaphore_wait(barrier, count)

    return wait_for_all


PARTS = NCOLS // 2
GROUP = PARTS // 2
LANES = 2
EACH = PARTS // LANES
PAIR = EACH // 2


class RowGather:
    def __init__(self, piece, sem_refs, where):
        self.piece = piece
        self.g_send, self.minus, self.plus, self.far, self.pair = sem_refs
        self.row, self.col, self.z, self.core = where
        self.sends = []

    def ref(self, step, p, h=None, core=None):
        return self.piece(
            lax.rem(self.z + step, NZ), self.core if core is None else core, p, h
        )

    def send(self, ref, device, recv_sem):
        copy = remote(ref, ref, self.g_send.at[len(self.sends)], recv_sem, device)
        copy.start()
        self.sends.append(copy)

    def arrived(self, ref, recv_sem):
        remote(ref, ref, self.g_send.at[0], recv_sem, self.partner()).wait_recv()

    def partner(self):
        return self.z * 2 + 1 - self.core, self.col

    def neighbour(self, step):
        return z_device(self.z, step, self.core, self.col)

    def begin(self, p):
        own = self.ref(0, p)
        self.send(own, self.neighbour(1), self.minus.at[p])
        self.send(own, self.neighbour(3), self.plus.at[p])
        self.send(own, self.partner(), self.pair.at[0, p])

    def pass_on(self, p):
        self.arrived(self.ref(3, p), self.minus.at[p])
        self.send(self.ref(3, p, 0), self.neighbour(1), self.far.at[0, p])
        self.arrived(self.ref(1, p), self.plus.at[p])
        self.send(self.ref(1, p, 1), self.neighbour(3), self.far.at[1, p])
        self.send(self.ref(3, p), self.partner(), self.pair.at[3, p])
        self.send(self.ref(1, p), self.partner(), self.pair.at[1, p])

    def finish(self, p):
        for h in range(2):
            half = self.ref(2, p, h)
            self.arrived(half, self.far.at[h, p])
            self.send(half, self.partner(), self.pair.at[2 + 2 * h, p])

    def close(self, pieces):
        other = 1 - self.core
        for p in range(pieces):
            for step in (0, 1, 3):
                self.arrived(self.ref(step, p, None, other), self.pair.at[step, p])
            for h in range(2):
                self.arrived(self.ref(2, p, h, other), self.pair.at[2 + 2 * h, p])
        for copy in self.sends:
            copy.wait_send()


def gather_sems(pieces):
    return [
        pltpu.SemaphoreType.DMA((9 * pieces,)),
        pltpu.SemaphoreType.DMA((pieces,)),
        pltpu.SemaphoreType.DMA((pieces,)),
        pltpu.SemaphoreType.DMA((2, pieces)),
        pltpu.SemaphoreType.DMA((5, pieces)),
    ]


class Parts:
    def __init__(self, where):
        self.row, self.col, self.z, self.core = where
        self.mine = lax.div(self.col, 2)
        self.first = jnp.where(self.core == lax.rem(self.col, 2), 1, 0)

    def slot(self, i):
        return lax.rem(self.mine + i, PARTS)

    def device_at(self, m):
        return self.z * 2 + lax.rem(self.col, 2), m * 2 + self.core

    def device(self, i):
        return self.device_at(self.slot(i))

    def own(self, m):
        return m * 2 + self.core == self.col


CELLS = COL_BLOCKS * BLK


def cells_of(body, block):
    return jnp.concatenate([body[2 * block], body[2 * block + 1]], axis=0)


def tabulate(neighbors, weights, tables, first_cell):
    def tile(t, carry):
        at = pl.ds(pl.multiple_of(t * BLK, BLK), BLK)
        near = (neighbors[:, at] - (first_cell + t * BLK - RIM)).astype(F32)
        tables[t] = jnp.concatenate([near, weights[:, at]], axis=0)
        return carry

    lax.fori_loop(0, COL_BLOCKS, tile, 0, unroll=4)


def window_of(body, rims, tile):
    last = COL_BLOCKS - 1
    low = jnp.where(tile == 0, rims[0], body[jnp.maximum(2 * tile - 1, 0)])
    high = jnp.where(tile == last, rims[1], body[jnp.minimum(2 * tile + 2, 2 * last)])
    return jnp.concatenate([low, cells_of(body, tile), high], axis=0)


def smooth_tile(window, table):
    table = table.T
    span = lax.broadcasted_iota(jnp.int32, (BLK, 2 * BLK), 1).astype(F32)
    mix = jnp.zeros((BLK, 2 * BLK), F32)
    for face in range(4):
        mix += jnp.where(table[:, face : face + 1] == span, table[:, 4 + face : 5 + face], 0.0)
    mix_high, mix_low = split(mix)
    center = window[RIM : RIM + BLK]
    near_high, near_low = split(window)
    mixed = dot(mix_high, near_high) + dot(mix_low, near_high) + dot(mix_high, near_low)
    total = table[:, 4:5] + table[:, 5:6] + table[:, 6:7] + table[:, 7:8]
    return total * center - mixed


RING_BLOCKS = COL_BLOCKS // 2


def ring_place(z, core, part):
    return (z * 2 + core) * GROUP + part


def plane_place(core, part):
    return RING_BLOCKS + (core * PARTS + part) * 2


def analyse_kernel(
    order,
    model,
    wavelet,
    windows,
    body,
    rims,
    ring_stage,
    plane_stage,
    sems,
    ring_send,
    ring_recv,
    plane_send,
    plane_recv,
    plane_pair,
    *sem_refs,
):
    where = place()
    row, col, z, core = where
    fill = pltpu.make_async_copy(model, body, sems.at[4])
    fill.start()
    parts = Parts(where)
    mine, lane = parts.mine, lax.div(z, 2)

    def ring_piece(at, k, p, h):
        first = ring_place(at, k, p * 2)
        return wavelet.at[pl.ds(first, 2) if h is None else pl.ds(first + h, 1)]

    gather = RowGather(ring_piece, sem_refs, where)
    below, above = (row, lax.rem(col + NCOLS - 1, NCOLS)), (row, lax.rem(col + 1, NCOLS))
    wait_for_all = greet(
        [gather.neighbour(1), gather.neighbour(3), gather.partner(), below, above],
        (parts.first, parts.device),
    )
    up = remote(
        model.at[2 * COL_BLOCKS - 1],
        rims.at[0],
        sems.at[0],
        sems.at[2],
        above,
    )
    down = remote(
        model.at[0],
        rims.at[1],
        sems.at[1],
        sems.at[3],
        below,
    )
    signs, scale = haar_tiles()
    sign_pair = jnp.concatenate([signs, signs], axis=1)
    fill.wait()

    def block_of(m, q):
        return order[0, (m * 2 + core) * 4 + q]

    def coefficients(m, q):
        high, low = split(cells_of(body, block_of(m, q)))
        product = dot(sign_pair, jnp.concatenate([high, low], axis=0))
        return (product * scale).astype(BF16)

    def ring_part(i):
        return i * 2 + lax.rem(lane + mine, 2)

    def make_ring(i, carry):
        ring_stage[i] = coefficients(ring_part(i), 2 + lax.rem(z, 2))
        return carry

    lax.fori_loop(0, GROUP, make_ring, 0)
    wait_for_all()

    def ring_copy(i):
        return remote(
            ring_stage.at[i],
            wavelet.at[ring_place(z, lax.rem(col, 2), lax.div(mine, 2))],
            ring_send.at[i],
            ring_recv.at[lax.div(mine, 2)],
            parts.device_at(ring_part(i)),
        )

    def spread_ring(i, carry):
        @pl.when(parts.own(ring_part(i)))
        def _():
            wavelet[ring_place(z, core, lax.div(mine, 2))] = ring_stage[i]

        @pl.when(jnp.logical_not(parts.own(ring_part(i))))
        def _():
            ring_copy(i).start()

        return carry

    lax.fori_loop(0, GROUP, spread_ring, 0)
    up.start()
    down.start()

    def plane_copy(i):
        return remote(
            plane_stage.at[i],
            wavelet.at[pl.ds(plane_place(lax.rem(col, 2), mine), 2)],
            plane_send.at[i],
            plane_recv.at[mine],
            parts.device(i),
        )

    def spread_plane(i, carry):
        for q in range(2):
            plane_stage[i, q] = coefficients(parts.slot(i), q)
        plane_copy(i).start()
        return carry

    lax.fori_loop(parts.first, PARTS, spread_plane, 0)

    @pl.when(parts.first == 1)
    def _():
        for q in range(2):
            wavelet[plane_place(core, mine) + q] = coefficients(mine, q)

    def wait_ring(i, carry):
        @pl.when(jnp.logical_not(parts.own(ring_part(i))))
        def _():
            ref = wavelet.at[ring_place(z, core, i)]
            remote(ref, ref, ring_send.at[0], ring_recv.at[i], gather.partner()).wait_recv()

        return carry

    def wait_plane(m, carry):
        @pl.when(jnp.logical_not(parts.own(m)))
        def _():
            ref = wavelet.at[pl.ds(plane_place(core, m), 2)]
            remote(ref, ref, plane_send.at[0], plane_recv.at[m], gather.partner()).wait_recv()

        return carry

    def half_plane(core_of, h):
        return wavelet.at[pl.ds(plane_place(core_of, h * GROUP), PARTS)]

    def swap(h):
        ref = half_plane(core, h)
        return remote(ref, ref, plane_pair.at[h], plane_pair.at[2 + h], gather.partner())

    for p in range(2):
        lax.fori_loop(2 * p, 2 * p + 2, wait_ring, 0)
        gather.begin(p)
    up.wait_recv()
    down.wait_recv()

    def keep_window(m, carry):
        windows[m] = window_of(body, rims, block_of(m, z))
        return carry

    lax.fori_loop(0, PARTS, keep_window, 0)
    for p in range(2):
        gather.pass_on(p)
    for h in range(2):
        lax.fori_loop(h * GROUP, (h + 1) * GROUP, wait_plane, 0)
        swap(h).start()
    for p in range(2):
        gather.finish(p)
    gather.close(2)
    for h in range(2):
        ref = half_plane(1 - core, h)
        remote(ref, ref, plane_pair.at[h], plane_pair.at[2 + h], gather.partner()).wait_recv()
        swap(h).wait_send()

    def drain_ring(i, carry):
        @pl.when(jnp.logical_not(parts.own(ring_part(i))))
        def _():
            ring_copy(i).wait_send()

        return carry

    def drain_plane(i, carry):
        plane_copy(i).wait_send()
        return carry

    lax.fori_loop(0, GROUP, drain_ring, 0)
    lax.fori_loop(parts.first, PARTS, drain_plane, 0)
    up.wait_send()
    down.wait_send()


def analyse(order, model):
    return pl.pallas_call(
        analyse_kernel,
        out_shape=(
            jax.ShapeDtypeStruct((COL_BLOCKS, BLK, BLK), BF16),
            jax.ShapeDtypeStruct((PARTS, 2 * BLK, BLK), F32),
        ),
        in_specs=[SMEM, ANY],
        out_specs=(VMEM, VMEM),
        scratch_shapes=[
            pltpu.VMEM((2 * COL_BLOCKS, RIM, BLK), F32),
            pltpu.VMEM((2, RIM, BLK), F32),
            pltpu.VMEM((GROUP, BLK, BLK), BF16),
            pltpu.VMEM((PARTS, 2, BLK, BLK), BF16),
            pltpu.SemaphoreType.DMA((5,)),
            pltpu.SemaphoreType.DMA((GROUP,)),
            pltpu.SemaphoreType.DMA((GROUP,)),
            pltpu.SemaphoreType.DMA((PARTS,)),
            pltpu.SemaphoreType.DMA((PARTS,)),
            pltpu.SemaphoreType.DMA((4,)),
            *gather_sems(2),
        ],
        compiler_params=pltpu.CompilerParams(
            collective_id=0, has_side_effects=True, vmem_limit_bytes=VMEM_LIMIT
        ),
        cost_estimate=cost(1 << 30, 60 << 20),
        name="analyse",
    )(order, model)


class Sensors:
    def __init__(self, count, source, held, sems):
        self.live, self.source, self.held, self.sems = count[0, 0], source, held, sems

    def copy(self, g):
        part = pl.ds(g * CHUNK, CHUNK)
        return pltpu.make_async_copy(self.source.at[0, part], self.held.at[part], self.sems.at[g])

    def start(self):
        def begin(g, carry):
            self.copy(g).start()
            return carry

        lax.fori_loop(0, pl.cdiv(self.live, CHUNK), begin, 0)

    def run(self, add):
        full = self.live // CHUNK

        def group(g, carry):
            self.copy(g).wait()
            add(g * CHUNK, CHUNK)
            return carry

        lax.fori_loop(0, full, group, 0)
        done = full * CHUNK

        @pl.when(done < self.live)
        def _():
            self.copy(full).wait()

        for width in (4, 1):

            def few(g, carry, width=width, done=done):
                add(done + g * width, width)
                return carry

            groups = (self.live - done) // width
            lax.fori_loop(0, groups, few, 0)
            done = done + groups * width


def forward_kernel(count, rows, cols, source, wavelet, image, held, places, sems):
    sensors = Sensors(count, source, held, sems)
    sensors.start()
    image[...] = jnp.zeros_like(image)
    mine = lax.axis_index("cols") >> 1

    def note(at, carry):
        q, core, part = at & 3, (at >> 2) & 1, at >> 3
        by_ring = ring_place(2 * ((part + mine) & 1) + (q & 1), core, part >> 1)
        places[at] = jnp.where(q >= 2, by_ring, plane_place(core, part) + q)
        return carry

    lax.fori_loop(0, COL_BLOCKS, note, 0)

    def add(first, width):
        terms = []
        for u in range(width):
            terms.append(dot(held[first + u], wavelet[places[cols[0, first + u]]]))
        for u in range(width):
            image[rows[0, first + u]] += terms[u]

    sensors.run(add)


SENSOR_SCRATCH = (
    pltpu.VMEM((SLOTS, BLK, BLK), BF16),
    pltpu.SemaphoreType.DMA((SLOTS // CHUNK,)),
)


def forward(count, rows, cols, sens, wavelet):
    held, sems = SENSOR_SCRATCH
    return pl.pallas_call(
        forward_kernel,
        out_shape=jax.ShapeDtypeStruct((ROW_BLOCKS, BLK, BLK), F32),
        in_specs=[SMEM, SMEM, SMEM, ANY, VMEM],
        out_specs=VMEM,
        scratch_shapes=[
            held,
            pltpu.SMEM((COL_BLOCKS,), jnp.int32),
            sems,
        ],
        compiler_params=pltpu.CompilerParams(vmem_limit_bytes=MIDDLE_LIMIT),
        name="forward",
    )(count, rows, cols, sens, wavelet)


class Ring:
    def __init__(self, me, plus, minus, send, recv, far=None):
        self.me, self.plus, self.minus = me, plus, minus
        self.others = ((2, far), (1, plus), (3, minus))
        self.send, self.recv = send, recv
        self.started = []

    def at(self, step):
        return lax.rem(self.me + step, 4)

    def copy(self, src, dst, device, slot):
        copy = remote(src, dst, self.send.at[slot], self.recv.at[slot], device)
        copy.start()
        self.started.append(copy)

    def arrived(self, ref, slot):
        remote(ref, ref, self.send.at[slot], self.recv.at[slot], self.plus).wait_recv()

    def drain(self):
        for copy in self.started:
            copy.wait_send()
        self.started = []


class Reduce:
    def __init__(self, ring, source, data, base, chunk, relay, landed):
        self.ring, self.source, self.data = ring, source, data
        self.base, self.chunk = base, chunk
        self.half = chunk // 2
        self.relay, self.landed = relay, landed

    def rows(self, step, h):
        start = self.base + self.ring.at(step) * self.chunk + h * self.half
        return pl.ds(pl.multiple_of(start, self.half), self.half)

    def relay_at(self, side):
        return self.relay.at[side, pl.ds(0, self.half)]

    def landed_at(self, side, h):
        return self.landed.at[side, pl.ds(h * self.half, self.half)]

    def begin(self):
        ring, source = self.ring, self.source
        ring.copy(source.at[self.rows(2, 0)], self.relay_at(0), ring.plus, 0)
        ring.copy(source.at[self.rows(2, 1)], self.relay_at(1), ring.minus, 1)
        ring.copy(source.at[self.rows(1, 1)], self.landed_at(0, 1), ring.plus, 2)
        ring.copy(source.at[self.rows(3, 0)], self.landed_at(1, 0), ring.minus, 3)

    def pass_on(self):
        ring, source, data = self.ring, self.source, self.data
        ring.arrived(self.relay_at(0), 0)
        data[self.rows(1, 0), :] = source[self.rows(1, 0), :] + self.relay[0, : self.half]
        ring.copy(data.at[self.rows(1, 0)], self.landed_at(0, 0), ring.plus, 4)
        ring.arrived(self.relay_at(1), 1)
        data[self.rows(3, 1), :] = source[self.rows(3, 1), :] + self.relay[1, : self.half]
        ring.copy(data.at[self.rows(3, 1)], self.landed_at(1, 1), ring.minus, 5)

    def finish(self):
        ring, source, data = self.ring, self.source, self.data
        ring.arrived(self.landed_at(0, 1), 2)
        ring.arrived(self.landed_at(1, 0), 3)
        ring.arrived(self.landed_at(0, 0), 4)
        ring.arrived(self.landed_at(1, 1), 5)
        for h in range(2):
            part = pl.ds(h * self.half, self.half)
            landed = self.landed[0, part, :] + self.landed[1, part, :]
            data[self.rows(0, h), :] = source[self.rows(0, h), :] + landed


class DirectReduce:
    def __init__(self, ring, data, base, chunk, landed):
        self.ring, self.data, self.base, self.chunk = ring, data, base, chunk
        self.landed = landed

    def rows(self, step):
        start = self.base + self.ring.at(step) * self.chunk
        return pl.ds(pl.multiple_of(start, self.chunk), self.chunk)

    def begin(self):
        for step, device in self.ring.others:
            self.ring.copy(
                self.data.at[self.rows(step)], self.landed.at[step - 1], device, step - 1
            )

    def pass_on(self):
        for step in range(3):
            self.ring.arrived(self.landed.at[step], step)

    def finish(self):
        own = self.rows(0)
        total = self.data[own, :] + self.landed[0]
        self.data[own, :] = total + (self.landed[1] + self.landed[2])


class DirectGather:
    def __init__(self, ring, data, base, chunk):
        self.ring, self.data, self.base, self.chunk = ring, data, base, chunk

    def rows(self, step):
        start = self.base + self.ring.at(step) * self.chunk
        return self.data.at[pl.ds(pl.multiple_of(start, self.chunk), self.chunk)]

    def begin(self):
        for step, device in self.ring.others:
            self.ring.copy(self.rows(0), self.rows(0), device, step - 1)

    def pass_on(self):
        pass

    def finish(self):
        for step in (1, 3, 2):
            self.ring.arrived(self.rows(4 - step), step - 1)


STREAMS = 2
STREAM = ROW_BLOCKS * BLK // STREAMS
BIG = STREAM // 4
SMALL = BIG // 4


def combine_kernel(source, image, partial, big_relay, big_landed, small_landed, send, recv):
    row, col, _, _ = place()
    y, x = lax.div(col, 4), lax.rem(col, 4)
    x_ring = [(row, y * 4 + lax.rem(x + step, 4)) for step in range(4)]
    y_ring = [(row, lax.rem(y + step, 4) * 4 + x) for step in range(4)]
    greet(x_ring[1:] + y_ring[1:])()

    def ring(axis, slot):
        me, devices = ((x, x_ring), (y, y_ring))[axis]
        return Ring(me, devices[1], devices[3], send.at[slot], recv.at[slot], devices[2])

    streams = range(STREAMS)
    axis = [a % 2 for a in streams]
    bases = [a * STREAM for a in streams]
    inner = [bases[a] + (x, y)[axis[a]] * BIG for a in streams]
    wide_rings = [ring(axis[a], a) for a in streams]
    cross_rings = [ring(1 - axis[a], STREAMS + a) for a in streams]
    back_rings = [ring(1 - axis[a], 2 * STREAMS + a) for a in streams]
    last_rings = [ring(axis[a], 3 * STREAMS + a) for a in streams]
    wide = [
        Reduce(wide_rings[a], source, partial, bases[a], BIG, big_relay.at[a], big_landed.at[a])
        for a in streams
    ]
    cross = [DirectReduce(cross_rings[a], partial, inner[a], SMALL, small_landed.at[a]) for a in streams]
    back = [DirectGather(back_rings[a], image, inner[a], SMALL) for a in streams]
    last = [DirectGather(last_rings[a], image, bases[a], BIG) for a in streams]

    def cast(a):
        start = inner[a] + (y, x)[axis[a]] * SMALL
        own = pl.ds(pl.multiple_of(start, SMALL), SMALL)
        image[own, :] = partial[own, :].astype(BF16)

    pairs = [(a, a + 1) for a in range(0, STREAMS, 2)]
    for a in streams:
        wide[a].begin()
    for a in streams:
        wide[a].pass_on()
    for pair in pairs:
        for a in pair:
            wide[a].finish()
            cross[a].begin()
    for pair in pairs:
        for a in pair:
            cross[a].pass_on()
            cross[a].finish()
            cast(a)
            back[a].begin()
    for pair in pairs:
        for a in pair:
            back[a].finish()
            last[a].begin()
    for a in streams:
        last[a].finish()
    for group in (wide_rings, cross_rings, back_rings, last_rings):
        for one in group:
            one.drain()


def combine(partial):
    vmem = pl.BlockSpec(memory_space=pltpu.VMEM)
    rows = ROW_BLOCKS * BLK

    return pl.pallas_call(
        combine_kernel,
        out_shape=jax.ShapeDtypeStruct((rows, BLK), BF16),
        in_specs=[vmem],
        out_specs=vmem,
        scratch_shapes=[
            pltpu.VMEM((rows, BLK), F32),
            pltpu.VMEM((STREAMS, 2, BIG // 2, BLK), F32),
            pltpu.VMEM((STREAMS, 2, BIG, BLK), F32),
            pltpu.VMEM((STREAMS, 3, SMALL, BLK), F32),
            pltpu.SemaphoreType.DMA((4 * STREAMS, 6)),
            pltpu.SemaphoreType.DMA((4 * STREAMS, 6)),
        ],
        compiler_params=pltpu.CompilerParams(
            collective_id=1, has_side_effects=True, vmem_limit_bytes=MIDDLE_LIMIT
        ),
        cost_estimate=cost(1 << 20, 80 << 20),
        name="combine",
    )(partial.reshape(rows, BLK))


def adjoint_kernel(
    count, rows, cols, source, image, data_image, adjoint, held, flipped, plain, sem, sems
):
    sensors = Sensors(count, source, held, sems)
    sensors.start()
    adjoint[...] = jnp.zeros_like(adjoint)

    def flip(b, carry):
        block = image[b].astype(F32)
        plain[b] = block
        flipped[b] = block.T.astype(BF16)
        return carry

    lax.fori_loop(0, ROW_BLOCKS, flip, 0, unroll=2)
    store = pltpu.make_async_copy(plain, data_image, sem)
    store.start()
    shift = lax.axis_index("cols") >> 1

    def add(first, width):
        terms = []
        for u in range(width):
            terms.append(dot(flipped[rows[0, first + u]], held[first + u]))
        for u in range(width):
            at = cols[0, first + u]
            part = at >> 3
            adjoint[(at >> 2) & 1, at & 3, (part + shift) & (LANES - 1), part >> (LANES // 2)] += terms[u]

    sensors.run(add)
    store.wait()


def adjoin(count, rows, cols, sens, image):
    held, sems = SENSOR_SCRATCH
    return pl.pallas_call(
        adjoint_kernel,
        out_shape=(
            jax.ShapeDtypeStruct((ROW_BLOCKS, BLK, BLK), F32),
            jax.ShapeDtypeStruct((2, NZ, LANES, EACH, BLK, BLK), F32),
        ),
        in_specs=[SMEM, SMEM, SMEM, ANY, VMEM],
        out_specs=(ANY, VMEM),
        scratch_shapes=[
            held,
            pltpu.VMEM((ROW_BLOCKS, BLK, BLK), BF16),
            pltpu.VMEM((ROW_BLOCKS, BLK, BLK), F32),
            pltpu.SemaphoreType.DMA,
            sems,
        ],
        compiler_params=pltpu.CompilerParams(vmem_limit_bytes=ADJOIN_LIMIT),
        name="adjoin",
    )(count, rows, cols, sens, image)


def return_kernel(
    order, partial, windows, neighbors, weights, scale, signs, out, tables, stage, pair, relay_out, relay, landed, gathered, send, recv, part_send, part_recv, *sem_refs
):
    where = place()
    row, col, z, core = where
    parts = Parts(where)
    mine = parts.mine

    def out_piece(at, k, p, h):
        first = p * EACH
        return out.at[at, k, pl.ds(first, EACH) if h is None else pl.ds(first + h * PAIR, PAIR)]

    gather = RowGather(out_piece, sem_refs, where)
    plus, minus, partner = gather.neighbour(1), gather.neighbour(3), gather.partner()
    greet([plus, minus, partner], (parts.first, parts.device))()
    rings = [Ring(z, plus, minus, send.at[p], recv.at[p]) for p in range(LANES)]
    for p in range(LANES):
        ring = rings[p]
        for slot, step in ((6, 2), (7, 1), (8, 3), (9, 0)):
            q = ring.at(step)
            ring.copy(partial.at[1 - core, q, p], pair.at[q, p], partner, slot)

    def total(p, step, h):
        q = rings[p].at(step)
        part = pl.ds(h * PAIR, PAIR)
        return partial[core, q, p, part] + pair[q, p, part]

    def paired(p, step, slot):
        rings[p].arrived(pair.at[rings[p].at(step), p], slot)

    def ship(p, value, slot, dst, device, sem):
        relay_out[p, slot] = value.astype(BF16)
        rings[p].copy(relay_out.at[p, slot], dst, device, sem)

    def launch(p):
        paired(p, 2, 6)
        ship(p, total(p, 2, 0), 0, relay.at[p, 0], plus, 0)
        ship(p, total(p, 2, 1), 1, relay.at[p, 1], minus, 1)
        paired(p, 1, 7)
        ship(p, total(p, 1, 1), 3, landed.at[p, 0, 1], plus, 2)
        paired(p, 3, 8)
        ship(p, total(p, 3, 0), 4, landed.at[p, 1, 0], minus, 3)

    def pass_on(p):
        ring = rings[p]
        ring.arrived(relay.at[p, 0], 0)
        ship(p, total(p, 1, 0) + relay[p, 0].astype(F32), 2, landed.at[p, 0, 0], plus, 4)
        ring.arrived(relay.at[p, 1], 1)
        ship(p, total(p, 3, 1) + relay[p, 1].astype(F32), 5, landed.at[p, 1, 1], minus, 5)

    lane_scale = scale[0:1, :]

    def member(p, i):
        return i * LANES + lax.rem(p + PARTS - mine, LANES)

    def part_copy(m):
        return remote(
            stage.at[m], gathered.at[mine], part_send.at[m], part_recv.at[mine], parts.device_at(m)
        )

    def hand_over(p):
        ring = rings[p]
        paired(p, 0, 9)
        for slot, (side, h) in ((2, (0, 1)), (3, (1, 0)), (4, (0, 0)), (5, (1, 1))):
            ring.arrived(landed.at[p, side, h], slot)
        for i in range(EACH):
            m, h, j = member(p, i), i // PAIR, i % PAIR
            landed_sum = landed[p, 0, h, j].astype(F32) + landed[p, 1, h, j].astype(F32)
            value = partial[core, z, p, i] + pair[z, p, i] + landed_sum
            stage[m] = (value * lane_scale).astype(BF16)

            @pl.when(parts.own(m))
            def _(m=m):
                gathered[m] = stage[m]

            @pl.when(jnp.logical_not(parts.own(m)))
            def _(m=m):
                part_copy(m).start()

    def synthesise(p):
        members = [member(p, h) for h in range(EACH)]
        smooth = [
            smooth_tile(windows[m], tables[order[0, (m * 2 + core) * 4 + z]]) for m in members
        ]
        for m in members:

            @pl.when(jnp.logical_not(parts.own(m)))
            def _(m=m):
                ref = gathered.at[m]
                remote(ref, ref, part_send.at[0], part_recv.at[m], partner).wait_recv()

        for h, m in enumerate(members):
            cells = lax.dot_general(
                signs[...], gathered[m], (((1,), (1,)), ((), ())), preferred_element_type=F32
            )
            out[z, core, p * EACH + h] = (cells + smooth[h]).astype(BF16)
        gather.begin(p)

    for p in range(LANES):
        launch(p)
    for p in range(LANES):
        pass_on(p)
    for p in range(LANES):
        hand_over(p)
    tabulate(neighbors, weights, tables, col * CELLS)
    for p in range(LANES):
        synthesise(p)
    for p in range(LANES):
        gather.pass_on(p)
    for p in range(LANES):
        gather.finish(p)
    gather.close(LANES)

    def drain(m, carry):
        @pl.when(jnp.logical_not(parts.own(m)))
        def _():
            part_copy(m).wait_send()

        return carry

    lax.fori_loop(0, PARTS, drain, 0)
    for ring in rings:
        ring.drain()


def give_back(order, partial, windows, neighbors, weights):
    return pl.pallas_call(
        return_kernel,
        out_shape=jax.ShapeDtypeStruct((NZ, 2, PARTS, BLK, BLK), BF16),
        in_specs=[SMEM, *[VMEM] * 6],
        out_specs=VMEM,
        scratch_shapes=[
            pltpu.VMEM((COL_BLOCKS, 8, BLK), F32),
            pltpu.VMEM((PARTS, BLK, BLK), BF16),
            pltpu.VMEM((NZ, LANES, EACH, BLK, BLK), F32),
            pltpu.VMEM((LANES, 6, PAIR, BLK, BLK), BF16),
            pltpu.VMEM((LANES, 2, PAIR, BLK, BLK), BF16),
            pltpu.VMEM((LANES, 2, 2, PAIR, BLK, BLK), BF16),
            pltpu.VMEM((PARTS, BLK, BLK), BF16),
            pltpu.SemaphoreType.DMA((LANES, 10)),
            pltpu.SemaphoreType.DMA((LANES, 10)),
            pltpu.SemaphoreType.DMA((PARTS,)),
            pltpu.SemaphoreType.DMA((PARTS,)),
            *gather_sems(LANES),
        ],
        compiler_params=pltpu.CompilerParams(
            collective_id=2, has_side_effects=True, vmem_limit_bytes=LATE_LIMIT
        ),
        cost_estimate=cost(1 << 30, 80 << 20),
        name="give_back",
    )(
        order,
        partial,
        windows,
        neighbors,
        weights,
        jnp.asarray(np.broadcast_to(SCALE[None, :], (8, BLK)), F32),
        jnp.asarray(SIGNS.T, BF16),
    )


def place_kernel(order, product, out, cells, out_sems):
    def store(i, block):
        return pltpu.make_async_copy(cells.at[i], out.at[block], out_sems.at[i])

    shift = lax.axis_index("cols") >> 1
    for i in range(2 * NZ):
        for n in range(PARTS):
            q, core, p = i // 2, i % 2, n // EACH
            at = i * PARTS + n
            cells[at] = product[q, core, n].astype(F32)
            m = (n % EACH) * LANES + ((p + PARTS - shift) & (LANES - 1))
            store(at, order[0, (m * 2 + core) * 4 + q]).start()

    def finish(i, carry):
        store(i, 0).wait()
        return carry

    lax.fori_loop(0, COL_BLOCKS, finish, 0)


def place_cells(order, product):
    return pl.pallas_call(
        place_kernel,
        out_shape=jax.ShapeDtypeStruct((COL_BLOCKS, BLK, BLK), F32),
        in_specs=[SMEM, VMEM],
        out_specs=ANY,
        scratch_shapes=[
            pltpu.VMEM((COL_BLOCKS, BLK, BLK), F32),
            pltpu.SemaphoreType.DMA((COL_BLOCKS,)),
        ],
        compiler_params=pltpu.CompilerParams(vmem_limit_bytes=MIDDLE_LIMIT),
        name="place_cells",
    )(order, product)


def local(model_dir, sens_blocks, blk_row, blk_col, blk_count, send_order, neighbors, face_weight):
    model = model_dir.reshape(2 * COL_BLOCKS, RIM, BLK)
    wavelet, windows = analyse(send_order, model)
    partial_image = forward(blk_count, blk_row, blk_col, sens_blocks, wavelet)
    image_half = combine(partial_image).reshape(ROW_BLOCKS, BLK, BLK)
    data_image, partial_adjoint = adjoin(blk_count, blk_row, blk_col, sens_blocks, image_half)
    product = give_back(send_order, partial_adjoint, windows, neighbors, face_weight)
    normal_product = place_cells(send_order, product)
    return data_image.reshape(ROW_BLOCKS * BLK, BLK), normal_product.reshape(CELLS, BLK)


def solution(mesh):
    placed = (
        P("cols", None),
        P("rows", "cols", None, None),
        P("rows", "cols"),
        P("rows", "cols"),
        P("rows", "cols"),
        P("cols", None),
        P(None, "cols"),
        P(None, "cols"),
    )
    return jax.shard_map(
        local,
        mesh=mesh,
        in_specs=placed,
        out_specs=(P("rows", None), P("cols", None)),
        check_vma=False,
    )
```
